32 devices in a mesh: ctx: 8 (over y, x, core), fsdp: 4 (over z).
Axes of the slice: x: 2, y: 2, z: 4, core: 2. Of those that a mesh axis runs over, the one named last changes fastest.
Arguments:
- tokens: bfloat16 [4, 2560, 768], P('fsdp', 'ctx'), may hold values from -6 to 6
- w_query: float32 [768, 768], P('fsdp'), may hold values from -0.21875 to 0.21875
- w_key: float32 [768, 768], P('fsdp'), may hold values from -0.21875 to 0.21875
- w_value: float32 [768, 768], P('fsdp'), may hold values from -0.21875 to 0.21875
- w_output: float32 [768, 768], P('fsdp'), may hold values from -4 to 4
- w_inner: float32 [768, 3072], P('fsdp'), may hold values from -0.21875 to 0.21875
- w_outer: float32 [3072, 768], P('fsdp'), may hold values from -0.109375 to 0.109375
- ln_gain: float32 [768, 2], P('fsdp'), may hold values from 0.5 to 1.5
- ln_bias: float32 [768, 2], P('fsdp'), may hold values from -1 to 1
- pairing: int32 [4, 12], P('fsdp'), may hold values from 0 to 1
- block_pairs: int32 [4, 8], P('fsdp'), may hold values from 0 to 7, each once within a row
- cotangent: bfloat16 [4, 2560, 768], P('fsdp', 'ctx'), may hold values from -6 to 6
Outputs:
- output: bfloat16 [4, 2560, 768], P('fsdp', 'ctx')
- d_tokens: bfloat16 [4, 2560, 768], P('fsdp', 'ctx')
- d_w_query: float32 [768, 768], P('fsdp')
- d_w_key: float32 [768, 768], P('fsdp')
- d_w_value: float32 [768, 768], P('fsdp')
- d_w_output: float32 [768, 768], P('fsdp')
- d_w_inner: float32 [768, 3072], P('fsdp')
- d_w_outer: float32 [3072, 768], P('fsdp')
- d_ln_gain: float32 [768, 2], P('fsdp')
- d_ln_bias: float32 [768, 2], P('fsdp')
The draws below stay inside these ranges and needn't reach their ends.
Inputs may be any that keep to these rules, and one draw needn't show every extreme that they name: `pairing`: 0 pairs each half of a sequence with itself for that head, 1 pairs the second half with the first. Each row is a permutation; index c of ctx holds lower segment block_pairs[n, c] and upper segment 2 * 8 - 1 - block_pairs[n, c] of sequence n.
All inputs are finite; a program needn't handle non-finite values.
Results may differ from the reference program's by a relative error of at most 0.023.
Values may be sent and summed in bfloat16 or wider, within the bound.
A program may use at most 192 MiB of HBM per device.

```python
import jax
import jax.numpy as jnp
from jax import lax

D = 768
H = 12
HD = 64
FF = 3072
TOK_DEV = 320
SEQLEN = 2560
SEQS = 4
SEG_LEN = 160
N_CTX = 8


def place_ends(entries, stream_key, low, top_value):
    spot = [jax.random.randint(jax.random.fold_in(stream_key, axis), (), 0, length) for axis, length in enumerate(entries.shape)]
    longest = entries.shape.index(max(entries.shape))
    beside = spot[:longest] + [(spot[longest] + 1) % entries.shape[longest]] + spot[longest + 1:]
    return entries.at[tuple(spot)].set(low).at[tuple(beside)].set(top_value)


def level_of(rng, shape, split, least, largest):
    def one(dim, parts):
        steps = jax.random.uniform(jax.random.fold_in(jax.random.fold_in(rng, 6), dim), (parts,), jnp.float32, least / len(split), largest / len(split))
        return jnp.repeat(jnp.exp(steps), shape[dim] // parts).reshape((-1,) + (1,) * (len(shape) - dim - 1))

    factor_of = one(*split[0])
    for cut in split[1:]:
        factor_of = factor_of * one(*cut)
    return factor_of


def scatter_about(own_key, extent, width, most, cuts=(), kind=jnp.bfloat16):
    gain = level_of(own_key, extent, cuts, -0.22, 0.18) if cuts else 1.0
    entries = jax.random.normal(own_key, extent, jnp.float32) * width * gain
    return jnp.minimum(jnp.maximum(entries, -most), most).astype(kind)


def setup_inputs(seed: int = 0) -> dict:
    arg_keys = jax.random.split(jax.random.key(seed), 13)
    tokens = scatter_about(arg_keys[0], (SEQS, SEQLEN, D), 1.0, 6.0, ((0, 4), (1, 8)))
    w_query = scatter_about(arg_keys[1], (D, D), D ** -0.5, 0.21875, ((0, 4),), jnp.float32)
    w_key = scatter_about(arg_keys[2], (D, D), D ** -0.5, 0.21875, ((0, 4),), jnp.float32)
    w_value = scatter_about(arg_keys[3], (D, D), D ** -0.5, 0.21875, ((0, 4),), jnp.float32)
    w_output = scatter_about(arg_keys[4], (D, D), (max(D * 8 // SEQLEN, 1)) ** -0.5, 4.0, ((0, 4),), jnp.float32)
    w_inner = scatter_about(arg_keys[5], (D, FF), D ** -0.5, 0.21875, ((0, 4),), jnp.float32)
    w_outer = scatter_about(arg_keys[6], (FF, D), FF ** -0.5, 0.109375, ((0, 4),), jnp.float32)
    ln_gain = jnp.clip(1.0 + 0.1 * jax.random.normal(arg_keys[7], (D, 2), jnp.float32), 0.5, 1.5)
    ln_bias = scatter_about(arg_keys[8], (D, 2), 0.2, 1.0, ((0, 4),), jnp.float32)
    pairing = place_ends(jax.random.randint(arg_keys[9], (SEQS, H), 0, 2), jax.random.fold_in(arg_keys[9], 1), 0, 1).astype(jnp.int32)
    block_pairs = jax.vmap(lambda own: jax.random.permutation(own, N_CTX))(jax.random.split(arg_keys[10], SEQS)).reshape((SEQS, N_CTX)).astype(jnp.int32)
    cotangent = scatter_about(arg_keys[11], (SEQS, SEQLEN, D), 1.0, 6.0, ((0, 4), (1, 8)))
    return dict(tokens=tokens, w_query=w_query, w_key=w_key, w_value=w_value, w_output=w_output, w_inner=w_inner, w_outer=w_outer, ln_gain=ln_gain, ln_bias=ln_bias, pairing=pairing, block_pairs=block_pairs, cotangent=cotangent)


norm_eps = 1e-05
score_scale = 0.125
very_low = -1e+30
high_prec = lax.Precision.HIGHEST

@jax.custom_vjp
def low(v):
    return lax.optimization_barrier(v.astype(jnp.bfloat16)).astype(jnp.float32)

@jax.custom_vjp
def low_back(v):
    return v

def low_keep(v):
    return (low(v), None)

def low_pass(kept, grad):
    return (grad,)

def back_keep(v):
    return (v, None)

def back_low(kept, grad):
    return (low(grad),)
low.defvjp(low_keep, low_pass)
low_back.defvjp(back_keep, back_low)

def layer_norm(values, norm_gain, norm_shift):
    center = values - lax.optimization_barrier(jnp.mean(values, axis=-1, keepdims=True))
    spread = lax.optimization_barrier(jnp.mean(center * center, axis=-1, keepdims=True))
    return center * lax.rsqrt(spread + norm_eps) * norm_gain + norm_shift

def matmul_high(left, right):
    return jnp.dot(left, right, precision=high_prec)

def seq_positions(pair_row):
    within = jnp.arange(TOK_DEV, dtype=jnp.int32)
    lower_pos = pair_row[:, None] * SEG_LEN + within[None, :]
    upper_pos = SEQLEN - (pair_row[:, None] + 1) * SEG_LEN + within[None, :] - SEG_LEN
    return jnp.where(within[None, :] < SEG_LEN, lower_pos, upper_pos).reshape(-1).astype(jnp.int32)

def pair_mask(query_pos, key_pos, head_flags, half_len):
    target = (query_pos[None, :] // half_len + head_flags[:, None]) % 2
    paired = key_pos[None, None, :] // half_len == target[:, :, None]
    causal = key_pos[None, :] <= query_pos[:, None]
    return jnp.logical_and(paired, causal[None, :, :])

def attend_sequence(q_one, k_one, v_one, head_flags, pair_row):
    pos_one = seq_positions(pair_row)
    half_len = SEQLEN // 2
    block_len = min(512, SEQLEN)

    def one_block(block_index):
        first_row = (block_index * block_len).astype(jnp.int32)
        q_block = lax.dynamic_slice_in_dim(q_one, first_row, block_len, 0)
        q_pos = lax.dynamic_slice_in_dim(pos_one, first_row, block_len, 0)
        allowed = pair_mask(q_pos, pos_one, head_flags, half_len)
        scores = low_back(jnp.einsum('qhd,khd->hqk', q_block, k_one, precision=high_prec)) * score_scale
        top_score = lax.optimization_barrier(jnp.max(jnp.where(allowed, scores, very_low), axis=2, keepdims=True))
        expos = jnp.where(allowed, jnp.exp(jnp.where(allowed, scores - top_score, 0.0)), 0.0)
        totals = lax.optimization_barrier(jnp.sum(expos, axis=2, keepdims=True))
        prob_rows = jnp.where(totals > 0, expos / jnp.where(totals > 0, totals, 1.0), 0.0)
        return jnp.einsum('hqk,khd->qhd', low(prob_rows), v_one, precision=high_prec)
    blocks = lax.map(jax.checkpoint(one_block), jnp.arange(SEQLEN // block_len, dtype=jnp.int32))
    return blocks.reshape(SEQLEN, H, HD)

def reference(tokens, w_query, w_key, w_value, w_output, w_inner, w_outer, ln_gain, ln_bias, pairing, block_pairs, cotangent):

    def forward(x_all, wq_in, wk_in, wv_in, wo_in, inner_in, outer_in, gain_in, shift_in):
        gains = low(gain_in)
        shifts = low(shift_in)
        flat = x_all.reshape(SEQS * SEQLEN, D)
        q_all = low_back(low(matmul_high(flat, low(wq_in))))
        k_all = low_back(low(matmul_high(flat, low(wk_in))))
        v_all = low_back(low(matmul_high(flat, low(wv_in))))

        def one_sequence(inputs):
            q_one, k_one, v_one, head_flags, pair_row = inputs
            return attend_sequence(q_one, k_one, v_one, head_flags, pair_row)
        attended = lax.map(one_sequence, (q_all.reshape(SEQS, SEQLEN, H, HD), k_all.reshape(SEQS, SEQLEN, H, HD), v_all.reshape(SEQS, SEQLEN, H, HD), pairing, block_pairs))
        attn_rows = low_back(low(attended.reshape(SEQS * SEQLEN, D)))
        branch = low_back(matmul_high(attn_rows, low(wo_in)))
        first_norm = layer_norm(flat + branch, gains[:, 0], shifts[:, 0])
        inner = low_back(matmul_high(low(first_norm), low(inner_in)))
        outer = low_back(matmul_high(low(jax.nn.gelu(inner, approximate=False)), low(outer_in)))
        result = layer_norm(first_norm + outer, gains[:, 1], shifts[:, 1])
        return result.reshape(SEQS, SEQLEN, D)
    output, pullback = jax.vjp(forward, tokens.astype(jnp.float32), w_query, w_key, w_value, w_output, w_inner, w_outer, ln_gain, ln_bias)
    grads = pullback(cotangent.astype(jnp.float32))
    return (output.astype(jnp.bfloat16), grads[0].astype(jnp.bfloat16), grads[1], grads[2], grads[3], grads[4], grads[5], grads[6], grads[7], grads[8])
```

```python
import functools

import jax
import jax.numpy as jnp
from jax import lax
from jax.experimental import pallas as pl
from jax.experimental.pallas import tpu as pltpu
from jax.sharding import PartitionSpec as P

norm_eps = 1e-05
score_scale = 0.125
very_low = -1e30


def shortened(value):

    def short(part):
        return part.astype(jnp.bfloat16) if part.dtype == jnp.float32 else part

    return jax.tree.map(short, value)


def layer_norm(values, norm_gain, norm_shift):
    center = values - jnp.mean(values, axis=-1, keepdims=True)
    spread = jnp.mean(center * center, axis=-1, keepdims=True)
    return center * lax.rsqrt(spread + norm_eps) * norm_gain + norm_shift


def exact_gelu(values):
    return jax.nn.gelu(values, approximate=False)


def project(rows_in, weight):
    return jnp.dot(rows_in, weight, preferred_element_type=jnp.float32)


def seq_positions(pair_row, tok_dev, seq_len):
    segment_len = tok_dev // 2
    within = jnp.arange(tok_dev, dtype=jnp.int32)
    lower_pos = pair_row[:, None] * segment_len + within[None, :]
    upper_pos = seq_len - (pair_row[:, None] + 1) * segment_len + within[None, :] - segment_len
    return jnp.where(within[None, :] < segment_len, lower_pos, upper_pos).reshape(-1)


def pair_mask(query_pos, key_pos, head_flags, half_len):
    target = (query_pos[None, :] // half_len + head_flags[:, None]) % 2
    paired = key_pos[None, None, :] // half_len == target[:, :, None]
    causal = key_pos[None, :] <= query_pos[:, None]
    return jnp.logical_and(paired, causal[None, :, :])


def block_rows(tok_dev):
    return 2 * tok_dev


def over_blocks(running, arrays, step_fn, tok_dev):
    row_count = arrays[0].shape[0]
    block_len = block_rows(tok_dev)

    def one_step(inner_carry, step_index):
        first_row = step_index * block_len
        sliced = tuple(
            (lax.dynamic_slice_in_dim(member, first_row, block_len, 0) for member in arrays)
        )
        return (step_fn(inner_carry, sliced, first_row), None)

    return lax.scan(one_step, running, jnp.arange(row_count // block_len, dtype=jnp.int32))[0]


def generic_body(
    tokens,
    w_query,
    w_key,
    w_value,
    w_output,
    w_inner,
    w_outer,
    ln_gain,
    ln_bias,
    pairing,
    block_pairs,
    cotangent,
):
    tok_dev = tokens.shape[1]
    width = tokens.shape[2]
    heads = pairing.shape[1]
    head_dim = width // heads
    n_ctx = lax.axis_size("ctx")
    seq_len = tok_dev * n_ctx
    half_len = seq_len // 2
    pos_all = seq_positions(block_pairs[0], tok_dev, seq_len)
    my_pos = lax.dynamic_slice_in_dim(pos_all, lax.axis_index("ctx") * tok_dev, tok_dev, 0)
    head_flags = pairing[0]
    masters = (w_query, w_key, w_value, w_output, w_inner, w_outer, ln_gain, ln_bias)
    low_masters = tuple((member.astype(jnp.bfloat16) for member in masters))
    gathered = jax.tree.map(
        lambda part, own: part.astype(own.dtype),
        lax.all_gather(shortened(low_masters), "fsdp", axis=0, tiled=True),
        low_masters,
    )
    wq_full, wk_full, wv_full, wo_full, inner_full, outer_full, gain_full, shift_full = gathered
    gain_wide = gain_full.astype(jnp.float32)
    shift_wide = shift_full.astype(jnp.float32)
    x_in = tokens[0]
    query_b = project(x_in, wq_full).astype(jnp.bfloat16)
    key_b = project(x_in, wk_full).astype(jnp.bfloat16)
    value_b = project(x_in, wv_full).astype(jnp.bfloat16)
    q_heads = query_b.reshape(tok_dev, heads, head_dim)

    def attend_step(running, sliced, offset):
        run_max, run_sum, run_acc = running
        key_block, value_block = sliced
        block_len = key_block.shape[0]
        key_pos = lax.dynamic_slice_in_dim(pos_all, offset, block_len, 0)
        allowed = pair_mask(my_pos, key_pos, head_flags, half_len)
        key_heads = key_block.reshape(block_len, heads, head_dim)
        value_heads = value_block.reshape(block_len, heads, head_dim)
        scores = (
            jnp.einsum("qhd,khd->hqk", q_heads, key_heads, preferred_element_type=jnp.float32)
            * score_scale
        )
        new_max = jnp.maximum(run_max, jnp.max(jnp.where(allowed, scores, very_low), axis=2))
        prob_rows = jnp.where(
            allowed, jnp.exp(jnp.where(allowed, scores - new_max[:, :, None], 0.0)), 0.0
        )
        decay = jnp.exp(run_max - new_max)
        new_sum = run_sum * decay + jnp.sum(prob_rows, axis=2)
        added = jnp.einsum(
            "hqk,khd->hqd",
            prob_rows.astype(jnp.bfloat16),
            value_heads,
            preferred_element_type=jnp.float32,
        )
        return (new_max, new_sum, run_acc * decay[:, :, None] + added)

    def pair_fold(step_fn, running, fetched):
        return over_blocks(running, fetched, step_fn, tok_dev)

    start_state = (
        jnp.full((heads, tok_dev), very_low, jnp.float32),
        jnp.zeros((heads, tok_dev), jnp.float32),
        jnp.zeros((heads, tok_dev, head_dim), jnp.float32),
    )
    run_max, run_sum, run_acc = pair_fold(
        attend_step,
        start_state,
        (
            lax.all_gather(key_b, "ctx", axis=0, tiled=True),
            lax.all_gather(value_b, "ctx", axis=0, tiled=True),
        ),
    )
    live_rows = run_sum > 0
    safe_sum = jnp.where(live_rows, run_sum, 1.0)
    attn_heads = jnp.where(live_rows[:, :, None], run_acc / safe_sum[:, :, None], 0.0)
    lse_rows = jnp.where(live_rows, run_max + jnp.log(safe_sum), 0.0)
    attn_rows = attn_heads.transpose(1, 0, 2).reshape(tok_dev, width)
    attn_b = attn_rows.astype(jnp.bfloat16)
    branch = project(attn_b, wo_full)
    first_norm, first_pull = jax.vjp(
        layer_norm, x_in.astype(jnp.float32) + branch, gain_wide[:, 0], shift_wide[:, 0]
    )
    first_b = first_norm.astype(jnp.bfloat16)
    inner = project(first_b, inner_full)
    active, gelu_pull = jax.vjp(exact_gelu, inner)
    active_b = active.astype(jnp.bfloat16)
    outer = project(active_b, outer_full)
    result, second_pull = jax.vjp(layer_norm, first_norm + outer, gain_wide[:, 1], shift_wide[:, 1])
    wq_back, wk_back, wv_back, wo_back, inner_back, outer_back, gain_back, shift_back = gathered
    d_h2, d_gain2, d_shift2 = second_pull(cotangent[0].astype(jnp.float32))
    d_f_b = d_h2.astype(jnp.bfloat16)
    d_outer = jnp.dot(active_b.T, d_f_b, preferred_element_type=jnp.float32)
    d_active = jnp.dot(d_f_b, outer_back.T, preferred_element_type=jnp.float32)
    d_u_b = gelu_pull(d_active)[0].astype(jnp.bfloat16)
    d_inner = jnp.dot(first_b.T, d_u_b, preferred_element_type=jnp.float32)
    d_x1 = d_h2 + jnp.dot(d_u_b, inner_back.T, preferred_element_type=jnp.float32)
    d_h1, d_gain1, d_shift1 = first_pull(d_x1)
    d_y_b = d_h1.astype(jnp.bfloat16)
    d_wo = jnp.dot(attn_b.T, d_y_b, preferred_element_type=jnp.float32)
    d_attn_b = jnp.dot(d_y_b, wo_back.T, preferred_element_type=jnp.float32).astype(jnp.bfloat16)
    delta_rows = (
        (d_attn_b.astype(jnp.float32) * attn_rows).reshape(tok_dev, heads, head_dim).sum(axis=2).T
    )
    dout_heads = d_attn_b.reshape(tok_dev, heads, head_dim)

    def query_grad_step(dq_acc, sliced, offset):
        key_block, value_block = sliced
        block_len = key_block.shape[0]
        key_pos = lax.dynamic_slice_in_dim(pos_all, offset, block_len, 0)
        allowed = pair_mask(my_pos, key_pos, head_flags, half_len)
        key_heads = key_block.reshape(block_len, heads, head_dim)
        value_heads = value_block.reshape(block_len, heads, head_dim)
        scores = (
            jnp.einsum("qhd,khd->hqk", q_heads, key_heads, preferred_element_type=jnp.float32)
            * score_scale
        )
        prob_rows = jnp.where(
            allowed, jnp.exp(jnp.where(allowed, scores - lse_rows[:, :, None], 0.0)), 0.0
        )
        prob_grad = jnp.einsum(
            "qhd,khd->hqk", dout_heads, value_heads, preferred_element_type=jnp.float32
        )
        dscore = (prob_rows * (prob_grad - delta_rows[:, :, None]) * score_scale).astype(
            jnp.bfloat16
        )
        return dq_acc + jnp.einsum(
            "hqk,khd->qhd", dscore, key_heads, preferred_element_type=jnp.float32
        )

    dq_start = jnp.zeros((tok_dev, heads, head_dim), jnp.float32)
    dq_acc = pair_fold(
        query_grad_step,
        dq_start,
        (
            lax.all_gather(key_b, "ctx", axis=0, tiled=True),
            lax.all_gather(value_b, "ctx", axis=0, tiled=True),
        ),
    )
    dq_b = dq_acc.reshape(tok_dev, width).astype(jnp.bfloat16)
    lse_all, delta_all = (
        lax.all_gather(lse_rows, "ctx", axis=1, tiled=True),
        lax.all_gather(delta_rows, "ctx", axis=1, tiled=True),
    )
    k_heads = key_b.reshape(tok_dev, heads, head_dim)
    v_heads = value_b.reshape(tok_dev, heads, head_dim)

    def key_grad_step(running, sliced, offset):
        dk_acc, dv_acc = running
        query_block, dout_block = sliced
        block_len = query_block.shape[0]
        query_pos = lax.dynamic_slice_in_dim(pos_all, offset, block_len, 0)
        lse_block = lax.dynamic_slice_in_dim(lse_all, offset, block_len, 1)
        delta_block = lax.dynamic_slice_in_dim(delta_all, offset, block_len, 1)
        allowed = pair_mask(query_pos, my_pos, head_flags, half_len)
        query_heads = query_block.reshape(block_len, heads, head_dim)
        dout_block_heads = dout_block.reshape(block_len, heads, head_dim)
        scores = (
            jnp.einsum("qhd,khd->hqk", query_heads, k_heads, preferred_element_type=jnp.float32)
            * score_scale
        )
        prob_rows = jnp.where(
            allowed, jnp.exp(jnp.where(allowed, scores - lse_block[:, :, None], 0.0)), 0.0
        )
        dv_acc = dv_acc + jnp.einsum(
            "hqk,qhd->khd",
            prob_rows.astype(jnp.bfloat16),
            dout_block_heads,
            preferred_element_type=jnp.float32,
        )
        prob_grad = jnp.einsum(
            "qhd,khd->hqk", dout_block_heads, v_heads, preferred_element_type=jnp.float32
        )
        dscore = (prob_rows * (prob_grad - delta_block[:, :, None]) * score_scale).astype(
            jnp.bfloat16
        )
        dk_acc = dk_acc + jnp.einsum(
            "hqk,qhd->khd", dscore, query_heads, preferred_element_type=jnp.float32
        )
        return (dk_acc, dv_acc)

    kv_start = (
        jnp.zeros((tok_dev, heads, head_dim), jnp.float32),
        jnp.zeros((tok_dev, heads, head_dim), jnp.float32),
    )
    dk_acc, dv_acc = pair_fold(
        key_grad_step,
        kv_start,
        (
            lax.all_gather(query_b, "ctx", axis=0, tiled=True),
            lax.all_gather(d_attn_b, "ctx", axis=0, tiled=True),
        ),
    )
    dk_b = dk_acc.reshape(tok_dev, width).astype(jnp.bfloat16)
    dv_b = dv_acc.reshape(tok_dev, width).astype(jnp.bfloat16)
    d_input = d_h1 + jnp.dot(dq_b, wq_back.T, preferred_element_type=jnp.float32)
    d_input = d_input + jnp.dot(dk_b, wk_back.T, preferred_element_type=jnp.float32)
    d_input = d_input + jnp.dot(dv_b, wv_back.T, preferred_element_type=jnp.float32)
    terms = (
        jnp.dot(x_in.T, dq_b, preferred_element_type=jnp.float32),
        jnp.dot(x_in.T, dk_b, preferred_element_type=jnp.float32),
        jnp.dot(x_in.T, dv_b, preferred_element_type=jnp.float32),
        d_wo,
        d_inner,
        d_outer,
        jnp.stack([d_gain1, d_gain2], axis=1),
        jnp.stack([d_shift1, d_shift2], axis=1),
    )
    shares = (
        lax.psum_scatter(
            terms[0].astype(jnp.bfloat16), "fsdp", scatter_dimension=0, tiled=True
        ).astype(jnp.float32),
        lax.psum_scatter(
            terms[1].astype(jnp.bfloat16), "fsdp", scatter_dimension=0, tiled=True
        ).astype(jnp.float32),
        lax.psum_scatter(
            terms[2].astype(jnp.bfloat16), "fsdp", scatter_dimension=0, tiled=True
        ).astype(jnp.float32),
        lax.psum_scatter(
            terms[3].astype(jnp.bfloat16), "fsdp", scatter_dimension=0, tiled=True
        ).astype(jnp.float32),
        lax.psum_scatter(
            terms[4].astype(jnp.bfloat16), "fsdp", scatter_dimension=0, tiled=True
        ).astype(jnp.float32),
        lax.psum_scatter(
            terms[5].astype(jnp.bfloat16), "fsdp", scatter_dimension=0, tiled=True
        ).astype(jnp.float32),
        lax.psum_scatter(
            terms[6].astype(jnp.bfloat16), "fsdp", scatter_dimension=0, tiled=True
        ).astype(jnp.float32),
        lax.psum_scatter(
            terms[7].astype(jnp.bfloat16), "fsdp", scatter_dimension=0, tiled=True
        ).astype(jnp.float32),
    )
    totals = (
        lax.psum(shares[0].astype(jnp.bfloat16), "ctx").astype(jnp.float32),
        lax.psum(shares[1].astype(jnp.bfloat16), "ctx").astype(jnp.float32),
        lax.psum(shares[2].astype(jnp.bfloat16), "ctx").astype(jnp.float32),
        lax.psum(shares[3].astype(jnp.bfloat16), "ctx").astype(jnp.float32),
        lax.psum(shares[4].astype(jnp.bfloat16), "ctx").astype(jnp.float32),
        lax.psum(shares[5].astype(jnp.bfloat16), "ctx").astype(jnp.float32),
        lax.psum(shares[6].astype(jnp.bfloat16), "ctx").astype(jnp.float32),
        lax.psum(shares[7].astype(jnp.bfloat16), "ctx").astype(jnp.float32),
    )
    return (
        result.astype(jnp.bfloat16)[None],
        d_input.astype(jnp.bfloat16)[None],
        totals[0],
        totals[1],
        totals[2],
        totals[3],
        totals[4],
        totals[5],
        totals[6],
        totals[7],
    )


MESH = pl.DeviceIdType.MESH
f32 = jnp.float32
bf16 = jnp.bfloat16


class Place:
    def __init__(self):
        me = lax.axis_index("ctx")
        self.me = me
        self.z = lax.axis_index("fsdp")
        self.core = lax.rem(me, 2)
        self.chip = me // 2
        self.x = lax.rem(self.chip, 2)
        self.y = self.chip // 2
        self.chip_x = self.chip + 1 - 2 * self.x
        self.chip_y = self.chip + 2 - 4 * self.y
        self.chip_d = 3 - self.chip
        self.sib = (2 * self.chip + 1 - self.core, self.z)
        self.xn = (2 * self.chip_x + self.core, self.z)
        self.yn = (2 * self.chip_y + self.core, self.z)
        self.dn = (2 * self.chip_d + self.core, self.z)
        self.up = (me, self.z + 1)
        self.down = (me, self.z - 1)


def greet(place, others, line_len=None):
    barrier = pltpu.get_barrier_semaphore()
    count = len(others)
    for other in others:
        pl.semaphore_signal(barrier, inc=1, device_id=other, device_id_type=MESH)
    if line_len is not None:

        @pl.when(place.z < line_len - 1)
        def _():
            pl.semaphore_signal(barrier, inc=1, device_id=place.up, device_id_type=MESH)

        @pl.when(place.z > 0)
        def _():
            pl.semaphore_signal(barrier, inc=1, device_id=place.down, device_id_type=MESH)

        count = count + jnp.where(place.z < line_len - 1, 1, 0) + jnp.where(place.z > 0, 1, 0)

    pl.semaphore_wait(barrier, count)


def maybe(cond, fn):
    if cond is None:
        fn()
    else:
        pl.when(cond)(fn)


class Net:
    def __init__(self, send_sems, recv_sems, count):
        self.send_sems, self.recv_sems, self.count = send_sems, recv_sems, count
        self.used = 0
        self.open = []

    def new(self):
        self.used += 1
        assert self.used <= self.count
        return self.used - 1

    def copy(self, idx, src, dst, dev):
        return pltpu.make_async_remote_copy(
            src_ref=src,
            dst_ref=dst,
            send_sem=self.send_sems.at[idx],
            recv_sem=self.recv_sems.at[idx],
            device_id=dev,
            device_id_type=MESH,
        )

    def send(self, idx, src, dst, dev, cond=None):
        cp = self.copy(idx, src, dst, dev)
        maybe(cond, cp.start)
        self.open.append((cond, cp))

    def recv(self, idx, dst, dev, cond=None):
        cp = self.copy(idx, dst, dst, dev)
        maybe(cond, cp.wait_recv)

    def finish(self):
        for cond, cp in self.open:
            maybe(cond, cp.wait_send)
        self.open = []


class PlaneGather:
    def __init__(self, net, place, own, slot, rows, cond=None):
        self.net, self.place, self.own, self.slot, self.cond = net, place, own, slot, cond
        self.h0, self.h1 = pl.ds(0, rows // 2), pl.ds(rows // 2, rows // 2)
        self.ids = [net.new() for _ in range(12)]

    def first(self):
        n, p, i, c = self.net, self.place, self.ids, self.cond
        mine = self.slot(p.core, p.chip)
        n.send(i[0], self.own.at[self.h0], mine.at[self.h0], p.xn, c)
        n.send(i[1], self.own.at[self.h1], mine.at[self.h1], p.yn, c)
        n.send(i[2], self.own.at[self.h1], mine.at[self.h1], p.xn, c)
        n.send(i[3], self.own.at[self.h0], mine.at[self.h0], p.yn, c)
        n.send(i[4], self.own, mine, p.sib, c)

    def second(self):
        n, p, i, c = self.net, self.place, self.ids, self.cond
        bx, by = self.slot(p.core, p.chip_x), self.slot(p.core, p.chip_y)
        n.recv(i[0], bx.at[self.h0], p.xn, c)
        n.send(i[5], bx.at[self.h0], bx.at[self.h0], p.yn, c)
        n.recv(i[1], by.at[self.h1], p.yn, c)
        n.send(i[6], by.at[self.h1], by.at[self.h1], p.xn, c)
        n.recv(i[2], bx.at[self.h1], p.xn, c)
        n.send(i[7], bx, bx, p.sib, c)
        n.recv(i[3], by.at[self.h0], p.yn, c)
        n.send(i[8], by, by, p.sib, c)

    def third(self):
        n, p, i, c = self.net, self.place, self.ids, self.cond
        bd = self.slot(p.core, p.chip_d)
        n.recv(i[5], bd.at[self.h0], p.yn, c)
        n.send(i[9], bd.at[self.h0], bd.at[self.h0], p.sib, c)
        n.recv(i[6], bd.at[self.h1], p.xn, c)
        n.send(i[10], bd.at[self.h1], bd.at[self.h1], p.sib, c)

    def last(self):
        n, p, i, c = self.net, self.place, self.ids, self.cond
        o = 1 - p.core
        n.recv(i[4], self.slot(o, p.chip), p.sib, c)
        n.recv(i[7], self.slot(o, p.chip_x), p.sib, c)
        n.recv(i[8], self.slot(o, p.chip_y), p.sib, c)
        bd = self.slot(o, p.chip_d)
        n.recv(i[9], bd.at[self.h0], p.sib, c)
        n.recv(i[10], bd.at[self.h1], p.sib, c)


def gather_kernel(
    nz, n_sem, x_ref, wsel_ref, wcat_ref, xall_ref, wqkv_ref, wfull_ref, ssem, rsem, lsem
):
    p = Place()
    z = p.z
    part_rows = wcat_ref.shape[2]
    half = wsel_ref.shape[0] // 2
    local = [
        pltpu.make_async_copy(x_ref, xall_ref.at[p.core, p.chip], lsem.at[0]),
        pltpu.make_async_copy(wsel_ref, wqkv_ref.at[z], lsem.at[1]),
        pltpu.make_async_copy(wcat_ref, wfull_ref.at[z], lsem.at[2]),
    ]
    for cp in local:
        cp.start()
    greet(p, (p.sib, p.xn, p.yn), nz)
    net = Net(ssem, rsem, n_sem)
    tokens_ag = PlaneGather(
        net, p, x_ref, lambda k, q: xall_ref.at[k, q], x_ref.shape[0]
    )
    tokens_ag.first()
    can_up, can_down = z < nz - 1, z > 0
    rows = pl.ds(p.core * half, half)
    sel_up = [net.new() for _ in range(nz)]
    sel_down = [net.new() for _ in range(nz)]
    cat_up = [net.new() for _ in range(nz)]
    cat_down = [net.new() for _ in range(nz)]
    net.send(sel_up[1], wsel_ref.at[rows], wqkv_ref.at[z, rows], p.up, can_up)
    net.send(sel_down[1], wsel_ref.at[rows], wqkv_ref.at[z, rows], p.down, can_down)
    mine = wcat_ref.at[p.core, p.chip]
    net.send(cat_up[1], mine, wfull_ref.at[z, p.core, p.chip], p.up, can_up)
    net.send(cat_down[1], mine, wfull_ref.at[z, p.core, p.chip], p.down, can_down)
    stages = [[tokens_ag]]
    sel_waits = []

    def line_step(t):
        gathers = []
        for sel, cat, src, frm, to, got, more in (
            (sel_up, cat_up, z - t, p.down, p.up, z >= t, can_up),
            (sel_down, cat_down, z + t, p.up, p.down, z + t < nz, can_down),
        ):
            block = wqkv_ref.at[src, rows]
            net.recv(sel[t], block, frm, got)
            idx = net.new()
            if t + 1 < nz:
                net.send(sel[t + 1], block, block, to, jnp.logical_and(got, more))
            net.send(idx, block, block, p.sib, got)
            other = pl.ds((1 - p.core) * half, half)
            sel_waits.append((idx, wqkv_ref.at[src, other], got))
            piece = wfull_ref.at[src, p.core, p.chip]
            net.recv(cat[t], piece, frm, got)
            if t + 1 < nz:
                net.send(cat[t + 1], piece, piece, to, jnp.logical_and(got, more))
            gather = PlaneGather(
                net, p, piece, lambda k, q, src=src: wfull_ref.at[src, k, q], part_rows, got
            )
            gather.first()
            gathers.append(gather)
        return gathers

    for t in range(1, nz + 2):
        if t < nz:
            stages.append(line_step(t))
        if t - 1 < len(stages):
            for gather in stages[t - 1]:
                gather.second()
        if 0 <= t - 2 < len(stages):
            for gather in stages[t - 2]:
                gather.third()
    for group in stages:
        for gather in group:
            gather.last()
    for idx, block, got in sel_waits:
        net.recv(idx, block, p.sib, got)
    net.finish()
    for cp in local:
        cp.wait()


def hbm(count):
    return [pl.BlockSpec(memory_space=pltpu.HBM)] * count


def comm_params(collective_id):
    return pltpu.CompilerParams(
        collective_id=collective_id, has_side_effects=True, vmem_limit_bytes=56 << 20
    )


def gather_all(nz, x_in, wsel, wcat):
    n_sem = 12 * (2 * nz - 1) + 6 * nz + 4
    return pl.pallas_call(
        functools.partial(gather_kernel, nz, n_sem),
        out_shape=(
            jax.ShapeDtypeStruct((2, 4) + x_in.shape, bf16),
            jax.ShapeDtypeStruct((nz,) + wsel.shape, bf16),
            jax.ShapeDtypeStruct((nz,) + wcat.shape, bf16),
        ),
        in_specs=hbm(3),
        out_specs=tuple(hbm(3)),
        scratch_shapes=[
            pltpu.SemaphoreType.DMA((n_sem,)),
            pltpu.SemaphoreType.DMA((n_sem,)),
            pltpu.SemaphoreType.DMA((3,)),
        ],
        compiler_params=comm_params(0),
        name="gather_all",
    )(x_in, wsel, wcat)


def exchange_kernel(in_ref, out_ref, ssem, rsem, lsem):
    p = Place()
    cp = pltpu.make_async_copy(in_ref.at[p.chip], out_ref.at[p.chip], lsem)
    cp.start()
    greet(p, (p.xn, p.yn, p.dn))
    net = Net(ssem, rsem, 3)
    pairs = ((p.chip_x, p.xn), (p.chip_y, p.yn), (p.chip_d, p.dn))
    for i, (chip, dev) in enumerate(pairs):
        net.send(i, in_ref.at[chip], out_ref.at[p.chip], dev)
    for i, (chip, dev) in enumerate(pairs):
        net.recv(i, out_ref.at[chip], dev)
    net.finish()
    cp.wait()


def exchange(blocks, collective_id):
    return pl.pallas_call(
        exchange_kernel,
        out_shape=jax.ShapeDtypeStruct(blocks.shape, blocks.dtype),
        in_specs=hbm(1),
        out_specs=hbm(1)[0],
        scratch_shapes=[
            pltpu.SemaphoreType.DMA((3,)),
            pltpu.SemaphoreType.DMA((3,)),
            pltpu.SemaphoreType.DMA,
        ],
        compiler_params=comm_params(collective_id),
        name="exchange",
    )(blocks)


def add_into(dst, src, rows, chunk=16):
    def step(i, _):
        at = pl.ds(pl.multiple_of(i * chunk, chunk), chunk)
        dst[at, :] = (dst[at, :].astype(f32) + src[at, :].astype(f32)).astype(dst.dtype)
        return 0

    lax.fori_loop(0, rows // chunk, step, 0)


class PlaneScatter:
    def __init__(self, net, place, rows, source, kept, from_sib, rx0, ry1, ry0, rx1, lsem):
        self.net, self.place, self.rows, self.source = net, place, rows, source
        self.kept, self.from_sib = kept, from_sib
        self.rx0, self.ry1, self.ry0, self.rx1, self.lsem = rx0, ry1, ry0, rx1, lsem
        self.h = rows // 2
        self.h0, self.h1 = pl.ds(0, self.h), pl.ds(self.h, self.h)
        self.ids = [net.new() for _ in range(9)]

    def start(self):
        p = self.place
        self.local = pltpu.make_async_copy(self.source.at[p.core], self.kept, self.lsem)
        self.local.start()
        self.net.send(self.ids[0], self.source.at[1 - p.core], self.from_sib, p.sib)

    def first(self):
        n, p, i, k = self.net, self.place, self.ids, self.kept
        n.recv(i[0], self.from_sib, p.sib)
        self.local.wait()
        for q in range(4):
            add_into(k.at[q], self.from_sib.at[q], self.rows)
        for j in range(2):
            n.send(i[1 + j], k.at[2 * j + 1 - p.x, self.h0], self.rx0.at[j], p.xn)
            n.send(i[3 + j], k.at[2 * (1 - p.y) + j, self.h1], self.ry1.at[j], p.yn)

    def second(self):
        n, p, i, k = self.net, self.place, self.ids, self.kept
        for j in range(2):
            n.recv(i[1 + j], self.rx0.at[j], p.xn)
            n.recv(i[3 + j], self.ry1.at[j], p.yn)
        far_y = 1 - p.y
        far_x = 1 - p.x
        add_into(k.at[2 * far_y + p.x, self.h0], self.rx0.at[far_y], self.h)
        n.send(i[5], k.at[2 * far_y + p.x, self.h0], self.ry0, p.yn)
        add_into(k.at[2 * p.y + far_x, self.h1], self.ry1.at[far_x], self.h)
        n.send(i[6], k.at[2 * p.y + far_x, self.h1], self.rx1, p.xn)
        add_into(k.at[p.chip, self.h0], self.rx0.at[p.y], self.h)
        add_into(k.at[p.chip, self.h1], self.ry1.at[p.x], self.h)

    def third(self):
        n, p, i, k = self.net, self.place, self.ids, self.kept
        n.recv(i[5], self.ry0, p.yn)
        add_into(k.at[p.chip, self.h0], self.ry0, self.h)
        n.recv(i[6], self.rx1, p.xn)
        add_into(k.at[p.chip, self.h1], self.rx1, self.h)


class LineScatter:
    def __init__(self, net, place, nz, block, rows, from_low, from_high):
        self.net, self.place, self.nz, self.block, self.rows = net, place, nz, block, rows
        self.from_low, self.from_high = from_low, from_high
        self.up = [net.new() for _ in range(nz)]
        self.down = [net.new() for _ in range(nz)]

    def upward(self, o):
        n, p, z = self.net, self.place, self.place.z
        sends = z < o
        takes = jnp.logical_and(z <= o, z > 0)

        def take():
            n.recv(self.up[o], self.from_low.at[o], p.down)
            add_into(self.block(o), self.from_low.at[o], self.rows)

        maybe(takes, take)
        n.send(self.up[o], self.block(o), self.from_low.at[o], p.up, sends)

    def downward(self, o):
        n, p, z = self.net, self.place, self.place.z
        sends = z > o
        takes = jnp.logical_and(z >= o, z < self.nz - 1)

        def take():
            n.recv(self.down[o], self.from_high.at[o], p.up)
            add_into(self.block(o), self.from_high.at[o], self.rows)

        maybe(takes, take)
        n.send(self.down[o], self.block(o), self.from_high.at[o], p.down, sends)


def line_order(nz):
    order = []
    for i in range((nz + 1) // 2):
        for o in (nz - 1 - i, i):
            if o not in order:
                order.append(o)
    return order


def reduce_kernel(
    nz,
    n_sem,
    g_ref,
    dx_ref,
    dw_ref,
    dh_ref,
    gsum_ref,
    dtok_ref,
    dwsum_ref,
    g_kept,
    g_sib,
    g_rx0,
    g_ry1,
    g_ry0,
    g_rx1,
    g_low,
    g_high,
    x_kept,
    x_sib,
    x_rx0,
    x_ry1,
    x_ry0,
    x_rx1,
    w_kept,
    w_sib,
    w_low,
    w_high,
    dh_buf,
    out_buf,
    ssem,
    rsem,
    lsem,
):
    p = Place()
    z = p.z
    greet(p, (p.sib, p.xn, p.yn), nz)
    net = Net(ssem, rsem, n_sem)
    rows = g_ref.shape[3]
    order = line_order(nz)
    scatters = {}
    for n, o in enumerate(order):
        scatters[o] = PlaneScatter(
            net, p, rows, g_ref.at[o], g_kept.at[o], g_sib.at[o], g_rx0.at[o], g_ry1.at[o],
            g_ry0.at[o], g_rx1.at[o], lsem.at[n],
        )
    xs = PlaneScatter(
        net, p, dx_ref.shape[2], dx_ref, x_kept, x_sib, x_rx0, x_ry1, x_ry0, x_rx1, lsem.at[nz]
    )
    half = dw_ref.shape[1] // 2
    mine = pl.ds(p.core * half, half)
    other = pl.ds((1 - p.core) * half, half)
    w_ids = net.new()
    net.send(w_ids, dw_ref.at[:, other], w_sib, p.sib)
    w_local = pltpu.make_async_copy(dw_ref.at[:, mine], w_kept, lsem.at[nz + 1])
    w_local.start()
    dh_local = pltpu.make_async_copy(dh_ref, dh_buf, lsem.at[nz + 2])
    dh_local.start()
    for o in order:
        scatters[o].start()
    xs.start()
    g_line = LineScatter(net, p, nz, lambda o: g_kept.at[o, p.chip], rows, g_low, g_high)
    w_line = LineScatter(net, p, nz, lambda o: w_kept.at[o], half, w_low, w_high)
    net.recv(w_ids, w_sib, p.sib)
    w_local.wait()
    for o in range(nz):
        add_into(w_kept.at[o], w_sib.at[o], half)
    steps = [scatters[o] for o in order] + [xs]

    def line_pair(line, i):
        line.upward(nz - 1 - i)
        line.downward(i)

    for i in range(len(steps) + 2):
        if i < len(steps):
            steps[i].first()
        if 1 <= i <= len(steps):
            steps[i - 1].second()
        if 2 <= i:
            steps[i - 2].third()
        if i == 0:
            line_pair(w_line, 0)
        if i == 1:
            line_pair(w_line, 1)
        if i == 2:
            line_pair(w_line, 2)
        if i == 3:
            line_pair(w_line, 3)
            line_pair(g_line, 0)
        if i == 5:
            line_pair(g_line, 1)
            line_pair(g_line, 2)
    line_pair(g_line, 3)
    dh_local.wait()
    xr = x_kept.shape[1]

    def tok(i, _):
        at = pl.ds(pl.multiple_of(i * 16, 16), 16)
        out_buf[at, :] = (dh_buf[at, :] + x_kept[p.chip, at, :].astype(f32)).astype(bf16)
        return 0

    lax.fori_loop(0, xr // 16, tok, 0)
    out_copy = pltpu.make_async_copy(out_buf, dtok_ref, lsem.at[nz + 3])
    out_copy.start()
    own_g = g_kept.at[z, p.chip]
    own_w = w_kept.at[z]
    lg = pltpu.make_async_copy(own_g, gsum_ref.at[p.core, p.chip], lsem.at[nz + 4])
    lw = pltpu.make_async_copy(own_w, dwsum_ref.at[p.core, p.chip], lsem.at[nz + 5])
    lg.start()
    lw.start()
    gathers = [
        PlaneGather(net, p, own_w, lambda k, q: dwsum_ref.at[k, q], half),
        PlaneGather(net, p, own_g, lambda k, q: gsum_ref.at[k, q], rows),
    ]
    for stage in ("first", "second", "third", "last"):
        for gather in gathers:
            getattr(gather, stage)()
    net.finish()
    out_copy.wait()
    lg.wait()
    lw.wait()


def reduce_all(nz, grads, dxp, dwp, dh):
    rows, width = grads.shape[3], grads.shape[4]
    trows = dxp.shape[2]
    half = dwp.shape[1] // 2
    n_sem = 9 * (nz + 1) + 2 + 4 * nz + 24
    vm = lambda *shape: pltpu.VMEM(shape, bf16)
    return pl.pallas_call(
        functools.partial(reduce_kernel, nz, n_sem),
        out_shape=(
            jax.ShapeDtypeStruct(grads.shape[1:], bf16),
            jax.ShapeDtypeStruct((trows, width), bf16),
            jax.ShapeDtypeStruct((2, 4, half, width), bf16),
        ),
        in_specs=hbm(4),
        out_specs=tuple(hbm(3)),
        scratch_shapes=[
            vm(nz, 4, rows, width),
            vm(nz, 4, rows, width),
            vm(nz, 2, rows // 2, width),
            vm(nz, 2, rows // 2, width),
            vm(nz, rows // 2, width),
            vm(nz, rows // 2, width),
            vm(nz, rows, width),
            vm(nz, rows, width),
            vm(4, trows, width),
            vm(4, trows, width),
            vm(2, trows // 2, width),
            vm(2, trows // 2, width),
            vm(trows // 2, width),
            vm(trows // 2, width),
            vm(nz, half, width),
            vm(nz, half, width),
            vm(nz, half, width),
            vm(nz, half, width),
            pltpu.VMEM((trows, width), f32),
            vm(trows, width),
            pltpu.SemaphoreType.DMA((n_sem,)),
            pltpu.SemaphoreType.DMA((n_sem,)),
            pltpu.SemaphoreType.DMA((nz + 6,)),
        ],
        compiler_params=comm_params(3),
        name="reduce_all",
    )(grads, dxp, dwp, dh)


LANES = 256
KT = 128


def slot_scalars(t, a, paired, seg, half):
    tiles = half // KT
    n_lo = jnp.where(paired == 1, 0, ((a + 1) * seg + KT - 1) // KT)
    lo = t < n_lo
    tile = jnp.where(paired == 1, jnp.minimum(t, tiles - 1), jnp.where(lo, t, t - n_lo))
    base = jnp.where(lo, a * seg, half - (a + 1) * seg)
    limit = jnp.where(paired == 1, jnp.where(t < tiles, 1 << 20, -(1 << 20)), base - tile * KT)
    key = jnp.where(jnp.logical_or(paired == 1, lo), tile, tile + tiles)
    return jnp.where(lo, 0, seg), key, limit


def head_lanes(h, head_dim, rows):
    lane = lax.broadcasted_iota(jnp.int32, (rows, LANES), 1)
    return jnp.logical_and(lane >= h * head_dim, lane < (h + 1) * head_dim)


def offsets(seg):
    col = lax.broadcasted_iota(jnp.int32, (seg, KT), 1)
    row = lax.broadcasted_iota(jnp.int32, (seg, KT), 0)
    return col - row


def attend_kernel(
    n_ctx, heads, head_dim, tab, x_ref, w_ref, q_ref, k_ref, v_ref, o_ref, o32_ref, lse_ref,
    qh_ref, s_ref, m_ref, l_ref, acc_ref,
):
    core = lax.rem(lax.axis_index("ctx"), 2)
    tok = x_ref.shape[2]
    seg = tok // 2
    half = seg * n_ctx
    slots = half // KT + 2

    def keys(i, _):
        upper = i // n_ctx
        a = jnp.where(upper == 1, 2 * n_ctx - 1 - i, i)
        c = tab[n_ctx + a]
        rows = x_ref[lax.rem(c, 2), c // 2, pl.ds(pl.multiple_of(upper * seg, seg), seg), :]
        kv = jnp.dot(rows, w_ref[:, LANES:], preferred_element_type=f32)
        at = pl.ds(pl.multiple_of(i * seg, seg), seg)
        k_ref[at, :] = kv[:, :LANES].astype(bf16)
        v_ref[at, :] = kv[:, LANES:].astype(bf16)
        return 0

    lax.fori_loop(0, 2 * n_ctx, keys, 0)

    def queries(j, _):
        q = jnp.dot(x_ref[core, j], w_ref[:, :LANES], preferred_element_type=f32)
        q_ref[j] = (q.astype(bf16).astype(f32) * score_scale).astype(bf16)
        o_ref[j] = jnp.zeros((tok, LANES), bf16)
        o32_ref[j] = jnp.zeros((tok, LANES), f32)
        lse_ref[j] = jnp.zeros((tok, 128), f32)
        return 0

    lax.fori_loop(0, n_ctx // 2, queries, 0)

    def one(jh, _):
        j, h = jh // heads, lax.rem(jh, heads)
        a = tab[2 * j + core]
        paired = tab[2 * n_ctx + h]
        mine = head_lanes(h, head_dim, tok)
        qh_ref[...] = jnp.where(mine, q_ref[j].astype(f32), 0.0).astype(bf16)
        m_ref[...] = jnp.full((tok, KT), very_low, f32)
        l_ref[...] = jnp.zeros((tok, KT), f32)
        acc_ref[...] = jnp.zeros((tok, LANES), f32)
        off = offsets(seg)
        for t in range(slots):
            at, key, limit = slot_scalars(t, a, paired, seg, half)
            rows = pl.ds(pl.multiple_of(at, seg), seg)
            cols = pl.ds(pl.multiple_of(key * KT, KT), KT)
            s = lax.dot_general(
                qh_ref[rows, :], k_ref[cols, :], (((1,), (1,)), ((), ())),
                preferred_element_type=f32,
            )
            s = jnp.where(off <= limit, s, very_low)
            s_ref[t] = s
            m_ref[rows, :] = jnp.maximum(m_ref[rows, :], s)
        top = jnp.max(m_ref[...], axis=1, keepdims=True)
        top = jnp.where(top > 0.5 * very_low, top, 0.0)
        m_ref[...] = jnp.broadcast_to(top, (tok, KT))
        for t in range(slots):
            at, key, limit = slot_scalars(t, a, paired, seg, half)
            rows = pl.ds(pl.multiple_of(at, seg), seg)
            cols = pl.ds(pl.multiple_of(key * KT, KT), KT)
            e = jnp.exp(s_ref[t] - m_ref[rows, :])
            l_ref[rows, :] += e
            acc_ref[rows, :] += jnp.dot(
                e.astype(bf16), v_ref[cols, :], preferred_element_type=f32
            )
        total = jnp.sum(l_ref[...], axis=1, keepdims=True)
        live = total > 0
        safe = jnp.where(live, total, 1.0)
        o = acc_ref[...] * (1.0 / safe)
        lse = jnp.where(live, top + jnp.log(safe), 0.0)
        o32 = jnp.where(mine, o, o32_ref[j])
        o32_ref[j] = o32
        o_ref[j] = o32.astype(bf16)
        lane = lax.broadcasted_iota(jnp.int32, (tok, 128), 1)
        lse_ref[j] = jnp.where(lane == h, lse, lse_ref[j])
        return 0

    lax.fori_loop(0, n_ctx // 2 * heads, one, 0)


def vmem(count):
    return [pl.BlockSpec(memory_space=pltpu.VMEM)] * count


def attend(tab, n_ctx, heads, head_dim, xall, wqkv):
    tok = xall.shape[2]
    seg = tok // 2
    seq = tok * n_ctx
    n_q = n_ctx // 2
    slots = seg * n_ctx // KT + 2
    return pl.pallas_call(
        functools.partial(attend_kernel, n_ctx, heads, head_dim),
        out_shape=(
            jax.ShapeDtypeStruct((n_q, tok, LANES), bf16),
            jax.ShapeDtypeStruct((seq, LANES), bf16),
            jax.ShapeDtypeStruct((seq, LANES), bf16),
            jax.ShapeDtypeStruct((n_q, tok, LANES), bf16),
            jax.ShapeDtypeStruct((n_q, tok, LANES), f32),
            jax.ShapeDtypeStruct((n_q, tok, 128), f32),
        ),
        in_specs=[pl.BlockSpec(memory_space=pltpu.SMEM)] + vmem(2),
        out_specs=tuple(vmem(6)),
        scratch_shapes=[
            pltpu.VMEM((tok, LANES), bf16),
            pltpu.VMEM((slots, seg, KT), f32),
            pltpu.VMEM((tok, KT), f32),
            pltpu.VMEM((tok, KT), f32),
            pltpu.VMEM((tok, LANES), f32),
        ],
        compiler_params=pltpu.CompilerParams(vmem_limit_bytes=56 << 20),
        name="attend",
    )(tab, xall, wqkv)


def attend_back_kernel(
    n_ctx, heads, head_dim, tab, x_ref, w_ref, q_ref, k_ref, v_ref, o32_ref, lse_ref, da_ref,
    dxp_ref, dwp_ref, dk_ref, dv_ref, dq_ref, qh_ref, dah_ref, lse_b, del_b, dcat_ref, dw_acc,
):
    core = lax.rem(lax.axis_index("ctx"), 2)
    tok = x_ref.shape[2]
    seg = tok // 2
    half = seg * n_ctx
    slots = half // KT + 2
    dk_ref[...] = jnp.zeros(dk_ref.shape, f32)
    dv_ref[...] = jnp.zeros(dv_ref.shape, f32)
    dcat_ref[...] = jnp.zeros(dcat_ref.shape, bf16)

    def one(jh, _):
        j, h = jh // heads, lax.rem(jh, heads)
        a = tab[2 * j + core]
        paired = tab[2 * n_ctx + h]
        mine = head_lanes(h, head_dim, tok)
        qh_ref[...] = jnp.where(mine, q_ref[j].astype(f32), 0.0).astype(bf16)
        da = jnp.where(mine, da_ref[j].astype(f32), 0.0)
        dah_ref[...] = da.astype(bf16)
        delta = jnp.sum(da * o32_ref[j], axis=1, keepdims=True)
        del_b[...] = jnp.broadcast_to(delta, (tok, KT))
        lane = lax.broadcasted_iota(jnp.int32, (tok, 128), 1)
        lse = jnp.sum(jnp.where(lane == h, lse_ref[j], 0.0), axis=1, keepdims=True)
        lse_b[...] = jnp.broadcast_to(lse, (tok, KT))
        dq_ref[...] = jnp.zeros((tok, LANES), f32)
        off = offsets(seg)
        for t in range(slots):
            at, key, limit = slot_scalars(t, a, paired, seg, half)
            rows = pl.ds(pl.multiple_of(at, seg), seg)
            cols = pl.ds(pl.multiple_of(key * KT, KT), KT)
            qh, dah = qh_ref[rows, :], dah_ref[rows, :]
            kt, vt = k_ref[cols, :], v_ref[cols, :]
            nt = (((1,), (1,)), ((), ()))
            tn = (((0,), (0,)), ((), ()))
            s = lax.dot_general(qh, kt, nt, preferred_element_type=f32)
            pr = jnp.where(off <= limit, jnp.exp(s - lse_b[rows, :]), 0.0)
            dp = lax.dot_general(dah, vt, nt, preferred_element_type=f32)
            ds = (pr * (dp - del_b[rows, :])).astype(bf16)
            dv_ref[cols, :] += lax.dot_general(pr.astype(bf16), dah, tn, preferred_element_type=f32)
            dk_ref[cols, :] += lax.dot_general(ds, qh, tn, preferred_element_type=f32)
            dq_ref[rows, :] += jnp.dot(ds, kt, preferred_element_type=f32)
        at = pl.ds(pl.multiple_of((2 * j + core) * tok, tok), tok)
        dq = dcat_ref[at, :LANES].astype(f32)
        dcat_ref[at, :LANES] = jnp.where(mine, dq_ref[...] * score_scale, dq).astype(bf16)
        return 0

    lax.fori_loop(0, n_ctx // 2 * heads, one, 0)
    dw_acc[...] = jnp.zeros(dw_acc.shape, f32)

    def block(c, _):
        a = tab[c]
        lo = pl.ds(pl.multiple_of(a * seg, seg), seg)
        up = pl.ds(pl.multiple_of((2 * n_ctx - 1 - a) * seg, seg), seg)
        base = pl.multiple_of(c * tok, tok)
        dcat_ref[pl.ds(base, seg), LANES : 2 * LANES] = dk_ref[lo, :].astype(bf16)
        dcat_ref[pl.ds(base + seg, seg), LANES : 2 * LANES] = dk_ref[up, :].astype(bf16)
        dcat_ref[pl.ds(base, seg), 2 * LANES :] = dv_ref[lo, :].astype(bf16)
        dcat_ref[pl.ds(base + seg, seg), 2 * LANES :] = dv_ref[up, :].astype(bf16)
        d = dcat_ref[pl.ds(base, tok), :]
        dx = lax.dot_general(d, w_ref[...], (((1,), (1,)), ((), ())), preferred_element_type=f32)
        dxp_ref[lax.rem(c, 2), c // 2] = dx.astype(bf16)
        dw_acc[...] += lax.dot_general(
            x_ref[lax.rem(c, 2), c // 2], d, (((0,), (0,)), ((), ())), preferred_element_type=f32
        )
        return 0

    lax.fori_loop(0, n_ctx, block, 0)
    dwp_ref[...] = dw_acc[...].astype(bf16)


def attend_back(tab, n_ctx, heads, head_dim, xall, wqkv, q, k, v, o32, lse, da):
    tok, width = xall.shape[2], xall.shape[3]
    seg = tok // 2
    seq = tok * n_ctx
    return pl.pallas_call(
        functools.partial(attend_back_kernel, n_ctx, heads, head_dim),
        out_shape=(
            jax.ShapeDtypeStruct(xall.shape, bf16),
            jax.ShapeDtypeStruct((width, 3 * LANES), bf16),
        ),
        in_specs=[pl.BlockSpec(memory_space=pltpu.SMEM)] + vmem(8),
        out_specs=tuple(vmem(2)),
        scratch_shapes=[
            pltpu.VMEM((seq, LANES), f32),
            pltpu.VMEM((seq, LANES), f32),
            pltpu.VMEM((tok, LANES), f32),
            pltpu.VMEM((tok, LANES), bf16),
            pltpu.VMEM((tok, LANES), bf16),
            pltpu.VMEM((tok, KT), f32),
            pltpu.VMEM((tok, KT), f32),
            pltpu.VMEM((seq, 3 * LANES), bf16),
            pltpu.VMEM((width, 3 * LANES), f32),
        ],
        compiler_params=pltpu.CompilerParams(vmem_limit_bytes=56 << 20),
        name="attend_back",
    )(tab, xall, wqkv, q, k, v, o32, lse, da)


def fast_body(
    tokens,
    w_query,
    w_key,
    w_value,
    w_output,
    w_inner,
    w_outer,
    ln_gain,
    ln_bias,
    pairing,
    block_pairs,
    cotangent,
):
    tok, width = tokens.shape[1], tokens.shape[2]
    n_ctx, nz = lax.axis_size("ctx"), lax.axis_size("fsdp")
    heads = pairing.shape[1]
    head_dim = width // heads
    my_heads = heads // 4
    cols = my_heads * head_dim
    chip = lax.axis_index("ctx") // 2
    d_rows = w_query.shape[0]
    f_rows, ff = w_outer.shape[0], w_inner.shape[1]
    n_f = ff // width
    x_in = tokens[0]

    def chip_cols(w):
        part = lax.dynamic_slice_in_dim(w, chip * cols, cols, 1).astype(bf16)
        return jnp.pad(part, ((0, 0), (0, LANES - cols)))

    wsel = jnp.concatenate([chip_cols(w) for w in (w_query, w_key, w_value)], axis=1)
    norms = jnp.concatenate([ln_gain.T, ln_bias.T], axis=0).reshape(1, 4 * d_rows)
    used = f_rows + n_f * d_rows + d_rows + 1
    total = -(-used // 256) * 256
    norms = jnp.pad(norms.astype(bf16), ((0, total - used), (0, 0)))
    wcat = jnp.concatenate(
        [w_outer.astype(bf16)]
        + [w_inner[:, i * width : (i + 1) * width].astype(bf16) for i in range(n_f)]
        + [w_output.astype(bf16), norms],
        axis=0,
    ).reshape(2, 4, total // 8, width)
    xall, wqkv, wfull = gather_all(nz, x_in, wsel, wcat)
    wqkv = wqkv.reshape(width, 3 * LANES)
    wfull = wfull.reshape(nz, total, width)
    o1, o2, o3 = f_rows, f_rows + n_f * d_rows, f_rows + n_f * d_rows + d_rows
    outer_full = wfull[:, :o1].reshape(ff, width)
    inner_full = (
        wfull[:, o1:o2].reshape(nz, n_f, d_rows, width).transpose(0, 2, 1, 3).reshape(width, ff)
    )
    wo_full = wfull[:, o2:o3].reshape(width, width)
    vec = wfull[:, o3].reshape(nz, 4, d_rows).transpose(1, 0, 2).reshape(4, width).astype(f32)

    lower = block_pairs[0]
    ranks = jnp.arange(n_ctx, dtype=jnp.int32)
    inverse = jnp.sum(
        jnp.where(lower[None, :] == ranks[:, None], ranks[None, :], 0), axis=1
    ).astype(jnp.int32)
    flags = lax.dynamic_slice_in_dim(pairing[0], chip * my_heads, my_heads, 0)
    tab = jnp.concatenate([lower, inverse, flags])
    q, k, v, o16, o32, lse = attend(tab, n_ctx, my_heads, head_dim, xall, wqkv)
    got = exchange(o16, 1)
    attn_b = got[:, :, :cols].transpose(1, 0, 2).reshape(tok, width)

    branch = project(attn_b, wo_full)
    first_norm, first_pull = jax.vjp(layer_norm, x_in.astype(f32) + branch, vec[0], vec[2])
    first_b = first_norm.astype(bf16)
    inner = project(first_b, inner_full)
    active, gelu_pull = jax.vjp(exact_gelu, inner)
    active_b = active.astype(bf16)
    outer = project(active_b, outer_full)
    result, second_pull = jax.vjp(layer_norm, first_norm + outer, vec[1], vec[3])
    d_h2, d_gain2, d_shift2 = second_pull(cotangent[0].astype(f32))
    d_f_b = d_h2.astype(bf16)
    d_outer = jnp.dot(active_b.T, d_f_b, preferred_element_type=f32)
    d_active = jnp.dot(d_f_b, outer_full.T, preferred_element_type=f32)
    d_u_b = gelu_pull(d_active)[0].astype(bf16)
    d_inner = jnp.dot(first_b.T, d_u_b, preferred_element_type=f32)
    d_x1 = d_h2 + jnp.dot(d_u_b, inner_full.T, preferred_element_type=f32)
    d_h1, d_gain1, d_shift1 = first_pull(d_x1)
    d_y_b = d_h1.astype(bf16)
    d_wo = jnp.dot(attn_b.T, d_y_b, preferred_element_type=f32)
    d_attn_b = jnp.dot(d_y_b, wo_full.T, preferred_element_type=f32).astype(bf16)
    d_norms = jnp.stack([d_gain1, d_gain2, d_shift1, d_shift2]).reshape(4, nz, d_rows)
    d_norms = jnp.pad(
        d_norms.transpose(1, 0, 2).reshape(nz, 1, width), ((0, 0), (0, total - used), (0, 0))
    )
    grads = jnp.concatenate(
        [
            d_outer.astype(bf16).reshape(nz, f_rows, width),
            d_inner.astype(bf16)
            .reshape(nz, d_rows, n_f, width)
            .transpose(0, 2, 1, 3)
            .reshape(nz, n_f * d_rows, width),
            d_wo.astype(bf16).reshape(nz, d_rows, width),
            d_norms.astype(bf16),
        ],
        axis=1,
    ).reshape(nz, 2, 4, total // 8, width)
    da = jnp.pad(
        d_attn_b.reshape(tok, 4, cols).transpose(1, 0, 2), ((0, 0), (0, 0), (0, LANES - cols))
    )
    da = exchange(da, 2)
    dxp, dwp = attend_back(tab, n_ctx, my_heads, head_dim, xall, wqkv, q, k, v, o32, lse, da)
    gsum, dtok, dwsum = reduce_all(nz, grads, dxp, dwp.reshape(nz, d_rows, width), d_h1)
    gsum = gsum.reshape(total, width)
    dwsum = dwsum.transpose(1, 0, 2, 3).reshape(4, d_rows, 3, LANES)[:, :, :, :cols]
    dwsum = dwsum.transpose(2, 1, 0, 3).reshape(3, d_rows, width).astype(f32)
    g_inner = (
        gsum[o1:o2].reshape(n_f, d_rows, width).transpose(1, 0, 2).reshape(d_rows, ff)
    )
    g_norms = gsum[o3].reshape(4, d_rows).astype(f32)
    return (
        result.astype(bf16)[None],
        dtok[None],
        dwsum[0],
        dwsum[1],
        dwsum[2],
        gsum[o2:o3].astype(f32),
        g_inner.astype(f32),
        gsum[:o1].astype(f32),
        g_norms[:2].T,
        g_norms[2:].T,
    )


def solution(mesh):
    in_specs = (
        P("fsdp", "ctx", None),
        P("fsdp", None),
        P("fsdp", None),
        P("fsdp", None),
        P("fsdp", None),
        P("fsdp", None),
        P("fsdp", None),
        P("fsdp", None),
        P("fsdp", None),
        P("fsdp", None),
        P("fsdp", None),
        P("fsdp", "ctx", None),
    )
    out_specs = (
        P("fsdp", "ctx", None),
        P("fsdp", "ctx", None),
        P("fsdp", None),
        P("fsdp", None),
        P("fsdp", None),
        P("fsdp", None),
        P("fsdp", None),
        P("fsdp", None),
        P("fsdp", None),
        P("fsdp", None),
    )
    fast = mesh.shape["ctx"] == 8
    chosen = fast_body if fast else generic_body
    return jax.shard_map(chosen, mesh=mesh, in_specs=in_specs, out_specs=out_specs, check_vma=False)
```

```python
import functools

import jax
import jax.numpy as jnp
from jax import lax
from jax.experimental import pallas as pl
from jax.experimental.pallas import tpu as pltpu
from jax.sharding import PartitionSpec as P

norm_eps = 1e-05
score_scale = 0.125
very_low = -1e30


def shortened(value):

    def short(part):
        return part.astype(jnp.bfloat16) if part.dtype == jnp.float32 else part

    return jax.tree.map(short, value)


def layer_norm(values, norm_gain, norm_shift):
    center = values - jnp.mean(values, axis=-1, keepdims=True)
    spread = jnp.mean(center * center, axis=-1, keepdims=True)
    return center * lax.rsqrt(spread + norm_eps) * norm_gain + norm_shift


def exact_gelu(values):
    return jax.nn.gelu(values, approximate=False)


def project(rows_in, weight):
    return jnp.dot(rows_in, weight, preferred_element_type=jnp.float32)


def seq_positions(pair_row, tok_dev, seq_len):
    segment_len = tok_dev // 2
    within = jnp.arange(tok_dev, dtype=jnp.int32)
    lower_pos = pair_row[:, None] * segment_len + within[None, :]
    upper_pos = seq_len - (pair_row[:, None] + 1) * segment_len + within[None, :] - segment_len
    return jnp.where(within[None, :] < segment_len, lower_pos, upper_pos).reshape(-1)


def pair_mask(query_pos, key_pos, head_flags, half_len):
    target = (query_pos[None, :] // half_len + head_flags[:, None]) % 2
    paired = key_pos[None, None, :] // half_len == target[:, :, None]
    causal = key_pos[None, :] <= query_pos[:, None]
    return jnp.logical_and(paired, causal[None, :, :])


def block_rows(tok_dev):
    return 2 * tok_dev


def over_blocks(running, arrays, step_fn, tok_dev):
    row_count = arrays[0].shape[0]
    block_len = block_rows(tok_dev)

    def one_step(inner_carry, step_index):
        first_row = step_index * block_len
        sliced = tuple(
            (lax.dynamic_slice_in_dim(member, first_row, block_len, 0) for member in arrays)
        )
        return (step_fn(inner_carry, sliced, first_row), None)

    return lax.scan(one_step, running, jnp.arange(row_count // block_len, dtype=jnp.int32))[0]


def generic_body(
    tokens,
    w_query,
    w_key,
    w_value,
    w_output,
    w_inner,
    w_outer,
    ln_gain,
    ln_bias,
    pairing,
    block_pairs,
    cotangent,
):
    tok_dev = tokens.shape[1]
    width = tokens.shape[2]
    heads = pairing.shape[1]
    head_dim = width // heads
    n_ctx = lax.axis_size("ctx")
    seq_len = tok_dev * n_ctx
    half_len = seq_len // 2
    pos_all = seq_positions(block_pairs[0], tok_dev, seq_len)
    my_pos = lax.dynamic_slice_in_dim(pos_all, lax.axis_index("ctx") * tok_dev, tok_dev, 0)
    head_flags = pairing[0]
    masters = (w_query, w_key, w_value, w_output, w_inner, w_outer, ln_gain, ln_bias)
    low_masters = tuple((member.astype(jnp.bfloat16) for member in masters))
    gathered = jax.tree.map(
        lambda part, own: part.astype(own.dtype),
        lax.all_gather(shortened(low_masters), "fsdp", axis=0, tiled=True),
        low_masters,
    )
    wq_full, wk_full, wv_full, wo_full, inner_full, outer_full, gain_full, shift_full = gathered
    gain_wide = gain_full.astype(jnp.float32)
    shift_wide = shift_full.astype(jnp.float32)
    x_in = tokens[0]
    query_b = project(x_in, wq_full).astype(jnp.bfloat16)
    key_b = project(x_in, wk_full).astype(jnp.bfloat16)
    value_b = project(x_in, wv_full).astype(jnp.bfloat16)
    q_heads = query_b.reshape(tok_dev, heads, head_dim)

    def attend_step(running, sliced, offset):
        run_max, run_sum, run_acc = running
        key_block, value_block = sliced
        block_len = key_block.shape[0]
        key_pos = lax.dynamic_slice_in_dim(pos_all, offset, block_len, 0)
        allowed = pair_mask(my_pos, key_pos, head_flags, half_len)
        key_heads = key_block.reshape(block_len, heads, head_dim)
        value_heads = value_block.reshape(block_len, heads, head_dim)
        scores = (
            jnp.einsum("qhd,khd->hqk", q_heads, key_heads, preferred_element_type=jnp.float32)
            * score_scale
        )
        new_max = jnp.maximum(run_max, jnp.max(jnp.where(allowed, scores, very_low), axis=2))
        prob_rows = jnp.where(
            allowed, jnp.exp(jnp.where(allowed, scores - new_max[:, :, None], 0.0)), 0.0
        )
        decay = jnp.exp(run_max - new_max)
        new_sum = run_sum * decay + jnp.sum(prob_rows, axis=2)
        added = jnp.einsum(
            "hqk,khd->hqd",
            prob_rows.astype(jnp.bfloat16),
            value_heads,
            preferred_element_type=jnp.float32,
        )
        return (new_max, new_sum, run_acc * decay[:, :, None] + added)

    def pair_fold(step_fn, running, fetched):
        return over_blocks(running, fetched, step_fn, tok_dev)

    start_state = (
        jnp.full((heads, tok_dev), very_low, jnp.float32),
        jnp.zeros((heads, tok_dev), jnp.float32),
        jnp.zeros((heads, tok_dev, head_dim), jnp.float32),
    )
    run_max, run_sum, run_acc = pair_fold(
        attend_step,
        start_state,
        (
            lax.all_gather(key_b, "ctx", axis=0, tiled=True),
            lax.all_gather(value_b, "ctx", axis=0, tiled=True),
        ),
    )
    live_rows = run_sum > 0
    safe_sum = jnp.where(live_rows, run_sum, 1.0)
    attn_heads = jnp.where(live_rows[:, :, None], run_acc / safe_sum[:, :, None], 0.0)
    lse_rows = jnp.where(live_rows, run_max + jnp.log(safe_sum), 0.0)
    attn_rows = attn_heads.transpose(1, 0, 2).reshape(tok_dev, width)
    attn_b = attn_rows.astype(jnp.bfloat16)
    branch = project(attn_b, wo_full)
    first_norm, first_pull = jax.vjp(
        layer_norm, x_in.astype(jnp.float32) + branch, gain_wide[:, 0], shift_wide[:, 0]
    )
    first_b = first_norm.astype(jnp.bfloat16)
    inner = project(first_b, inner_full)
    active, gelu_pull = jax.vjp(exact_gelu, inner)
    active_b = active.astype(jnp.bfloat16)
    outer = project(active_b, outer_full)
    result, second_pull = jax.vjp(layer_norm, first_norm + outer, gain_wide[:, 1], shift_wide[:, 1])
    wq_back, wk_back, wv_back, wo_back, inner_back, outer_back, gain_back, shift_back = gathered
    d_h2, d_gain2, d_shift2 = second_pull(cotangent[0].astype(jnp.float32))
    d_f_b = d_h2.astype(jnp.bfloat16)
    d_outer = jnp.dot(active_b.T, d_f_b, preferred_element_type=jnp.float32)
    d_active = jnp.dot(d_f_b, outer_back.T, preferred_element_type=jnp.float32)
    d_u_b = gelu_pull(d_active)[0].astype(jnp.bfloat16)
    d_inner = jnp.dot(first_b.T, d_u_b, preferred_element_type=jnp.float32)
    d_x1 = d_h2 + jnp.dot(d_u_b, inner_back.T, preferred_element_type=jnp.float32)
    d_h1, d_gain1, d_shift1 = first_pull(d_x1)
    d_y_b = d_h1.astype(jnp.bfloat16)
    d_wo = jnp.dot(attn_b.T, d_y_b, preferred_element_type=jnp.float32)
    d_attn_b = jnp.dot(d_y_b, wo_back.T, preferred_element_type=jnp.float32).astype(jnp.bfloat16)
    delta_rows = (
        (d_attn_b.astype(jnp.float32) * attn_rows).reshape(tok_dev, heads, head_dim).sum(axis=2).T
    )
    dout_heads = d_attn_b.reshape(tok_dev, heads, head_dim)

    def query_grad_step(dq_acc, sliced, offset):
        key_block, value_block = sliced
        block_len = key_block.shape[0]
        key_pos = lax.dynamic_slice_in_dim(pos_all, offset, block_len, 0)
        allowed = pair_mask(my_pos, key_pos, head_flags, half_len)
        key_heads = key_block.reshape(block_len, heads, head_dim)
        value_heads = value_block.reshape(block_len, heads, head_dim)
        scores = (
            jnp.einsum("qhd,khd->hqk", q_heads, key_heads, preferred_element_type=jnp.float32)
            * score_scale
        )
        prob_rows = jnp.where(
            allowed, jnp.exp(jnp.where(allowed, scores - lse_rows[:, :, None], 0.0)), 0.0
        )
        prob_grad = jnp.einsum(
            "qhd,khd->hqk", dout_heads, value_heads, preferred_element_type=jnp.float32
        )
        dscore = (prob_rows * (prob_grad - delta_rows[:, :, None]) * score_scale).astype(
            jnp.bfloat16
        )
        return dq_acc + jnp.einsum(
            "hqk,khd->qhd", dscore, key_heads, preferred_element_type=jnp.float32
        )

    dq_start = jnp.zeros((tok_dev, heads, head_dim), jnp.float32)
    dq_acc = pair_fold(
        query_grad_step,
        dq_start,
        (
            lax.all_gather(key_b, "ctx", axis=0, tiled=True),
            lax.all_gather(value_b, "ctx", axis=0, tiled=True),
        ),
    )
    dq_b = dq_acc.reshape(tok_dev, width).astype(jnp.bfloat16)
    lse_all, delta_all = (
        lax.all_gather(lse_rows, "ctx", axis=1, tiled=True),
        lax.all_gather(delta_rows, "ctx", axis=1, tiled=True),
    )
    k_heads = key_b.reshape(tok_dev, heads, head_dim)
    v_heads = value_b.reshape(tok_dev, heads, head_dim)

    def key_grad_step(running, sliced, offset):
        dk_acc, dv_acc = running
        query_block, dout_block = sliced
        block_len = query_block.shape[0]
        query_pos = lax.dynamic_slice_in_dim(pos_all, offset, block_len, 0)
        lse_block = lax.dynamic_slice_in_dim(lse_all, offset, block_len, 1)
        delta_block = lax.dynamic_slice_in_dim(delta_all, offset, block_len, 1)
        allowed = pair_mask(query_pos, my_pos, head_flags, half_len)
        query_heads = query_block.reshape(block_len, heads, head_dim)
        dout_block_heads = dout_block.reshape(block_len, heads, head_dim)
        scores = (
            jnp.einsum("qhd,khd->hqk", query_heads, k_heads, preferred_element_type=jnp.float32)
            * score_scale
        )
        prob_rows = jnp.where(
            allowed, jnp.exp(jnp.where(allowed, scores - lse_block[:, :, None], 0.0)), 0.0
        )
        dv_acc = dv_acc + jnp.einsum(
            "hqk,qhd->khd",
            prob_rows.astype(jnp.bfloat16),
            dout_block_heads,
            preferred_element_type=jnp.float32,
        )
        prob_grad = jnp.einsum(
            "qhd,khd->hqk", dout_block_heads, v_heads, preferred_element_type=jnp.float32
        )
        dscore = (prob_rows * (prob_grad - delta_block[:, :, None]) * score_scale).astype(
            jnp.bfloat16
        )
        dk_acc = dk_acc + jnp.einsum(
            "hqk,qhd->khd", dscore, query_heads, preferred_element_type=jnp.float32
        )
        return (dk_acc, dv_acc)

    kv_start = (
        jnp.zeros((tok_dev, heads, head_dim), jnp.float32),
        jnp.zeros((tok_dev, heads, head_dim), jnp.float32),
    )
    dk_acc, dv_acc = pair_fold(
        key_grad_step,
        kv_start,
        (
            lax.all_gather(query_b, "ctx", axis=0, tiled=True),
            lax.all_gather(d_attn_b, "ctx", axis=0, tiled=True),
        ),
    )
    dk_b = dk_acc.reshape(tok_dev, width).astype(jnp.bfloat16)
    dv_b = dv_acc.reshape(tok_dev, width).astype(jnp.bfloat16)
    d_input = d_h1 + jnp.dot(dq_b, wq_back.T, preferred_element_type=jnp.float32)
    d_input = d_input + jnp.dot(dk_b, wk_back.T, preferred_element_type=jnp.float32)
    d_input = d_input + jnp.dot(dv_b, wv_back.T, preferred_element_type=jnp.float32)
    terms = (
        jnp.dot(x_in.T, dq_b, preferred_element_type=jnp.float32),
        jnp.dot(x_in.T, dk_b, preferred_element_type=jnp.float32),
        jnp.dot(x_in.T, dv_b, preferred_element_type=jnp.float32),
        d_wo,
        d_inner,
        d_outer,
        jnp.stack([d_gain1, d_gain2], axis=1),
        jnp.stack([d_shift1, d_shift2], axis=1),
    )
    shares = (
        lax.psum_scatter(
            terms[0].astype(jnp.bfloat16), "fsdp", scatter_dimension=0, tiled=True
        ).astype(jnp.float32),
        lax.psum_scatter(
            terms[1].astype(jnp.bfloat16), "fsdp", scatter_dimension=0, tiled=True
        ).astype(jnp.float32),
        lax.psum_scatter(
            terms[2].astype(jnp.bfloat16), "fsdp", scatter_dimension=0, tiled=True
        ).astype(jnp.float32),
        lax.psum_scatter(
            terms[3].astype(jnp.bfloat16), "fsdp", scatter_dimension=0, tiled=True
        ).astype(jnp.float32),
        lax.psum_scatter(
            terms[4].astype(jnp.bfloat16), "fsdp", scatter_dimension=0, tiled=True
        ).astype(jnp.float32),
        lax.psum_scatter(
            terms[5].astype(jnp.bfloat16), "fsdp", scatter_dimension=0, tiled=True
        ).astype(jnp.float32),
        lax.psum_scatter(
            terms[6].astype(jnp.bfloat16), "fsdp", scatter_dimension=0, tiled=True
        ).astype(jnp.float32),
        lax.psum_scatter(
            terms[7].astype(jnp.bfloat16), "fsdp", scatter_dimension=0, tiled=True
        ).astype(jnp.float32),
    )
    totals = (
        lax.psum(shares[0].astype(jnp.bfloat16), "ctx").astype(jnp.float32),
        lax.psum(shares[1].astype(jnp.bfloat16), "ctx").astype(jnp.float32),
        lax.psum(shares[2].astype(jnp.bfloat16), "ctx").astype(jnp.float32),
        lax.psum(shares[3].astype(jnp.bfloat16), "ctx").astype(jnp.float32),
        lax.psum(shares[4].astype(jnp.bfloat16), "ctx").astype(jnp.float32),
        lax.psum(shares[5].astype(jnp.bfloat16), "ctx").astype(jnp.float32),
        lax.psum(shares[6].astype(jnp.bfloat16), "ctx").astype(jnp.float32),
        lax.psum(shares[7].astype(jnp.bfloat16), "ctx").astype(jnp.float32),
    )
    return (
        result.astype(jnp.bfloat16)[None],
        d_input.astype(jnp.bfloat16)[None],
        totals[0],
        totals[1],
        totals[2],
        totals[3],
        totals[4],
        totals[5],
        totals[6],
        totals[7],
    )


MESH = pl.DeviceIdType.MESH
f32 = jnp.float32
bf16 = jnp.bfloat16


class Place:
    def __init__(self):
        me = lax.axis_index("ctx")
        self.me = me
        self.z = lax.axis_index("fsdp")
        self.core = lax.rem(me, 2)
        self.chip = me // 2
        self.x = lax.rem(self.chip, 2)
        self.y = self.chip // 2
        self.chip_x = self.chip + 1 - 2 * self.x
        self.chip_y = self.chip + 2 - 4 * self.y
        self.chip_d = 3 - self.chip
        self.sib = (2 * self.chip + 1 - self.core, self.z)
        self.xn = (2 * self.chip_x + self.core, self.z)
        self.yn = (2 * self.chip_y + self.core, self.z)
        self.dn = (2 * self.chip_d + self.core, self.z)
        self.up = (me, self.z + 1)
        self.down = (me, self.z - 1)


def greet(place, others, line_len=None):
    barrier = pltpu.get_barrier_semaphore()
    count = len(others)
    for other in others:
        pl.semaphore_signal(barrier, inc=1, device_id=other, device_id_type=MESH)
    if line_len is not None:

        @pl.when(place.z < line_len - 1)
        def _():
            pl.semaphore_signal(barrier, inc=1, device_id=place.up, device_id_type=MESH)

        @pl.when(place.z > 0)
        def _():
            pl.semaphore_signal(barrier, inc=1, device_id=place.down, device_id_type=MESH)

        count = count + jnp.where(place.z < line_len - 1, 1, 0) + jnp.where(place.z > 0, 1, 0)

    pl.semaphore_wait(barrier, count)


def maybe(cond, fn):
    if cond is None:
        fn()
    else:
        pl.when(cond)(fn)


class Net:
    def __init__(self, send_sems, recv_sems, count):
        self.send_sems, self.recv_sems, self.count = send_sems, recv_sems, count
        self.used = 0
        self.open = []

    def new(self):
        self.used += 1
        assert self.used <= self.count
        return self.used - 1

    def copy(self, idx, src, dst, dev):
        return pltpu.make_async_remote_copy(
            src_ref=src,
            dst_ref=dst,
            send_sem=self.send_sems.at[idx],
            recv_sem=self.recv_sems.at[idx],
            device_id=dev,
            device_id_type=MESH,
        )

    def send(self, idx, src, dst, dev, cond=None):
        cp = self.copy(idx, src, dst, dev)
        maybe(cond, cp.start)
        self.open.append((cond, cp))

    def recv(self, idx, dst, dev, cond=None):
        cp = self.copy(idx, dst, dst, dev)
        maybe(cond, cp.wait_recv)

    def finish(self):
        for cond, cp in self.open:
            maybe(cond, cp.wait_send)
        self.open = []


class PlaneGather:
    def __init__(self, net, place, own, slot, rows, cond=None):
        self.net, self.place, self.own, self.slot, self.cond = net, place, own, slot, cond
        self.h0, self.h1 = pl.ds(0, rows // 2), pl.ds(rows // 2, rows // 2)
        self.ids = [net.new() for _ in range(12)]

    def first(self):
        n, p, i, c = self.net, self.place, self.ids, self.cond
        mine = self.slot(p.core, p.chip)
        n.send(i[0], self.own.at[self.h0], mine.at[self.h0], p.xn, c)
        n.send(i[1], self.own.at[self.h1], mine.at[self.h1], p.yn, c)
        n.send(i[2], self.own.at[self.h1], mine.at[self.h1], p.xn, c)
        n.send(i[3], self.own.at[self.h0], mine.at[self.h0], p.yn, c)
        n.send(i[4], self.own, mine, p.sib, c)

    def second(self):
        n, p, i, c = self.net, self.place, self.ids, self.cond
        bx, by = self.slot(p.core, p.chip_x), self.slot(p.core, p.chip_y)
        n.recv(i[0], bx.at[self.h0], p.xn, c)
        n.send(i[5], bx.at[self.h0], bx.at[self.h0], p.yn, c)
        n.recv(i[1], by.at[self.h1], p.yn, c)
        n.send(i[6], by.at[self.h1], by.at[self.h1], p.xn, c)
        n.recv(i[2], bx.at[self.h1], p.xn, c)
        n.send(i[7], bx, bx, p.sib, c)
        n.recv(i[3], by.at[self.h0], p.yn, c)
        n.send(i[8], by, by, p.sib, c)

    def third(self):
        n, p, i, c = self.net, self.place, self.ids, self.cond
        bd = self.slot(p.core, p.chip_d)
        n.recv(i[5], bd.at[self.h0], p.yn, c)
        n.send(i[9], bd.at[self.h0], bd.at[self.h0], p.sib, c)
        n.recv(i[6], bd.at[self.h1], p.xn, c)
        n.send(i[10], bd.at[self.h1], bd.at[self.h1], p.sib, c)

    def last(self):
        n, p, i, c = self.net, self.place, self.ids, self.cond
        o = 1 - p.core
        n.recv(i[4], self.slot(o, p.chip), p.sib, c)
        n.recv(i[7], self.slot(o, p.chip_x), p.sib, c)
        n.recv(i[8], self.slot(o, p.chip_y), p.sib, c)
        bd = self.slot(o, p.chip_d)
        n.recv(i[9], bd.at[self.h0], p.sib, c)
        n.recv(i[10], bd.at[self.h1], p.sib, c)


def gather_kernel(
    nz, n_sem, x_ref, wsel_ref, wcat_ref, xall_ref, wqkv_ref, wfull_ref, ssem, rsem, lsem
):
    p = Place()
    z = p.z
    part_rows = wcat_ref.shape[2]
    half = wsel_ref.shape[0] // 2
    local = [
        pltpu.make_async_copy(x_ref, xall_ref.at[p.core, p.chip], lsem.at[0]),
        pltpu.make_async_copy(wsel_ref, wqkv_ref.at[z], lsem.at[1]),
        pltpu.make_async_copy(wcat_ref, wfull_ref.at[z], lsem.at[2]),
    ]
    for cp in local:
        cp.start()
    greet(p, (p.sib, p.xn, p.yn), nz)
    net = Net(ssem, rsem, n_sem)
    tokens_ag = PlaneGather(
        net, p, x_ref, lambda k, q: xall_ref.at[k, q], x_ref.shape[0]
    )
    tokens_ag.first()
    can_up, can_down = z < nz - 1, z > 0
    rows = pl.ds(p.core * half, half)
    sel_up = [net.new() for _ in range(nz)]
    sel_down = [net.new() for _ in range(nz)]
    cat_up = [net.new() for _ in range(nz)]
    cat_down = [net.new() for _ in range(nz)]
    net.send(sel_up[1], wsel_ref.at[rows], wqkv_ref.at[z, rows], p.up, can_up)
    net.send(sel_down[1], wsel_ref.at[rows], wqkv_ref.at[z, rows], p.down, can_down)
    mine = wcat_ref.at[p.core, p.chip]
    net.send(cat_up[1], mine, wfull_ref.at[z, p.core, p.chip], p.up, can_up)
    net.send(cat_down[1], mine, wfull_ref.at[z, p.core, p.chip], p.down, can_down)
    stages = [[tokens_ag]]
    sel_waits = []

    def line_step(t):
        gathers = []
        for sel, cat, src, frm, to, got, more in (
            (sel_up, cat_up, z - t, p.down, p.up, z >= t, can_up),
            (sel_down, cat_down, z + t, p.up, p.down, z + t < nz, can_down),
        ):
            block = wqkv_ref.at[src, rows]
            net.recv(sel[t], block, frm, got)
            idx = net.new()
            if t + 1 < nz:
                net.send(sel[t + 1], block, block, to, jnp.logical_and(got, more))
            net.send(idx, block, block, p.sib, got)
            other = pl.ds((1 - p.core) * half, half)
            sel_waits.append((idx, wqkv_ref.at[src, other], got))
            piece = wfull_ref.at[src, p.core, p.chip]
            net.recv(cat[t], piece, frm, got)
            if t + 1 < nz:
                net.send(cat[t + 1], piece, piece, to, jnp.logical_and(got, more))
            gather = PlaneGather(
                net, p, piece, lambda k, q, src=src: wfull_ref.at[src, k, q], part_rows, got
            )
            gather.first()
            gathers.append(gather)
        return gathers

    for t in range(1, nz + 2):
        if t < nz:
            stages.append(line_step(t))
        if t - 1 < len(stages):
            for gather in stages[t - 1]:
                gather.second()
        if 0 <= t - 2 < len(stages):
            for gather in stages[t - 2]:
                gather.third()
    for group in stages:
        for gather in group:
            gather.last()
    for idx, block, got in sel_waits:
        net.recv(idx, block, p.sib, got)
    net.finish()
    for cp in local:
        cp.wait()


def hbm(count):
    return [pl.BlockSpec(memory_space=pltpu.HBM)] * count


def comm_params(collective_id):
    return pltpu.CompilerParams(
        collective_id=collective_id, has_side_effects=True, vmem_limit_bytes=56 << 20
    )


def gather_all(nz, x_in, wsel, wcat):
    n_sem = 12 * (2 * nz - 1) + 6 * nz + 4
    return pl.pallas_call(
        functools.partial(gather_kernel, nz, n_sem),
        out_shape=(
            jax.ShapeDtypeStruct((2, 4) + x_in.shape, bf16),
            jax.ShapeDtypeStruct((nz,) + wsel.shape, bf16),
            jax.ShapeDtypeStruct((nz,) + wcat.shape, bf16),
        ),
        in_specs=vmem(3),
        out_specs=tuple(hbm(3)),
        scratch_shapes=[
            pltpu.SemaphoreType.DMA((n_sem,)),
            pltpu.SemaphoreType.DMA((n_sem,)),
            pltpu.SemaphoreType.DMA((3,)),
        ],
        compiler_params=comm_params(0),
        name="gather_all",
    )(x_in, wsel, wcat)


def to_owners_kernel(in_ref, out_ref, part_ref, sum_ref, ssem, rsem):
    p = Place()
    greet(p, (p.sib, p.xn, p.yn, p.dn))
    net = Net(ssem, rsem, 4)
    net.send(3, in_ref.at[1 - p.core], part_ref, p.sib)
    net.recv(3, part_ref, p.sib)
    pairs = ((p.chip_d, p.dn), (p.chip_x, p.xn), (p.chip_y, p.yn))
    for i, (chip, dev) in enumerate(pairs):
        sum_ref[chip] = in_ref[p.core, chip] + part_ref[chip]
        net.send(i, sum_ref.at[chip], out_ref.at[p.chip], dev)
    out_ref[p.chip] = in_ref[p.core, p.chip] + part_ref[p.chip]
    for i, (chip, dev) in enumerate(pairs):
        net.recv(i, out_ref.at[chip], dev)
    net.finish()


def to_owners(blocks):
    shape = blocks.shape[1:]
    return pl.pallas_call(
        to_owners_kernel,
        out_shape=jax.ShapeDtypeStruct(shape, bf16),
        in_specs=vmem(1),
        out_specs=vmem(1)[0],
        scratch_shapes=[
            pltpu.VMEM(shape, bf16),
            pltpu.VMEM(shape, bf16),
            pltpu.SemaphoreType.DMA((4,)),
            pltpu.SemaphoreType.DMA((4,)),
        ],
        compiler_params=comm_params(1),
        name="to_owners",
    )(blocks)


def to_heads_kernel(in_ref, out_ref, ssem, rsem):
    p = Place()
    greet(p, (p.sib, p.xn, p.yn, p.dn))
    net = Net(ssem, rsem, 7)
    pairs = ((p.chip_d, p.dn), (p.chip_x, p.xn), (p.chip_y, p.yn))
    for i, (chip, dev) in enumerate(pairs):
        net.send(i, in_ref.at[chip], out_ref.at[p.core, p.chip], dev)
    net.send(3, in_ref.at[p.chip], out_ref.at[p.core, p.chip], p.sib)
    out_ref[p.core, p.chip] = in_ref[p.chip]
    for i, chip, dev in ((1, p.chip_x, p.xn), (2, p.chip_y, p.yn), (0, p.chip_d, p.dn)):
        block = out_ref.at[p.core, chip]
        net.recv(i, block, dev)
        net.send(4 + i, block, block, p.sib)
    for i, chip in ((3, p.chip), (5, p.chip_x), (6, p.chip_y), (4, p.chip_d)):
        net.recv(i, out_ref.at[1 - p.core, chip], p.sib)
    net.finish()


def to_heads(blocks):
    return pl.pallas_call(
        to_heads_kernel,
        out_shape=jax.ShapeDtypeStruct((2,) + blocks.shape, bf16),
        in_specs=vmem(1),
        out_specs=vmem(1)[0],
        scratch_shapes=[pltpu.SemaphoreType.DMA((7,)), pltpu.SemaphoreType.DMA((7,))],
        compiler_params=comm_params(2),
        name="to_heads",
    )(blocks)


def add_into(dst, src, rows, chunk=32):
    if rows % chunk:
        chunk = 16

    def step(i, _):
        at = pl.ds(pl.multiple_of(i * chunk, chunk), chunk)
        dst[at, :] = dst[at, :] + src[at, :]
        return 0

    lax.fori_loop(0, rows // chunk, step, 0)


class PlaneScatter:
    def __init__(self, net, place, rows, source, kept, from_sib, rx0, ry1, ry0, rx1, lsem):
        self.net, self.place, self.rows, self.source = net, place, rows, source
        self.kept, self.from_sib = kept, from_sib
        self.rx0, self.ry1, self.ry0, self.rx1, self.lsem = rx0, ry1, ry0, rx1, lsem
        self.h = rows // 2
        self.h0, self.h1 = pl.ds(0, self.h), pl.ds(self.h, self.h)
        self.ids = [net.new() for _ in range(9)]

    def start(self):
        p = self.place
        self.local = pltpu.make_async_copy(self.source.at[p.core], self.kept, self.lsem)
        self.local.start()
        self.net.send(self.ids[0], self.source.at[1 - p.core], self.from_sib, p.sib)

    def first(self):
        n, p, i, k = self.net, self.place, self.ids, self.kept
        n.recv(i[0], self.from_sib, p.sib)
        self.local.wait()
        for q in range(4):
            add_into(k.at[q], self.from_sib.at[q], self.rows)
        for j in range(2):
            n.send(i[1 + j], k.at[2 * j + 1 - p.x, self.h0], self.rx0.at[j], p.xn)
            n.send(i[3 + j], k.at[2 * (1 - p.y) + j, self.h1], self.ry1.at[j], p.yn)

    def second(self):
        n, p, i, k = self.net, self.place, self.ids, self.kept
        for j in range(2):
            n.recv(i[1 + j], self.rx0.at[j], p.xn)
            n.recv(i[3 + j], self.ry1.at[j], p.yn)
        far_y = 1 - p.y
        far_x = 1 - p.x
        add_into(k.at[2 * far_y + p.x, self.h0], self.rx0.at[far_y], self.h)
        n.send(i[5], k.at[2 * far_y + p.x, self.h0], self.ry0, p.yn)
        add_into(k.at[2 * p.y + far_x, self.h1], self.ry1.at[far_x], self.h)
        n.send(i[6], k.at[2 * p.y + far_x, self.h1], self.rx1, p.xn)
        add_into(k.at[p.chip, self.h0], self.rx0.at[p.y], self.h)
        add_into(k.at[p.chip, self.h1], self.ry1.at[p.x], self.h)

    def third(self):
        n, p, i, k = self.net, self.place, self.ids, self.kept
        n.recv(i[5], self.ry0, p.yn)
        add_into(k.at[p.chip, self.h0], self.ry0, self.h)
        n.recv(i[6], self.rx1, p.xn)
        add_into(k.at[p.chip, self.h1], self.rx1, self.h)


class LineScatter:
    def __init__(self, net, place, nz, block, rows, from_low, from_high):
        self.net, self.place, self.nz, self.block, self.rows = net, place, nz, block, rows
        self.from_low, self.from_high = from_low, from_high
        self.up = [net.new() for _ in range(nz)]
        self.down = [net.new() for _ in range(nz)]

    def step(self, t):
        n, p, z, top = self.net, self.place, self.place.z, self.nz - 1
        sides = (
            (self.up, self.from_low, z, top - t + z, p.down, p.up),
            (self.down, self.from_high, top - z, t + z - top, p.up, p.down),
        )
        for ids, buf, depth, owner, frm, to in sides:
            owner = jnp.clip(owner, 0, top)

            def take(ids=ids, buf=buf, owner=owner, frm=frm):
                n.recv(ids[t - 1], buf.at[owner], frm)
                add_into(self.block(owner), buf.at[owner], self.rows)

            if t > 0:
                maybe(jnp.logical_and(depth > 0, depth <= t), take)
            if t < top:
                n.send(ids[t], self.block(owner), buf.at[owner], to, depth <= t)


def line_order(nz):
    order = []
    for i in range((nz + 1) // 2):
        for o in (nz - 1 - i, i):
            if o not in order:
                order.append(o)
    return order


def reduce_kernel(
    nz,
    n_sem,
    g_ref,
    dx_ref,
    dw_ref,
    dh_ref,
    gsum_ref,
    dtok_ref,
    dwsum_ref,
    g_kept,
    g_sib,
    g_rx0,
    g_ry1,
    g_ry0,
    g_rx1,
    g_low,
    g_high,
    x_kept,
    x_sib,
    x_rx0,
    x_ry1,
    x_ry0,
    x_rx1,
    w_kept,
    w_sib,
    w_low,
    w_high,
    dh_buf,
    out_buf,
    ssem,
    rsem,
    lsem,
):
    p = Place()
    z = p.z
    greet(p, (p.sib, p.xn, p.yn), nz)
    net = Net(ssem, rsem, n_sem)
    rows = g_ref.shape[3]
    order = line_order(nz)
    scatters = {}
    for n, o in enumerate(order):
        scatters[o] = PlaneScatter(
            net, p, rows, g_ref.at[o], g_kept.at[o], g_sib.at[o], g_rx0.at[o], g_ry1.at[o],
            g_ry0.at[o], g_rx1.at[o], lsem.at[n],
        )
    xs = PlaneScatter(
        net, p, dx_ref.shape[2], dx_ref, x_kept, x_sib, x_rx0, x_ry1, x_ry0, x_rx1, lsem.at[nz]
    )
    half = dw_ref.shape[1] // 2
    mine = pl.ds(p.core * half, half)
    other = pl.ds((1 - p.core) * half, half)
    w_ids = net.new()
    net.send(w_ids, dw_ref.at[:, other], w_sib, p.sib)
    w_local = pltpu.make_async_copy(dw_ref.at[:, mine], w_kept, lsem.at[nz + 1])
    w_local.start()
    dh_local = pltpu.make_async_copy(dh_ref, dh_buf, lsem.at[nz + 2])
    dh_local.start()
    for o in order:
        scatters[o].start()
    xs.start()
    g_line = LineScatter(net, p, nz, lambda o: g_kept.at[o, p.chip], rows, g_low, g_high)
    w_line = LineScatter(net, p, nz, lambda o: w_kept.at[o], half, w_low, w_high)
    net.recv(w_ids, w_sib, p.sib)
    w_local.wait()
    for o in range(nz):
        add_into(w_kept.at[o], w_sib.at[o], half)
    steps = [scatters[o] for o in order] + [xs]

    for i in range(len(steps) + 2):
        if i < len(steps):
            steps[i].first()
        if 1 <= i <= len(steps):
            steps[i - 1].second()
        if 2 <= i:
            steps[i - 2].third()
        if i < nz:
            w_line.step(i)
        if i in (3, 5, 6):
            g_line.step({3: 0, 5: 1, 6: 2}[i])
    g_line.step(nz - 1)
    dh_local.wait()
    xr = x_kept.shape[1]

    def tok(i, _):
        at = pl.ds(pl.multiple_of(i * 16, 16), 16)
        out_buf[at, :] = (dh_buf[at, :] + x_kept[p.chip, at, :].astype(f32)).astype(bf16)
        return 0

    lax.fori_loop(0, xr // 16, tok, 0)
    out_copy = pltpu.make_async_copy(out_buf, dtok_ref, lsem.at[nz + 3])
    out_copy.start()
    own_g = g_kept.at[z, p.chip]
    own_w = w_kept.at[z]
    lg = pltpu.make_async_copy(own_g, gsum_ref.at[p.core, p.chip], lsem.at[nz + 4])
    lw = pltpu.make_async_copy(own_w, dwsum_ref.at[p.core, p.chip], lsem.at[nz + 5])
    lg.start()
    lw.start()
    gathers = [
        PlaneGather(net, p, own_w, lambda k, q: dwsum_ref.at[k, q], half),
        PlaneGather(net, p, own_g, lambda k, q: gsum_ref.at[k, q], rows),
    ]
    for stage in ("first", "second", "third", "last"):
        for gather in gathers:
            getattr(gather, stage)()
    net.finish()
    out_copy.wait()
    lg.wait()
    lw.wait()


def reduce_all(nz, grads, dxp, dwp, dh):
    rows, width = grads.shape[3], grads.shape[4]
    trows = dxp.shape[2]
    half = dwp.shape[1] // 2
    n_sem = 9 * (nz + 1) + 2 + 4 * nz + 24
    vm = lambda *shape: pltpu.VMEM(shape, bf16)
    return pl.pallas_call(
        functools.partial(reduce_kernel, nz, n_sem),
        out_shape=(
            jax.ShapeDtypeStruct(grads.shape[1:], bf16),
            jax.ShapeDtypeStruct((trows, width), bf16),
            jax.ShapeDtypeStruct((2, 4, half, width), bf16),
        ),
        in_specs=hbm(4),
        out_specs=tuple(hbm(3)),
        scratch_shapes=[
            vm(nz, 4, rows, width),
            vm(nz, 4, rows, width),
            vm(nz, 2, rows // 2, width),
            vm(nz, 2, rows // 2, width),
            vm(nz, rows // 2, width),
            vm(nz, rows // 2, width),
            vm(nz, rows, width),
            vm(nz, rows, width),
            vm(4, trows, width),
            vm(4, trows, width),
            vm(2, trows // 2, width),
            vm(2, trows // 2, width),
            vm(trows // 2, width),
            vm(trows // 2, width),
            vm(nz, half, width),
            vm(nz, half, width),
            vm(nz, half, width),
            vm(nz, half, width),
            pltpu.VMEM((trows, width), f32),
            vm(trows, width),
            pltpu.SemaphoreType.DMA((n_sem,)),
            pltpu.SemaphoreType.DMA((n_sem,)),
            pltpu.SemaphoreType.DMA((nz + 6,)),
        ],
        compiler_params=comm_params(3),
        name="reduce_all",
    )(grads, dxp, dwp, dh)


LANES = 256
KT = 128
NT = (((1,), (1,)), ((), ()))
TN = (((0,), (0,)), ((), ()))
NN = (((1,), (0,)), ((), ()))


def mm(a, b, dims=NN):
    return lax.dot_general(a, b, dims, preferred_element_type=f32)


def head_mask(h, head_dim, dtype):
    lane = lax.broadcasted_iota(jnp.int32, (1, LANES), 1)
    inside = jnp.logical_and(lane >= h * head_dim, lane < (h + 1) * head_dim)
    return jnp.where(inside, 1.0, 0.0).astype(dtype)


class Fold:
    def __init__(self, n, seg):
        self.n, self.seg, self.half = n, seg, n * seg
        self.tiles = self.half // KT

    def ranges(self, i):
        a = -(-(self.n - i) * self.seg // KT)
        b = -(-(i + 1) * self.seg // KT)
        assert a + b == self.tiles + 2
        return a, b

    def places(self, i, core, paired):
        a, b = self.ranges(i)
        n, seg = self.n, self.seg
        mine = core * self.half
        up = self.half + (core * (n // 2) + i) * seg
        rows_a = jnp.where(paired == 1, up, mine + (n - 1 - i) * seg)
        rows_b = jnp.where(paired == 1, up, mine + i * seg)
        keys_a = jnp.where(paired == 1, 0, mine)
        keys_b = jnp.where(paired == 1, a * KT, mine)
        lim_a = jnp.where(paired == 1, 1 << 20, (n - 1 - i) * seg - (a - 2) * KT)
        lim_b = jnp.where(paired == 1, -(1 << 20), i * seg - (b - 2) * KT)
        return (rows_a, keys_a, lim_a, a), (rows_b, keys_b, lim_b, b)


def natural(tab, n, s):
    upper = s // n
    c = tab[n + jnp.where(upper == 1, 2 * n - 1 - s, s)]
    return lax.rem(c, 2), c // 2, upper


def key_slice(base, first, count):
    return pl.ds(pl.multiple_of(base + first * KT, 32), count * KT)


def tail_mask(seg, limit):
    col = lax.broadcasted_iota(jnp.int32, (seg, 2 * KT), 1)
    row = lax.broadcasted_iota(jnp.int32, (seg, 2 * KT), 0)
    return col - row <= limit


def project_tokens(n, seg, tab, x_ref, w_ref, q_ref, k_ref, v_ref):
    def two(i, _):
        rows = []
        for u in range(2):
            k, q, upper = natural(tab, n, 2 * i + u)
            rows.append(x_ref[k, q, pl.ds(pl.multiple_of(upper * seg, seg), seg), :])
        qkv = mm(jnp.concatenate(rows, axis=0), w_ref[...])
        at = pl.ds(pl.multiple_of(i * 2 * seg, 2 * seg), 2 * seg)
        q_ref[at, :] = (qkv[:, :LANES].astype(bf16).astype(f32) * score_scale).astype(bf16)
        k_ref[at, :] = qkv[:, LANES : 2 * LANES].astype(bf16)
        v_ref[at, :] = qkv[:, 2 * LANES :].astype(bf16)
        return 0

    lax.fori_loop(0, n, two, 0)


def attend_heads(fold, core, heads, head_dim, tab, q_ref, k_ref, v_ref, o_ref, lse_ref):
    n, seg = fold.n, fold.seg
    rows_of = lambda at: pl.ds(pl.multiple_of(at, 32), seg)
    o_ref[...] = jnp.zeros(o_ref.shape, f32)

    def head(h, _):
        paired = tab[2 * n + h]
        pf = paired.astype(f32)
        lanes = head_mask(h, head_dim, f32)
        lanes16 = head_mask(h, head_dim, bf16)
        for i in range(n // 2):
            parts = []
            for rows, keys, limit, count in fold.places(i, core, paired):
                q = q_ref[rows_of(rows), :] * lanes16
                tail = mm(q, k_ref[key_slice(keys, count - 2, 2), :], NT)
                tail = jnp.where(tail_mask(seg, limit), tail, very_low)
                top = jnp.max(tail, axis=1, keepdims=True)
                main = None
                if count > 2:
                    main = mm(q, k_ref[key_slice(keys, 0, count - 2), :], NT)
                    top = jnp.maximum(top, jnp.max(main, axis=1, keepdims=True))
                parts.append((keys, count, main, tail, top))
            both = jnp.maximum(parts[0][4], parts[1][4])
            outs = []
            for keys, count, main, tail, top in parts:
                top = jnp.where(paired == 1, both, top)
                e = jnp.exp(tail - top)
                total = jnp.sum(e, axis=1, keepdims=True)
                acc = mm(e.astype(bf16), v_ref[key_slice(keys, count - 2, 2), :])
                if main is not None:
                    e = jnp.exp(main - top)
                    total += jnp.sum(e, axis=1, keepdims=True)
                    acc += mm(e.astype(bf16), v_ref[key_slice(keys, 0, count - 2), :])
                outs.append((top, total, acc))
            (top_a, sum_a, acc_a), (top_b, sum_b, acc_b) = outs
            sum_a, sum_b = sum_a + pf * sum_b, jnp.where(paired == 1, sum_a + sum_b, sum_b)
            acc_a = acc_a + pf * acc_b
            out_a = acc_a * (lanes / sum_a)
            out_b = acc_b * (lanes / sum_b)
            lse_ref[h, i, 0] = jnp.broadcast_to(top_a + jnp.log(sum_a), (seg, KT))
            lse_ref[h, i, 1] = jnp.broadcast_to(top_b + jnp.log(sum_b), (seg, KT))
            far = rows_of(core * fold.half + (n - 1 - i) * seg)
            near = rows_of(core * fold.half + i * seg)
            up = rows_of(fold.half + (core * (n // 2) + i) * seg)
            o_ref[far, :] += (1.0 - pf) * out_a
            o_ref[near, :] += (1.0 - pf) * out_b
            o_ref[up, :] += pf * out_a
        return 0

    lax.fori_loop(0, heads, head, 0)


def attend_kernel(
    n, heads, head_dim, tab, x_ref, w_ref, q_ref, k_ref, v_ref, o_ref, o32_ref, lse_ref
):
    core = lax.rem(lax.axis_index("ctx"), 2)
    seg = x_ref.shape[2] // 2
    fold = Fold(n, seg)
    project_tokens(n, seg, tab, x_ref, w_ref, q_ref, k_ref, v_ref)
    attend_heads(fold, core, heads, head_dim, tab, q_ref, k_ref, v_ref, o32_ref, lse_ref)
    for c in range(n):
        a = tab[c]
        for u, s in ((0, a), (1, 2 * n - 1 - a)):
            at = pl.ds(pl.multiple_of(s * seg, seg), seg)
            o_ref[c % 2, c // 2, u * seg : (u + 1) * seg, :] = o32_ref[at, :].astype(bf16)


def vmem(count):
    return [pl.BlockSpec(memory_space=pltpu.VMEM)] * count


def attend(tab, n, heads, head_dim, xall, wqkv):
    tok = xall.shape[2]
    seq = tok * n
    return pl.pallas_call(
        functools.partial(attend_kernel, n, heads, head_dim),
        out_shape=(
            jax.ShapeDtypeStruct((seq, LANES), bf16),
            jax.ShapeDtypeStruct((seq, LANES), bf16),
            jax.ShapeDtypeStruct((seq, LANES), bf16),
            jax.ShapeDtypeStruct((2, n // 2, tok, LANES), bf16),
            jax.ShapeDtypeStruct((seq, LANES), f32),
            jax.ShapeDtypeStruct((heads, n // 2, 2, tok // 2, KT), f32),
        ),
        in_specs=[pl.BlockSpec(memory_space=pltpu.SMEM)] + vmem(2),
        out_specs=tuple(vmem(6)),
        compiler_params=pltpu.CompilerParams(vmem_limit_bytes=56 << 20),
        name="attend",
    )(tab, xall, wqkv)


def attend_back_heads(
    fold, core, heads, head_dim, tab, q_ref, k_ref, v_ref, o_ref, lse_ref, da_ref,
    dq_ref, dkn_ref, dvn_ref, dk_ref, dv_ref,
):
    n, seg, half = fold.n, fold.seg, fold.half
    rows_of = lambda at: pl.ds(pl.multiple_of(at, 32), seg)
    for ref in (dq_ref, dkn_ref, dvn_ref):
        ref[...] = jnp.zeros(ref.shape, f32)

    def head(h, _):
        paired = tab[2 * n + h]
        pf = paired.astype(f32)
        lanes = head_mask(h, head_dim, f32)
        lanes16 = head_mask(h, head_dim, bf16)
        dk_ref[...] = jnp.zeros(dk_ref.shape, f32)
        dv_ref[...] = jnp.zeros(dv_ref.shape, f32)
        for i in range(n // 2):
            dqs = []
            places = fold.places(i, core, paired)
            for g, (rows, keys, limit, count) in enumerate(places):
                q = q_ref[rows_of(rows), :] * lanes16
                k, c, upper = natural(tab, n, rows // seg)
                da = da_ref[k, c, pl.ds(pl.multiple_of(upper * seg, seg), seg), :] * lanes16
                delta = jnp.sum(da.astype(f32) * o_ref[rows_of(rows), :], axis=1, keepdims=True)
                lse = lse_ref[h, i, g, :, :1]
                dq = None
                pieces = [(count - 2, 2, True)]
                if count > 2:
                    pieces.append((0, count - 2, False))
                for first, size, masked in pieces:
                    kt = k_ref[key_slice(keys, first, size), :]
                    vt = v_ref[key_slice(keys, first, size), :]
                    pr = jnp.exp(mm(q, kt, NT) - lse)
                    if masked:
                        pr = jnp.where(tail_mask(seg, limit), pr, 0.0)
                    ds = (pr * (mm(da, vt, NT) - delta)).astype(bf16)
                    part = mm(ds, kt)
                    dq = part if dq is None else dq + part
                    dv = mm(pr.astype(bf16), da, TN)
                    dk = mm(ds, q, TN)
                    at = pl.ds(first * KT, size * KT)
                    if g == 0 or masked:
                        dk_ref[at, :] += dk
                        dv_ref[at, :] += dv
                    else:
                        beyond = pl.ds(places[0][3] * KT, size * KT)
                        dk_ref[at, :] += (1.0 - pf) * dk
                        dv_ref[at, :] += (1.0 - pf) * dv
                        dk_ref[beyond, :] += pf * dk
                        dv_ref[beyond, :] += pf * dv
                dqs.append(dq)
            scaled = lanes * score_scale
            dq_a, dq_b = (dqs[0] + pf * dqs[1]) * scaled, dqs[1] * scaled
            far = rows_of(core * half + (n - 1 - i) * seg)
            near = rows_of(core * half + i * seg)
            up = rows_of(half + (core * (n // 2) + i) * seg)
            dq_ref[far, :] += (1.0 - pf) * dq_a
            dq_ref[near, :] += (1.0 - pf) * dq_b
            dq_ref[up, :] += pf * dq_a

        def spread(j, _):
            at = pl.ds(pl.multiple_of(j * seg, seg), seg)
            mine = pl.ds(pl.multiple_of(core * half + j * seg, seg), seg)
            for src, dst in ((dk_ref, dkn_ref), (dv_ref, dvn_ref)):
                dst[mine, :] += (1.0 - pf) * src[at, :]
                dst[at, :] += pf * src[at, :]
            return 0

        lax.fori_loop(0, n, spread, 0)
        return 0

    lax.fori_loop(0, heads, head, 0)


def attend_back_kernel(
    n, heads, head_dim, tab, x_ref, w_ref, q_ref, k_ref, v_ref, o_ref, lse_ref, da_ref,
    dxp_ref, dwp_ref, dq_ref, dkn_ref, dvn_ref, dk_ref, dv_ref, dw_acc,
):
    core = lax.rem(lax.axis_index("ctx"), 2)
    tok = x_ref.shape[2]
    seg = tok // 2
    fold = Fold(n, seg)
    attend_back_heads(
        fold, core, heads, head_dim, tab, q_ref, k_ref, v_ref, o_ref, lse_ref, da_ref,
        dq_ref, dkn_ref, dvn_ref, dk_ref, dv_ref,
    )
    dw_acc[...] = jnp.zeros(dw_acc.shape, f32)

    def block(c, _):
        a = tab[c]
        lo = pl.ds(pl.multiple_of(a * seg, seg), seg)
        up = pl.ds(pl.multiple_of((2 * n - 1 - a) * seg, seg), seg)
        d = jnp.concatenate(
            [
                jnp.concatenate([r[lo, :].astype(bf16), r[up, :].astype(bf16)], axis=0)
                for r in (dq_ref, dkn_ref, dvn_ref)
            ],
            axis=1,
        )
        dxp_ref[lax.rem(c, 2), c // 2] = mm(d, w_ref[...], NT).astype(bf16)
        dw_acc[...] += mm(x_ref[lax.rem(c, 2), c // 2], d, TN)
        return 0

    lax.fori_loop(0, n, block, 0)
    dwp_ref[...] = dw_acc[...].astype(bf16)


def attend_back(tab, n, heads, head_dim, xall, wqkv, q, k, v, o32, lse, da):
    tok, width = xall.shape[2], xall.shape[3]
    seq = tok * n
    full = pltpu.VMEM((seq, LANES), f32)
    half = pltpu.VMEM((seq // 2, LANES), f32)
    return pl.pallas_call(
        functools.partial(attend_back_kernel, n, heads, head_dim),
        out_shape=(
            jax.ShapeDtypeStruct(xall.shape, bf16),
            jax.ShapeDtypeStruct((width, 3 * LANES), bf16),
        ),
        in_specs=[pl.BlockSpec(memory_space=pltpu.SMEM)] + vmem(8),
        out_specs=tuple(vmem(2)),
        scratch_shapes=[full, full, full, half, half, pltpu.VMEM((width, 3 * LANES), f32)],
        compiler_params=pltpu.CompilerParams(vmem_limit_bytes=56 << 20),
        name="attend_back",
    )(tab, xall, wqkv, q, k, v, o32, lse, da)


def norm_forward(h, gain, shift):
    mean = jnp.mean(h, axis=1, keepdims=True)
    center = h - mean
    scale = lax.rsqrt(jnp.mean(center * center, axis=1, keepdims=True) + norm_eps)
    n = center * scale
    return n, scale, n * gain + shift


def norm_backward(cot, n, scale, gain):
    dn = cot * gain
    mean = jnp.mean(dn, axis=1, keepdims=True)
    along = jnp.mean(dn * n, axis=1, keepdims=True)
    return scale * (dn - mean - n * along)


def middle_kernel(
    nz, cols, n_f, x_ref, a_ref, w_ref, cot_ref, out_ref, da_ref, g_ref, dh_ref,
    w1, w2, wo, lnb, u_ref, z_ref, x1b_ref, acc_ref, n1_ref, r1_ref, dx1_ref, sems,
):
    tok, width = x_ref.shape
    f_rows = w2.shape[1]
    d_rows = cols
    o1, o2, o3 = f_rows, f_rows + n_f * d_rows, f_rows + n_f * d_rows + d_rows
    copies = []

    def fetch(src, dst):
        cp = pltpu.make_async_copy(src, dst, sems.at[len(copies)])
        cp.start()
        copies.append(cp)
        return cp

    first = [fetch(w_ref.at[o, o2:o3], wo.at[o]) for o in range(nz)]
    first += [fetch(w_ref.at[o, o3 : o3 + 16], lnb.at[o]) for o in range(nz)]
    inner = [
        [
            fetch(
                w_ref.at[o, o1 + f * d_rows : o1 + (f + 1) * d_rows],
                w1.at[f, o * d_rows : (o + 1) * d_rows],
            )
            for o in range(nz)
        ]
        for f in range(n_f)
    ]
    outer = [fetch(w_ref.at[o, :f_rows], w2.at[o]) for o in range(nz)]
    for cp in first:
        cp.wait()
    vec = lnb[0].astype(f32)
    for o in range(1, nz):
        vec = vec + lnb[o].astype(f32)
    gain1, gain2, shift1, shift2 = vec[0:1], vec[1:2], vec[2:3], vec[3:4]
    h1 = x_ref[...].astype(f32)
    for o in range(nz):
        h1 = h1 + mm(a_ref[o, :, :cols], wo[o])
    n1, r1, x1 = norm_forward(h1, gain1, shift1)
    n1_ref[...] = n1
    r1_ref[...] = jnp.broadcast_to(r1, (tok, 128))
    x1b_ref[...] = x1.astype(bf16)
    acc_ref[...] = x1
    for group in inner:
        for cp in group:
            cp.wait()
    for cp in outer:
        cp.wait()

    def up(f, _):
        u = mm(x1b_ref[...], w1[f])
        cdf = 0.5 + 0.5 * lax.erf(u * (0.5**0.5))
        z = (u * cdf).astype(bf16)
        z_ref[f] = z
        u_ref[f] = (cdf + u * jnp.exp(-0.5 * u * u) * 0.3989422804014327).astype(u_ref.dtype)
        acc_ref[...] += mm(z, w2[f])
        return 0

    lax.fori_loop(0, n_f, up, 0)
    n2, r2, out = norm_forward(acc_ref[...], gain2, shift2)
    out_ref[...] = out.astype(bf16)
    cot = cot_ref[...].astype(f32)
    d_gain2 = jnp.sum(cot * n2, axis=0, keepdims=True)
    d_shift2 = jnp.sum(cot, axis=0, keepdims=True)
    dh2 = norm_backward(cot, n2, r2, gain2)
    dx1_ref[...] = dh2
    df = dh2.astype(bf16)

    def back(f, _):
        g_ref[f, :f_rows, :] = mm(z_ref[f], df, TN).astype(bf16)
        du = (mm(df, w2[f], NT) * u_ref[f].astype(f32)).astype(bf16)
        dw = mm(x1b_ref[...], du, TN).astype(bf16)
        for o in range(nz):
            at = pl.ds(pl.multiple_of(o1 + f * d_rows, 16), d_rows)
            g_ref[o, at, :] = dw[o * d_rows : (o + 1) * d_rows]
        dx1_ref[...] += mm(du, w1[f], NT)
        return 0

    lax.fori_loop(0, n_f, back, 0)
    d_x1 = dx1_ref[...]
    n1 = n1_ref[...]
    d_gain1 = jnp.sum(d_x1 * n1, axis=0, keepdims=True)
    d_shift1 = jnp.sum(d_x1, axis=0, keepdims=True)
    dh1 = norm_backward(d_x1, n1, r1_ref[:, :1], gain1)
    dh_ref[...] = dh1
    dy = dh1.astype(bf16)
    total = g_ref.shape[1]
    norms = jnp.concatenate([d_gain1, d_gain2, d_shift1, d_shift2], axis=0).astype(bf16)
    for o in range(nz):
        g_ref[o, o2:o3, :] = mm(a_ref[o, :, :cols], dy, TN).astype(bf16)
        g_ref[o, o3:, :] = jnp.zeros((total - o3, width), bf16)
        g_ref[o, o3 : o3 + 4, :] = norms
        da_ref[o, :, :cols] = mm(dy, wo[o], NT).astype(bf16)
        da_ref[o, :, cols:] = jnp.zeros((tok, LANES - cols), bf16)


def middle(nz, cols, n_f, x_in, attn, wfull, cot):
    tok, width = x_in.shape
    vm = lambda dt, *shape: pltpu.VMEM(shape, dt)
    return pl.pallas_call(
        functools.partial(middle_kernel, nz, cols, n_f),
        out_shape=(
            jax.ShapeDtypeStruct((tok, width), bf16),
            jax.ShapeDtypeStruct((nz, tok, LANES), bf16),
            jax.ShapeDtypeStruct(wfull.shape, bf16),
            jax.ShapeDtypeStruct((tok, width), f32),
        ),
        in_specs=vmem(2) + hbm(1) + vmem(1),
        out_specs=tuple(vmem(4)),
        scratch_shapes=[
            vm(bf16, n_f, width, width),
            vm(bf16, nz, width, width),
            vm(bf16, nz, cols, width),
            vm(bf16, nz, 16, width),
            vm(f32, n_f, tok, width),
            vm(bf16, n_f, tok, width),
            vm(bf16, tok, width),
            vm(f32, tok, width),
            vm(f32, tok, width),
            vm(f32, tok, 128),
            vm(f32, tok, width),
            pltpu.SemaphoreType.DMA((3 * nz + n_f * nz,)),
        ],
        compiler_params=pltpu.CompilerParams(vmem_limit_bytes=60 << 20),
        name="middle",
    )(x_in, attn, wfull, cot)


def fast_body(
    tokens,
    w_query,
    w_key,
    w_value,
    w_output,
    w_inner,
    w_outer,
    ln_gain,
    ln_bias,
    pairing,
    block_pairs,
    cotangent,
):
    tok, width = tokens.shape[1], tokens.shape[2]
    n_ctx, nz = lax.axis_size("ctx"), lax.axis_size("fsdp")
    heads = pairing.shape[1]
    head_dim = width // heads
    my_heads = heads // 4
    cols = my_heads * head_dim
    chip = lax.axis_index("ctx") // 2
    d_rows = w_query.shape[0]
    f_rows, ff = w_outer.shape[0], w_inner.shape[1]
    n_f = ff // width
    x_in = tokens[0]

    def chip_cols(w):
        part = lax.dynamic_slice_in_dim(w, chip * cols, cols, 1).astype(bf16)
        return jnp.pad(part, ((0, 0), (0, LANES - cols)))

    wsel = jnp.concatenate([chip_cols(w) for w in (w_query, w_key, w_value)], axis=1)
    z = lax.axis_index("fsdp")
    norms = jnp.concatenate([ln_gain.T, ln_bias.T], axis=0).astype(bf16)
    used = f_rows + n_f * d_rows + d_rows
    total = -(-(used + 4) // 256) * 256
    norms = lax.dynamic_update_slice(jnp.zeros((total - used, width), bf16), norms, (0, z * d_rows))
    wcat = jnp.concatenate(
        [w_outer.astype(bf16)]
        + [w_inner[:, i * width : (i + 1) * width].astype(bf16) for i in range(n_f)]
        + [w_output.astype(bf16), norms],
        axis=0,
    ).reshape(2, 4, total // 8, width)
    xall, wqkv, wfull = gather_all(nz, x_in, wsel, wcat)
    wqkv = wqkv.reshape(width, 3 * LANES)
    wfull = wfull.reshape(nz, total, width)

    lower = block_pairs[0]
    ranks = jnp.arange(n_ctx, dtype=jnp.int32)
    inverse = jnp.sum(
        jnp.where(lower[None, :] == ranks[:, None], ranks[None, :], 0), axis=1
    ).astype(jnp.int32)
    flags = lax.dynamic_slice_in_dim(pairing[0], chip * my_heads, my_heads, 0)
    tab = jnp.concatenate([lower, inverse, flags])
    q, k, v, o16, o32, lse = attend(tab, n_ctx, my_heads, head_dim, xall, wqkv)
    attn = to_owners(o16)
    result, da, grads, d_h1 = middle(nz, cols, n_f, x_in, attn, wfull, cotangent[0])
    da = to_heads(da)
    dxp, dwp = attend_back(tab, n_ctx, my_heads, head_dim, xall, wqkv, q, k, v, o32, lse, da)
    grads = grads.reshape(nz, 2, 4, total // 8, width)
    gsum, dtok, dwsum = reduce_all(nz, grads, dxp, dwp.reshape(nz, d_rows, width), d_h1)
    gsum = gsum.reshape(total, width)
    dwsum = dwsum.transpose(1, 0, 2, 3).reshape(4, d_rows, 3, LANES)[:, :, :, :cols]
    dwsum = dwsum.transpose(2, 1, 0, 3).reshape(3, d_rows, width).astype(f32)
    o1, o2 = f_rows, f_rows + n_f * d_rows
    g_inner = [gsum[o1 + i * d_rows : o1 + (i + 1) * d_rows] for i in range(n_f)]
    g_norms = lax.dynamic_slice(gsum[used : used + 4], (0, z * d_rows), (4, d_rows)).astype(f32)
    return (
        result[None],
        dtok[None],
        dwsum[0],
        dwsum[1],
        dwsum[2],
        gsum[o2:used].astype(f32),
        jnp.concatenate(g_inner, axis=1).astype(f32),
        gsum[:o1].astype(f32),
        g_norms[:2].T,
        g_norms[2:].T,
    )


def solution(mesh):
    in_specs = (
        P("fsdp", "ctx", None),
        P("fsdp", None),
        P("fsdp", None),
        P("fsdp", None),
        P("fsdp", None),
        P("fsdp", None),
        P("fsdp", None),
        P("fsdp", None),
        P("fsdp", None),
        P("fsdp", None),
        P("fsdp", None),
        P("fsdp", "ctx", None),
    )
    out_specs = (
        P("fsdp", "ctx", None),
        P("fsdp", "ctx", None),
        P("fsdp", None),
        P("fsdp", None),
        P("fsdp", None),
        P("fsdp", None),
        P("fsdp", None),
        P("fsdp", None),
        P("fsdp", None),
        P("fsdp", None),
    )
    fast = mesh.shape["ctx"] == 8 and mesh.shape["fsdp"] == 4
    chosen = fast_body if fast else generic_body
    return jax.shard_map(chosen, mesh=mesh, in_specs=in_specs, out_specs=out_specs, check_vma=False)
```

```python
import functools

import jax
import jax.numpy as jnp
from jax import lax
from jax.experimental import pallas as pl
from jax.experimental.pallas import tpu as pltpu
from jax.sharding import PartitionSpec as P

norm_eps = 1e-05
score_scale = 0.125
very_low = -1e30


def shortened(value):

    def short(part):
        return part.astype(jnp.bfloat16) if part.dtype == jnp.float32 else part

    return jax.tree.map(short, value)


def layer_norm(values, norm_gain, norm_shift):
    center = values - jnp.mean(values, axis=-1, keepdims=True)
    spread = jnp.mean(center * center, axis=-1, keepdims=True)
    return center * lax.rsqrt(spread + norm_eps) * norm_gain + norm_shift


def exact_gelu(values):
    return jax.nn.gelu(values, approximate=False)


def project(rows_in, weight):
    return jnp.dot(rows_in, weight, preferred_element_type=jnp.float32)


def seq_positions(pair_row, tok_dev, seq_len):
    segment_len = tok_dev // 2
    within = jnp.arange(tok_dev, dtype=jnp.int32)
    lower_pos = pair_row[:, None] * segment_len + within[None, :]
    upper_pos = seq_len - (pair_row[:, None] + 1) * segment_len + within[None, :] - segment_len
    return jnp.where(within[None, :] < segment_len, lower_pos, upper_pos).reshape(-1)


def pair_mask(query_pos, key_pos, head_flags, half_len):
    target = (query_pos[None, :] // half_len + head_flags[:, None]) % 2
    paired = key_pos[None, None, :] // half_len == target[:, :, None]
    causal = key_pos[None, :] <= query_pos[:, None]
    return jnp.logical_and(paired, causal[None, :, :])


def block_rows(tok_dev):
    return 2 * tok_dev


def over_blocks(running, arrays, step_fn, tok_dev):
    row_count = arrays[0].shape[0]
    block_len = block_rows(tok_dev)

    def one_step(inner_carry, step_index):
        first_row = step_index * block_len
        sliced = tuple(
            (lax.dynamic_slice_in_dim(member, first_row, block_len, 0) for member in arrays)
        )
        return (step_fn(inner_carry, sliced, first_row), None)

    return lax.scan(one_step, running, jnp.arange(row_count // block_len, dtype=jnp.int32))[0]


def generic_body(
    tokens,
    w_query,
    w_key,
    w_value,
    w_output,
    w_inner,
    w_outer,
    ln_gain,
    ln_bias,
    pairing,
    block_pairs,
    cotangent,
):
    tok_dev = tokens.shape[1]
    width = tokens.shape[2]
    heads = pairing.shape[1]
    head_dim = width // heads
    n_ctx = lax.axis_size("ctx")
    seq_len = tok_dev * n_ctx
    half_len = seq_len // 2
    pos_all = seq_positions(block_pairs[0], tok_dev, seq_len)
    my_pos = lax.dynamic_slice_in_dim(pos_all, lax.axis_index("ctx") * tok_dev, tok_dev, 0)
    head_flags = pairing[0]
    masters = (w_query, w_key, w_value, w_output, w_inner, w_outer, ln_gain, ln_bias)
    low_masters = tuple((member.astype(jnp.bfloat16) for member in masters))
    gathered = jax.tree.map(
        lambda part, own: part.astype(own.dtype),
        lax.all_gather(shortened(low_masters), "fsdp", axis=0, tiled=True),
        low_masters,
    )
    wq_full, wk_full, wv_full, wo_full, inner_full, outer_full, gain_full, shift_full = gathered
    gain_wide = gain_full.astype(jnp.float32)
    shift_wide = shift_full.astype(jnp.float32)
    x_in = tokens[0]
    query_b = project(x_in, wq_full).astype(jnp.bfloat16)
    key_b = project(x_in, wk_full).astype(jnp.bfloat16)
    value_b = project(x_in, wv_full).astype(jnp.bfloat16)
    q_heads = query_b.reshape(tok_dev, heads, head_dim)

    def attend_step(running, sliced, offset):
        run_max, run_sum, run_acc = running
        key_block, value_block = sliced
        block_len = key_block.shape[0]
        key_pos = lax.dynamic_slice_in_dim(pos_all, offset, block_len, 0)
        allowed = pair_mask(my_pos, key_pos, head_flags, half_len)
        key_heads = key_block.reshape(block_len, heads, head_dim)
        value_heads = value_block.reshape(block_len, heads, head_dim)
        scores = (
            jnp.einsum("qhd,khd->hqk", q_heads, key_heads, preferred_element_type=jnp.float32)
            * score_scale
        )
        new_max = jnp.maximum(run_max, jnp.max(jnp.where(allowed, scores, very_low), axis=2))
        prob_rows = jnp.where(
            allowed, jnp.exp(jnp.where(allowed, scores - new_max[:, :, None], 0.0)), 0.0
        )
        decay = jnp.exp(run_max - new_max)
        new_sum = run_sum * decay + jnp.sum(prob_rows, axis=2)
        added = jnp.einsum(
            "hqk,khd->hqd",
            prob_rows.astype(jnp.bfloat16),
            value_heads,
            preferred_element_type=jnp.float32,
        )
        return (new_max, new_sum, run_acc * decay[:, :, None] + added)

    def pair_fold(step_fn, running, fetched):
        return over_blocks(running, fetched, step_fn, tok_dev)

    start_state = (
        jnp.full((heads, tok_dev), very_low, jnp.float32),
        jnp.zeros((heads, tok_dev), jnp.float32),
        jnp.zeros((heads, tok_dev, head_dim), jnp.float32),
    )
    run_max, run_sum, run_acc = pair_fold(
        attend_step,
        start_state,
        (
            lax.all_gather(key_b, "ctx", axis=0, tiled=True),
            lax.all_gather(value_b, "ctx", axis=0, tiled=True),
        ),
    )
    live_rows = run_sum > 0
    safe_sum = jnp.where(live_rows, run_sum, 1.0)
    attn_heads = jnp.where(live_rows[:, :, None], run_acc / safe_sum[:, :, None], 0.0)
    lse_rows = jnp.where(live_rows, run_max + jnp.log(safe_sum), 0.0)
    attn_rows = attn_heads.transpose(1, 0, 2).reshape(tok_dev, width)
    attn_b = attn_rows.astype(jnp.bfloat16)
    branch = project(attn_b, wo_full)
    first_norm, first_pull = jax.vjp(
        layer_norm, x_in.astype(jnp.float32) + branch, gain_wide[:, 0], shift_wide[:, 0]
    )
    first_b = first_norm.astype(jnp.bfloat16)
    inner = project(first_b, inner_full)
    active, gelu_pull = jax.vjp(exact_gelu, inner)
    active_b = active.astype(jnp.bfloat16)
    outer = project(active_b, outer_full)
    result, second_pull = jax.vjp(layer_norm, first_norm + outer, gain_wide[:, 1], shift_wide[:, 1])
    wq_back, wk_back, wv_back, wo_back, inner_back, outer_back, gain_back, shift_back = gathered
    d_h2, d_gain2, d_shift2 = second_pull(cotangent[0].astype(jnp.float32))
    d_f_b = d_h2.astype(jnp.bfloat16)
    d_outer = jnp.dot(active_b.T, d_f_b, preferred_element_type=jnp.float32)
    d_active = jnp.dot(d_f_b, outer_back.T, preferred_element_type=jnp.float32)
    d_u_b = gelu_pull(d_active)[0].astype(jnp.bfloat16)
    d_inner = jnp.dot(first_b.T, d_u_b, preferred_element_type=jnp.float32)
    d_x1 = d_h2 + jnp.dot(d_u_b, inner_back.T, preferred_element_type=jnp.float32)
    d_h1, d_gain1, d_shift1 = first_pull(d_x1)
    d_y_b = d_h1.astype(jnp.bfloat16)
    d_wo = jnp.dot(attn_b.T, d_y_b, preferred_element_type=jnp.float32)
    d_attn_b = jnp.dot(d_y_b, wo_back.T, preferred_element_type=jnp.float32).astype(jnp.bfloat16)
    delta_rows = (
        (d_attn_b.astype(jnp.float32) * attn_rows).reshape(tok_dev, heads, head_dim).sum(axis=2).T
    )
    dout_heads = d_attn_b.reshape(tok_dev, heads, head_dim)

    def query_grad_step(dq_acc, sliced, offset):
        key_block, value_block = sliced
        block_len = key_block.shape[0]
        key_pos = lax.dynamic_slice_in_dim(pos_all, offset, block_len, 0)
        allowed = pair_mask(my_pos, key_pos, head_flags, half_len)
        key_heads = key_block.reshape(block_len, heads, head_dim)
        value_heads = value_block.reshape(block_len, heads, head_dim)
        scores = (
            jnp.einsum("qhd,khd->hqk", q_heads, key_heads, preferred_element_type=jnp.float32)
            * score_scale
        )
        prob_rows = jnp.where(
            allowed, jnp.exp(jnp.where(allowed, scores - lse_rows[:, :, None], 0.0)), 0.0
        )
        prob_grad = jnp.einsum(
            "qhd,khd->hqk", dout_heads, value_heads, preferred_element_type=jnp.float32
        )
        dscore = (prob_rows * (prob_grad - delta_rows[:, :, None]) * score_scale).astype(
            jnp.bfloat16
        )
        return dq_acc + jnp.einsum(
            "hqk,khd->qhd", dscore, key_heads, preferred_element_type=jnp.float32
        )

    dq_start = jnp.zeros((tok_dev, heads, head_dim), jnp.float32)
    dq_acc = pair_fold(
        query_grad_step,
        dq_start,
        (
            lax.all_gather(key_b, "ctx", axis=0, tiled=True),
            lax.all_gather(value_b, "ctx", axis=0, tiled=True),
        ),
    )
    dq_b = dq_acc.reshape(tok_dev, width).astype(jnp.bfloat16)
    lse_all, delta_all = (
        lax.all_gather(lse_rows, "ctx", axis=1, tiled=True),
        lax.all_gather(delta_rows, "ctx", axis=1, tiled=True),
    )
    k_heads = key_b.reshape(tok_dev, heads, head_dim)
    v_heads = value_b.reshape(tok_dev, heads, head_dim)

    def key_grad_step(running, sliced, offset):
        dk_acc, dv_acc = running
        query_block, dout_block = sliced
        block_len = query_block.shape[0]
        query_pos = lax.dynamic_slice_in_dim(pos_all, offset, block_len, 0)
        lse_block = lax.dynamic_slice_in_dim(lse_all, offset, block_len, 1)
        delta_block = lax.dynamic_slice_in_dim(delta_all, offset, block_len, 1)
        allowed = pair_mask(query_pos, my_pos, head_flags, half_len)
        query_heads = query_block.reshape(block_len, heads, head_dim)
        dout_block_heads = dout_block.reshape(block_len, heads, head_dim)
        scores = (
            jnp.einsum("qhd,khd->hqk", query_heads, k_heads, preferred_element_type=jnp.float32)
            * score_scale
        )
        prob_rows = jnp.where(
            allowed, jnp.exp(jnp.where(allowed, scores - lse_block[:, :, None], 0.0)), 0.0
        )
        dv_acc = dv_acc + jnp.einsum(
            "hqk,qhd->khd",
            prob_rows.astype(jnp.bfloat16),
            dout_block_heads,
            preferred_element_type=jnp.float32,
        )
        prob_grad = jnp.einsum(
            "qhd,khd->hqk", dout_block_heads, v_heads, preferred_element_type=jnp.float32
        )
        dscore = (prob_rows * (prob_grad - delta_block[:, :, None]) * score_scale).astype(
            jnp.bfloat16
        )
        dk_acc = dk_acc + jnp.einsum(
            "hqk,qhd->khd", dscore, query_heads, preferred_element_type=jnp.float32
        )
        return (dk_acc, dv_acc)

    kv_start = (
        jnp.zeros((tok_dev, heads, head_dim), jnp.float32),
        jnp.zeros((tok_dev, heads, head_dim), jnp.float32),
    )
    dk_acc, dv_acc = pair_fold(
        key_grad_step,
        kv_start,
        (
            lax.all_gather(query_b, "ctx", axis=0, tiled=True),
            lax.all_gather(d_attn_b, "ctx", axis=0, tiled=True),
        ),
    )
    dk_b = dk_acc.reshape(tok_dev, width).astype(jnp.bfloat16)
    dv_b = dv_acc.reshape(tok_dev, width).astype(jnp.bfloat16)
    d_input = d_h1 + jnp.dot(dq_b, wq_back.T, preferred_element_type=jnp.float32)
    d_input = d_input + jnp.dot(dk_b, wk_back.T, preferred_element_type=jnp.float32)
    d_input = d_input + jnp.dot(dv_b, wv_back.T, preferred_element_type=jnp.float32)
    terms = (
        jnp.dot(x_in.T, dq_b, preferred_element_type=jnp.float32),
        jnp.dot(x_in.T, dk_b, preferred_element_type=jnp.float32),
        jnp.dot(x_in.T, dv_b, preferred_element_type=jnp.float32),
        d_wo,
        d_inner,
        d_outer,
        jnp.stack([d_gain1, d_gain2], axis=1),
        jnp.stack([d_shift1, d_shift2], axis=1),
    )
    shares = (
        lax.psum_scatter(
            terms[0].astype(jnp.bfloat16), "fsdp", scatter_dimension=0, tiled=True
        ).astype(jnp.float32),
        lax.psum_scatter(
            terms[1].astype(jnp.bfloat16), "fsdp", scatter_dimension=0, tiled=True
        ).astype(jnp.float32),
        lax.psum_scatter(
            terms[2].astype(jnp.bfloat16), "fsdp", scatter_dimension=0, tiled=True
        ).astype(jnp.float32),
        lax.psum_scatter(
            terms[3].astype(jnp.bfloat16), "fsdp", scatter_dimension=0, tiled=True
        ).astype(jnp.float32),
        lax.psum_scatter(
            terms[4].astype(jnp.bfloat16), "fsdp", scatter_dimension=0, tiled=True
        ).astype(jnp.float32),
        lax.psum_scatter(
            terms[5].astype(jnp.bfloat16), "fsdp", scatter_dimension=0, tiled=True
        ).astype(jnp.float32),
        lax.psum_scatter(
            terms[6].astype(jnp.bfloat16), "fsdp", scatter_dimension=0, tiled=True
        ).astype(jnp.float32),
        lax.psum_scatter(
            terms[7].astype(jnp.bfloat16), "fsdp", scatter_dimension=0, tiled=True
        ).astype(jnp.float32),
    )
    totals = (
        lax.psum(shares[0].astype(jnp.bfloat16), "ctx").astype(jnp.float32),
        lax.psum(shares[1].astype(jnp.bfloat16), "ctx").astype(jnp.float32),
        lax.psum(shares[2].astype(jnp.bfloat16), "ctx").astype(jnp.float32),
        lax.psum(shares[3].astype(jnp.bfloat16), "ctx").astype(jnp.float32),
        lax.psum(shares[4].astype(jnp.bfloat16), "ctx").astype(jnp.float32),
        lax.psum(shares[5].astype(jnp.bfloat16), "ctx").astype(jnp.float32),
        lax.psum(shares[6].astype(jnp.bfloat16), "ctx").astype(jnp.float32),
        lax.psum(shares[7].astype(jnp.bfloat16), "ctx").astype(jnp.float32),
    )
    return (
        result.astype(jnp.bfloat16)[None],
        d_input.astype(jnp.bfloat16)[None],
        totals[0],
        totals[1],
        totals[2],
        totals[3],
        totals[4],
        totals[5],
        totals[6],
        totals[7],
    )


MESH = pl.DeviceIdType.MESH
f32 = jnp.float32
bf16 = jnp.bfloat16


class Place:
    def __init__(self):
        me = lax.axis_index("ctx")
        self.me = me
        self.z = lax.axis_index("fsdp")
        self.core = lax.rem(me, 2)
        self.chip = me // 2
        self.x = lax.rem(self.chip, 2)
        self.y = self.chip // 2
        self.chip_x = self.chip + 1 - 2 * self.x
        self.chip_y = self.chip + 2 - 4 * self.y
        self.chip_d = 3 - self.chip
        self.sib = (2 * self.chip + 1 - self.core, self.z)
        self.xn = (2 * self.chip_x + self.core, self.z)
        self.yn = (2 * self.chip_y + self.core, self.z)
        self.dn = (2 * self.chip_d + self.core, self.z)
        self.up = (me, self.z + 1)
        self.down = (me, self.z - 1)


def greet(place, others, line_len=None):
    barrier = pltpu.get_barrier_semaphore()
    count = len(others)
    for other in others:
        pl.semaphore_signal(barrier, inc=1, device_id=other, device_id_type=MESH)
    if line_len is not None:

        @pl.when(place.z < line_len - 1)
        def _():
            pl.semaphore_signal(barrier, inc=1, device_id=place.up, device_id_type=MESH)

        @pl.when(place.z > 0)
        def _():
            pl.semaphore_signal(barrier, inc=1, device_id=place.down, device_id_type=MESH)

        count = count + jnp.where(place.z < line_len - 1, 1, 0) + jnp.where(place.z > 0, 1, 0)

    pl.semaphore_wait(barrier, count)


def maybe(cond, fn):
    if cond is None:
        fn()
    else:
        pl.when(cond)(fn)


class Net:
    def __init__(self, send_sems, recv_sems, count):
        self.send_sems, self.recv_sems, self.count = send_sems, recv_sems, count
        self.used = 0
        self.open = []

    def new(self):
        self.used += 1
        assert self.used <= self.count
        return self.used - 1

    def copy(self, idx, src, dst, dev):
        return pltpu.make_async_remote_copy(
            src_ref=src,
            dst_ref=dst,
            send_sem=self.send_sems.at[idx],
            recv_sem=self.recv_sems.at[idx],
            device_id=dev,
            device_id_type=MESH,
        )

    def send(self, idx, src, dst, dev, cond=None):
        cp = self.copy(idx, src, dst, dev)
        maybe(cond, cp.start)
        self.open.append((cond, cp))

    def recv(self, idx, dst, dev, cond=None):
        cp = self.copy(idx, dst, dst, dev)
        maybe(cond, cp.wait_recv)

    def finish(self):
        for cond, cp in self.open:
            maybe(cond, cp.wait_send)
        self.open = []


class PlaneGather:
    def __init__(self, net, place, own, slot, rows, cond=None):
        self.net, self.place, self.own, self.slot, self.cond = net, place, own, slot, cond
        self.h0, self.h1 = pl.ds(0, rows // 2), pl.ds(rows // 2, rows // 2)
        self.ids = [net.new() for _ in range(12)]

    def first(self):
        n, p, i, c = self.net, self.place, self.ids, self.cond
        mine = self.slot(p.core, p.chip)
        n.send(i[0], self.own.at[self.h0], mine.at[self.h0], p.xn, c)
        n.send(i[1], self.own.at[self.h1], mine.at[self.h1], p.yn, c)
        n.send(i[2], self.own.at[self.h1], mine.at[self.h1], p.xn, c)
        n.send(i[3], self.own.at[self.h0], mine.at[self.h0], p.yn, c)
        n.send(i[4], self.own, mine, p.sib, c)

    def second(self):
        n, p, i, c = self.net, self.place, self.ids, self.cond
        bx, by = self.slot(p.core, p.chip_x), self.slot(p.core, p.chip_y)
        n.recv(i[0], bx.at[self.h0], p.xn, c)
        n.send(i[5], bx.at[self.h0], bx.at[self.h0], p.yn, c)
        n.recv(i[1], by.at[self.h1], p.yn, c)
        n.send(i[6], by.at[self.h1], by.at[self.h1], p.xn, c)
        n.recv(i[2], bx.at[self.h1], p.xn, c)
        n.send(i[7], bx, bx, p.sib, c)
        n.recv(i[3], by.at[self.h0], p.yn, c)
        n.send(i[8], by, by, p.sib, c)

    def third(self):
        n, p, i, c = self.net, self.place, self.ids, self.cond
        bd = self.slot(p.core, p.chip_d)
        n.recv(i[5], bd.at[self.h0], p.yn, c)
        n.send(i[9], bd.at[self.h0], bd.at[self.h0], p.sib, c)
        n.recv(i[6], bd.at[self.h1], p.xn, c)
        n.send(i[10], bd.at[self.h1], bd.at[self.h1], p.sib, c)

    def last(self):
        n, p, i, c = self.net, self.place, self.ids, self.cond
        o = 1 - p.core
        n.recv(i[4], self.slot(o, p.chip), p.sib, c)
        n.recv(i[7], self.slot(o, p.chip_x), p.sib, c)
        n.recv(i[8], self.slot(o, p.chip_y), p.sib, c)
        bd = self.slot(o, p.chip_d)
        n.recv(i[9], bd.at[self.h0], p.sib, c)
        n.recv(i[10], bd.at[self.h1], p.sib, c)


def hbm(count):
    return [pl.BlockSpec(memory_space=pltpu.HBM)] * count


def comm_params(collective_id):
    return pltpu.CompilerParams(
        collective_id=collective_id, has_side_effects=True, vmem_limit_bytes=56 << 20
    )


def vmem(count):
    return [pl.BlockSpec(memory_space=pltpu.VMEM)] * count


def smem(count):
    return [pl.BlockSpec(memory_space=pltpu.SMEM)] * count


LANES = 256
KT = 128
NT = (((1,), (1,)), ((), ()))
TN = (((0,), (0,)), ((), ()))
NN = (((1,), (0,)), ((), ()))


def mm(a, b, dims=NN):
    return lax.dot_general(a, b, dims, preferred_element_type=f32)


def head_mask(h, head_dim, dtype):
    lane = lax.broadcasted_iota(jnp.int32, (1, LANES), 1)
    inside = jnp.logical_and(lane >= h * head_dim, lane < (h + 1) * head_dim)
    return jnp.where(inside, 1.0, 0.0).astype(dtype)


class Fold:
    def __init__(self, n, seg):
        self.n, self.seg, self.half = n, seg, n * seg
        self.tiles = self.half // KT

    def ranges(self, i):
        a = -(-(self.n - i) * self.seg // KT)
        b = -(-(i + 1) * self.seg // KT)
        assert a + b == self.tiles + 2
        return a, b

    def places(self, i, core, paired):
        a, b = self.ranges(i)
        n, seg = self.n, self.seg
        causal = 1 - paired
        up = n + core * (n // 2) + i
        rows_a = (core * n + n - 1 - i) * causal + up * paired
        rows_b = (core * n + i) * causal + up * paired
        keys_a = core * self.tiles * causal
        keys_b = core * self.tiles * causal + a * paired
        lim_a = (n - 1 - i) * seg - (a - 2) * KT + (1 << 20) * paired
        lim_b = i * seg - (b - 2) * KT - (1 << 20) * paired
        return (rows_a, keys_a, lim_a, a), (rows_b, keys_b, lim_b, b)


def natural(tab, n, s):
    upper = lax.div(s, n)
    c = tab[n + s + upper * (2 * n - 1 - 2 * s)]
    return lax.rem(c, 2), lax.div(c, 2), upper


def key_tiles(ref, base, first, count):
    return ref[pl.ds(base + first, count)].reshape(count * KT, LANES)


def tail_mask(seg, limit):
    col = lax.broadcasted_iota(jnp.int32, (seg, 2 * KT), 1)
    row = lax.broadcasted_iota(jnp.int32, (seg, 2 * KT), 0)
    return col - row <= limit


def fill_table(tab, pairs, pairing, chip, n, heads):
    for c in range(n):
        tab[c] = pairs[0, c]
    for a in range(n):
        found = jnp.int32(0)
        for c in range(n):
            found = found + (pairs[0, c] == a).astype(jnp.int32) * c
        tab[n + a] = jnp.minimum(found, n - 1)
    for h in range(heads):
        tab[2 * n + h] = pairing[0, chip * heads + h]


def lse_lane(fold, h, i, g):
    return (h * (fold.n // 2) + i) * 2 + g


def attend_unit(fold, core, h, i, head_dim, tab, q_ref, k_ref, v_ref, o_ref, lse_ref):
    n, seg = fold.n, fold.seg
    paired = tab[2 * n + h]
    pf = paired.astype(f32)
    lanes = head_mask(h, head_dim, f32)
    lanes16 = head_mask(h, head_dim, bf16)
    parts = []
    for rows, keys, limit, count in fold.places(i, core, paired):
        q = q_ref[rows] * lanes16
        tail = mm(q, key_tiles(k_ref, keys, count - 2, 2), NT)
        tail = jnp.where(tail_mask(seg, limit), tail, very_low)
        top = jnp.max(tail, axis=1, keepdims=True)
        main = None
        if count > 2:
            main = mm(q, key_tiles(k_ref, keys, 0, count - 2), NT)
            top = jnp.maximum(top, jnp.max(main, axis=1, keepdims=True))
        parts.append((keys, count, main, tail, top))
    both = jnp.maximum(parts[0][4], parts[1][4])
    joined = jnp.broadcast_to(paired, both.shape) == 1
    outs = []
    for keys, count, main, tail, top in parts:
        top = jnp.where(joined, both, top)
        e = jnp.exp(tail - top)
        total = jnp.sum(e, axis=1, keepdims=True)
        acc = mm(e.astype(bf16), key_tiles(v_ref, keys, count - 2, 2))
        if main is not None:
            e = jnp.exp(main - top)
            total += jnp.sum(e, axis=1, keepdims=True)
            acc += mm(e.astype(bf16), key_tiles(v_ref, keys, 0, count - 2))
        outs.append((top, total, acc))
    (top_a, sum_a, acc_a), (top_b, sum_b, acc_b) = outs
    sum_a, sum_b = sum_a + pf * sum_b, jnp.where(joined, sum_a + sum_b, sum_b)
    acc_a = acc_a + pf * acc_b
    out_a = acc_a * (lanes / sum_a)
    out_b = acc_b * (lanes / sum_b)
    lane = lax.broadcasted_iota(jnp.int32, (1, KT), 1)
    lse = jnp.where(lane == lse_lane(fold, h, i, 0), top_a + jnp.log(sum_a), lse_ref[...])
    lse_ref[...] = jnp.where(lane == lse_lane(fold, h, i, 1), top_b + jnp.log(sum_b), lse)
    far, near, up = core * n + n - 1 - i, core * n + i, n + core * (n // 2) + i
    for at, value in ((far, (1.0 - pf) * out_a), (near, (1.0 - pf) * out_b), (up, pf * out_a)):
        o_ref[at] += value.astype(bf16)


def forward_kernel(
    nz, n, heads, head_dim, rb, n_sem,
    pairs, pairing, x_ref, wsel_ref, wcat_ref,
    xall_o, wqkv_o, q_o, k_o, v_o, on_o, lse_o, attn_o, wfull_o,
    tab, xall, wqkv, q_ref, k_ref, v_ref, o_nat, o_ctx, o_part, o_sum, ssem, rsem, lsem,
):
    p = Place()
    z = p.z
    seg = x_ref.shape[1]
    fold = Fold(n, seg)
    ra = wcat_ref.shape[2] - rb
    ax, bx = pl.ds(0, ra), pl.ds(ra, rb)
    half = wsel_ref.shape[0] // 2
    locals_ = []

    def keep(src, dst):
        cp = pltpu.make_async_copy(src, dst, lsem.at[len(locals_)])
        cp.start()
        locals_.append(cp)
        return cp

    own_x = keep(x_ref, xall.at[p.core, p.chip])
    own_w = keep(wsel_ref, wqkv.at[z])
    greet(p, (p.sib, p.xn, p.yn, p.dn), nz)
    net = Net(ssem, rsem, n_sem)
    tokens_ag = PlaneGather(net, p, x_ref, lambda k, q: xall.at[k, q], 2)
    tokens_ag.first()
    keep(wcat_ref, wfull_o.at[z])
    can_up, can_down = z < nz - 1, z > 0
    rows = pl.ds(p.core * half, half)
    other = pl.ds((1 - p.core) * half, half)

    class Stream:
        def __init__(self, own, at, after):
            self.up = [net.new() for _ in range(nz)]
            self.down = [net.new() for _ in range(nz)]
            self.own, self.at, self.after = own, at, after

        def begin(self):
            net.send(self.up[1], self.own, self.at(z), p.up, can_up)
            net.send(self.down[1], self.own, self.at(z), p.down, can_down)

        def step(self, t):
            for ids, src, frm, to, got, more in (
                (self.up, z - t, p.down, p.up, z >= t, can_up),
                (self.down, z + t, p.up, p.down, z + t < nz, can_down),
            ):
                src = jnp.clip(src, 0, nz - 1)
                block = self.at(src)
                net.recv(ids[t], block, frm, got)
                if t + 1 < nz:
                    net.send(ids[t + 1], block, block, to, jnp.logical_and(got, more))
                self.after(t, src, block, got)

    waits = []

    def share(block_of):
        def after(t, src, block, got):
            idx = net.new()
            net.send(idx, block, block, p.sib, got)
            waits.append((idx, block_of(src), got))

        return after

    gathers = {t: [] for t in range(1, nz)}

    def spread(t, src, block, got):
        gather = PlaneGather(
            net, p, block, lambda k, q: wfull_o.at[src, k, q].at[ax], ra, got
        )
        gather.first()
        gathers[t].append(gather)

    sel = Stream(
        wsel_ref.at[rows], lambda o: wqkv.at[o, rows], share(lambda o: wqkv.at[o, other])
    )
    cat_a = Stream(
        wcat_ref.at[p.core, p.chip].at[ax], lambda o: wfull_o.at[o, p.core, p.chip].at[ax], spread
    )
    cat_b = Stream(
        wcat_ref.at[p.core, :, bx],
        lambda o: wfull_o.at[o, p.core, :, bx],
        share(lambda o: wfull_o.at[o, 1 - p.core, :, bx]),
    )
    sel.begin()
    cat_a.begin()
    fill_table(tab, pairs, pairing, p.chip, n, heads)
    o_nat[...] = jnp.zeros(o_nat.shape, bf16)
    lse_o[...] = jnp.zeros(lse_o.shape, f32)
    sel.step(1)
    tokens_ag.second()
    cat_a.step(1)
    cat_b.begin()
    for t in range(2, nz):
        sel.step(t)
    tokens_ag.third()
    own_x.wait()
    own_w.wait()
    tokens_ag.last()
    for idx, block, got in waits:
        net.recv(idx, block, p.sib, got)
    del waits[:]
    keep(xall, xall_o)
    keep(wqkv, wqkv_o)

    def four(i, _):
        tokens = jnp.concatenate([xall[natural(tab, n, 4 * i + u)] for u in range(4)], axis=0)
        qkv = mm(tokens, wqkv[...].reshape(-1, 3 * LANES))
        q = (qkv[:, :LANES].astype(bf16).astype(f32) * score_scale).astype(bf16)
        q_ref[pl.ds(4 * i, 4)] = q.reshape(4, seg, LANES)
        at = pl.ds(i * (4 * seg // KT), 4 * seg // KT)
        k_ref[at] = qkv[:, LANES : 2 * LANES].astype(bf16).reshape(-1, KT, LANES)
        v_ref[at] = qkv[:, 2 * LANES :].astype(bf16).reshape(-1, KT, LANES)
        return 0

    lax.fori_loop(0, n // 2, four, 0)
    for src, dst in ((q_ref, q_o), (k_ref, k_o), (v_ref, v_o)):
        keep(src, dst)

    def second(t):
        for gather in gathers.get(t, ()):
            gather.second()

    def third(t):
        for gather in gathers.get(t, ()):
            gather.third()

    todo = {
        (0, 0): lambda: (second(1), cat_a.step(2)),
        (0, 2): lambda: (third(1), cat_b.step(1)),
        (1, 0): lambda: (second(2), cat_a.step(3)),
        (1, 2): lambda: (third(2), cat_b.step(2)),
        (2, 0): lambda: second(3),
        (2, 2): lambda: third(3),
    }
    for h in range(heads):
        for i in range(n // 2):
            attend_unit(fold, p.core, h, i, head_dim, tab, q_ref, k_ref, v_ref, o_nat, lse_o)
            if (h, i) in todo:
                todo[h, i]()
    keep(o_nat, on_o)
    for core_is in range(2):
        for q in range(n // 2):
            a = tab[2 * q + core_is]
            for u, s in ((0, a), (1, 2 * n - 1 - a)):
                o_ctx[core_is, q, u * seg : (u + 1) * seg, :] = o_nat[s]
    part, swaps = net.new(), [net.new() for _ in range(3)]
    net.send(part, o_ctx.at[1 - p.core], o_part, p.sib)
    net.recv(part, o_part, p.sib)
    pairs_ = ((p.chip_d, p.dn), (p.chip_x, p.xn), (p.chip_y, p.yn))
    for idx, (chip, dev) in zip(swaps, pairs_):
        o_sum[chip] = o_ctx[p.core, chip] + o_part[chip]
        net.send(idx, o_sum.at[chip], attn_o.at[p.chip], dev)
    attn_o[p.chip] = o_ctx[p.core, p.chip] + o_part[p.chip]
    cat_b.step(3)
    for t in gathers:
        for gather in gathers[t]:
            gather.last()
    for idx, (chip, dev) in zip(swaps, pairs_):
        net.recv(idx, attn_o.at[chip], dev)
    for idx, block, got in waits:
        net.recv(idx, block, p.sib, got)
    net.finish()
    for cp in locals_[2:]:
        cp.wait()


def forward(nz, n, heads, head_dim, rb, pairs, pairing, x_in, wsel, wcat):
    tok, width = x_in.shape
    seg = tok // 2
    n_sem = 12 * (2 * nz - 1) + 3 * 2 * nz + 4 * nz + 8
    wide, tiled = (2 * n, seg, LANES), (tok * n // KT, KT, LANES)
    shapes = [(2, 4, 2, seg, width), (nz,) + wsel.shape, wide, tiled, tiled]
    block = (4, tok, LANES)
    sds = jax.ShapeDtypeStruct
    return pl.pallas_call(
        functools.partial(forward_kernel, nz, n, heads, head_dim, rb, n_sem),
        out_shape=tuple(sds(s, bf16) for s in shapes)
        + (sds(wide, bf16), sds((tok // 2, KT), f32), sds(block, bf16), sds((nz,) + wcat.shape, bf16)),
        in_specs=smem(2) + vmem(3),
        out_specs=tuple(hbm(6) + vmem(2) + hbm(1)),
        scratch_shapes=[pltpu.SMEM((2 * n + heads,), jnp.int32)]
        + [pltpu.VMEM(s, bf16) for s in shapes]
        + [
            pltpu.VMEM(wide, bf16),
            pltpu.VMEM((2,) + block, bf16),
            pltpu.VMEM(block, bf16),
            pltpu.VMEM(block, bf16),
            pltpu.SemaphoreType.DMA((n_sem,)),
            pltpu.SemaphoreType.DMA((n_sem,)),
            pltpu.SemaphoreType.DMA((12,)),
        ],
        compiler_params=comm_params(0),
        name="forward",
    )(pairs, pairing, x_in.reshape(2, seg, width), wsel, wcat)


def add_into(dst, src, rows, chunk=32):
    if rows % chunk:
        chunk = 16

    def step(i, _):
        at = pl.ds(pl.multiple_of(i * chunk, chunk), chunk)
        dst[at, :] = dst[at, :] + src[at, :]
        return 0

    lax.fori_loop(0, rows // chunk, step, 0)


class PlaneSum:
    def __init__(self, net, place, block, rows, rx0, ry1, ry0, rx1):
        self.net, self.place, self.block = net, place, block
        self.rx0, self.ry1, self.ry0, self.rx1 = rx0, ry1, ry0, rx1
        self.h = rows // 2
        self.h0, self.h1 = pl.ds(0, self.h), pl.ds(self.h, self.h)
        self.ids = [net.new() for _ in range(6)]

    def first(self):
        n, p, i = self.net, self.place, self.ids
        for j in range(2):
            n.send(i[j], self.block(2 * j + 1 - p.x).at[self.h0], self.rx0.at[j], p.xn)
            n.send(i[2 + j], self.block(2 * (1 - p.y) + j).at[self.h1], self.ry1.at[j], p.yn)

    def second(self):
        n, p, i = self.net, self.place, self.ids
        far_y, far_x = 1 - p.y, 1 - p.x
        for j in range(2):
            n.recv(i[j], self.rx0.at[j], p.xn)
        to_y = self.block(2 * far_y + p.x).at[self.h0]
        add_into(to_y, self.rx0.at[far_y], self.h)
        n.send(i[4], to_y, self.ry0, p.yn)
        for j in range(2):
            n.recv(i[2 + j], self.ry1.at[j], p.yn)
        to_x = self.block(2 * p.y + far_x).at[self.h1]
        add_into(to_x, self.ry1.at[far_x], self.h)
        n.send(i[5], to_x, self.rx1, p.xn)
        mine = self.block(p.chip)
        add_into(mine.at[self.h0], self.rx0.at[p.y], self.h)
        add_into(mine.at[self.h1], self.ry1.at[p.x], self.h)

    def third(self):
        n, p, i = self.net, self.place, self.ids
        mine = self.block(p.chip)
        n.recv(i[4], self.ry0, p.yn)
        add_into(mine.at[self.h0], self.ry0, self.h)
        n.recv(i[5], self.rx1, p.xn)
        add_into(mine.at[self.h1], self.rx1, self.h)


class LineSum:
    def __init__(self, net, place, nz, whole, low, high, parts, rows):
        self.net, self.place, self.nz, self.whole = net, place, nz, whole
        self.low, self.high, self.parts, self.rows = low, high, parts, rows
        self.up = [net.new() for _ in range(nz)]
        self.down = [net.new() for _ in range(nz)]

    def step(self, t):
        n, p, z, top = self.net, self.place, self.place.z, self.nz - 1
        sides = (
            (self.up, self.low, z, top - t + z, p.down, p.up),
            (self.down, self.high, top - z, t + z - top, p.up, p.down),
        )
        for ids, buf, depth, owner, frm, to in sides:
            owner = jnp.clip(owner, 0, top)
            whole, landed = self.whole(owner), buf.at[owner]

            def take(ids=ids, whole=whole, landed=landed, frm=frm):
                n.recv(ids[t - 1], landed, frm)
                if self.parts is None:
                    add_into(whole, landed, self.rows)
                else:
                    for j in range(self.parts):
                        add_into(whole.at[j], landed.at[j], self.rows)

            if t > 0:
                maybe(jnp.logical_and(depth > 0, depth <= t), take)
            if t < top:
                n.send(ids[t], whole, landed, to, depth <= t)


def attend_back_unit(
    fold, core, h, i, head_dim, tab, q_ref, k_ref, v_ref, o_ref, lse_ref, da_ref,
    dcat_ref, dk_ref, dv_ref,
):
    n, seg, half = fold.n, fold.seg, fold.half
    paired = tab[2 * n + h]
    pf = paired.astype(f32)
    lanes = head_mask(h, head_dim, f32)
    lanes16 = head_mask(h, head_dim, bf16)
    dqs = []
    places = fold.places(i, core, paired)
    for g, (rows, keys, limit, count) in enumerate(places):
        q = q_ref[rows] * lanes16
        k, c, upper = natural(tab, n, rows)
        da = da_ref[k, c, upper] * lanes16
        delta = jnp.sum(
            da.astype(f32) * o_ref[rows].astype(f32), axis=1, keepdims=True
        )
        lane = lse_lane(fold, h, i, g)
        lse = lse_ref[:, lane : lane + 1]
        dq = None
        pieces = [(count - 2, 2, True)]
        if count > 2:
            pieces.append((0, count - 2, False))
        for first, size, masked in pieces:
            kt = key_tiles(k_ref, keys, first, size)
            vt = key_tiles(v_ref, keys, first, size)
            pr = jnp.exp(mm(q, kt, NT) - lse)
            if masked:
                pr = jnp.where(tail_mask(seg, limit), pr, 0.0)
            ds = (pr * (mm(da, vt, NT) - delta)).astype(bf16)
            part = mm(ds, kt)
            dq = part if dq is None else dq + part
            dv = mm(pr.astype(bf16), da, TN)
            dk = mm(ds, q, TN)
            at = pl.ds(first * KT, size * KT)
            if g == 0 or masked:
                dk_ref[at, :] += dk
                dv_ref[at, :] += dv
            else:
                beyond = pl.ds(places[0][3] * KT, size * KT)
                dk_ref[at, :] += (1.0 - pf) * dk
                dv_ref[at, :] += (1.0 - pf) * dv
                dk_ref[beyond, :] += pf * dk
                dv_ref[beyond, :] += pf * dv
        dqs.append(dq)
    scaled = lanes * score_scale
    dq_a, dq_b = (dqs[0] + pf * dqs[1]) * scaled, dqs[1] * scaled
    far, near, up = core * n + n - 1 - i, core * n + i, n + core * (n // 2) + i
    for at, value in ((far, (1.0 - pf) * dq_a), (near, (1.0 - pf) * dq_b), (up, pf * dq_a)):
        dcat_ref[at, :, :LANES] += value.astype(bf16)


def place_key_grads(fold, core, paired, dk_ref, dv_ref, dcat_ref):
    n, seg, half = fold.n, fold.seg, fold.half
    pf = paired.astype(f32)

    def spread(j, _):
        at = pl.ds(pl.multiple_of(j * seg, seg), seg)
        for src, lanes in ((dk_ref, slice(LANES, 2 * LANES)), (dv_ref, slice(2 * LANES, None))):
            value = src[at, :]
            dcat_ref[core * n + j, :, lanes] += ((1.0 - pf) * value).astype(bf16)
            dcat_ref[j, :, lanes] += (pf * value).astype(bf16)
        return 0

    lax.fori_loop(0, n, spread, 0)


def backward_kernel(
    nz, n, heads, head_dim, rb, n_sem,
    pairs, pairing, g_ref, da_in, dh_ref, xall_i, wqkv_i, q_i, k_i, v_i, on_i, lse_ref,
    gsum_o, dtok_o, dw_o,
    tab, g_kept, g_sib, g_rx0, g_ry1, g_ry0, g_rx1, g_low, g_high,
    b_low, b_high, b_rx0, b_ry1, b_ry0, b_rx1,
    x_part, x_sib, x_rx0, x_ry1, x_ry0, x_rx1, w_part, w_sib, w_low, w_high, w_all,
    da_all, xall, wqkv, q_ref, k_ref, v_ref, on_ref, dcat, dk_ref, dv_ref, dw_acc,
    ssem, rsem, lsem,
):
    p = Place()
    z = p.z
    seg, width = xall.shape[3], xall.shape[4]
    tok = 2 * seg
    fold = Fold(n, seg)
    rows = g_ref.shape[3]
    ra = rows - rb
    ax, bx = pl.ds(0, ra), pl.ds(ra, rb)
    order = line_order(nz)
    local = []

    def fetch(src, dst):
        cp = pltpu.make_async_copy(src, dst, lsem.at[len(local)])
        cp.start()
        local.append(cp)
        return cp

    net = Net(ssem, rsem, n_sem)
    own_da = fetch(da_in.at[p.chip], da_all.at[p.core, p.chip])
    own_g = {o: fetch(g_ref.at[o, p.core], g_kept.at[o]) for o in order}
    greet(p, (p.sib, p.xn, p.yn, p.dn), nz)
    swaps = [net.new() for _ in range(7)]
    partners = ((p.chip_d, p.dn), (p.chip_x, p.xn), (p.chip_y, p.yn))
    for i, (chip, dev) in enumerate(partners):
        net.send(swaps[i], da_in.at[chip], da_all.at[p.core, p.chip], dev)
    net.send(swaps[3], da_in.at[p.chip], da_all.at[p.core, p.chip], p.sib)
    sib_ids = {}
    for o in order:
        sib_ids[o] = net.new()
        net.send(sib_ids[o], g_ref.at[o, 1 - p.core], g_sib.at[o], p.sib)
    att_in = [
        fetch(src, dst)
        for src, dst in (
            (q_i, q_ref), (k_i, k_ref), (v_i, v_ref), (on_i, on_ref), (xall_i, xall), (wqkv_i, wqkv),
        )
    ]
    fill_table(tab, pairs, pairing, p.chip, n, heads)
    dcat[...] = jnp.zeros(dcat.shape, bf16)

    plane = {
        o: PlaneSum(
            net, p, lambda q, o=o: g_kept.at[o, q].at[ax], ra,
            g_rx0.at[o], g_ry1.at[o], g_ry0.at[o], g_rx1.at[o],
        )
        for o in order
    }
    line_a = LineSum(net, p, nz, lambda o: g_kept.at[o, p.chip].at[ax], g_low, g_high, None, ra)
    line_b = LineSum(net, p, nz, lambda o: g_kept.at[o, :, bx], b_low, b_high, n // 2, rb)
    plane_b = PlaneSum(
        net, p, lambda q: g_kept.at[z, q].at[bx], rb, b_rx0, b_ry1, b_ry0, b_rx1
    )

    def chip_sum(o):
        net.recv(sib_ids[o], g_sib.at[o], p.sib)
        own_g[o].wait()
        for q in range(n // 2):
            add_into(g_kept.at[o, q], g_sib.at[o, q], rows)

    for o in order[:2]:
        chip_sum(o)
        plane[o].first()
    line_b.step(0)
    for i, chip, dev in ((1, p.chip_x, p.xn), (2, p.chip_y, p.yn), (0, p.chip_d, p.dn)):
        block = da_all.at[p.core, chip]
        net.recv(swaps[i], block, dev)
        net.send(swaps[4 + i], block, block, p.sib)
    for o in order[2:]:
        chip_sum(o)
        plane[o].first()
    for i, chip in ((3, p.chip), (5, p.chip_x), (6, p.chip_y), (4, p.chip_d)):
        net.recv(swaps[i], da_all.at[1 - p.core, chip], p.sib)
    own_da.wait()
    for cp in att_in:
        cp.wait()

    todo = {
        0: lambda: plane[order[0]].second(),
        1: lambda: plane[order[1]].second(),
        2: lambda: (plane[order[0]].third(), plane[order[1]].third(), line_a.step(0)),
        3: lambda: plane[order[2]].second(),
        4: lambda: (plane[order[3]].second(), line_b.step(1)),
        5: lambda: (plane[order[2]].third(), plane[order[3]].third(), line_a.step(1)),
        7: lambda: line_b.step(2),
        8: lambda: line_a.step(2),
        10: lambda: (line_b.step(3), plane_b.first()),
        11: lambda: line_a.step(3),
    }
    units = n // 2
    for h in range(heads):
        dk_ref[...] = jnp.zeros(dk_ref.shape, f32)
        dv_ref[...] = jnp.zeros(dv_ref.shape, f32)
        for i in range(units):
            attend_back_unit(
                fold, p.core, h, i, head_dim, tab, q_ref, k_ref, v_ref, on_ref, lse_ref, da_all,
                dcat, dk_ref, dv_ref,
            )
            step = todo.get(h * units + i)
            if step:
                step()
        place_key_grads(fold, p.core, tab[2 * n + h], dk_ref, dv_ref, dcat)

    def block_grads(k, q):
        a = tab[2 * q + k]
        return jnp.concatenate([dcat[a], dcat[2 * n - 1 - a]], axis=0)

    dw_acc[...] = jnp.zeros(dw_acc.shape, f32)

    def weights(c, _):
        k, q = lax.rem(c, 2), c // 2
        dw_acc[...] += mm(xall[k, q].reshape(tok, width), block_grads(k, q), TN)
        return 0

    lax.fori_loop(0, n, weights, 0)
    d = wqkv.shape[1]
    half = d // 2
    for o in range(nz):
        w_part[0, o] = dw_acc[o * d : o * d + half].astype(bf16)
        w_part[1, o] = dw_acc[o * d + half : (o + 1) * d].astype(bf16)
    w_id = net.new()
    net.send(w_id, w_part.at[1 - p.core], w_sib, p.sib)
    plane_b.second()
    w_line = LineSum(net, p, nz, lambda o: w_part.at[p.core, o], w_low, w_high, None, half)

    def tokens_of(k):
        def one(q, _):
            w = wqkv[...].reshape(-1, 3 * LANES)
            x_part[k, q] = mm(block_grads(k, q), w, NT).astype(bf16)
            return 0

        lax.fori_loop(0, n // 2, one, 0)

    tokens_of(1 - p.core)
    x_id = net.new()
    net.send(x_id, x_part.at[1 - p.core], x_sib, p.sib)
    net.recv(w_id, w_sib, p.sib)
    for o in range(nz):
        add_into(w_part.at[p.core, o], w_sib.at[o], half)
    w_line.step(0)
    plane_b.third()
    final = PlaneGather(net, p, g_kept.at[z, p.chip], lambda k, q: gsum_o.at[k, q], rows)
    final.first()
    own_sum = fetch(g_kept.at[z, p.chip], gsum_o.at[p.core, p.chip])
    tokens_of(p.core)
    net.recv(x_id, x_sib, p.sib)
    for q in range(n // 2):
        add_into(x_part.at[p.core, q], x_sib.at[q], tok)
    xs = PlaneSum(net, p, lambda q: x_part.at[p.core, q], tok, x_rx0, x_ry1, x_ry0, x_rx1)
    xs.first()
    w_line.step(1)
    final.second()
    w_line.step(2)
    xs.second()
    w_line.step(3)
    w_final = PlaneGather(net, p, w_part.at[p.core, z], lambda k, q: w_all.at[k, q], half)
    w_final.first()
    own_w = pltpu.make_async_copy(w_part.at[p.core, z], w_all.at[p.core, p.chip], lsem.at[31])
    own_w.start()
    final.third()
    w_final.second()
    xs.third()

    def add_tokens(i, _):
        at = pl.ds(pl.multiple_of(i * 32, 32), 32)
        dtok_o[at, :] = (dh_ref[at, :] + x_part[p.core, p.chip, at, :].astype(f32)).astype(bf16)
        return 0

    lax.fori_loop(0, tok // 32, add_tokens, 0)
    w_final.third()
    w_final.last()
    own_w.wait()
    cols = heads * head_dim
    for j in range(3):
        for k in range(2):
            dw_o[j, k * half : (k + 1) * half, :] = jnp.concatenate(
                [w_all[k, q][:, j * LANES : j * LANES + cols] for q in range(4)], axis=1
            )
    final.last()
    own_sum.wait()
    net.finish()


def line_order(nz):
    order = []
    for i in range((nz + 1) // 2):
        for o in (nz - 1 - i, i):
            if o not in order:
                order.append(o)
    return order


def backward(
    nz, n, heads, head_dim, rb, pairs, pairing, grads, da, dh, xall, wqkv, q, k, v, on, lse
):
    rows, width = grads.shape[3], grads.shape[4]
    seg = xall.shape[3]
    tok = 2 * seg
    d_rows = wqkv.shape[1]
    half = d_rows // 2
    ra = rows - rb
    n_sem = 6 * (nz + 2) + 6 * nz + nz + 9 + 24 + 2
    sds = jax.ShapeDtypeStruct
    vm = lambda *shape: pltpu.VMEM(shape, bf16)
    wide, tiled = (2 * n, seg, LANES), (tok * n // KT, KT, LANES)
    da = da.reshape(4, 2, seg, LANES)
    return pl.pallas_call(
        functools.partial(backward_kernel, nz, n, heads, head_dim, rb, n_sem),
        out_shape=(
            sds(grads.shape[1:], bf16),
            sds((tok, width), bf16),
            sds((3, d_rows, width), bf16),
        ),
        in_specs=smem(2) + hbm(2) + vmem(1) + hbm(6) + vmem(1),
        out_specs=tuple(hbm(1) + vmem(2)),
        scratch_shapes=[
            pltpu.SMEM((2 * n + heads,), jnp.int32),
            vm(nz, 4, rows, width),
            vm(nz, 4, rows, width),
            vm(nz, 2, ra // 2, width),
            vm(nz, 2, ra // 2, width),
            vm(nz, ra // 2, width),
            vm(nz, ra // 2, width),
            vm(nz, ra, width),
            vm(nz, ra, width),
            vm(nz, 4, rb, width),
            vm(nz, 4, rb, width),
            vm(2, rb // 2, width),
            vm(2, rb // 2, width),
            vm(rb // 2, width),
            vm(rb // 2, width),
            vm(2, 4, tok, width),
            vm(4, tok, width),
            vm(2, tok // 2, width),
            vm(2, tok // 2, width),
            vm(tok // 2, width),
            vm(tok // 2, width),
            vm(2, nz, half, width),
            vm(nz, half, width),
            vm(nz, half, width),
            vm(nz, half, width),
            vm(2, 4, half, width),
            vm(2, 4, 2, seg, LANES),
            vm(2, 4, 2, seg, width),
            vm(nz, d_rows, width),
            vm(*wide),
            vm(*tiled),
            vm(*tiled),
            vm(*wide),
            vm(2 * n, seg, 3 * LANES),
            pltpu.VMEM((seg * n, LANES), f32),
            pltpu.VMEM((seg * n, LANES), f32),
            pltpu.VMEM((width, 3 * LANES), f32),
            pltpu.SemaphoreType.DMA((n_sem,)),
            pltpu.SemaphoreType.DMA((n_sem,)),
            pltpu.SemaphoreType.DMA((32,)),
        ],
        compiler_params=comm_params(1),
        name="backward",
    )(pairs, pairing, grads, da, dh, xall, wqkv, q, k, v, on, lse)


def norm_forward(h, gain, shift):
    mean = jnp.mean(h, axis=1, keepdims=True)
    center = h - mean
    scale = lax.rsqrt(jnp.mean(center * center, axis=1, keepdims=True) + norm_eps)
    n = center * scale
    return n, scale, n * gain + shift


def norm_backward(cot, n, scale, gain):
    dn = cot * gain
    mean = jnp.mean(dn, axis=1, keepdims=True)
    along = jnp.mean(dn * n, axis=1, keepdims=True)
    return scale * (dn - mean - n * along)


def middle_kernel(
    nz, cols, n_f, x_ref, a_ref, w_ref, cot_ref, out_ref, da_ref, g_ref, dh_ref,
    w1, w2, wo, lnb, u_ref, z_ref, x1b_ref, acc_ref, n1_ref, r1_ref, dx1_ref, sems,
):
    tok, width = x_ref.shape
    f_rows = w2.shape[1]
    d_rows = cols
    o1, o2, o3 = f_rows, f_rows + n_f * d_rows, f_rows + n_f * d_rows + d_rows
    copies = []

    def fetch(src, dst):
        cp = pltpu.make_async_copy(src, dst, sems.at[len(copies)])
        cp.start()
        copies.append(cp)
        return cp

    first = [fetch(w_ref.at[o, o2:o3], wo.at[o]) for o in range(nz)]
    first += [fetch(w_ref.at[o, o3 : o3 + 16], lnb.at[o]) for o in range(nz)]
    inner = [
        [
            fetch(
                w_ref.at[o, o1 + f * d_rows : o1 + (f + 1) * d_rows],
                w1.at[f, o * d_rows : (o + 1) * d_rows],
            )
            for o in range(nz)
        ]
        for f in range(n_f)
    ]
    outer = [fetch(w_ref.at[o, :f_rows], w2.at[o]) for o in range(nz)]
    for cp in first:
        cp.wait()
    vec = lnb[0].astype(f32)
    for o in range(1, nz):
        vec = vec + lnb[o].astype(f32)
    gain1, gain2, shift1, shift2 = vec[0:1], vec[1:2], vec[2:3], vec[3:4]
    h1 = x_ref[...].astype(f32)
    for o in range(nz):
        h1 = h1 + mm(a_ref[o, :, :cols], wo[o])
    n1, r1, x1 = norm_forward(h1, gain1, shift1)
    n1_ref[...] = n1
    r1_ref[...] = jnp.broadcast_to(r1, (tok, 128))
    x1b_ref[...] = x1.astype(bf16)
    acc_ref[...] = x1
    for group in inner:
        for cp in group:
            cp.wait()
    for cp in outer:
        cp.wait()

    def up(f, _):
        u = mm(x1b_ref[...], w1[f])
        cdf = 0.5 + 0.5 * lax.erf(u * (0.5**0.5))
        z = (u * cdf).astype(bf16)
        z_ref[f] = z
        u_ref[f] = (cdf + u * jnp.exp(-0.5 * u * u) * 0.3989422804014327).astype(u_ref.dtype)
        acc_ref[...] += mm(z, w2[f])
        return 0

    lax.fori_loop(0, n_f, up, 0)
    n2, r2, out = norm_forward(acc_ref[...], gain2, shift2)
    out_ref[...] = out.astype(bf16)
    cot = cot_ref[...].astype(f32)
    d_gain2 = jnp.sum(cot * n2, axis=0, keepdims=True)
    d_shift2 = jnp.sum(cot, axis=0, keepdims=True)
    dh2 = norm_backward(cot, n2, r2, gain2)
    dx1_ref[...] = dh2
    df = dh2.astype(bf16)

    def back(f, _):
        g_ref[f, :f_rows, :] = mm(z_ref[f], df, TN).astype(bf16)
        du = (mm(df, w2[f], NT) * u_ref[f].astype(f32)).astype(bf16)
        dw = mm(x1b_ref[...], du, TN).astype(bf16)
        for o in range(nz):
            at = pl.ds(pl.multiple_of(o1 + f * d_rows, 16), d_rows)
            g_ref[o, at, :] = dw[o * d_rows : (o + 1) * d_rows]
        dx1_ref[...] += mm(du, w1[f], NT)
        return 0

    lax.fori_loop(0, n_f, back, 0)
    d_x1 = dx1_ref[...]
    n1 = n1_ref[...]
    d_gain1 = jnp.sum(d_x1 * n1, axis=0, keepdims=True)
    d_shift1 = jnp.sum(d_x1, axis=0, keepdims=True)
    dh1 = norm_backward(d_x1, n1, r1_ref[:, :1], gain1)
    dh_ref[...] = dh1
    dy = dh1.astype(bf16)
    total = g_ref.shape[1]
    norms = jnp.concatenate([d_gain1, d_gain2, d_shift1, d_shift2], axis=0).astype(bf16)
    for o in range(nz):
        g_ref[o, o2:o3, :] = mm(a_ref[o, :, :cols], dy, TN).astype(bf16)
        g_ref[o, o3:, :] = jnp.zeros((total - o3, width), bf16)
        g_ref[o, o3 : o3 + 4, :] = norms
        da_ref[o, :, :cols] = mm(dy, wo[o], NT).astype(bf16)
        da_ref[o, :, cols:] = jnp.zeros((tok, LANES - cols), bf16)


def middle(nz, cols, n_f, x_in, attn, wfull, cot):
    tok, width = x_in.shape
    vm = lambda dt, *shape: pltpu.VMEM(shape, dt)
    return pl.pallas_call(
        functools.partial(middle_kernel, nz, cols, n_f),
        out_shape=(
            jax.ShapeDtypeStruct((tok, width), bf16),
            jax.ShapeDtypeStruct((nz, tok, LANES), bf16),
            jax.ShapeDtypeStruct(wfull.shape, bf16),
            jax.ShapeDtypeStruct((tok, width), f32),
        ),
        in_specs=vmem(2) + hbm(1) + vmem(1),
        out_specs=tuple(vmem(4)),
        scratch_shapes=[
            vm(bf16, n_f, width, width),
            vm(bf16, nz, width, width),
            vm(bf16, nz, cols, width),
            vm(bf16, nz, 16, width),
            vm(f32, n_f, tok, width),
            vm(bf16, n_f, tok, width),
            vm(bf16, tok, width),
            vm(f32, tok, width),
            vm(f32, tok, width),
            vm(f32, tok, 128),
            vm(f32, tok, width),
            pltpu.SemaphoreType.DMA((3 * nz + n_f * nz,)),
        ],
        compiler_params=pltpu.CompilerParams(vmem_limit_bytes=60 << 20),
        name="middle",
    )(x_in, attn, wfull, cot)


def fast_body(
    tokens,
    w_query,
    w_key,
    w_value,
    w_output,
    w_inner,
    w_outer,
    ln_gain,
    ln_bias,
    pairing,
    block_pairs,
    cotangent,
):
    tok, width = tokens.shape[1], tokens.shape[2]
    n_ctx, nz = lax.axis_size("ctx"), lax.axis_size("fsdp")
    heads = pairing.shape[1]
    head_dim = width // heads
    my_heads = heads // 4
    cols = my_heads * head_dim
    chip = lax.axis_index("ctx") // 2
    d_rows = w_query.shape[0]
    f_rows, ff = w_outer.shape[0], w_inner.shape[1]
    n_f = ff // width
    x_in = tokens[0]

    def chip_cols(w):
        part = lax.dynamic_slice_in_dim(w, chip * cols, cols, 1).astype(bf16)
        return jnp.pad(part, ((0, 0), (0, LANES - cols)))

    wsel = jnp.concatenate([chip_cols(w) for w in (w_query, w_key, w_value)], axis=1)
    z = lax.axis_index("fsdp")
    norms = jnp.concatenate([ln_gain.T, ln_bias.T], axis=0).astype(bf16)
    used = f_rows + n_f * d_rows + d_rows
    total = -(-(used + 4) // 256) * 256
    norms = lax.dynamic_update_slice(jnp.zeros((total - used, width), bf16), norms, (0, z * d_rows))
    wcat = jnp.concatenate(
        [w_outer.astype(bf16)]
        + [w_inner[:, i * width : (i + 1) * width].astype(bf16) for i in range(n_f)]
        + [w_output.astype(bf16), norms],
        axis=0,
    ).reshape(2, 4, total // 8, width)
    xall, wqkv, q, k, v, on, lse, attn, wfull = forward(
        nz, n_ctx, my_heads, head_dim, 64, block_pairs, pairing, x_in, wsel, wcat
    )
    wfull = wfull.reshape(nz, total, width)
    result, da, grads, d_h1 = middle(nz, cols, n_f, x_in, attn, wfull, cotangent[0])
    grads = grads.reshape(nz, 2, 4, total // 8, width)
    gsum, dtok, dw = backward(
        nz, n_ctx, my_heads, head_dim, 64, block_pairs, pairing, grads, da, d_h1,
        xall, wqkv, q, k, v, on, lse,
    )
    gsum = gsum.reshape(total, width)
    o1, o2 = f_rows, f_rows + n_f * d_rows
    g_inner = [gsum[o1 + i * d_rows : o1 + (i + 1) * d_rows] for i in range(n_f)]
    g_norms = lax.dynamic_slice(gsum[used : used + 4], (0, z * d_rows), (4, d_rows)).astype(f32)
    return (
        result[None],
        dtok[None],
        dw[0].astype(f32),
        dw[1].astype(f32),
        dw[2].astype(f32),
        gsum[o2:used].astype(f32),
        jnp.concatenate(g_inner, axis=1).astype(f32),
        gsum[:o1].astype(f32),
        g_norms[:2].T,
        g_norms[2:].T,
    )


def solution(mesh):
    in_specs = (
        P("fsdp", "ctx", None),
        P("fsdp", None),
        P("fsdp", None),
        P("fsdp", None),
        P("fsdp", None),
        P("fsdp", None),
        P("fsdp", None),
        P("fsdp", None),
        P("fsdp", None),
        P("fsdp", None),
        P("fsdp", None),
        P("fsdp", "ctx", None),
    )
    out_specs = (
        P("fsdp", "ctx", None),
        P("fsdp", "ctx", None),
        P("fsdp", None),
        P("fsdp", None),
        P("fsdp", None),
        P("fsdp", None),
        P("fsdp", None),
        P("fsdp", None),
        P("fsdp", None),
        P("fsdp", None),
    )
    fast = mesh.shape["ctx"] == 8 and mesh.shape["fsdp"] == 4
    chosen = fast_body if fast else generic_body
    return jax.shard_map(chosen, mesh=mesh, in_specs=in_specs, out_specs=out_specs, check_vma=False)
```

```python
import functools

import jax
import jax.numpy as jnp
from jax import lax
from jax.experimental import pallas as pl
from jax.experimental.pallas import tpu as pltpu
from jax.sharding import PartitionSpec as P

norm_eps = 1e-05
score_scale = 0.125
very_low = -1e30


def shortened(value):

    def short(part):
        return part.astype(jnp.bfloat16) if part.dtype == jnp.float32 else part

    return jax.tree.map(short, value)


def layer_norm(values, norm_gain, norm_shift):
    center = values - jnp.mean(values, axis=-1, keepdims=True)
    spread = jnp.mean(center * center, axis=-1, keepdims=True)
    return center * lax.rsqrt(spread + norm_eps) * norm_gain + norm_shift


def exact_gelu(values):
    return jax.nn.gelu(values, approximate=False)


def project(rows_in, weight):
    return jnp.dot(rows_in, weight, preferred_element_type=jnp.float32)


def seq_positions(pair_row, tok_dev, seq_len):
    segment_len = tok_dev // 2
    within = jnp.arange(tok_dev, dtype=jnp.int32)
    lower_pos = pair_row[:, None] * segment_len + within[None, :]
    upper_pos = seq_len - (pair_row[:, None] + 1) * segment_len + within[None, :] - segment_len
    return jnp.where(within[None, :] < segment_len, lower_pos, upper_pos).reshape(-1)


def pair_mask(query_pos, key_pos, head_flags, half_len):
    target = (query_pos[None, :] // half_len + head_flags[:, None]) % 2
    paired = key_pos[None, None, :] // half_len == target[:, :, None]
    causal = key_pos[None, :] <= query_pos[:, None]
    return jnp.logical_and(paired, causal[None, :, :])


def block_rows(tok_dev):
    return 2 * tok_dev


def over_blocks(running, arrays, step_fn, tok_dev):
    row_count = arrays[0].shape[0]
    block_len = block_rows(tok_dev)

    def one_step(inner_carry, step_index):
        first_row = step_index * block_len
        sliced = tuple(
            (lax.dynamic_slice_in_dim(member, first_row, block_len, 0) for member in arrays)
        )
        return (step_fn(inner_carry, sliced, first_row), None)

    return lax.scan(one_step, running, jnp.arange(row_count // block_len, dtype=jnp.int32))[0]


def generic_body(
    tokens,
    w_query,
    w_key,
    w_value,
    w_output,
    w_inner,
    w_outer,
    ln_gain,
    ln_bias,
    pairing,
    block_pairs,
    cotangent,
):
    tok_dev = tokens.shape[1]
    width = tokens.shape[2]
    heads = pairing.shape[1]
    head_dim = width // heads
    n_ctx = lax.axis_size("ctx")
    seq_len = tok_dev * n_ctx
    half_len = seq_len // 2
    pos_all = seq_positions(block_pairs[0], tok_dev, seq_len)
    my_pos = lax.dynamic_slice_in_dim(pos_all, lax.axis_index("ctx") * tok_dev, tok_dev, 0)
    head_flags = pairing[0]
    masters = (w_query, w_key, w_value, w_output, w_inner, w_outer, ln_gain, ln_bias)
    low_masters = tuple((member.astype(jnp.bfloat16) for member in masters))
    gathered = jax.tree.map(
        lambda part, own: part.astype(own.dtype),
        lax.all_gather(shortened(low_masters), "fsdp", axis=0, tiled=True),
        low_masters,
    )
    wq_full, wk_full, wv_full, wo_full, inner_full, outer_full, gain_full, shift_full = gathered
    gain_wide = gain_full.astype(jnp.float32)
    shift_wide = shift_full.astype(jnp.float32)
    x_in = tokens[0]
    query_b = project(x_in, wq_full).astype(jnp.bfloat16)
    key_b = project(x_in, wk_full).astype(jnp.bfloat16)
    value_b = project(x_in, wv_full).astype(jnp.bfloat16)
    q_heads = query_b.reshape(tok_dev, heads, head_dim)

    def attend_step(running, sliced, offset):
        run_max, run_sum, run_acc = running
        key_block, value_block = sliced
        block_len = key_block.shape[0]
        key_pos = lax.dynamic_slice_in_dim(pos_all, offset, block_len, 0)
        allowed = pair_mask(my_pos, key_pos, head_flags, half_len)
        key_heads = key_block.reshape(block_len, heads, head_dim)
        value_heads = value_block.reshape(block_len, heads, head_dim)
        scores = (
            jnp.einsum("qhd,khd->hqk", q_heads, key_heads, preferred_element_type=jnp.float32)
            * score_scale
        )
        new_max = jnp.maximum(run_max, jnp.max(jnp.where(allowed, scores, very_low), axis=2))
        prob_rows = jnp.where(
            allowed, jnp.exp(jnp.where(allowed, scores - new_max[:, :, None], 0.0)), 0.0
        )
        decay = jnp.exp(run_max - new_max)
        new_sum = run_sum * decay + jnp.sum(prob_rows, axis=2)
        added = jnp.einsum(
            "hqk,khd->hqd",
            prob_rows.astype(jnp.bfloat16),
            value_heads,
            preferred_element_type=jnp.float32,
        )
        return (new_max, new_sum, run_acc * decay[:, :, None] + added)

    def pair_fold(step_fn, running, fetched):
        return over_blocks(running, fetched, step_fn, tok_dev)

    start_state = (
        jnp.full((heads, tok_dev), very_low, jnp.float32),
        jnp.zeros((heads, tok_dev), jnp.float32),
        jnp.zeros((heads, tok_dev, head_dim), jnp.float32),
    )
    run_max, run_sum, run_acc = pair_fold(
        attend_step,
        start_state,
        (
            lax.all_gather(key_b, "ctx", axis=0, tiled=True),
            lax.all_gather(value_b, "ctx", axis=0, tiled=True),
        ),
    )
    live_rows = run_sum > 0
    safe_sum = jnp.where(live_rows, run_sum, 1.0)
    attn_heads = jnp.where(live_rows[:, :, None], run_acc / safe_sum[:, :, None], 0.0)
    lse_rows = jnp.where(live_rows, run_max + jnp.log(safe_sum), 0.0)
    attn_rows = attn_heads.transpose(1, 0, 2).reshape(tok_dev, width)
    attn_b = attn_rows.astype(jnp.bfloat16)
    branch = project(attn_b, wo_full)
    first_norm, first_pull = jax.vjp(
        layer_norm, x_in.astype(jnp.float32) + branch, gain_wide[:, 0], shift_wide[:, 0]
    )
    first_b = first_norm.astype(jnp.bfloat16)
    inner = project(first_b, inner_full)
    active, gelu_pull = jax.vjp(exact_gelu, inner)
    active_b = active.astype(jnp.bfloat16)
    outer = project(active_b, outer_full)
    result, second_pull = jax.vjp(layer_norm, first_norm + outer, gain_wide[:, 1], shift_wide[:, 1])
    wq_back, wk_back, wv_back, wo_back, inner_back, outer_back, gain_back, shift_back = gathered
    d_h2, d_gain2, d_shift2 = second_pull(cotangent[0].astype(jnp.float32))
    d_f_b = d_h2.astype(jnp.bfloat16)
    d_outer = jnp.dot(active_b.T, d_f_b, preferred_element_type=jnp.float32)
    d_active = jnp.dot(d_f_b, outer_back.T, preferred_element_type=jnp.float32)
    d_u_b = gelu_pull(d_active)[0].astype(jnp.bfloat16)
    d_inner = jnp.dot(first_b.T, d_u_b, preferred_element_type=jnp.float32)
    d_x1 = d_h2 + jnp.dot(d_u_b, inner_back.T, preferred_element_type=jnp.float32)
    d_h1, d_gain1, d_shift1 = first_pull(d_x1)
    d_y_b = d_h1.astype(jnp.bfloat16)
    d_wo = jnp.dot(attn_b.T, d_y_b, preferred_element_type=jnp.float32)
    d_attn_b = jnp.dot(d_y_b, wo_back.T, preferred_element_type=jnp.float32).astype(jnp.bfloat16)
    delta_rows = (
        (d_attn_b.astype(jnp.float32) * attn_rows).reshape(tok_dev, heads, head_dim).sum(axis=2).T
    )
    dout_heads = d_attn_b.reshape(tok_dev, heads, head_dim)

    def query_grad_step(dq_acc, sliced, offset):
        key_block, value_block = sliced
        block_len = key_block.shape[0]
        key_pos = lax.dynamic_slice_in_dim(pos_all, offset, block_len, 0)
        allowed = pair_mask(my_pos, key_pos, head_flags, half_len)
        key_heads = key_block.reshape(block_len, heads, head_dim)
        value_heads = value_block.reshape(block_len, heads, head_dim)
        scores = (
            jnp.einsum("qhd,khd->hqk", q_heads, key_heads, preferred_element_type=jnp.float32)
            * score_scale
        )
        prob_rows = jnp.where(
            allowed, jnp.exp(jnp.where(allowed, scores - lse_rows[:, :, None], 0.0)), 0.0
        )
        prob_grad = jnp.einsum(
            "qhd,khd->hqk", dout_heads, value_heads, preferred_element_type=jnp.float32
        )
        dscore = (prob_rows * (prob_grad - delta_rows[:, :, None]) * score_scale).astype(
            jnp.bfloat16
        )
        return dq_acc + jnp.einsum(
            "hqk,khd->qhd", dscore, key_heads, preferred_element_type=jnp.float32
        )

    dq_start = jnp.zeros((tok_dev, heads, head_dim), jnp.float32)
    dq_acc = pair_fold(
        query_grad_step,
        dq_start,
        (
            lax.all_gather(key_b, "ctx", axis=0, tiled=True),
            lax.all_gather(value_b, "ctx", axis=0, tiled=True),
        ),
    )
    dq_b = dq_acc.reshape(tok_dev, width).astype(jnp.bfloat16)
    lse_all, delta_all = (
        lax.all_gather(lse_rows, "ctx", axis=1, tiled=True),
        lax.all_gather(delta_rows, "ctx", axis=1, tiled=True),
    )
    k_heads = key_b.reshape(tok_dev, heads, head_dim)
    v_heads = value_b.reshape(tok_dev, heads, head_dim)

    def key_grad_step(running, sliced, offset):
        dk_acc, dv_acc = running
        query_block, dout_block = sliced
        block_len = query_block.shape[0]
        query_pos = lax.dynamic_slice_in_dim(pos_all, offset, block_len, 0)
        lse_block = lax.dynamic_slice_in_dim(lse_all, offset, block_len, 1)
        delta_block = lax.dynamic_slice_in_dim(delta_all, offset, block_len, 1)
        allowed = pair_mask(query_pos, my_pos, head_flags, half_len)
        query_heads = query_block.reshape(block_len, heads, head_dim)
        dout_block_heads = dout_block.reshape(block_len, heads, head_dim)
        scores = (
            jnp.einsum("qhd,khd->hqk", query_heads, k_heads, preferred_element_type=jnp.float32)
            * score_scale
        )
        prob_rows = jnp.where(
            allowed, jnp.exp(jnp.where(allowed, scores - lse_block[:, :, None], 0.0)), 0.0
        )
        dv_acc = dv_acc + jnp.einsum(
            "hqk,qhd->khd",
            prob_rows.astype(jnp.bfloat16),
            dout_block_heads,
            preferred_element_type=jnp.float32,
        )
        prob_grad = jnp.einsum(
            "qhd,khd->hqk", dout_block_heads, v_heads, preferred_element_type=jnp.float32
        )
        dscore = (prob_rows * (prob_grad - delta_block[:, :, None]) * score_scale).astype(
            jnp.bfloat16
        )
        dk_acc = dk_acc + jnp.einsum(
            "hqk,qhd->khd", dscore, query_heads, preferred_element_type=jnp.float32
        )
        return (dk_acc, dv_acc)

    kv_start = (
        jnp.zeros((tok_dev, heads, head_dim), jnp.float32),
        jnp.zeros((tok_dev, heads, head_dim), jnp.float32),
    )
    dk_acc, dv_acc = pair_fold(
        key_grad_step,
        kv_start,
        (
            lax.all_gather(query_b, "ctx", axis=0, tiled=True),
            lax.all_gather(d_attn_b, "ctx", axis=0, tiled=True),
        ),
    )
    dk_b = dk_acc.reshape(tok_dev, width).astype(jnp.bfloat16)
    dv_b = dv_acc.reshape(tok_dev, width).astype(jnp.bfloat16)
    d_input = d_h1 + jnp.dot(dq_b, wq_back.T, preferred_element_type=jnp.float32)
    d_input = d_input + jnp.dot(dk_b, wk_back.T, preferred_element_type=jnp.float32)
    d_input = d_input + jnp.dot(dv_b, wv_back.T, preferred_element_type=jnp.float32)
    terms = (
        jnp.dot(x_in.T, dq_b, preferred_element_type=jnp.float32),
        jnp.dot(x_in.T, dk_b, preferred_element_type=jnp.float32),
        jnp.dot(x_in.T, dv_b, preferred_element_type=jnp.float32),
        d_wo,
        d_inner,
        d_outer,
        jnp.stack([d_gain1, d_gain2], axis=1),
        jnp.stack([d_shift1, d_shift2], axis=1),
    )
    shares = (
        lax.psum_scatter(
            terms[0].astype(jnp.bfloat16), "fsdp", scatter_dimension=0, tiled=True
        ).astype(jnp.float32),
        lax.psum_scatter(
            terms[1].astype(jnp.bfloat16), "fsdp", scatter_dimension=0, tiled=True
        ).astype(jnp.float32),
        lax.psum_scatter(
            terms[2].astype(jnp.bfloat16), "fsdp", scatter_dimension=0, tiled=True
        ).astype(jnp.float32),
        lax.psum_scatter(
            terms[3].astype(jnp.bfloat16), "fsdp", scatter_dimension=0, tiled=True
        ).astype(jnp.float32),
        lax.psum_scatter(
            terms[4].astype(jnp.bfloat16), "fsdp", scatter_dimension=0, tiled=True
        ).astype(jnp.float32),
        lax.psum_scatter(
            terms[5].astype(jnp.bfloat16), "fsdp", scatter_dimension=0, tiled=True
        ).astype(jnp.float32),
        lax.psum_scatter(
            terms[6].astype(jnp.bfloat16), "fsdp", scatter_dimension=0, tiled=True
        ).astype(jnp.float32),
        lax.psum_scatter(
            terms[7].astype(jnp.bfloat16), "fsdp", scatter_dimension=0, tiled=True
        ).astype(jnp.float32),
    )
    totals = (
        lax.psum(shares[0].astype(jnp.bfloat16), "ctx").astype(jnp.float32),
        lax.psum(shares[1].astype(jnp.bfloat16), "ctx").astype(jnp.float32),
        lax.psum(shares[2].astype(jnp.bfloat16), "ctx").astype(jnp.float32),
        lax.psum(shares[3].astype(jnp.bfloat16), "ctx").astype(jnp.float32),
        lax.psum(shares[4].astype(jnp.bfloat16), "ctx").astype(jnp.float32),
        lax.psum(shares[5].astype(jnp.bfloat16), "ctx").astype(jnp.float32),
        lax.psum(shares[6].astype(jnp.bfloat16), "ctx").astype(jnp.float32),
        lax.psum(shares[7].astype(jnp.bfloat16), "ctx").astype(jnp.float32),
    )
    return (
        result.astype(jnp.bfloat16)[None],
        d_input.astype(jnp.bfloat16)[None],
        totals[0],
        totals[1],
        totals[2],
        totals[3],
        totals[4],
        totals[5],
        totals[6],
        totals[7],
    )


MESH = pl.DeviceIdType.MESH
f32 = jnp.float32
bf16 = jnp.bfloat16


class Place:
    def __init__(self):
        me = lax.axis_index("ctx")
        self.me = me
        self.z = lax.axis_index("fsdp")
        self.core = lax.rem(me, 2)
        self.chip = me // 2
        self.x = lax.rem(self.chip, 2)
        self.y = self.chip // 2
        self.chip_x = self.chip + 1 - 2 * self.x
        self.chip_y = self.chip + 2 - 4 * self.y
        self.chip_d = 3 - self.chip
        self.other = 1 - self.core
        self.sib = (2 * self.chip + 1 - self.core, self.z)
        self.xn = (2 * self.chip_x + self.core, self.z)
        self.yn = (2 * self.chip_y + self.core, self.z)
        self.dn = (2 * self.chip_d + self.core, self.z)
        self.up = (me, self.z + 1)
        self.down = (me, self.z - 1)


def greet(place, others, line_len=None):
    barrier = pltpu.get_barrier_semaphore()
    count = len(others)
    for other in others:
        pl.semaphore_signal(barrier, inc=1, device_id=other, device_id_type=MESH)
    if line_len is not None:

        @pl.when(place.z < line_len - 1)
        def _():
            pl.semaphore_signal(barrier, inc=1, device_id=place.up, device_id_type=MESH)

        @pl.when(place.z > 0)
        def _():
            pl.semaphore_signal(barrier, inc=1, device_id=place.down, device_id_type=MESH)

        count = count + jnp.where(place.z < line_len - 1, 1, 0) + jnp.where(place.z > 0, 1, 0)

    pl.semaphore_wait(barrier, count)


def maybe(cond, fn):
    if cond is None:
        fn()
    else:
        pl.when(cond)(fn)


def of(ref):
    return ref() if callable(ref) else ref


class Net:
    def __init__(self, send_sems, recv_sems, count):
        self.send_sems, self.recv_sems, self.count = send_sems, recv_sems, count
        self.used = 0
        self.open = []

    def new(self):
        self.used += 1
        assert self.used <= self.count
        return self.used - 1

    def copy(self, idx, src, dst, dev):
        return pltpu.make_async_remote_copy(
            src_ref=src,
            dst_ref=dst,
            send_sem=self.send_sems.at[idx],
            recv_sem=self.recv_sems.at[idx],
            device_id=dev,
            device_id_type=MESH,
        )

    def send(self, idx, src, dst, dev, cond=None):
        make = lambda: self.copy(idx, of(src), of(dst), dev)
        maybe(cond, lambda: make().start())
        self.open.append((cond, make))

    def recv(self, idx, dst, dev, cond=None):
        maybe(cond, lambda: self.copy(idx, of(dst), of(dst), dev).wait_recv())

    def finish(self):
        for cond, make in self.open:
            maybe(cond, lambda make=make: make().wait_send())
        self.open = []


class PlaneGather:
    def __init__(self, net, place, own, slot, rows, cond=None):
        p = place
        self.net, self.place, self.cond = net, place, cond
        self.own_of, self.slot = own, slot
        self.h0, self.h1 = pl.ds(0, rows // 2), pl.ds(rows // 2, rows // 2)
        self.ids = [net.new() for _ in range(11)]

    def at(self, core, chip, half=0):
        def view():
            ref = self.slot(core, chip)
            return ref if half == 0 else ref.at[self.h0 if half == 1 else self.h1]

        return view

    def mine(self, half=0):
        def view():
            ref = self.own_of()
            return ref if half == 0 else ref.at[self.h0 if half == 1 else self.h1]

        return view

    def first(self):
        n, p, i, c = self.net, self.place, self.ids, self.cond
        at = functools.partial(self.at, p.core, p.chip)
        n.send(i[0], self.mine(1), at(1), p.xn, c)
        n.send(i[1], self.mine(2), at(2), p.yn, c)
        n.send(i[2], self.mine(2), at(2), p.xn, c)
        n.send(i[3], self.mine(1), at(1), p.yn, c)
        n.send(i[4], self.mine(), at(), p.sib, c)

    def second(self):
        n, p, i, c = self.net, self.place, self.ids, self.cond
        bx = functools.partial(self.at, p.core, p.chip_x)
        by = functools.partial(self.at, p.core, p.chip_y)
        n.recv(i[0], bx(1), p.xn, c)
        n.send(i[5], bx(1), bx(1), p.yn, c)
        n.recv(i[1], by(2), p.yn, c)
        n.send(i[6], by(2), by(2), p.xn, c)
        n.recv(i[2], bx(2), p.xn, c)
        n.send(i[7], bx(), bx(), p.sib, c)
        n.recv(i[3], by(1), p.yn, c)
        n.send(i[8], by(), by(), p.sib, c)

    def third(self):
        n, p, i, c = self.net, self.place, self.ids, self.cond
        bd = functools.partial(self.at, p.core, p.chip_d)
        n.recv(i[5], bd(1), p.yn, c)
        n.send(i[9], bd(1), bd(1), p.sib, c)
        n.recv(i[6], bd(2), p.xn, c)
        n.send(i[10], bd(2), bd(2), p.sib, c)

    def last(self):
        n, p, i, c = self.net, self.place, self.ids, self.cond
        for idx, q in ((4, p.chip), (7, p.chip_x), (8, p.chip_y)):
            n.recv(i[idx], self.at(p.other, q), p.sib, c)
        n.recv(i[9], self.at(p.other, p.chip_d, 1), p.sib, c)
        n.recv(i[10], self.at(p.other, p.chip_d, 2), p.sib, c)


def hbm(count):
    return [pl.BlockSpec(memory_space=pltpu.HBM)] * count


def comm_params(collective_id):
    return pltpu.CompilerParams(
        collective_id=collective_id, has_side_effects=True, vmem_limit_bytes=56 << 20
    )


def vmem(count):
    return [pl.BlockSpec(memory_space=pltpu.VMEM)] * count


def smem(count):
    return [pl.BlockSpec(memory_space=pltpu.SMEM)] * count


LANES = 256
KT = 128
NT = (((1,), (1,)), ((), ()))
TN = (((0,), (0,)), ((), ()))
NN = (((1,), (0,)), ((), ()))


def mm(a, b, dims=NN):
    return lax.dot_general(a, b, dims, preferred_element_type=f32)


def head_mask(h, head_dim, dtype):
    lane = lax.broadcasted_iota(jnp.int32, (1, LANES), 1)
    inside = jnp.logical_and(lane >= h * head_dim, lane < (h + 1) * head_dim)
    return jnp.where(inside, 1.0, 0.0).astype(dtype)


class Fold:
    def __init__(self, n, seg):
        self.n, self.seg, self.half = n, seg, n * seg
        self.tiles = self.half // KT

    def ranges(self, i):
        a = -(-(self.n - i) * self.seg // KT)
        b = -(-(i + 1) * self.seg // KT)
        assert a + b == self.tiles + 2
        return a, b

    def places(self, i, core, paired):
        a, b = self.ranges(i)
        n, seg = self.n, self.seg
        causal = 1 - paired
        up = n + core * (n // 2) + i
        rows_a = (core * n + n - 1 - i) * causal + up * paired
        rows_b = (core * n + i) * causal + up * paired
        keys_a = core * self.tiles * causal
        keys_b = core * self.tiles * causal + a * paired
        lim_a = (n - 1 - i) * seg - (a - 2) * KT + (1 << 20) * paired
        lim_b = i * seg - (b - 2) * KT - (1 << 20) * paired
        return (rows_a, keys_a, lim_a, a), (rows_b, keys_b, lim_b, b)


def natural(tab, n, s):
    upper = lax.div(s, n)
    c = tab[n + s + upper * (2 * n - 1 - 2 * s)]
    return lax.rem(c, 2), lax.div(c, 2), upper


def key_tiles(ref, base, first, count):
    return ref[pl.ds(base + first, count)].reshape(count * KT, LANES)


def tail_mask(seg, limit):
    col = lax.broadcasted_iota(jnp.int32, (seg, 2 * KT), 1)
    row = lax.broadcasted_iota(jnp.int32, (seg, 2 * KT), 0)
    return col - row <= limit


def chain(*steps):
    def run():
        for fn, *args in steps:
            fn(*args)

    return run


def fill_table(tab, pairs, pairing, chip, n, heads):
    for c in range(n):
        tab[c] = pairs[0, c]
    for a in range(n):
        found = jnp.int32(0)
        for c in range(n):
            found = found + (pairs[0, c] == a).astype(jnp.int32) * c
        tab[n + a] = jnp.minimum(found, n - 1)
    for h in range(heads):
        tab[2 * n + h] = pairing[0, chip * heads + h]


def lse_lane(fold, h, i, g):
    return (h * (fold.n // 2) + i) * 2 + g


def attend_unit(fold, core, h, i, head_dim, tab, q_ref, k_ref, v_ref, o_ref, lse_ref):
    n, seg = fold.n, fold.seg
    paired = tab[2 * n + h]
    pf = paired.astype(f32)
    lanes = head_mask(h, head_dim, f32)
    lanes16 = head_mask(h, head_dim, bf16)
    parts = []
    for rows, keys, limit, count in fold.places(i, core, paired):
        q = q_ref[rows] * lanes16
        tail = mm(q, key_tiles(k_ref, keys, count - 2, 2), NT)
        tail = jnp.where(tail_mask(seg, limit), tail, very_low)
        top = jnp.max(tail, axis=1, keepdims=True)
        main = None
        if count > 2:
            main = mm(q, key_tiles(k_ref, keys, 0, count - 2), NT)
            top = jnp.maximum(top, jnp.max(main, axis=1, keepdims=True))
        parts.append((keys, count, main, tail, top))
    both = jnp.maximum(parts[0][4], parts[1][4])
    joined = jnp.broadcast_to(paired, both.shape) == 1
    outs = []
    for keys, count, main, tail, top in parts:
        top = jnp.where(joined, both, top)
        e = jnp.exp(tail - top)
        total = jnp.sum(e, axis=1, keepdims=True)
        acc = mm(e.astype(bf16), key_tiles(v_ref, keys, count - 2, 2))
        if main is not None:
            e = jnp.exp(main - top)
            total += jnp.sum(e, axis=1, keepdims=True)
            acc += mm(e.astype(bf16), key_tiles(v_ref, keys, 0, count - 2))
        outs.append((top, total, acc))
    (top_a, sum_a, acc_a), (top_b, sum_b, acc_b) = outs
    sum_a, sum_b = sum_a + pf * sum_b, jnp.where(joined, sum_a + sum_b, sum_b)
    acc_a = acc_a + pf * acc_b
    out_a = acc_a * (lanes / sum_a)
    out_b = acc_b * (lanes / sum_b)
    lane = lax.broadcasted_iota(jnp.int32, (1, KT), 1)
    lse = jnp.where(lane == lse_lane(fold, h, i, 0), top_a + jnp.log(sum_a), lse_ref[...])
    lse_ref[...] = jnp.where(lane == lse_lane(fold, h, i, 1), top_b + jnp.log(sum_b), lse)
    far, near, up = core * n + n - 1 - i, core * n + i, n + core * (n // 2) + i
    for at, value in ((far, (1.0 - pf) * out_a), (near, (1.0 - pf) * out_b), (up, pf * out_a)):
        o_ref[at] += value.astype(bf16)


def forward_kernel(
    nz, n, heads, head_dim, rb, n_sem,
    pairs, pairing, x_ref, wsel_ref, wcat_ref,
    xall_o, wqkv_o, q_o, k_o, v_o, on_o, lse_o, attn_o, wfull_o,
    tab, xall, wqkv, q_ref, k_ref, v_ref, o_nat, o_ctx, o_part, o_sum, ssem, rsem, lsem,
):
    p = Place()
    z = p.z
    seg = x_ref.shape[1]
    fold = Fold(n, seg)
    ra = wcat_ref.shape[2] - rb
    ax, bx = pl.ds(0, ra), pl.ds(ra, rb)
    half = wsel_ref.shape[0] // 2
    locals_ = []

    def keep(src, dst):
        cp = pltpu.make_async_copy(src, dst, lsem.at[len(locals_)])
        cp.start()
        locals_.append(cp)
        return cp

    own_x = keep(x_ref, xall.at[p.core, p.chip])
    own_w = keep(wsel_ref, wqkv.at[z])
    greet(p, (p.sib, p.xn, p.yn, p.dn), nz)
    net = Net(ssem, rsem, n_sem)
    tokens_ag = PlaneGather(net, p, lambda: x_ref, lambda k, q: xall.at[k, q], 2)
    tokens_ag.first()
    keep(wcat_ref, wfull_o.at[z])
    can_up, can_down = z < nz - 1, z > 0
    rows = pl.ds(p.core * half, half)
    other = pl.ds(p.other * half, half)

    class Stream:
        def __init__(self, own, at, after):
            self.up = [net.new() for _ in range(nz)]
            self.down = [net.new() for _ in range(nz)]
            self.own, self.at, self.todo = own, at, {}
            for t in range(1, nz):
                self.todo[t] = []
                for ids, src, frm, to, got, more in (
                    (self.up, z - t, p.down, p.up, z >= t, can_up),
                    (self.down, z + t, p.up, p.down, z + t < nz, can_down),
                ):
                    src = jnp.clip(src, 0, nz - 1)
                    on = jnp.logical_and(got, more)
                    self.todo[t].append((ids, src, frm, to, got, on, after(t, src, at, got)))

        def begin(self):
            net.send(self.up[1], self.own, lambda: self.at(z), p.up, can_up)
            net.send(self.down[1], self.own, lambda: self.at(z), p.down, can_down)

        def step(self, t):
            for ids, src, frm, to, got, on, then in self.todo[t]:
                block = functools.partial(self.at, src)
                net.recv(ids[t], block, frm, got)
                if t + 1 < nz:
                    net.send(ids[t + 1], block, block, to, on)
                then()

    def share(waits, block_of):
        def after(t, src, at, got):
            idx = net.new()
            waits.append((idx, lambda: block_of(src), got))
            return lambda: net.send(idx, lambda: at(src), lambda: at(src), p.sib, got)

        return after

    gathers = {t: [] for t in range(1, nz)}

    def spread(t, src, at, got):
        gather = PlaneGather(net, p, lambda: at(src), lambda k, q: wfull_o.at[src, k, q].at[ax], ra, got)
        gathers[t].append(gather)
        return gather.first

    sel_waits, b_waits = [], []
    sel = Stream(
        lambda: wsel_ref.at[rows], lambda o: wqkv.at[o, rows],
        share(sel_waits, lambda o: wqkv.at[o, other]),
    )
    cat_a = Stream(
        lambda: wcat_ref.at[p.core, p.chip].at[ax],
        lambda o: wfull_o.at[o, p.core, p.chip].at[ax],
        spread,
    )
    cat_b = Stream(
        lambda: wcat_ref.at[p.core, :, bx],
        lambda o: wfull_o.at[o, p.core, :, bx],
        share(b_waits, lambda o: wfull_o.at[o, p.other, :, bx]),
    )
    sel.begin()
    cat_a.begin()
    fill_table(tab, pairs, pairing, p.chip, n, heads)
    o_nat[...] = jnp.zeros(o_nat.shape, bf16)
    lse_o[...] = jnp.zeros(lse_o.shape, f32)
    sel.step(1)
    tokens_ag.second()
    cat_a.step(1)
    cat_b.begin()
    for t in range(2, nz):
        sel.step(t)
    tokens_ag.third()
    own_x.wait()
    own_w.wait()
    tokens_ag.last()
    for idx, block, got in sel_waits:
        net.recv(idx, block, p.sib, got)
    keep(xall, xall_o)
    keep(wqkv, wqkv_o)

    def four(i, _):
        tokens = jnp.concatenate([xall[natural(tab, n, 4 * i + u)] for u in range(4)], axis=0)
        qkv = mm(tokens, wqkv[...].reshape(-1, 3 * LANES))
        q = (qkv[:, :LANES].astype(bf16).astype(f32) * score_scale).astype(bf16)
        q_ref[pl.ds(4 * i, 4)] = q.reshape(4, seg, LANES)
        at = pl.ds(i * (4 * seg // KT), 4 * seg // KT)
        k_ref[at] = qkv[:, LANES : 2 * LANES].astype(bf16).reshape(-1, KT, LANES)
        v_ref[at] = qkv[:, 2 * LANES :].astype(bf16).reshape(-1, KT, LANES)
        return 0

    lax.fori_loop(0, n // 2, four, 0)
    for src, dst in ((q_ref, q_o), (k_ref, k_o), (v_ref, v_o)):
        keep(src, dst)

    def second(t):
        for gather in gathers.get(t, ()):
            gather.second()

    def third(t):
        for gather in gathers.get(t, ()):
            gather.third()

    todo = {
        (0, 0): chain((second, 1), (cat_a.step, 2)),
        (0, 2): chain((third, 1), (cat_b.step, 1)),
        (1, 0): chain((second, 2), (cat_a.step, 3)),
        (1, 2): chain((third, 2), (cat_b.step, 2)),
        (2, 0): chain((second, 3)),
        (2, 2): chain((third, 3)),
    }
    def head(h, _):
        for i in range(n // 2):
            attend_unit(fold, p.core, h, i, head_dim, tab, q_ref, k_ref, v_ref, o_nat, lse_o)
            for (at_h, at_i), step in todo.items():
                if at_i == i:
                    pl.when(h == at_h)(step)
        return 0

    lax.fori_loop(0, heads, head, 0)
    keep(o_nat, on_o)
    for core_is in range(2):
        for q in range(n // 2):
            a = tab[2 * q + core_is]
            for u, s in ((0, a), (1, 2 * n - 1 - a)):
                o_ctx[core_is, q, u * seg : (u + 1) * seg, :] = o_nat[s]
    part, swaps = net.new(), [net.new() for _ in range(3)]
    net.send(part, o_ctx.at[p.other], o_part, p.sib)
    net.recv(part, o_part, p.sib)
    pairs_ = ((p.chip_d, p.dn), (p.chip_x, p.xn), (p.chip_y, p.yn))
    for idx, (chip, dev) in zip(swaps, pairs_):
        o_sum[chip] = o_ctx[p.core, chip] + o_part[chip]
        net.send(idx, o_sum.at[chip], attn_o.at[p.chip], dev)
    attn_o[p.chip] = o_ctx[p.core, p.chip] + o_part[p.chip]
    cat_b.step(3)
    for t in gathers:
        for gather in gathers[t]:
            gather.last()
    for idx, (chip, dev) in zip(swaps, pairs_):
        net.recv(idx, attn_o.at[chip], dev)
    for idx, block, got in b_waits:
        net.recv(idx, block, p.sib, got)
    net.finish()
    for cp in locals_[2:]:
        cp.wait()


def forward(nz, n, heads, head_dim, rb, pairs, pairing, x_in, wsel, wcat):
    tok, width = x_in.shape
    seg = tok // 2
    n_sem = 12 * (2 * nz - 1) + 3 * 2 * nz + 4 * nz + 8
    wide, tiled = (2 * n, seg, LANES), (tok * n // KT, KT, LANES)
    shapes = [(2, 4, 2, seg, width), (nz,) + wsel.shape, wide, tiled, tiled]
    block = (4, tok, LANES)
    sds = jax.ShapeDtypeStruct
    return pl.pallas_call(
        functools.partial(forward_kernel, nz, n, heads, head_dim, rb, n_sem),
        out_shape=tuple(sds(s, bf16) for s in shapes)
        + (sds(wide, bf16), sds((tok // 2, KT), f32), sds(block, bf16), sds((nz,) + wcat.shape, bf16)),
        in_specs=smem(2) + vmem(3),
        out_specs=tuple(hbm(6) + vmem(2) + hbm(1)),
        scratch_shapes=[pltpu.SMEM((2 * n + heads,), jnp.int32)]
        + [pltpu.VMEM(s, bf16) for s in shapes]
        + [
            pltpu.VMEM(wide, bf16),
            pltpu.VMEM((2,) + block, bf16),
            pltpu.VMEM(block, bf16),
            pltpu.VMEM(block, bf16),
            pltpu.SemaphoreType.DMA((n_sem,)),
            pltpu.SemaphoreType.DMA((n_sem,)),
            pltpu.SemaphoreType.DMA((12,)),
        ],
        compiler_params=comm_params(0),
        name="forward",
    )(pairs, pairing, x_in.reshape(2, seg, width), wsel, wcat)


def add_into(dst, src, rows, chunk=32):
    if rows % chunk:
        chunk = 16

    def step(i, _):
        at = pl.ds(pl.multiple_of(i * chunk, chunk), chunk)
        to, frm = of(dst), of(src)
        to[at, :] = to[at, :] + frm[at, :]
        return 0

    lax.fori_loop(0, rows // chunk, step, 0)


class Slot:
    def __init__(self, ref, o):
        self.ref, self.o = ref, o

    def __call__(self):
        return self.ref.at[self.o]

    @property
    def at(self):
        return self().at


class PlaneSum:
    def __init__(self, net, place, block, rows, rx0, ry1, ry0, rx1):
        p = place
        self.net, self.place = net, place
        self.rx0, self.ry1, self.ry0, self.rx1 = rx0, ry1, ry0, rx1
        self.h = rows // 2
        h0, h1 = pl.ds(0, self.h), pl.ds(self.h, self.h)
        far_x, far_y = 1 - p.x, 1 - p.y
        self.block, self.h0, self.h1 = block, h0, h1
        self.far_x, self.far_y = far_x, far_y
        self.to_x = [2 * j + far_x for j in range(2)]
        self.to_y = [2 * far_y + j for j in range(2)]
        self.on_y, self.on_x = 2 * far_y + p.x, 2 * p.y + far_x
        self.ids = [net.new() for _ in range(6)]

    def part(self, index, half):
        return lambda: self.block(index).at[half]

    def first(self):
        n, p, i = self.net, self.place, self.ids
        for j in range(2):
            n.send(i[j], self.part(self.to_x[j], self.h0), lambda j=j: self.rx0.at[j], p.xn)
            n.send(i[2 + j], self.part(self.to_y[j], self.h1), lambda j=j: self.ry1.at[j], p.yn)

    def second(self):
        n, p, i = self.net, self.place, self.ids
        on_y, on_x = self.part(self.on_y, self.h0), self.part(self.on_x, self.h1)
        mine0, mine1 = self.part(p.chip, self.h0), self.part(p.chip, self.h1)
        for j in range(2):
            n.recv(i[j], lambda j=j: self.rx0.at[j], p.xn)
        add_into(on_y, lambda: self.rx0.at[self.far_y], self.h)
        n.send(i[4], on_y, self.ry0, p.yn)
        for j in range(2):
            n.recv(i[2 + j], lambda j=j: self.ry1.at[j], p.yn)
        add_into(on_x, lambda: self.ry1.at[self.far_x], self.h)
        n.send(i[5], on_x, self.rx1, p.xn)
        add_into(mine0, lambda: self.rx0.at[p.y], self.h)
        add_into(mine1, lambda: self.ry1.at[p.x], self.h)

    def third(self):
        n, p, i = self.net, self.place, self.ids
        n.recv(i[4], self.ry0, p.yn)
        add_into(self.part(p.chip, self.h0), self.ry0, self.h)
        n.recv(i[5], self.rx1, p.xn)
        add_into(self.part(p.chip, self.h1), self.rx1, self.h)


class LineSum:
    def __init__(self, net, place, nz, whole, low, high, parts, rows):
        p, z, top = place, place.z, nz - 1
        self.net, self.top, self.parts, self.rows, self.whole = net, top, parts, rows, whole
        sides = (
            ([net.new() for _ in range(nz)], low, z, -1, p.down, p.up),
            ([net.new() for _ in range(nz)], high, top - z, 1, p.up, p.down),
        )
        self.todo = {}
        for t in range(nz):
            self.todo[t] = []
            for ids, buf, depth, sign, frm, to in sides:
                owner = jnp.clip(top - t + z if sign < 0 else t + z - top, 0, top)
                takes = jnp.logical_and(depth > 0, depth <= t)
                self.todo[t].append(
                    (ids, owner, buf, takes, depth <= t, frm, to)
                )

    def step(self, t):
        n = self.net
        for ids, owner, buf, takes, sends, frm, to in self.todo[t]:
            whole = functools.partial(self.whole, owner)
            landed = lambda buf=buf, owner=owner: buf.at[owner]

            def take(ids=ids, whole=whole, landed=landed, frm=frm):
                n.recv(ids[t - 1], landed, frm)
                if self.parts is None:
                    add_into(whole, landed, self.rows)
                else:
                    for j in range(self.parts):
                        add_into(
                            lambda j=j: whole().at[j], lambda j=j: landed().at[j], self.rows
                        )

            if t > 0:
                maybe(takes, take)
            if t < self.top:
                n.send(ids[t], whole, landed, to, sends)


def attend_back_unit(
    fold, core, h, i, head_dim, tab, q_ref, k_ref, v_ref, o_ref, lse_ref, da_ref,
    dcat_ref, dk_ref, dv_ref,
):
    n, seg, half = fold.n, fold.seg, fold.half
    paired = tab[2 * n + h]
    pf = paired.astype(f32)
    lanes = head_mask(h, head_dim, f32)
    lanes16 = head_mask(h, head_dim, bf16)
    dqs = []
    places = fold.places(i, core, paired)
    for g, (rows, keys, limit, count) in enumerate(places):
        q = q_ref[rows] * lanes16
        k, c, upper = natural(tab, n, rows)
        da = da_ref[k, c, upper] * lanes16
        delta = jnp.sum(
            da.astype(f32) * o_ref[rows].astype(f32), axis=1, keepdims=True
        )
        lane = lax.broadcasted_iota(jnp.int32, (1, KT), 1) == lse_lane(fold, h, i, g)
        lse = jnp.sum(jnp.where(lane, lse_ref[...], 0.0), axis=1, keepdims=True)
        dq = None
        pieces = [(count - 2, 2, True)]
        if count > 2:
            pieces.append((0, count - 2, False))
        for first, size, masked in pieces:
            kt = key_tiles(k_ref, keys, first, size)
            vt = key_tiles(v_ref, keys, first, size)
            pr = jnp.exp(mm(q, kt, NT) - lse)
            if masked:
                pr = jnp.where(tail_mask(seg, limit), pr, 0.0)
            ds = (pr * (mm(da, vt, NT) - delta)).astype(bf16)
            part = mm(ds, kt)
            dq = part if dq is None else dq + part
            dv = mm(pr.astype(bf16), da, TN)
            dk = mm(ds, q, TN)
            at = pl.ds(first * KT, size * KT)
            if g == 0 or masked:
                dk_ref[at, :] += dk
                dv_ref[at, :] += dv
            else:
                beyond = pl.ds(places[0][3] * KT, size * KT)
                dk_ref[at, :] += (1.0 - pf) * dk
                dv_ref[at, :] += (1.0 - pf) * dv
                dk_ref[beyond, :] += pf * dk
                dv_ref[beyond, :] += pf * dv
        dqs.append(dq)
    scaled = lanes * score_scale
    dq_a, dq_b = (dqs[0] + pf * dqs[1]) * scaled, dqs[1] * scaled
    far, near, up = core * n + n - 1 - i, core * n + i, n + core * (n // 2) + i
    for at, value in ((far, (1.0 - pf) * dq_a), (near, (1.0 - pf) * dq_b), (up, pf * dq_a)):
        dcat_ref[at, :, :LANES] += value.astype(bf16)


def place_key_grads(fold, core, paired, dk_ref, dv_ref, dcat_ref):
    n, seg, half = fold.n, fold.seg, fold.half
    pf = paired.astype(f32)

    def spread(j, _):
        at = pl.ds(pl.multiple_of(j * seg, seg), seg)
        for src, lanes in ((dk_ref, slice(LANES, 2 * LANES)), (dv_ref, slice(2 * LANES, None))):
            value = src[at, :]
            dcat_ref[core * n + j, :, lanes] += ((1.0 - pf) * value).astype(bf16)
            dcat_ref[j, :, lanes] += (pf * value).astype(bf16)
        return 0

    lax.fori_loop(0, n, spread, 0)


def backward_kernel(
    nz, n, heads, head_dim, rb, n_sem,
    pairs, pairing, g_ref, da_in, dh_ref, xall_i, wqkv_i, q_i, k_i, v_i, on_i, lse_ref,
    gsum_o, dtok_o, dw_o,
    tab, g_kept, g_sib, g_rx0, g_ry1, g_ry0, g_rx1, g_low, g_high,
    b_low, b_high, b_rx0, b_ry1, b_ry0, b_rx1,
    x_part, x_sib, x_rx0, x_ry1, x_ry0, x_rx1, w_part, w_sib, w_low, w_high, w_all,
    da_all, xall, wqkv, q_ref, k_ref, v_ref, on_ref, dcat, dk_ref, dv_ref, dw_acc,
    ssem, rsem, lsem,
):
    p = Place()
    z = p.z
    seg, width = xall.shape[3], xall.shape[4]
    tok = 2 * seg
    fold = Fold(n, seg)
    rows = g_ref.shape[3]
    ra = rows - rb
    ax, bx = pl.ds(0, ra), pl.ds(ra, rb)
    order = line_order(nz)
    local = []

    def fetch(src, dst):
        cp = pltpu.make_async_copy(src, dst, lsem.at[len(local)])
        cp.start()
        local.append(cp)
        return cp

    net = Net(ssem, rsem, n_sem)
    own_da = fetch(da_in.at[p.chip], da_all.at[p.core, p.chip])
    own_g = {o: fetch(g_ref.at[o, p.core], g_kept.at[o]) for o in order}
    greet(p, (p.sib, p.xn, p.yn, p.dn), nz)
    swaps = [net.new() for _ in range(7)]
    partners = ((p.chip_d, p.dn), (p.chip_x, p.xn), (p.chip_y, p.yn))
    for i, (chip, dev) in enumerate(partners):
        net.send(swaps[i], da_in.at[chip], da_all.at[p.core, p.chip], dev)
    net.send(swaps[3], da_in.at[p.chip], da_all.at[p.core, p.chip], p.sib)
    sib_ids = {}
    for o in order:
        sib_ids[o] = net.new()
        net.send(sib_ids[o], g_ref.at[o, p.other], g_sib.at[o], p.sib)
    att_in = [
        fetch(src, dst)
        for src, dst in (
            (q_i, q_ref), (k_i, k_ref), (v_i, v_ref), (on_i, on_ref), (xall_i, xall), (wqkv_i, wqkv),
        )
    ]
    fill_table(tab, pairs, pairing, p.chip, n, heads)
    dcat[...] = jnp.zeros(dcat.shape, bf16)

    plane = {
        o: PlaneSum(
            net, p, lambda q, o=o: g_kept.at[o, q].at[ax], ra,
            *(Slot(r, o) for r in (g_rx0, g_ry1, g_ry0, g_rx1)),
        )
        for o in order
    }
    line_a = LineSum(net, p, nz, lambda o: g_kept.at[o, p.chip].at[ax], g_low, g_high, None, ra)
    line_b = LineSum(net, p, nz, lambda o: g_kept.at[o, :, bx], b_low, b_high, n // 2, rb)
    plane_b = PlaneSum(
        net, p, lambda q: g_kept.at[z, q].at[bx], rb, b_rx0, b_ry1, b_ry0, b_rx1
    )

    def chip_sum(o):
        net.recv(sib_ids[o], g_sib.at[o], p.sib)
        own_g[o].wait()
        for q in range(n // 2):
            add_into(g_kept.at[o, q], g_sib.at[o, q], rows)

    for o in order[:2]:
        chip_sum(o)
        plane[o].first()
    line_b.step(0)
    for i, chip, dev in ((1, p.chip_x, p.xn), (2, p.chip_y, p.yn), (0, p.chip_d, p.dn)):
        block = da_all.at[p.core, chip]
        net.recv(swaps[i], block, dev)
        net.send(swaps[4 + i], block, block, p.sib)
    for o in order[2:]:
        chip_sum(o)
        plane[o].first()
    for i, chip in ((3, p.chip), (5, p.chip_x), (6, p.chip_y), (4, p.chip_d)):
        net.recv(swaps[i], da_all.at[p.other, chip], p.sib)
    own_da.wait()
    for cp in att_in:
        cp.wait()

    p0, p1, p2, p3 = (plane[o] for o in order)
    todo = {
        0: chain((p0.second,)),
        1: chain((p1.second,)),
        2: chain((p0.third,), (p1.third,), (line_a.step, 0)),
        3: chain((p2.second,)),
        4: chain((p3.second,), (line_b.step, 1)),
        5: chain((p2.third,), (p3.third,), (line_a.step, 1)),
        7: chain((line_b.step, 2)),
        8: chain((line_a.step, 2)),
        10: chain((line_b.step, 3), (plane_b.first,)),
        11: chain((line_a.step, 3)),
    }
    units = n // 2

    def head(h, _):
        dk_ref[...] = jnp.zeros(dk_ref.shape, f32)
        dv_ref[...] = jnp.zeros(dv_ref.shape, f32)
        for i in range(units):
            attend_back_unit(
                fold, p.core, h, i, head_dim, tab, q_ref, k_ref, v_ref, on_ref, lse_ref, da_all,
                dcat, dk_ref, dv_ref,
            )
            for hh in range(heads):
                if hh * units + i in todo:
                    pl.when(h == hh)(todo[hh * units + i])
        place_key_grads(fold, p.core, tab[2 * n + h], dk_ref, dv_ref, dcat)
        return 0

    lax.fori_loop(0, heads, head, 0)

    def block_grads(k, q):
        a = tab[2 * q + k]
        return jnp.concatenate([dcat[a], dcat[2 * n - 1 - a]], axis=0)

    dw_acc[...] = jnp.zeros(dw_acc.shape, f32)

    def weights(c, _):
        k, q = lax.rem(c, 2), c // 2
        dw_acc[...] += mm(xall[k, q].reshape(tok, width), block_grads(k, q), TN)
        return 0

    lax.fori_loop(0, n, weights, 0)
    d = wqkv.shape[1]
    half = d // 2
    for o in range(nz):
        w_part[0, o] = dw_acc[o * d : o * d + half].astype(bf16)
        w_part[1, o] = dw_acc[o * d + half : (o + 1) * d].astype(bf16)
    w_id = net.new()
    net.send(w_id, w_part.at[p.other], w_sib, p.sib)
    plane_b.second()
    w_line = LineSum(net, p, nz, lambda o: w_part.at[p.core, o], w_low, w_high, None, half)

    def tokens_of(k):
        def one(q, _):
            w = wqkv[...].reshape(-1, 3 * LANES)
            x_part[k, q] = mm(block_grads(k, q), w, NT).astype(bf16)
            return 0

        lax.fori_loop(0, n // 2, one, 0)

    tokens_of(p.other)
    x_id = net.new()
    net.send(x_id, x_part.at[p.other], x_sib, p.sib)
    net.recv(w_id, w_sib, p.sib)
    for o in range(nz):
        add_into(w_part.at[p.core, o], w_sib.at[o], half)
    w_line.step(0)
    plane_b.third()
    final = PlaneGather(net, p, lambda: g_kept.at[z, p.chip], lambda k, q: gsum_o.at[k, q], rows)
    final.first()
    own_sum = fetch(g_kept.at[z, p.chip], gsum_o.at[p.core, p.chip])
    tokens_of(p.core)
    net.recv(x_id, x_sib, p.sib)
    for q in range(n // 2):
        add_into(x_part.at[p.core, q], x_sib.at[q], tok)
    xs = PlaneSum(net, p, lambda q: x_part.at[p.core, q], tok, x_rx0, x_ry1, x_ry0, x_rx1)
    xs.first()
    w_line.step(1)
    final.second()
    w_line.step(2)
    xs.second()
    w_line.step(3)
    w_final = PlaneGather(net, p, lambda: w_part.at[p.core, z], lambda k, q: w_all.at[k, q], half)
    w_final.first()
    own_w = pltpu.make_async_copy(w_part.at[p.core, z], w_all.at[p.core, p.chip], lsem.at[31])
    own_w.start()
    final.third()
    w_final.second()
    xs.third()

    def add_tokens(i, _):
        at = pl.ds(pl.multiple_of(i * 32, 32), 32)
        dtok_o[at, :] = (dh_ref[at, :] + x_part[p.core, p.chip, at, :].astype(f32)).astype(bf16)
        return 0

    lax.fori_loop(0, tok // 32, add_tokens, 0)
    w_final.third()
    w_final.last()
    own_w.wait()
    cols = heads * head_dim
    for j in range(3):
        for k in range(2):
            dw_o[j, k * half : (k + 1) * half, :] = jnp.concatenate(
                [w_all[k, q][:, j * LANES : j * LANES + cols] for q in range(4)], axis=1
            )
    final.last()
    own_sum.wait()
    net.finish()


def line_order(nz):
    order = []
    for i in range((nz + 1) // 2):
        for o in (nz - 1 - i, i):
            if o not in order:
                order.append(o)
    return order


def backward(
    nz, n, heads, head_dim, rb, pairs, pairing, grads, da, dh, xall, wqkv, q, k, v, on, lse
):
    rows, width = grads.shape[3], grads.shape[4]
    seg = xall.shape[3]
    tok = 2 * seg
    d_rows = wqkv.shape[1]
    half = d_rows // 2
    ra = rows - rb
    n_sem = 6 * (nz + 2) + 6 * nz + nz + 9 + 24 + 2
    sds = jax.ShapeDtypeStruct
    vm = lambda *shape: pltpu.VMEM(shape, bf16)
    wide, tiled = (2 * n, seg, LANES), (tok * n // KT, KT, LANES)
    da = da.reshape(4, 2, seg, LANES)
    return pl.pallas_call(
        functools.partial(backward_kernel, nz, n, heads, head_dim, rb, n_sem),
        out_shape=(
            sds(grads.shape[1:], bf16),
            sds((tok, width), bf16),
            sds((3, d_rows, width), bf16),
        ),
        in_specs=smem(2) + hbm(2) + vmem(1) + hbm(6) + vmem(1),
        out_specs=tuple(hbm(1) + vmem(2)),
        scratch_shapes=[
            pltpu.SMEM((2 * n + heads,), jnp.int32),
            vm(nz, 4, rows, width),
            vm(nz, 4, rows, width),
            vm(nz, 2, ra // 2, width),
            vm(nz, 2, ra // 2, width),
            vm(nz, ra // 2, width),
            vm(nz, ra // 2, width),
            vm(nz, ra, width),
            vm(nz, ra, width),
            vm(nz, 4, rb, width),
            vm(nz, 4, rb, width),
            vm(2, rb // 2, width),
            vm(2, rb // 2, width),
            vm(rb // 2, width),
            vm(rb // 2, width),
            vm(2, 4, tok, width),
            vm(4, tok, width),
            vm(2, tok // 2, width),
            vm(2, tok // 2, width),
            vm(tok // 2, width),
            vm(tok // 2, width),
            vm(2, nz, half, width),
            vm(nz, half, width),
            vm(nz, half, width),
            vm(nz, half, width),
            vm(2, 4, half, width),
            vm(2, 4, 2, seg, LANES),
            vm(2, 4, 2, seg, width),
            vm(nz, d_rows, width),
            vm(*wide),
            vm(*tiled),
            vm(*tiled),
            vm(*wide),
            vm(2 * n, seg, 3 * LANES),
            pltpu.VMEM((seg * n, LANES), f32),
            pltpu.VMEM((seg * n, LANES), f32),
            pltpu.VMEM((width, 3 * LANES), f32),
            pltpu.SemaphoreType.DMA((n_sem,)),
            pltpu.SemaphoreType.DMA((n_sem,)),
            pltpu.SemaphoreType.DMA((32,)),
        ],
        compiler_params=comm_params(1),
        name="backward",
    )(pairs, pairing, grads, da, dh, xall, wqkv, q, k, v, on, lse)


def norm_forward(h, gain, shift):
    mean = jnp.mean(h, axis=1, keepdims=True)
    center = h - mean
    scale = lax.rsqrt(jnp.mean(center * center, axis=1, keepdims=True) + norm_eps)
    n = center * scale
    return n, scale, n * gain + shift


def norm_backward(cot, n, scale, gain):
    dn = cot * gain
    mean = jnp.mean(dn, axis=1, keepdims=True)
    along = jnp.mean(dn * n, axis=1, keepdims=True)
    return scale * (dn - mean - n * along)


def middle_kernel(
    nz, cols, n_f, x_ref, a_ref, w_ref, cot_ref, out_ref, da_ref, g_ref, dh_ref,
    w1, w2, wo, lnb, u_ref, z_ref, x1b_ref, acc_ref, n1_ref, r1_ref, dx1_ref, sems,
):
    tok, width = x_ref.shape
    f_rows = w2.shape[1]
    d_rows = cols
    o1, o2, o3 = f_rows, f_rows + n_f * d_rows, f_rows + n_f * d_rows + d_rows
    copies = []

    def fetch(src, dst):
        cp = pltpu.make_async_copy(src, dst, sems.at[len(copies)])
        cp.start()
        copies.append(cp)
        return cp

    first = [fetch(w_ref.at[o, o2:o3], wo.at[o]) for o in range(nz)]
    first += [fetch(w_ref.at[o, o3 : o3 + 16], lnb.at[o]) for o in range(nz)]
    inner = [
        [
            fetch(
                w_ref.at[o, o1 + f * d_rows : o1 + (f + 1) * d_rows],
                w1.at[f, o * d_rows : (o + 1) * d_rows],
            )
            for o in range(nz)
        ]
        for f in range(n_f)
    ]
    outer = [fetch(w_ref.at[o, :f_rows], w2.at[o]) for o in range(nz)]
    for cp in first:
        cp.wait()
    vec = lnb[0].astype(f32)
    for o in range(1, nz):
        vec = vec + lnb[o].astype(f32)
    gain1, gain2, shift1, shift2 = vec[0:1], vec[1:2], vec[2:3], vec[3:4]
    h1 = x_ref[...].astype(f32)
    for o in range(nz):
        h1 = h1 + mm(a_ref[o, :, :cols], wo[o])
    n1, r1, x1 = norm_forward(h1, gain1, shift1)
    n1_ref[...] = n1
    r1_ref[...] = jnp.broadcast_to(r1, (tok, 128))
    x1b_ref[...] = x1.astype(bf16)
    acc_ref[...] = x1
    for group in inner:
        for cp in group:
            cp.wait()
    for cp in outer:
        cp.wait()

    def up(f, _):
        u = mm(x1b_ref[...], w1[f])
        cdf = 0.5 + 0.5 * lax.erf(u * (0.5**0.5))
        z = (u * cdf).astype(bf16)
        z_ref[f] = z
        u_ref[f] = (cdf + u * jnp.exp(-0.5 * u * u) * 0.3989422804014327).astype(u_ref.dtype)
        acc_ref[...] += mm(z, w2[f])
        return 0

    lax.fori_loop(0, n_f, up, 0)
    n2, r2, out = norm_forward(acc_ref[...], gain2, shift2)
    out_ref[...] = out.astype(bf16)
    cot = cot_ref[...].astype(f32)
    d_gain2 = jnp.sum(cot * n2, axis=0, keepdims=True)
    d_shift2 = jnp.sum(cot, axis=0, keepdims=True)
    dh2 = norm_backward(cot, n2, r2, gain2)
    dx1_ref[...] = dh2
    df = dh2.astype(bf16)

    def back(f, _):
        g_ref[f, :f_rows, :] = mm(z_ref[f], df, TN).astype(bf16)
        du = (mm(df, w2[f], NT) * u_ref[f].astype(f32)).astype(bf16)
        dw = mm(x1b_ref[...], du, TN).astype(bf16)
        for o in range(nz):
            at = pl.ds(pl.multiple_of(o1 + f * d_rows, 16), d_rows)
            g_ref[o, at, :] = dw[o * d_rows : (o + 1) * d_rows]
        dx1_ref[...] += mm(du, w1[f], NT)
        return 0

    lax.fori_loop(0, n_f, back, 0)
    d_x1 = dx1_ref[...]
    n1 = n1_ref[...]
    d_gain1 = jnp.sum(d_x1 * n1, axis=0, keepdims=True)
    d_shift1 = jnp.sum(d_x1, axis=0, keepdims=True)
    dh1 = norm_backward(d_x1, n1, r1_ref[:, :1], gain1)
    dh_ref[...] = dh1
    dy = dh1.astype(bf16)
    total = g_ref.shape[1]
    norms = jnp.concatenate([d_gain1, d_gain2, d_shift1, d_shift2], axis=0).astype(bf16)
    for o in range(nz):
        g_ref[o, o2:o3, :] = mm(a_ref[o, :, :cols], dy, TN).astype(bf16)
        g_ref[o, o3:, :] = jnp.zeros((total - o3, width), bf16)
        g_ref[o, o3 : o3 + 4, :] = norms
        da_ref[o, :, :cols] = mm(dy, wo[o], NT).astype(bf16)
        da_ref[o, :, cols:] = jnp.zeros((tok, LANES - cols), bf16)


def middle(nz, cols, n_f, x_in, attn, wfull, cot):
    tok, width = x_in.shape
    vm = lambda dt, *shape: pltpu.VMEM(shape, dt)
    return pl.pallas_call(
        functools.partial(middle_kernel, nz, cols, n_f),
        out_shape=(
            jax.ShapeDtypeStruct((tok, width), bf16),
            jax.ShapeDtypeStruct((nz, tok, LANES), bf16),
            jax.ShapeDtypeStruct(wfull.shape, bf16),
            jax.ShapeDtypeStruct((tok, width), f32),
        ),
        in_specs=vmem(2) + hbm(1) + vmem(1),
        out_specs=tuple(vmem(4)),
        scratch_shapes=[
            vm(bf16, n_f, width, width),
            vm(bf16, nz, width, width),
            vm(bf16, nz, cols, width),
            vm(bf16, nz, 16, width),
            vm(f32, n_f, tok, width),
            vm(bf16, n_f, tok, width),
            vm(bf16, tok, width),
            vm(f32, tok, width),
            vm(f32, tok, width),
            vm(f32, tok, 128),
            vm(f32, tok, width),
            pltpu.SemaphoreType.DMA((3 * nz + n_f * nz,)),
        ],
        compiler_params=pltpu.CompilerParams(vmem_limit_bytes=60 << 20),
        name="middle",
    )(x_in, attn, wfull, cot)


def fast_body(
    tokens,
    w_query,
    w_key,
    w_value,
    w_output,
    w_inner,
    w_outer,
    ln_gain,
    ln_bias,
    pairing,
    block_pairs,
    cotangent,
):
    tok, width = tokens.shape[1], tokens.shape[2]
    n_ctx, nz = lax.axis_size("ctx"), lax.axis_size("fsdp")
    heads = pairing.shape[1]
    head_dim = width // heads
    my_heads = heads // 4
    cols = my_heads * head_dim
    chip = lax.axis_index("ctx") // 2
    d_rows = w_query.shape[0]
    f_rows, ff = w_outer.shape[0], w_inner.shape[1]
    n_f = ff // width
    x_in = tokens[0]

    def chip_cols(w):
        part = lax.dynamic_slice_in_dim(w, chip * cols, cols, 1).astype(bf16)
        return jnp.pad(part, ((0, 0), (0, LANES - cols)))

    wsel = jnp.concatenate([chip_cols(w) for w in (w_query, w_key, w_value)], axis=1)
    z = lax.axis_index("fsdp")
    norms = jnp.concatenate([ln_gain.T, ln_bias.T], axis=0).astype(bf16)
    used = f_rows + n_f * d_rows + d_rows
    total = -(-(used + 4) // 256) * 256
    norms = lax.dynamic_update_slice(jnp.zeros((total - used, width), bf16), norms, (0, z * d_rows))
    wcat = jnp.concatenate(
        [w_outer.astype(bf16)]
        + [w_inner[:, i * width : (i + 1) * width].astype(bf16) for i in range(n_f)]
        + [w_output.astype(bf16), norms],
        axis=0,
    ).reshape(2, 4, total // 8, width)
    xall, wqkv, q, k, v, on, lse, attn, wfull = forward(
        nz, n_ctx, my_heads, head_dim, 64, block_pairs, pairing, x_in, wsel, wcat
    )
    wfull = wfull.reshape(nz, total, width)
    result, da, grads, d_h1 = middle(nz, cols, n_f, x_in, attn, wfull, cotangent[0])
    grads = grads.reshape(nz, 2, 4, total // 8, width)
    gsum, dtok, dw = backward(
        nz, n_ctx, my_heads, head_dim, 64, block_pairs, pairing, grads, da, d_h1,
        xall, wqkv, q, k, v, on, lse,
    )
    gsum = gsum.reshape(total, width)
    o1, o2 = f_rows, f_rows + n_f * d_rows
    g_inner = [gsum[o1 + i * d_rows : o1 + (i + 1) * d_rows] for i in range(n_f)]
    g_norms = lax.dynamic_slice(gsum[used : used + 4], (0, z * d_rows), (4, d_rows)).astype(f32)
    return (
        result[None],
        dtok[None],
        dw[0].astype(f32),
        dw[1].astype(f32),
        dw[2].astype(f32),
        gsum[o2:used].astype(f32),
        jnp.concatenate(g_inner, axis=1).astype(f32),
        gsum[:o1].astype(f32),
        g_norms[:2].T,
        g_norms[2:].T,
    )


def solution(mesh):
    in_specs = (
        P("fsdp", "ctx", None),
        P("fsdp", None),
        P("fsdp", None),
        P("fsdp", None),
        P("fsdp", None),
        P("fsdp", None),
        P("fsdp", None),
        P("fsdp", None),
        P("fsdp", None),
        P("fsdp", None),
        P("fsdp", None),
        P("fsdp", "ctx", None),
    )
    out_specs = (
        P("fsdp", "ctx", None),
        P("fsdp", "ctx", None),
        P("fsdp", None),
        P("fsdp", None),
        P("fsdp", None),
        P("fsdp", None),
        P("fsdp", None),
        P("fsdp", None),
        P("fsdp", None),
        P("fsdp", None),
    )
    fast = mesh.shape["ctx"] == 8 and mesh.shape["fsdp"] == 4
    chosen = fast_body if fast else generic_body
    return jax.shard_map(chosen, mesh=mesh, in_specs=in_specs, out_specs=out_specs, check_vma=False)
```

```python
import functools

import jax
import jax.numpy as jnp
from jax import lax
from jax.experimental import pallas as pl
from jax.experimental.pallas import tpu as pltpu
from jax.sharding import PartitionSpec as P

norm_eps = 1e-05
score_scale = 0.125
very_low = -1e30


def shortened(value):

    def short(part):
        return part.astype(jnp.bfloat16) if part.dtype == jnp.float32 else part

    return jax.tree.map(short, value)


def layer_norm(values, norm_gain, norm_shift):
    center = values - jnp.mean(values, axis=-1, keepdims=True)
    spread = jnp.mean(center * center, axis=-1, keepdims=True)
    return center * lax.rsqrt(spread + norm_eps) * norm_gain + norm_shift


def exact_gelu(values):
    return jax.nn.gelu(values, approximate=False)


def project(rows_in, weight):
    return jnp.dot(rows_in, weight, preferred_element_type=jnp.float32)


def seq_positions(pair_row, tok_dev, seq_len):
    segment_len = tok_dev // 2
    within = jnp.arange(tok_dev, dtype=jnp.int32)
    lower_pos = pair_row[:, None] * segment_len + within[None, :]
    upper_pos = seq_len - (pair_row[:, None] + 1) * segment_len + within[None, :] - segment_len
    return jnp.where(within[None, :] < segment_len, lower_pos, upper_pos).reshape(-1)


def pair_mask(query_pos, key_pos, head_flags, half_len):
    target = (query_pos[None, :] // half_len + head_flags[:, None]) % 2
    paired = key_pos[None, None, :] // half_len == target[:, :, None]
    causal = key_pos[None, :] <= query_pos[:, None]
    return jnp.logical_and(paired, causal[None, :, :])


def block_rows(tok_dev):
    return 2 * tok_dev


def over_blocks(running, arrays, step_fn, tok_dev):
    row_count = arrays[0].shape[0]
    block_len = block_rows(tok_dev)

    def one_step(inner_carry, step_index):
        first_row = step_index * block_len
        sliced = tuple(
            (lax.dynamic_slice_in_dim(member, first_row, block_len, 0) for member in arrays)
        )
        return (step_fn(inner_carry, sliced, first_row), None)

    return lax.scan(one_step, running, jnp.arange(row_count // block_len, dtype=jnp.int32))[0]


def generic_body(
    tokens,
    w_query,
    w_key,
    w_value,
    w_output,
    w_inner,
    w_outer,
    ln_gain,
    ln_bias,
    pairing,
    block_pairs,
    cotangent,
):
    tok_dev = tokens.shape[1]
    width = tokens.shape[2]
    heads = pairing.shape[1]
    head_dim = width // heads
    n_ctx = lax.axis_size("ctx")
    seq_len = tok_dev * n_ctx
    half_len = seq_len // 2
    pos_all = seq_positions(block_pairs[0], tok_dev, seq_len)
    my_pos = lax.dynamic_slice_in_dim(pos_all, lax.axis_index("ctx") * tok_dev, tok_dev, 0)
    head_flags = pairing[0]
    masters = (w_query, w_key, w_value, w_output, w_inner, w_outer, ln_gain, ln_bias)
    low_masters = tuple((member.astype(jnp.bfloat16) for member in masters))
    gathered = jax.tree.map(
        lambda part, own: part.astype(own.dtype),
        lax.all_gather(shortened(low_masters), "fsdp", axis=0, tiled=True),
        low_masters,
    )
    wq_full, wk_full, wv_full, wo_full, inner_full, outer_full, gain_full, shift_full = gathered
    gain_wide = gain_full.astype(jnp.float32)
    shift_wide = shift_full.astype(jnp.float32)
    x_in = tokens[0]
    query_b = project(x_in, wq_full).astype(jnp.bfloat16)
    key_b = project(x_in, wk_full).astype(jnp.bfloat16)
    value_b = project(x_in, wv_full).astype(jnp.bfloat16)
    q_heads = query_b.reshape(tok_dev, heads, head_dim)

    def attend_step(running, sliced, offset):
        run_max, run_sum, run_acc = running
        key_block, value_block = sliced
        block_len = key_block.shape[0]
        key_pos = lax.dynamic_slice_in_dim(pos_all, offset, block_len, 0)
        allowed = pair_mask(my_pos, key_pos, head_flags, half_len)
        key_heads = key_block.reshape(block_len, heads, head_dim)
        value_heads = value_block.reshape(block_len, heads, head_dim)
        scores = (
            jnp.einsum("qhd,khd->hqk", q_heads, key_heads, preferred_element_type=jnp.float32)
            * score_scale
        )
        new_max = jnp.maximum(run_max, jnp.max(jnp.where(allowed, scores, very_low), axis=2))
        prob_rows = jnp.where(
            allowed, jnp.exp(jnp.where(allowed, scores - new_max[:, :, None], 0.0)), 0.0
        )
        decay = jnp.exp(run_max - new_max)
        new_sum = run_sum * decay + jnp.sum(prob_rows, axis=2)
        added = jnp.einsum(
            "hqk,khd->hqd",
            prob_rows.astype(jnp.bfloat16),
            value_heads,
            preferred_element_type=jnp.float32,
        )
        return (new_max, new_sum, run_acc * decay[:, :, None] + added)

    def pair_fold(step_fn, running, fetched):
        return over_blocks(running, fetched, step_fn, tok_dev)

    start_state = (
        jnp.full((heads, tok_dev), very_low, jnp.float32),
        jnp.zeros((heads, tok_dev), jnp.float32),
        jnp.zeros((heads, tok_dev, head_dim), jnp.float32),
    )
    run_max, run_sum, run_acc = pair_fold(
        attend_step,
        start_state,
        (
            lax.all_gather(key_b, "ctx", axis=0, tiled=True),
            lax.all_gather(value_b, "ctx", axis=0, tiled=True),
        ),
    )
    live_rows = run_sum > 0
    safe_sum = jnp.where(live_rows, run_sum, 1.0)
    attn_heads = jnp.where(live_rows[:, :, None], run_acc / safe_sum[:, :, None], 0.0)
    lse_rows = jnp.where(live_rows, run_max + jnp.log(safe_sum), 0.0)
    attn_rows = attn_heads.transpose(1, 0, 2).reshape(tok_dev, width)
    attn_b = attn_rows.astype(jnp.bfloat16)
    branch = project(attn_b, wo_full)
    first_norm, first_pull = jax.vjp(
        layer_norm, x_in.astype(jnp.float32) + branch, gain_wide[:, 0], shift_wide[:, 0]
    )
    first_b = first_norm.astype(jnp.bfloat16)
    inner = project(first_b, inner_full)
    active, gelu_pull = jax.vjp(exact_gelu, inner)
    active_b = active.astype(jnp.bfloat16)
    outer = project(active_b, outer_full)
    result, second_pull = jax.vjp(layer_norm, first_norm + outer, gain_wide[:, 1], shift_wide[:, 1])
    wq_back, wk_back, wv_back, wo_back, inner_back, outer_back, gain_back, shift_back = gathered
    d_h2, d_gain2, d_shift2 = second_pull(cotangent[0].astype(jnp.float32))
    d_f_b = d_h2.astype(jnp.bfloat16)
    d_outer = jnp.dot(active_b.T, d_f_b, preferred_element_type=jnp.float32)
    d_active = jnp.dot(d_f_b, outer_back.T, preferred_element_type=jnp.float32)
    d_u_b = gelu_pull(d_active)[0].astype(jnp.bfloat16)
    d_inner = jnp.dot(first_b.T, d_u_b, preferred_element_type=jnp.float32)
    d_x1 = d_h2 + jnp.dot(d_u_b, inner_back.T, preferred_element_type=jnp.float32)
    d_h1, d_gain1, d_shift1 = first_pull(d_x1)
    d_y_b = d_h1.astype(jnp.bfloat16)
    d_wo = jnp.dot(attn_b.T, d_y_b, preferred_element_type=jnp.float32)
    d_attn_b = jnp.dot(d_y_b, wo_back.T, preferred_element_type=jnp.float32).astype(jnp.bfloat16)
    delta_rows = (
        (d_attn_b.astype(jnp.float32) * attn_rows).reshape(tok_dev, heads, head_dim).sum(axis=2).T
    )
    dout_heads = d_attn_b.reshape(tok_dev, heads, head_dim)

    def query_grad_step(dq_acc, sliced, offset):
        key_block, value_block = sliced
        block_len = key_block.shape[0]
        key_pos = lax.dynamic_slice_in_dim(pos_all, offset, block_len, 0)
        allowed = pair_mask(my_pos, key_pos, head_flags, half_len)
        key_heads = key_block.reshape(block_len, heads, head_dim)
        value_heads = value_block.reshape(block_len, heads, head_dim)
        scores = (
            jnp.einsum("qhd,khd->hqk", q_heads, key_heads, preferred_element_type=jnp.float32)
            * score_scale
        )
        prob_rows = jnp.where(
            allowed, jnp.exp(jnp.where(allowed, scores - lse_rows[:, :, None], 0.0)), 0.0
        )
        prob_grad = jnp.einsum(
            "qhd,khd->hqk", dout_heads, value_heads, preferred_element_type=jnp.float32
        )
        dscore = (prob_rows * (prob_grad - delta_rows[:, :, None]) * score_scale).astype(
            jnp.bfloat16
        )
        return dq_acc + jnp.einsum(
            "hqk,khd->qhd", dscore, key_heads, preferred_element_type=jnp.float32
        )

    dq_start = jnp.zeros((tok_dev, heads, head_dim), jnp.float32)
    dq_acc = pair_fold(
        query_grad_step,
        dq_start,
        (
            lax.all_gather(key_b, "ctx", axis=0, tiled=True),
            lax.all_gather(value_b, "ctx", axis=0, tiled=True),
        ),
    )
    dq_b = dq_acc.reshape(tok_dev, width).astype(jnp.bfloat16)
    lse_all, delta_all = (
        lax.all_gather(lse_rows, "ctx", axis=1, tiled=True),
        lax.all_gather(delta_rows, "ctx", axis=1, tiled=True),
    )
    k_heads = key_b.reshape(tok_dev, heads, head_dim)
    v_heads = value_b.reshape(tok_dev, heads, head_dim)

    def key_grad_step(running, sliced, offset):
        dk_acc, dv_acc = running
        query_block, dout_block = sliced
        block_len = query_block.shape[0]
        query_pos = lax.dynamic_slice_in_dim(pos_all, offset, block_len, 0)
        lse_block = lax.dynamic_slice_in_dim(lse_all, offset, block_len, 1)
        delta_block = lax.dynamic_slice_in_dim(delta_all, offset, block_len, 1)
        allowed = pair_mask(query_pos, my_pos, head_flags, half_len)
        query_heads = query_block.reshape(block_len, heads, head_dim)
        dout_block_heads = dout_block.reshape(block_len, heads, head_dim)
        scores = (
            jnp.einsum("qhd,khd->hqk", query_heads, k_heads, preferred_element_type=jnp.float32)
            * score_scale
        )
        prob_rows = jnp.where(
            allowed, jnp.exp(jnp.where(allowed, scores - lse_block[:, :, None], 0.0)), 0.0
        )
        dv_acc = dv_acc + jnp.einsum(
            "hqk,qhd->khd",
            prob_rows.astype(jnp.bfloat16),
            dout_block_heads,
            preferred_element_type=jnp.float32,
        )
        prob_grad = jnp.einsum(
            "qhd,khd->hqk", dout_block_heads, v_heads, preferred_element_type=jnp.float32
        )
        dscore = (prob_rows * (prob_grad - delta_block[:, :, None]) * score_scale).astype(
            jnp.bfloat16
        )
        dk_acc = dk_acc + jnp.einsum(
            "hqk,qhd->khd", dscore, query_heads, preferred_element_type=jnp.float32
        )
        return (dk_acc, dv_acc)

    kv_start = (
        jnp.zeros((tok_dev, heads, head_dim), jnp.float32),
        jnp.zeros((tok_dev, heads, head_dim), jnp.float32),
    )
    dk_acc, dv_acc = pair_fold(
        key_grad_step,
        kv_start,
        (
            lax.all_gather(query_b, "ctx", axis=0, tiled=True),
            lax.all_gather(d_attn_b, "ctx", axis=0, tiled=True),
        ),
    )
    dk_b = dk_acc.reshape(tok_dev, width).astype(jnp.bfloat16)
    dv_b = dv_acc.reshape(tok_dev, width).astype(jnp.bfloat16)
    d_input = d_h1 + jnp.dot(dq_b, wq_back.T, preferred_element_type=jnp.float32)
    d_input = d_input + jnp.dot(dk_b, wk_back.T, preferred_element_type=jnp.float32)
    d_input = d_input + jnp.dot(dv_b, wv_back.T, preferred_element_type=jnp.float32)
    terms = (
        jnp.dot(x_in.T, dq_b, preferred_element_type=jnp.float32),
        jnp.dot(x_in.T, dk_b, preferred_element_type=jnp.float32),
        jnp.dot(x_in.T, dv_b, preferred_element_type=jnp.float32),
        d_wo,
        d_inner,
        d_outer,
        jnp.stack([d_gain1, d_gain2], axis=1),
        jnp.stack([d_shift1, d_shift2], axis=1),
    )
    shares = (
        lax.psum_scatter(
            terms[0].astype(jnp.bfloat16), "fsdp", scatter_dimension=0, tiled=True
        ).astype(jnp.float32),
        lax.psum_scatter(
            terms[1].astype(jnp.bfloat16), "fsdp", scatter_dimension=0, tiled=True
        ).astype(jnp.float32),
        lax.psum_scatter(
            terms[2].astype(jnp.bfloat16), "fsdp", scatter_dimension=0, tiled=True
        ).astype(jnp.float32),
        lax.psum_scatter(
            terms[3].astype(jnp.bfloat16), "fsdp", scatter_dimension=0, tiled=True
        ).astype(jnp.float32),
        lax.psum_scatter(
            terms[4].astype(jnp.bfloat16), "fsdp", scatter_dimension=0, tiled=True
        ).astype(jnp.float32),
        lax.psum_scatter(
            terms[5].astype(jnp.bfloat16), "fsdp", scatter_dimension=0, tiled=True
        ).astype(jnp.float32),
        lax.psum_scatter(
            terms[6].astype(jnp.bfloat16), "fsdp", scatter_dimension=0, tiled=True
        ).astype(jnp.float32),
        lax.psum_scatter(
            terms[7].astype(jnp.bfloat16), "fsdp", scatter_dimension=0, tiled=True
        ).astype(jnp.float32),
    )
    totals = (
        lax.psum(shares[0].astype(jnp.bfloat16), "ctx").astype(jnp.float32),
        lax.psum(shares[1].astype(jnp.bfloat16), "ctx").astype(jnp.float32),
        lax.psum(shares[2].astype(jnp.bfloat16), "ctx").astype(jnp.float32),
        lax.psum(shares[3].astype(jnp.bfloat16), "ctx").astype(jnp.float32),
        lax.psum(shares[4].astype(jnp.bfloat16), "ctx").astype(jnp.float32),
        lax.psum(shares[5].astype(jnp.bfloat16), "ctx").astype(jnp.float32),
        lax.psum(shares[6].astype(jnp.bfloat16), "ctx").astype(jnp.float32),
        lax.psum(shares[7].astype(jnp.bfloat16), "ctx").astype(jnp.float32),
    )
    return (
        result.astype(jnp.bfloat16)[None],
        d_input.astype(jnp.bfloat16)[None],
        totals[0],
        totals[1],
        totals[2],
        totals[3],
        totals[4],
        totals[5],
        totals[6],
        totals[7],
    )


MESH = pl.DeviceIdType.MESH
f32 = jnp.float32
bf16 = jnp.bfloat16


class Place:
    def __init__(self):
        me = lax.axis_index("ctx")
        self.me = me
        self.z = lax.axis_index("fsdp")
        self.core = lax.rem(me, 2)
        self.chip = me // 2
        self.x = lax.rem(self.chip, 2)
        self.y = self.chip // 2
        self.chip_x = self.chip + 1 - 2 * self.x
        self.chip_y = self.chip + 2 - 4 * self.y
        self.chip_d = 3 - self.chip
        self.other = 1 - self.core
        self.sib = (2 * self.chip + 1 - self.core, self.z)
        self.xn = (2 * self.chip_x + self.core, self.z)
        self.yn = (2 * self.chip_y + self.core, self.z)
        self.dn = (2 * self.chip_d + self.core, self.z)
        self.up = (me, self.z + 1)
        self.down = (me, self.z - 1)


def greet(place, others, line_len=None):
    barrier = pltpu.get_barrier_semaphore()
    count = len(others)
    for other in others:
        pl.semaphore_signal(barrier, inc=1, device_id=other, device_id_type=MESH)
    if line_len is not None:

        @pl.when(place.z < line_len - 1)
        def _():
            pl.semaphore_signal(barrier, inc=1, device_id=place.up, device_id_type=MESH)

        @pl.when(place.z > 0)
        def _():
            pl.semaphore_signal(barrier, inc=1, device_id=place.down, device_id_type=MESH)

        count = count + jnp.where(place.z < line_len - 1, 1, 0) + jnp.where(place.z > 0, 1, 0)

    pl.semaphore_wait(barrier, count)


def maybe(cond, fn):
    if cond is None:
        fn()
    else:
        pl.when(cond)(fn)


def of(ref):
    return ref() if callable(ref) else ref


class Net:
    def __init__(self, send_sems, recv_sems, count):
        self.send_sems, self.recv_sems, self.count = send_sems, recv_sems, count
        self.used = 0
        self.open = []

    def new(self):
        self.used += 1
        assert self.used <= self.count
        return self.used - 1

    def copy(self, idx, src, dst, dev):
        return pltpu.make_async_remote_copy(
            src_ref=src,
            dst_ref=dst,
            send_sem=self.send_sems.at[idx],
            recv_sem=self.recv_sems.at[idx],
            device_id=dev,
            device_id_type=MESH,
        )

    def send(self, idx, src, dst, dev, cond=None):
        make = lambda: self.copy(idx, of(src), of(dst), dev)
        maybe(cond, lambda: make().start())
        self.open.append((cond, make))

    def recv(self, idx, dst, dev, cond=None):
        maybe(cond, lambda: self.copy(idx, of(dst), of(dst), dev).wait_recv())

    def finish(self):
        for cond, make in self.open:
            maybe(cond, lambda make=make: make().wait_send())
        self.open = []


class PlaneGather:
    def __init__(self, net, place, own, slot, rows, cond=None):
        p = place
        self.net, self.place, self.cond = net, place, cond
        self.own_of, self.slot = own, slot
        self.h0, self.h1 = pl.ds(0, rows // 2), pl.ds(rows // 2, rows // 2)
        self.ids = [net.new() for _ in range(11)]

    def at(self, core, chip, half=0):
        def view():
            ref = self.slot(core, chip)
            return ref if half == 0 else ref.at[self.h0 if half == 1 else self.h1]

        return view

    def mine(self, half=0):
        def view():
            ref = self.own_of()
            return ref if half == 0 else ref.at[self.h0 if half == 1 else self.h1]

        return view

    def first(self):
        n, p, i, c = self.net, self.place, self.ids, self.cond
        at = functools.partial(self.at, p.core, p.chip)
        n.send(i[0], self.mine(1), at(1), p.xn, c)
        n.send(i[1], self.mine(2), at(2), p.yn, c)
        n.send(i[2], self.mine(2), at(2), p.xn, c)
        n.send(i[3], self.mine(1), at(1), p.yn, c)
        n.send(i[4], self.mine(), at(), p.sib, c)

    def second(self):
        n, p, i, c = self.net, self.place, self.ids, self.cond
        bx = functools.partial(self.at, p.core, p.chip_x)
        by = functools.partial(self.at, p.core, p.chip_y)
        n.recv(i[0], bx(1), p.xn, c)
        n.send(i[5], bx(1), bx(1), p.yn, c)
        n.recv(i[1], by(2), p.yn, c)
        n.send(i[6], by(2), by(2), p.xn, c)
        n.recv(i[2], bx(2), p.xn, c)
        n.send(i[7], bx(), bx(), p.sib, c)
        n.recv(i[3], by(1), p.yn, c)
        n.send(i[8], by(), by(), p.sib, c)

    def third(self):
        n, p, i, c = self.net, self.place, self.ids, self.cond
        bd = functools.partial(self.at, p.core, p.chip_d)
        n.recv(i[5], bd(1), p.yn, c)
        n.send(i[9], bd(1), bd(1), p.sib, c)
        n.recv(i[6], bd(2), p.xn, c)
        n.send(i[10], bd(2), bd(2), p.sib, c)

    def last(self):
        n, p, i, c = self.net, self.place, self.ids, self.cond
        for idx, q in ((4, p.chip), (7, p.chip_x), (8, p.chip_y)):
            n.recv(i[idx], self.at(p.other, q), p.sib, c)
        n.recv(i[9], self.at(p.other, p.chip_d, 1), p.sib, c)
        n.recv(i[10], self.at(p.other, p.chip_d, 2), p.sib, c)


def hbm(count):
    return [pl.BlockSpec(memory_space=pltpu.HBM)] * count


def comm_params(collective_id):
    return pltpu.CompilerParams(
        collective_id=collective_id, has_side_effects=True, vmem_limit_bytes=56 << 20
    )


def vmem(count):
    return [pl.BlockSpec(memory_space=pltpu.VMEM)] * count


def smem(count):
    return [pl.BlockSpec(memory_space=pltpu.SMEM)] * count


LANES = 256
KT = 128
NT = (((1,), (1,)), ((), ()))
TN = (((0,), (0,)), ((), ()))
NN = (((1,), (0,)), ((), ()))


def mm(a, b, dims=NN):
    return lax.dot_general(a, b, dims, preferred_element_type=f32)


def head_mask(h, head_dim, dtype):
    lane = lax.broadcasted_iota(jnp.int32, (1, LANES), 1)
    inside = jnp.logical_and(lane >= h * head_dim, lane < (h + 1) * head_dim)
    return jnp.where(inside, 1.0, 0.0).astype(dtype)


class Fold:
    def __init__(self, n, seg):
        self.n, self.seg, self.half = n, seg, n * seg
        self.tiles = self.half // KT

    def ranges(self, i):
        a = -(-(self.n - i) * self.seg // KT)
        b = -(-(i + 1) * self.seg // KT)
        assert a + b == self.tiles + 2
        return a, b

    def places(self, i, core, paired):
        a, b = self.ranges(i)
        n, seg = self.n, self.seg
        causal = 1 - paired
        up = n + core * (n // 2) + i
        rows_a = (core * n + n - 1 - i) * causal + up * paired
        rows_b = (core * n + i) * causal + up * paired
        keys_a = core * self.tiles * causal
        keys_b = core * self.tiles * causal + a * paired
        lim_a = (n - 1 - i) * seg - (a - 2) * KT + (1 << 20) * paired
        lim_b = i * seg - (b - 2) * KT - (1 << 20) * paired
        return (rows_a, keys_a, lim_a, a), (rows_b, keys_b, lim_b, b)


def natural(tab, n, s):
    upper = lax.div(s, n)
    c = tab[n + s + upper * (2 * n - 1 - 2 * s)]
    return lax.rem(c, 2), lax.div(c, 2), upper


def key_tiles(ref, base, first, count):
    return ref[pl.ds(base + first, count)].reshape(count * KT, LANES)


def tail_mask(seg, limit):
    col = lax.broadcasted_iota(jnp.int32, (seg, 2 * KT), 1)
    row = lax.broadcasted_iota(jnp.int32, (seg, 2 * KT), 0)
    return col - row <= limit


def chain(*steps):
    def run():
        for fn, *args in steps:
            fn(*args)

    return run


def fill_table(tab, pairs, pairing, chip, n, heads):
    for c in range(n):
        tab[c] = pairs[0, c]
    for a in range(n):
        found = jnp.int32(0)
        for c in range(n):
            found = found + (pairs[0, c] == a).astype(jnp.int32) * c
        tab[n + a] = jnp.minimum(found, n - 1)
    for h in range(heads):
        tab[2 * n + h] = pairing[0, chip * heads + h]


def lse_lane(fold, h, i, g):
    return (h * (fold.n // 2) + i) * 2 + g


def attend_unit(fold, core, h, i, head_dim, tab, q_ref, k_ref, v_ref, o_ref, lse_ref):
    n, seg = fold.n, fold.seg
    paired = tab[2 * n + h]
    pf = paired.astype(f32)
    lanes = head_mask(h, head_dim, f32)
    lanes16 = head_mask(h, head_dim, bf16)
    parts = []
    for rows, keys, limit, count in fold.places(i, core, paired):
        q = q_ref[rows] * lanes16
        tail = mm(q, key_tiles(k_ref, keys, count - 2, 2), NT)
        tail = jnp.where(tail_mask(seg, limit), tail, very_low)
        top = jnp.max(tail, axis=1, keepdims=True)
        main = None
        if count > 2:
            main = mm(q, key_tiles(k_ref, keys, 0, count - 2), NT)
            top = jnp.maximum(top, jnp.max(main, axis=1, keepdims=True))
        parts.append((keys, count, main, tail, top))
    both = jnp.maximum(parts[0][4], parts[1][4])
    joined = jnp.broadcast_to(paired, both.shape) == 1
    outs = []
    for keys, count, main, tail, top in parts:
        top = jnp.where(joined, both, top)
        e = jnp.exp(tail - top)
        total = jnp.sum(e, axis=1, keepdims=True)
        acc = mm(e.astype(bf16), key_tiles(v_ref, keys, count - 2, 2))
        if main is not None:
            e = jnp.exp(main - top)
            total += jnp.sum(e, axis=1, keepdims=True)
            acc += mm(e.astype(bf16), key_tiles(v_ref, keys, 0, count - 2))
        outs.append((top, total, acc))
    (top_a, sum_a, acc_a), (top_b, sum_b, acc_b) = outs
    sum_a, sum_b = sum_a + pf * sum_b, jnp.where(joined, sum_a + sum_b, sum_b)
    acc_a = acc_a + pf * acc_b
    out_a = acc_a * (lanes / sum_a)
    out_b = acc_b * (lanes / sum_b)
    lane = lax.broadcasted_iota(jnp.int32, (1, KT), 1)
    lse = jnp.where(lane == lse_lane(fold, h, i, 0), top_a + jnp.log(sum_a), lse_ref[...])
    lse_ref[...] = jnp.where(lane == lse_lane(fold, h, i, 1), top_b + jnp.log(sum_b), lse)
    far, near, up = core * n + n - 1 - i, core * n + i, n + core * (n // 2) + i
    for at, value in ((far, (1.0 - pf) * out_a), (near, (1.0 - pf) * out_b), (up, pf * out_a)):
        o_ref[at] += value.astype(bf16)


def forward_kernel(
    nz, n, heads, head_dim, rb, n_sem,
    pairs, pairing, x_ref, wsel_ref, wcat_ref,
    xall_o, wqkv_o, q_o, k_o, v_o, on_o, lse_o, attn_o, wfull_o,
    tab, xall, wqkv, q_ref, k_ref, v_ref, o_nat, o_ctx, o_part, o_sum, ssem, rsem, lsem,
):
    p = Place()
    z = p.z
    seg = x_ref.shape[1]
    fold = Fold(n, seg)
    ra = wcat_ref.shape[2] - rb
    ax, bx = pl.ds(0, ra), pl.ds(ra, rb)
    half = wsel_ref.shape[0] // 2
    locals_ = []

    def keep(src, dst):
        cp = pltpu.make_async_copy(src, dst, lsem.at[len(locals_)])
        cp.start()
        locals_.append(cp)
        return cp

    own_x = keep(x_ref, xall.at[p.core, p.chip])
    own_w = keep(wsel_ref, wqkv.at[z])
    greet(p, (p.sib, p.xn, p.yn, p.dn), nz)
    net = Net(ssem, rsem, n_sem)
    tokens_ag = PlaneGather(net, p, lambda: x_ref, lambda k, q: xall.at[k, q], 2)
    tokens_ag.first()
    keep(wcat_ref, wfull_o.at[z])
    can_up, can_down = z < nz - 1, z > 0
    rows = pl.ds(p.core * half, half)
    other = pl.ds(p.other * half, half)

    class Stream:
        def __init__(self, own, at, after):
            self.up = [net.new() for _ in range(nz)]
            self.down = [net.new() for _ in range(nz)]
            self.own, self.at, self.todo = own, at, {}
            for t in range(1, nz):
                self.todo[t] = []
                for ids, src, frm, to, got, more in (
                    (self.up, z - t, p.down, p.up, z >= t, can_up),
                    (self.down, z + t, p.up, p.down, z + t < nz, can_down),
                ):
                    src = jnp.clip(src, 0, nz - 1)
                    on = jnp.logical_and(got, more)
                    self.todo[t].append((ids, src, frm, to, got, on, after(t, src, at, got)))

        def begin(self):
            net.send(self.up[1], self.own, lambda: self.at(z), p.up, can_up)
            net.send(self.down[1], self.own, lambda: self.at(z), p.down, can_down)

        def step(self, t):
            for ids, src, frm, to, got, on, then in self.todo[t]:
                block = functools.partial(self.at, src)
                net.recv(ids[t], block, frm, got)
                if t + 1 < nz:
                    net.send(ids[t + 1], block, block, to, on)
                then()

    def share(waits, block_of):
        def after(t, src, at, got):
            idx = net.new()
            waits.append((idx, lambda: block_of(src), got))
            return lambda: net.send(idx, lambda: at(src), lambda: at(src), p.sib, got)

        return after

    gathers = {t: [] for t in range(1, nz)}

    def spread(t, src, at, got):
        gather = PlaneGather(net, p, lambda: at(src), lambda k, q: wfull_o.at[src, k, q].at[ax], ra, got)
        gathers[t].append(gather)
        return gather.first

    sel_waits, b_waits = [], []
    sel = Stream(
        lambda: wsel_ref.at[rows], lambda o: wqkv.at[o, rows],
        share(sel_waits, lambda o: wqkv.at[o, other]),
    )
    cat_a = Stream(
        lambda: wcat_ref.at[p.core, p.chip].at[ax],
        lambda o: wfull_o.at[o, p.core, p.chip].at[ax],
        spread,
    )
    cat_b = Stream(
        lambda: wcat_ref.at[p.core, :, bx],
        lambda o: wfull_o.at[o, p.core, :, bx],
        share(b_waits, lambda o: wfull_o.at[o, p.other, :, bx]),
    )
    sel.begin()
    fill_table(tab, pairs, pairing, p.chip, n, heads)
    o_nat[...] = jnp.zeros(o_nat.shape, bf16)
    lse_o[...] = jnp.zeros(lse_o.shape, f32)
    sel.step(1)
    cat_a.begin()
    for t in range(2, nz):
        sel.step(t)
    tokens_ag.second()
    cat_a.step(1)
    tokens_ag.third()
    cat_a.step(2)
    cat_b.begin()
    own_x.wait()
    own_w.wait()
    tokens_ag.last()
    for idx, block, got in sel_waits:
        net.recv(idx, block, p.sib, got)
    keep(xall, xall_o)
    keep(wqkv, wqkv_o)

    def four(i, _):
        tokens = jnp.concatenate([xall[natural(tab, n, 4 * i + u)] for u in range(4)], axis=0)
        qkv = mm(tokens, wqkv[...].reshape(-1, 3 * LANES))
        q = (qkv[:, :LANES].astype(bf16).astype(f32) * score_scale).astype(bf16)
        q_ref[pl.ds(4 * i, 4)] = q.reshape(4, seg, LANES)
        at = pl.ds(i * (4 * seg // KT), 4 * seg // KT)
        k_ref[at] = qkv[:, LANES : 2 * LANES].astype(bf16).reshape(-1, KT, LANES)
        v_ref[at] = qkv[:, 2 * LANES :].astype(bf16).reshape(-1, KT, LANES)
        return 0

    lax.fori_loop(0, n // 2, four, 0)
    for src, dst in ((q_ref, q_o), (k_ref, k_o), (v_ref, v_o)):
        keep(src, dst)

    def second(t):
        for gather in gathers.get(t, ()):
            gather.second()

    def third(t):
        for gather in gathers.get(t, ()):
            gather.third()

    todo = {
        (0, 1): chain((second, 1)),
        (0, 2): chain((cat_a.step, 3)),
        (1, 1): chain((third, 1), (second, 2)),
        (2, 0): chain((cat_b.step, 1), (third, 2)),
        (2, 2): chain((second, 3)),
    }

    def head(h, _):
        for i in range(n // 2):
            attend_unit(fold, p.core, h, i, head_dim, tab, q_ref, k_ref, v_ref, o_nat, lse_o)
            for (at_h, at_i), step in todo.items():
                if at_i == i:
                    pl.when(h == at_h)(step)
        return 0

    lax.fori_loop(0, heads, head, 0)
    keep(o_nat, on_o)
    for core_is in range(2):
        for q in range(n // 2):
            a = tab[2 * q + core_is]
            for u, s in ((0, a), (1, 2 * n - 1 - a)):
                o_ctx[core_is, q, u * seg : (u + 1) * seg, :] = o_nat[s]
    part, swaps = net.new(), [net.new() for _ in range(3)]
    net.send(part, o_ctx.at[p.other], o_part, p.sib)
    cat_b.step(2)
    net.recv(part, o_part, p.sib)
    pairs_ = ((p.chip_d, p.dn), (p.chip_x, p.xn), (p.chip_y, p.yn))
    for idx, (chip, dev) in zip(swaps, pairs_):
        o_sum[chip] = o_ctx[p.core, chip] + o_part[chip]
        net.send(idx, o_sum.at[chip], attn_o.at[p.chip], dev)
    attn_o[p.chip] = o_ctx[p.core, p.chip] + o_part[p.chip]
    third(3)
    cat_b.step(3)
    for t in gathers:
        for gather in gathers[t]:
            gather.last()
    for idx, (chip, dev) in zip(swaps, pairs_):
        net.recv(idx, attn_o.at[chip], dev)
    for idx, block, got in b_waits:
        net.recv(idx, block, p.sib, got)
    net.finish()
    for cp in locals_[2:]:
        cp.wait()


def forward(nz, n, heads, head_dim, rb, pairs, pairing, x_in, wsel, wcat):
    tok, width = x_in.shape
    seg = tok // 2
    n_sem = 12 * (2 * nz - 1) + 3 * 2 * nz + 4 * nz + 8
    wide, tiled = (2 * n, seg, LANES), (tok * n // KT, KT, LANES)
    shapes = [(2, 4, 2, seg, width), (nz,) + wsel.shape, wide, tiled, tiled]
    block = (4, tok, LANES)
    sds = jax.ShapeDtypeStruct
    return pl.pallas_call(
        functools.partial(forward_kernel, nz, n, heads, head_dim, rb, n_sem),
        out_shape=tuple(sds(s, bf16) for s in shapes)
        + (sds(wide, bf16), sds((tok // 2, KT), f32), sds(block, bf16), sds((nz,) + wcat.shape, bf16)),
        in_specs=smem(2) + vmem(3),
        out_specs=tuple(hbm(6) + vmem(2) + hbm(1)),
        scratch_shapes=[pltpu.SMEM((2 * n + heads,), jnp.int32)]
        + [pltpu.VMEM(s, bf16) for s in shapes]
        + [
            pltpu.VMEM(wide, bf16),
            pltpu.VMEM((2,) + block, bf16),
            pltpu.VMEM(block, bf16),
            pltpu.VMEM(block, bf16),
            pltpu.SemaphoreType.DMA((n_sem,)),
            pltpu.SemaphoreType.DMA((n_sem,)),
            pltpu.SemaphoreType.DMA((12,)),
        ],
        compiler_params=comm_params(0),
        name="forward",
    )(pairs, pairing, x_in.reshape(2, seg, width), wsel, wcat)


def add_into(dst, src, rows, chunk=32):
    if rows % chunk:
        chunk = 16

    def step(i, _):
        at = pl.ds(pl.multiple_of(i * chunk, chunk), chunk)
        to, frm = of(dst), of(src)
        to[at, :] = to[at, :] + frm[at, :]
        return 0

    lax.fori_loop(0, rows // chunk, step, 0)


class Slot:
    def __init__(self, ref, o):
        self.ref, self.o = ref, o

    def __call__(self):
        return self.ref.at[self.o]

    @property
    def at(self):
        return self().at


class PlaneSum:
    def __init__(self, net, place, block, rows, rx0, ry1, ry0, rx1):
        p = place
        self.net, self.place = net, place
        self.rx0, self.ry1, self.ry0, self.rx1 = rx0, ry1, ry0, rx1
        self.h = rows // 2
        h0, h1 = pl.ds(0, self.h), pl.ds(self.h, self.h)
        far_x, far_y = 1 - p.x, 1 - p.y
        self.block, self.h0, self.h1 = block, h0, h1
        self.far_x, self.far_y = far_x, far_y
        self.to_x = [2 * j + far_x for j in range(2)]
        self.to_y = [2 * far_y + j for j in range(2)]
        self.on_y, self.on_x = 2 * far_y + p.x, 2 * p.y + far_x
        self.ids = [net.new() for _ in range(6)]

    def part(self, index, half):
        return lambda: self.block(index).at[half]

    def first(self):
        n, p, i = self.net, self.place, self.ids
        for j in range(2):
            n.send(i[j], self.part(self.to_x[j], self.h0), lambda j=j: self.rx0.at[j], p.xn)
            n.send(i[2 + j], self.part(self.to_y[j], self.h1), lambda j=j: self.ry1.at[j], p.yn)

    def second(self):
        n, p, i = self.net, self.place, self.ids
        on_y, on_x = self.part(self.on_y, self.h0), self.part(self.on_x, self.h1)
        mine0, mine1 = self.part(p.chip, self.h0), self.part(p.chip, self.h1)
        for j in range(2):
            n.recv(i[j], lambda j=j: self.rx0.at[j], p.xn)
        add_into(on_y, lambda: self.rx0.at[self.far_y], self.h)
        n.send(i[4], on_y, self.ry0, p.yn)
        for j in range(2):
            n.recv(i[2 + j], lambda j=j: self.ry1.at[j], p.yn)
        add_into(on_x, lambda: self.ry1.at[self.far_x], self.h)
        n.send(i[5], on_x, self.rx1, p.xn)
        add_into(mine0, lambda: self.rx0.at[p.y], self.h)
        add_into(mine1, lambda: self.ry1.at[p.x], self.h)

    def third(self):
        n, p, i = self.net, self.place, self.ids
        n.recv(i[4], self.ry0, p.yn)
        add_into(self.part(p.chip, self.h0), self.ry0, self.h)
        n.recv(i[5], self.rx1, p.xn)
        add_into(self.part(p.chip, self.h1), self.rx1, self.h)


class LineSum:
    def __init__(self, net, place, nz, whole, low, high, parts, rows):
        p, z, top = place, place.z, nz - 1
        self.net, self.top, self.parts, self.rows, self.whole = net, top, parts, rows, whole
        sides = (
            ([net.new() for _ in range(nz)], low, z, -1, p.down, p.up),
            ([net.new() for _ in range(nz)], high, top - z, 1, p.up, p.down),
        )
        self.todo = {}
        for t in range(nz):
            self.todo[t] = []
            for ids, buf, depth, sign, frm, to in sides:
                owner = jnp.clip(top - t + z if sign < 0 else t + z - top, 0, top)
                takes = jnp.logical_and(depth > 0, depth <= t)
                self.todo[t].append(
                    (ids, owner, buf, takes, depth <= t, frm, to)
                )

    def step(self, t):
        n = self.net
        for ids, owner, buf, takes, sends, frm, to in self.todo[t]:
            whole = functools.partial(self.whole, owner)
            landed = lambda buf=buf, owner=owner: buf.at[owner]

            def take(ids=ids, whole=whole, landed=landed, frm=frm):
                n.recv(ids[t - 1], landed, frm)
                if self.parts is None:
                    add_into(whole, landed, self.rows)
                else:
                    for j in range(self.parts):
                        add_into(
                            lambda j=j: whole().at[j], lambda j=j: landed().at[j], self.rows
                        )

            if t > 0:
                maybe(takes, take)
            if t < self.top:
                n.send(ids[t], whole, landed, to, sends)


def attend_back_unit(
    fold, core, h, i, head_dim, tab, q_ref, k_ref, v_ref, o_ref, lse_ref, da_ref,
    dcat_ref, dk_ref, dv_ref,
):
    n, seg, half = fold.n, fold.seg, fold.half
    paired = tab[2 * n + h]
    pf = paired.astype(f32)
    lanes = head_mask(h, head_dim, f32)
    lanes16 = head_mask(h, head_dim, bf16)
    dqs = []
    places = fold.places(i, core, paired)
    for g, (rows, keys, limit, count) in enumerate(places):
        q = q_ref[rows] * lanes16
        k, c, upper = natural(tab, n, rows)
        da = da_ref[k, c, upper] * lanes16
        delta = jnp.sum(
            da.astype(f32) * o_ref[rows].astype(f32), axis=1, keepdims=True
        )
        lane = lax.broadcasted_iota(jnp.int32, (1, KT), 1) == lse_lane(fold, h, i, g)
        lse = jnp.sum(jnp.where(lane, lse_ref[...], 0.0), axis=1, keepdims=True)
        dq = None
        pieces = [(count - 2, 2, True)]
        if count > 2:
            pieces.append((0, count - 2, False))
        for first, size, masked in pieces:
            kt = key_tiles(k_ref, keys, first, size)
            vt = key_tiles(v_ref, keys, first, size)
            pr = jnp.exp(mm(q, kt, NT) - lse)
            if masked:
                pr = jnp.where(tail_mask(seg, limit), pr, 0.0)
            ds = (pr * (mm(da, vt, NT) - delta)).astype(bf16)
            part = mm(ds, kt)
            dq = part if dq is None else dq + part
            dv = mm(pr.astype(bf16), da, TN)
            dk = mm(ds, q, TN)
            at = pl.ds(first * KT, size * KT)
            if g == 0 or masked:
                dk_ref[at, :] += dk
                dv_ref[at, :] += dv
            else:
                beyond = pl.ds(places[0][3] * KT, size * KT)
                dk_ref[at, :] += (1.0 - pf) * dk
                dv_ref[at, :] += (1.0 - pf) * dv
                dk_ref[beyond, :] += pf * dk
                dv_ref[beyond, :] += pf * dv
        dqs.append(dq)
    scaled = lanes * score_scale
    dq_a, dq_b = (dqs[0] + pf * dqs[1]) * scaled, dqs[1] * scaled
    far, near, up = core * n + n - 1 - i, core * n + i, n + core * (n // 2) + i
    for at, value in ((far, (1.0 - pf) * dq_a), (near, (1.0 - pf) * dq_b), (up, pf * dq_a)):
        dcat_ref[at, :, :LANES] += value.astype(bf16)


def place_key_grads(fold, core, paired, dk_ref, dv_ref, dcat_ref):
    n, seg, half = fold.n, fold.seg, fold.half
    pf = paired.astype(f32)

    def spread(j, _):
        at = pl.ds(pl.multiple_of(j * seg, seg), seg)
        for src, lanes in ((dk_ref, slice(LANES, 2 * LANES)), (dv_ref, slice(2 * LANES, None))):
            value = src[at, :]
            dcat_ref[core * n + j, :, lanes] += ((1.0 - pf) * value).astype(bf16)
            dcat_ref[j, :, lanes] += (pf * value).astype(bf16)
        return 0

    lax.fori_loop(0, n, spread, 0)


def backward_kernel(
    nz, n, heads, head_dim, rb, n_sem,
    pairs, pairing, g_ref, da_in, dh_ref, xall_i, wqkv_i, q_i, k_i, v_i, on_i, lse_ref,
    gsum_o, dtok_o, dw_o,
    tab, g_kept, g_sib, g_rx0, g_ry1, g_ry0, g_rx1, g_low, g_high,
    b_low, b_high, b_rx0, b_ry1, b_ry0, b_rx1,
    x_part, x_sib, x_rx0, x_ry1, x_ry0, x_rx1, w_part, w_sib, w_low, w_high, w_all,
    da_all, xall, wqkv, q_ref, k_ref, v_ref, on_ref, dcat, dk_ref, dv_ref, dw_acc,
    ssem, rsem, lsem,
):
    p = Place()
    z = p.z
    seg, width = xall.shape[3], xall.shape[4]
    tok = 2 * seg
    fold = Fold(n, seg)
    rows = g_ref.shape[3]
    ra = rows - rb
    ax, bx = pl.ds(0, ra), pl.ds(ra, rb)
    order = line_order(nz)
    local = []

    def fetch(src, dst):
        cp = pltpu.make_async_copy(src, dst, lsem.at[len(local)])
        cp.start()
        local.append(cp)
        return cp

    net = Net(ssem, rsem, n_sem)
    own_da = fetch(da_in.at[p.chip], da_all.at[p.core, p.chip])
    own_g = {o: fetch(g_ref.at[o, p.core], g_kept.at[o]) for o in order}
    greet(p, (p.sib, p.xn, p.yn, p.dn), nz)
    swaps = [net.new() for _ in range(7)]
    partners = ((p.chip_d, p.dn), (p.chip_x, p.xn), (p.chip_y, p.yn))
    for i, (chip, dev) in enumerate(partners):
        net.send(swaps[i], da_in.at[chip], da_all.at[p.core, p.chip], dev)
    net.send(swaps[3], da_in.at[p.chip], da_all.at[p.core, p.chip], p.sib)
    sib_ids = {o: net.new() for o in order}

    def to_sib(o):
        net.send(sib_ids[o], lambda: g_ref.at[o, p.other], lambda: g_sib.at[o], p.sib)

    to_sib(order[0])
    to_sib(order[1])
    att_in = [
        fetch(src, dst)
        for src, dst in (
            (q_i, q_ref), (k_i, k_ref), (v_i, v_ref), (on_i, on_ref), (xall_i, xall), (wqkv_i, wqkv),
        )
    ]
    fill_table(tab, pairs, pairing, p.chip, n, heads)
    dcat[...] = jnp.zeros(dcat.shape, bf16)

    plane = {
        o: PlaneSum(
            net, p, lambda q, o=o: g_kept.at[o, q].at[ax], ra,
            *(Slot(r, o) for r in (g_rx0, g_ry1, g_ry0, g_rx1)),
        )
        for o in order
    }
    line_a = LineSum(net, p, nz, lambda o: g_kept.at[o, p.chip].at[ax], g_low, g_high, None, ra)
    line_b = LineSum(net, p, nz, lambda o: g_kept.at[o, :, bx], b_low, b_high, n // 2, rb)
    plane_b = PlaneSum(
        net, p, lambda q: g_kept.at[z, q].at[bx], rb, b_rx0, b_ry1, b_ry0, b_rx1
    )

    def chip_sum(o):
        net.recv(sib_ids[o], lambda: g_sib.at[o], p.sib)
        pltpu.make_async_copy(g_ref.at[o, p.core], g_kept.at[o], lsem.at[1 + order.index(o)]).wait()
        for q in range(n // 2):
            add_into(lambda q=q: g_kept.at[o, q], lambda q=q: g_sib.at[o, q], rows)

    p0, p1, p2, p3 = (plane[o] for o in order)
    chip_sum(order[0])
    p0.first()
    to_sib(order[2])
    chip_sum(order[1])
    p1.first()
    to_sib(order[3])
    line_b.step(0)
    for i, chip, dev in ((1, p.chip_x, p.xn), (2, p.chip_y, p.yn), (0, p.chip_d, p.dn)):
        block = da_all.at[p.core, chip]
        net.recv(swaps[i], block, dev)
        net.send(swaps[4 + i], block, block, p.sib)
    for i, chip in ((3, p.chip), (5, p.chip_x), (6, p.chip_y), (4, p.chip_d)):
        net.recv(swaps[i], da_all.at[p.other, chip], p.sib)
    own_da.wait()
    for cp in att_in:
        cp.wait()

    todo = {
        0: chain((chip_sum, order[2]), (chip_sum, order[3])),
        1: chain((p0.second,)),
        2: chain((p1.second,), (p2.first,), (line_b.step, 1)),
        3: chain((p0.third,), (p3.first,)),
        4: chain((p1.third,), (line_a.step, 0)),
        5: chain((p2.second,)),
        6: chain((line_b.step, 2), (p3.second,)),
        7: chain((p2.third,)),
        8: chain((p3.third,), (line_a.step, 1)),
        9: chain((line_b.step, 3), (plane_b.first,)),
        10: chain((line_a.step, 2)),
        11: chain((plane_b.second,)),
    }
    units = n // 2

    def head(h, _):
        dk_ref[...] = jnp.zeros(dk_ref.shape, f32)
        dv_ref[...] = jnp.zeros(dv_ref.shape, f32)
        for i in range(units):
            attend_back_unit(
                fold, p.core, h, i, head_dim, tab, q_ref, k_ref, v_ref, on_ref, lse_ref, da_all,
                dcat, dk_ref, dv_ref,
            )
            for hh in range(heads):
                if hh * units + i in todo:
                    pl.when(h == hh)(todo[hh * units + i])
        place_key_grads(fold, p.core, tab[2 * n + h], dk_ref, dv_ref, dcat)
        return 0

    lax.fori_loop(0, heads, head, 0)

    def block_grads(k, q):
        a = tab[2 * q + k]
        return jnp.concatenate([dcat[a], dcat[2 * n - 1 - a]], axis=0)

    dw_acc[...] = jnp.zeros(dw_acc.shape, f32)

    def weights(c, _):
        k, q = lax.rem(c, 2), c // 2
        dw_acc[...] += mm(xall[k, q].reshape(tok, width), block_grads(k, q), TN)
        return 0

    lax.fori_loop(0, n, weights, 0)
    d = wqkv.shape[1]
    half = d // 2
    for o in range(nz):
        w_part[0, o] = dw_acc[o * d : o * d + half].astype(bf16)
        w_part[1, o] = dw_acc[o * d + half : (o + 1) * d].astype(bf16)
    w_id = net.new()
    net.send(w_id, w_part.at[p.other], w_sib, p.sib)
    w_line = LineSum(net, p, nz, lambda o: w_part.at[p.core, o], w_low, w_high, None, half)

    def tokens_of(k):
        def one(q, _):
            w = wqkv[...].reshape(-1, 3 * LANES)
            x_part[k, q] = mm(block_grads(k, q), w, NT).astype(bf16)
            return 0

        lax.fori_loop(0, n // 2, one, 0)

    tokens_of(p.other)
    x_id = net.new()
    net.send(x_id, x_part.at[p.other], x_sib, p.sib)
    net.recv(w_id, w_sib, p.sib)
    for o in range(nz):
        add_into(w_part.at[p.core, o], w_sib.at[o], half)
    w_line.step(0)
    tokens_of(p.core)
    net.recv(x_id, x_sib, p.sib)
    for q in range(n // 2):
        add_into(x_part.at[p.core, q], x_sib.at[q], tok)
    xs = PlaneSum(net, p, lambda q: x_part.at[p.core, q], tok, x_rx0, x_ry1, x_ry0, x_rx1)
    xs.first()
    line_a.step(3)
    plane_b.third()
    final = PlaneGather(net, p, lambda: g_kept.at[z, p.chip], lambda k, q: gsum_o.at[k, q], rows)
    final.first()
    own_sum = fetch(g_kept.at[z, p.chip], gsum_o.at[p.core, p.chip])
    w_line.step(1)
    xs.second()
    w_line.step(2)
    final.second()
    w_line.step(3)
    w_final = PlaneGather(net, p, lambda: w_part.at[p.core, z], lambda k, q: w_all.at[k, q], half)
    w_final.first()
    own_w = pltpu.make_async_copy(w_part.at[p.core, z], w_all.at[p.core, p.chip], lsem.at[31])
    own_w.start()
    final.third()
    w_final.second()
    xs.third()

    def add_tokens(i, _):
        at = pl.ds(pl.multiple_of(i * 32, 32), 32)
        dtok_o[at, :] = (dh_ref[at, :] + x_part[p.core, p.chip, at, :].astype(f32)).astype(bf16)
        return 0

    lax.fori_loop(0, tok // 32, add_tokens, 0)
    w_final.third()
    w_final.last()
    own_w.wait()
    cols = heads * head_dim
    for j in range(3):
        for k in range(2):
            dw_o[j, k * half : (k + 1) * half, :] = jnp.concatenate(
                [w_all[k, q][:, j * LANES : j * LANES + cols] for q in range(4)], axis=1
            )
    final.last()
    own_sum.wait()
    net.finish()


def line_order(nz):
    order = []
    for i in range((nz + 1) // 2):
        for o in (nz - 1 - i, i):
            if o not in order:
                order.append(o)
    return order


def backward(
    nz, n, heads, head_dim, rb, pairs, pairing, grads, da, dh, xall, wqkv, q, k, v, on, lse
):
    rows, width = grads.shape[3], grads.shape[4]
    seg = xall.shape[3]
    tok = 2 * seg
    d_rows = wqkv.shape[1]
    half = d_rows // 2
    ra = rows - rb
    n_sem = 6 * (nz + 2) + 6 * nz + nz + 9 + 24 + 2
    sds = jax.ShapeDtypeStruct
    vm = lambda *shape: pltpu.VMEM(shape, bf16)
    wide, tiled = (2 * n, seg, LANES), (tok * n // KT, KT, LANES)
    da = da.reshape(4, 2, seg, LANES)
    return pl.pallas_call(
        functools.partial(backward_kernel, nz, n, heads, head_dim, rb, n_sem),
        out_shape=(
            sds(grads.shape[1:], bf16),
            sds((tok, width), bf16),
            sds((3, d_rows, width), bf16),
        ),
        in_specs=smem(2) + hbm(2) + vmem(1) + hbm(6) + vmem(1),
        out_specs=tuple(hbm(1) + vmem(2)),
        scratch_shapes=[
            pltpu.SMEM((2 * n + heads,), jnp.int32),
            vm(nz, 4, rows, width),
            vm(nz, 4, rows, width),
            vm(nz, 2, ra // 2, width),
            vm(nz, 2, ra // 2, width),
            vm(nz, ra // 2, width),
            vm(nz, ra // 2, width),
            vm(nz, ra, width),
            vm(nz, ra, width),
            vm(nz, 4, rb, width),
            vm(nz, 4, rb, width),
            vm(2, rb // 2, width),
            vm(2, rb // 2, width),
            vm(rb // 2, width),
            vm(rb // 2, width),
            vm(2, 4, tok, width),
            vm(4, tok, width),
            vm(2, tok // 2, width),
            vm(2, tok // 2, width),
            vm(tok // 2, width),
            vm(tok // 2, width),
            vm(2, nz, half, width),
            vm(nz, half, width),
            vm(nz, half, width),
            vm(nz, half, width),
            vm(2, 4, half, width),
            vm(2, 4, 2, seg, LANES),
            vm(2, 4, 2, seg, width),
            vm(nz, d_rows, width),
            vm(*wide),
            vm(*tiled),
            vm(*tiled),
            vm(*wide),
            vm(2 * n, seg, 3 * LANES),
            pltpu.VMEM((seg * n, LANES), f32),
            pltpu.VMEM((seg * n, LANES), f32),
            pltpu.VMEM((width, 3 * LANES), f32),
            pltpu.SemaphoreType.DMA((n_sem,)),
            pltpu.SemaphoreType.DMA((n_sem,)),
            pltpu.SemaphoreType.DMA((32,)),
        ],
        compiler_params=comm_params(1),
        name="backward",
    )(pairs, pairing, grads, da, dh, xall, wqkv, q, k, v, on, lse)


def norm_forward(h, gain, shift):
    mean = jnp.mean(h, axis=1, keepdims=True)
    center = h - mean
    scale = lax.rsqrt(jnp.mean(center * center, axis=1, keepdims=True) + norm_eps)
    n = center * scale
    return n, scale, n * gain + shift


def norm_backward(cot, n, scale, gain):
    dn = cot * gain
    mean = jnp.mean(dn, axis=1, keepdims=True)
    along = jnp.mean(dn * n, axis=1, keepdims=True)
    return scale * (dn - mean - n * along)


def middle_kernel(
    nz, cols, n_f, x_ref, a_ref, w_ref, cot_ref, out_ref, da_ref, g_ref, dh_ref,
    w1, w2, wo, lnb, u_ref, z_ref, x1b_ref, acc_ref, n1_ref, r1_ref, dx1_ref, sems,
):
    tok, width = x_ref.shape
    f_rows = w2.shape[1]
    d_rows = cols
    o1, o2, o3 = f_rows, f_rows + n_f * d_rows, f_rows + n_f * d_rows + d_rows
    copies = []

    def fetch(src, dst):
        cp = pltpu.make_async_copy(src, dst, sems.at[len(copies)])
        cp.start()
        copies.append(cp)
        return cp

    first = [fetch(w_ref.at[o, o2:o3], wo.at[o]) for o in range(nz)]
    first += [fetch(w_ref.at[o, o3 : o3 + 16], lnb.at[o]) for o in range(nz)]
    inner = [
        [
            fetch(
                w_ref.at[o, o1 + f * d_rows : o1 + (f + 1) * d_rows],
                w1.at[f, o * d_rows : (o + 1) * d_rows],
            )
            for o in range(nz)
        ]
        for f in range(n_f)
    ]
    outer = [fetch(w_ref.at[o, :f_rows], w2.at[o]) for o in range(nz)]
    for cp in first:
        cp.wait()
    vec = lnb[0].astype(f32)
    for o in range(1, nz):
        vec = vec + lnb[o].astype(f32)
    gain1, gain2, shift1, shift2 = vec[0:1], vec[1:2], vec[2:3], vec[3:4]
    h1 = x_ref[...].astype(f32)
    for o in range(nz):
        h1 = h1 + mm(a_ref[o, :, :cols], wo[o])
    n1, r1, x1 = norm_forward(h1, gain1, shift1)
    n1_ref[...] = n1
    r1_ref[...] = jnp.broadcast_to(r1, (tok, 128))
    x1b_ref[...] = x1.astype(bf16)
    acc_ref[...] = x1
    for group in inner:
        for cp in group:
            cp.wait()
    for cp in outer:
        cp.wait()

    def up(f, _):
        u = mm(x1b_ref[...], w1[f])
        cdf = 0.5 + 0.5 * lax.erf(u * (0.5**0.5))
        z = (u * cdf).astype(bf16)
        z_ref[f] = z
        u_ref[f] = (cdf + u * jnp.exp(-0.5 * u * u) * 0.3989422804014327).astype(u_ref.dtype)
        acc_ref[...] += mm(z, w2[f])
        return 0

    lax.fori_loop(0, n_f, up, 0)
    n2, r2, out = norm_forward(acc_ref[...], gain2, shift2)
    out_ref[...] = out.astype(bf16)
    cot = cot_ref[...].astype(f32)
    d_gain2 = jnp.sum(cot * n2, axis=0, keepdims=True)
    d_shift2 = jnp.sum(cot, axis=0, keepdims=True)
    dh2 = norm_backward(cot, n2, r2, gain2)
    dx1_ref[...] = dh2
    df = dh2.astype(bf16)

    def back(f, _):
        g_ref[f, :f_rows, :] = mm(z_ref[f], df, TN).astype(bf16)
        du = (mm(df, w2[f], NT) * u_ref[f].astype(f32)).astype(bf16)
        dw = mm(x1b_ref[...], du, TN).astype(bf16)
        for o in range(nz):
            at = pl.ds(pl.multiple_of(o1 + f * d_rows, 16), d_rows)
            g_ref[o, at, :] = dw[o * d_rows : (o + 1) * d_rows]
        dx1_ref[...] += mm(du, w1[f], NT)
        return 0

    lax.fori_loop(0, n_f, back, 0)
    d_x1 = dx1_ref[...]
    n1 = n1_ref[...]
    d_gain1 = jnp.sum(d_x1 * n1, axis=0, keepdims=True)
    d_shift1 = jnp.sum(d_x1, axis=0, keepdims=True)
    dh1 = norm_backward(d_x1, n1, r1_ref[:, :1], gain1)
    dh_ref[...] = dh1
    dy = dh1.astype(bf16)
    total = g_ref.shape[1]
    norms = jnp.concatenate([d_gain1, d_gain2, d_shift1, d_shift2], axis=0).astype(bf16)
    for o in range(nz):
        g_ref[o, o2:o3, :] = mm(a_ref[o, :, :cols], dy, TN).astype(bf16)
        g_ref[o, o3:, :] = jnp.zeros((total - o3, width), bf16)
        g_ref[o, o3 : o3 + 4, :] = norms
        da_ref[o, :, :cols] = mm(dy, wo[o], NT).astype(bf16)
        da_ref[o, :, cols:] = jnp.zeros((tok, LANES - cols), bf16)


def middle(nz, cols, n_f, x_in, attn, wfull, cot):
    tok, width = x_in.shape
    vm = lambda dt, *shape: pltpu.VMEM(shape, dt)
    return pl.pallas_call(
        functools.partial(middle_kernel, nz, cols, n_f),
        out_shape=(
            jax.ShapeDtypeStruct((tok, width), bf16),
            jax.ShapeDtypeStruct((nz, tok, LANES), bf16),
            jax.ShapeDtypeStruct(wfull.shape, bf16),
            jax.ShapeDtypeStruct((tok, width), f32),
        ),
        in_specs=vmem(2) + hbm(1) + vmem(1),
        out_specs=tuple(vmem(4)),
        scratch_shapes=[
            vm(bf16, n_f, width, width),
            vm(bf16, nz, width, width),
            vm(bf16, nz, cols, width),
            vm(bf16, nz, 16, width),
            vm(f32, n_f, tok, width),
            vm(bf16, n_f, tok, width),
            vm(bf16, tok, width),
            vm(f32, tok, width),
            vm(f32, tok, width),
            vm(f32, tok, 128),
            vm(f32, tok, width),
            pltpu.SemaphoreType.DMA((3 * nz + n_f * nz,)),
        ],
        compiler_params=pltpu.CompilerParams(vmem_limit_bytes=60 << 20),
        name="middle",
    )(x_in, attn, wfull, cot)


def fast_body(
    tokens,
    w_query,
    w_key,
    w_value,
    w_output,
    w_inner,
    w_outer,
    ln_gain,
    ln_bias,
    pairing,
    block_pairs,
    cotangent,
):
    tok, width = tokens.shape[1], tokens.shape[2]
    n_ctx, nz = lax.axis_size("ctx"), lax.axis_size("fsdp")
    heads = pairing.shape[1]
    head_dim = width // heads
    my_heads = heads // 4
    cols = my_heads * head_dim
    chip = lax.axis_index("ctx") // 2
    d_rows = w_query.shape[0]
    f_rows, ff = w_outer.shape[0], w_inner.shape[1]
    n_f = ff // width
    x_in = tokens[0]

    def chip_cols(w):
        part = lax.dynamic_slice_in_dim(w, chip * cols, cols, 1).astype(bf16)
        return jnp.pad(part, ((0, 0), (0, LANES - cols)))

    wsel = jnp.concatenate([chip_cols(w) for w in (w_query, w_key, w_value)], axis=1)
    z = lax.axis_index("fsdp")
    norms = jnp.concatenate([ln_gain.T, ln_bias.T], axis=0).astype(bf16)
    used = f_rows + n_f * d_rows + d_rows
    total = -(-(used + 4) // 256) * 256
    norms = lax.dynamic_update_slice(jnp.zeros((total - used, width), bf16), norms, (0, z * d_rows))
    wcat = jnp.concatenate(
        [w_outer.astype(bf16)]
        + [w_inner[:, i * width : (i + 1) * width].astype(bf16) for i in range(n_f)]
        + [w_output.astype(bf16), norms],
        axis=0,
    ).reshape(2, 4, total // 8, width)
    xall, wqkv, q, k, v, on, lse, attn, wfull = forward(
        nz, n_ctx, my_heads, head_dim, 64, block_pairs, pairing, x_in, wsel, wcat
    )
    wfull = wfull.reshape(nz, total, width)
    result, da, grads, d_h1 = middle(nz, cols, n_f, x_in, attn, wfull, cotangent[0])
    grads = grads.reshape(nz, 2, 4, total // 8, width)
    gsum, dtok, dw = backward(
        nz, n_ctx, my_heads, head_dim, 64, block_pairs, pairing, grads, da, d_h1,
        xall, wqkv, q, k, v, on, lse,
    )
    gsum = gsum.reshape(total, width)
    o1, o2 = f_rows, f_rows + n_f * d_rows
    g_inner = [gsum[o1 + i * d_rows : o1 + (i + 1) * d_rows] for i in range(n_f)]
    g_norms = lax.dynamic_slice(gsum[used : used + 4], (0, z * d_rows), (4, d_rows)).astype(f32)
    return (
        result[None],
        dtok[None],
        dw[0].astype(f32),
        dw[1].astype(f32),
        dw[2].astype(f32),
        gsum[o2:used].astype(f32),
        jnp.concatenate(g_inner, axis=1).astype(f32),
        gsum[:o1].astype(f32),
        g_norms[:2].T,
        g_norms[2:].T,
    )


def solution(mesh):
    in_specs = (
        P("fsdp", "ctx", None),
        P("fsdp", None),
        P("fsdp", None),
        P("fsdp", None),
        P("fsdp", None),
        P("fsdp", None),
        P("fsdp", None),
        P("fsdp", None),
        P("fsdp", None),
        P("fsdp", None),
        P("fsdp", None),
        P("fsdp", "ctx", None),
    )
    out_specs = (
        P("fsdp", "ctx", None),
        P("fsdp", "ctx", None),
        P("fsdp", None),
        P("fsdp", None),
        P("fsdp", None),
        P("fsdp", None),
        P("fsdp", None),
        P("fsdp", None),
        P("fsdp", None),
        P("fsdp", None),
    )
    fast = mesh.shape["ctx"] == 8 and mesh.shape["fsdp"] == 4
    chosen = fast_body if fast else generic_body
    return jax.shard_map(chosen, mesh=mesh, in_specs=in_specs, out_specs=out_specs, check_vma=False)
```

```python
import functools

import jax
import jax.numpy as jnp
from jax import lax
from jax.experimental import pallas as pl
from jax.experimental.pallas import tpu as pltpu
from jax.sharding import PartitionSpec as P

norm_eps = 1e-05
score_scale = 0.125
very_low = -1e30


def shortened(value):

    def short(part):
        return part.astype(jnp.bfloat16) if part.dtype == jnp.float32 else part

    return jax.tree.map(short, value)


def layer_norm(values, norm_gain, norm_shift):
    center = values - jnp.mean(values, axis=-1, keepdims=True)
    spread = jnp.mean(center * center, axis=-1, keepdims=True)
    return center * lax.rsqrt(spread + norm_eps) * norm_gain + norm_shift


def exact_gelu(values):
    return jax.nn.gelu(values, approximate=False)


def project(rows_in, weight):
    return jnp.dot(rows_in, weight, preferred_element_type=jnp.float32)


def seq_positions(pair_row, tok_dev, seq_len):
    segment_len = tok_dev // 2
    within = jnp.arange(tok_dev, dtype=jnp.int32)
    lower_pos = pair_row[:, None] * segment_len + within[None, :]
    upper_pos = seq_len - (pair_row[:, None] + 1) * segment_len + within[None, :] - segment_len
    return jnp.where(within[None, :] < segment_len, lower_pos, upper_pos).reshape(-1)


def pair_mask(query_pos, key_pos, head_flags, half_len):
    target = (query_pos[None, :] // half_len + head_flags[:, None]) % 2
    paired = key_pos[None, None, :] // half_len == target[:, :, None]
    causal = key_pos[None, :] <= query_pos[:, None]
    return jnp.logical_and(paired, causal[None, :, :])


def block_rows(tok_dev):
    return 2 * tok_dev


def over_blocks(running, arrays, step_fn, tok_dev):
    row_count = arrays[0].shape[0]
    block_len = block_rows(tok_dev)

    def one_step(inner_carry, step_index):
        first_row = step_index * block_len
        sliced = tuple(
            (lax.dynamic_slice_in_dim(member, first_row, block_len, 0) for member in arrays)
        )
        return (step_fn(inner_carry, sliced, first_row), None)

    return lax.scan(one_step, running, jnp.arange(row_count // block_len, dtype=jnp.int32))[0]


def generic_body(
    tokens,
    w_query,
    w_key,
    w_value,
    w_output,
    w_inner,
    w_outer,
    ln_gain,
    ln_bias,
    pairing,
    block_pairs,
    cotangent,
):
    tok_dev = tokens.shape[1]
    width = tokens.shape[2]
    heads = pairing.shape[1]
    head_dim = width // heads
    n_ctx = lax.axis_size("ctx")
    seq_len = tok_dev * n_ctx
    half_len = seq_len // 2
    pos_all = seq_positions(block_pairs[0], tok_dev, seq_len)
    my_pos = lax.dynamic_slice_in_dim(pos_all, lax.axis_index("ctx") * tok_dev, tok_dev, 0)
    head_flags = pairing[0]
    masters = (w_query, w_key, w_value, w_output, w_inner, w_outer, ln_gain, ln_bias)
    low_masters = tuple((member.astype(jnp.bfloat16) for member in masters))
    gathered = jax.tree.map(
        lambda part, own: part.astype(own.dtype),
        lax.all_gather(shortened(low_masters), "fsdp", axis=0, tiled=True),
        low_masters,
    )
    wq_full, wk_full, wv_full, wo_full, inner_full, outer_full, gain_full, shift_full = gathered
    gain_wide = gain_full.astype(jnp.float32)
    shift_wide = shift_full.astype(jnp.float32)
    x_in = tokens[0]
    query_b = project(x_in, wq_full).astype(jnp.bfloat16)
    key_b = project(x_in, wk_full).astype(jnp.bfloat16)
    value_b = project(x_in, wv_full).astype(jnp.bfloat16)
    q_heads = query_b.reshape(tok_dev, heads, head_dim)

    def attend_step(running, sliced, offset):
        run_max, run_sum, run_acc = running
        key_block, value_block = sliced
        block_len = key_block.shape[0]
        key_pos = lax.dynamic_slice_in_dim(pos_all, offset, block_len, 0)
        allowed = pair_mask(my_pos, key_pos, head_flags, half_len)
        key_heads = key_block.reshape(block_len, heads, head_dim)
        value_heads = value_block.reshape(block_len, heads, head_dim)
        scores = (
            jnp.einsum("qhd,khd->hqk", q_heads, key_heads, preferred_element_type=jnp.float32)
            * score_scale
        )
        new_max = jnp.maximum(run_max, jnp.max(jnp.where(allowed, scores, very_low), axis=2))
        prob_rows = jnp.where(
            allowed, jnp.exp(jnp.where(allowed, scores - new_max[:, :, None], 0.0)), 0.0
        )
        decay = jnp.exp(run_max - new_max)
        new_sum = run_sum * decay + jnp.sum(prob_rows, axis=2)
        added = jnp.einsum(
            "hqk,khd->hqd",
            prob_rows.astype(jnp.bfloat16),
            value_heads,
            preferred_element_type=jnp.float32,
        )
        return (new_max, new_sum, run_acc * decay[:, :, None] + added)

    def pair_fold(step_fn, running, fetched):
        return over_blocks(running, fetched, step_fn, tok_dev)

    start_state = (
        jnp.full((heads, tok_dev), very_low, jnp.float32),
        jnp.zeros((heads, tok_dev), jnp.float32),
        jnp.zeros((heads, tok_dev, head_dim), jnp.float32),
    )
    run_max, run_sum, run_acc = pair_fold(
        attend_step,
        start_state,
        (
            lax.all_gather(key_b, "ctx", axis=0, tiled=True),
            lax.all_gather(value_b, "ctx", axis=0, tiled=True),
        ),
    )
    live_rows = run_sum > 0
    safe_sum = jnp.where(live_rows, run_sum, 1.0)
    attn_heads = jnp.where(live_rows[:, :, None], run_acc / safe_sum[:, :, None], 0.0)
    lse_rows = jnp.where(live_rows, run_max + jnp.log(safe_sum), 0.0)
    attn_rows = attn_heads.transpose(1, 0, 2).reshape(tok_dev, width)
    attn_b = attn_rows.astype(jnp.bfloat16)
    branch = project(attn_b, wo_full)
    first_norm, first_pull = jax.vjp(
        layer_norm, x_in.astype(jnp.float32) + branch, gain_wide[:, 0], shift_wide[:, 0]
    )
    first_b = first_norm.astype(jnp.bfloat16)
    inner = project(first_b, inner_full)
    active, gelu_pull = jax.vjp(exact_gelu, inner)
    active_b = active.astype(jnp.bfloat16)
    outer = project(active_b, outer_full)
    result, second_pull = jax.vjp(layer_norm, first_norm + outer, gain_wide[:, 1], shift_wide[:, 1])
    wq_back, wk_back, wv_back, wo_back, inner_back, outer_back, gain_back, shift_back = gathered
    d_h2, d_gain2, d_shift2 = second_pull(cotangent[0].astype(jnp.float32))
    d_f_b = d_h2.astype(jnp.bfloat16)
    d_outer = jnp.dot(active_b.T, d_f_b, preferred_element_type=jnp.float32)
    d_active = jnp.dot(d_f_b, outer_back.T, preferred_element_type=jnp.float32)
    d_u_b = gelu_pull(d_active)[0].astype(jnp.bfloat16)
    d_inner = jnp.dot(first_b.T, d_u_b, preferred_element_type=jnp.float32)
    d_x1 = d_h2 + jnp.dot(d_u_b, inner_back.T, preferred_element_type=jnp.float32)
    d_h1, d_gain1, d_shift1 = first_pull(d_x1)
    d_y_b = d_h1.astype(jnp.bfloat16)
    d_wo = jnp.dot(attn_b.T, d_y_b, preferred_element_type=jnp.float32)
    d_attn_b = jnp.dot(d_y_b, wo_back.T, preferred_element_type=jnp.float32).astype(jnp.bfloat16)
    delta_rows = (
        (d_attn_b.astype(jnp.float32) * attn_rows).reshape(tok_dev, heads, head_dim).sum(axis=2).T
    )
    dout_heads = d_attn_b.reshape(tok_dev, heads, head_dim)

    def query_grad_step(dq_acc, sliced, offset):
        key_block, value_block = sliced
        block_len = key_block.shape[0]
        key_pos = lax.dynamic_slice_in_dim(pos_all, offset, block_len, 0)
        allowed = pair_mask(my_pos, key_pos, head_flags, half_len)
        key_heads = key_block.reshape(block_len, heads, head_dim)
        value_heads = value_block.reshape(block_len, heads, head_dim)
        scores = (
            jnp.einsum("qhd,khd->hqk", q_heads, key_heads, preferred_element_type=jnp.float32)
            * score_scale
        )
        prob_rows = jnp.where(
            allowed, jnp.exp(jnp.where(allowed, scores - lse_rows[:, :, None], 0.0)), 0.0
        )
        prob_grad = jnp.einsum(
            "qhd,khd->hqk", dout_heads, value_heads, preferred_element_type=jnp.float32
        )
        dscore = (prob_rows * (prob_grad - delta_rows[:, :, None]) * score_scale).astype(
            jnp.bfloat16
        )
        return dq_acc + jnp.einsum(
            "hqk,khd->qhd", dscore, key_heads, preferred_element_type=jnp.float32
        )

    dq_start = jnp.zeros((tok_dev, heads, head_dim), jnp.float32)
    dq_acc = pair_fold(
        query_grad_step,
        dq_start,
        (
            lax.all_gather(key_b, "ctx", axis=0, tiled=True),
            lax.all_gather(value_b, "ctx", axis=0, tiled=True),
        ),
    )
    dq_b = dq_acc.reshape(tok_dev, width).astype(jnp.bfloat16)
    lse_all, delta_all = (
        lax.all_gather(lse_rows, "ctx", axis=1, tiled=True),
        lax.all_gather(delta_rows, "ctx", axis=1, tiled=True),
    )
    k_heads = key_b.reshape(tok_dev, heads, head_dim)
    v_heads = value_b.reshape(tok_dev, heads, head_dim)

    def key_grad_step(running, sliced, offset):
        dk_acc, dv_acc = running
        query_block, dout_block = sliced
        block_len = query_block.shape[0]
        query_pos = lax.dynamic_slice_in_dim(pos_all, offset, block_len, 0)
        lse_block = lax.dynamic_slice_in_dim(lse_all, offset, block_len, 1)
        delta_block = lax.dynamic_slice_in_dim(delta_all, offset, block_len, 1)
        allowed = pair_mask(query_pos, my_pos, head_flags, half_len)
        query_heads = query_block.reshape(block_len, heads, head_dim)
        dout_block_heads = dout_block.reshape(block_len, heads, head_dim)
        scores = (
            jnp.einsum("qhd,khd->hqk", query_heads, k_heads, preferred_element_type=jnp.float32)
            * score_scale
        )
        prob_rows = jnp.where(
            allowed, jnp.exp(jnp.where(allowed, scores - lse_block[:, :, None], 0.0)), 0.0
        )
        dv_acc = dv_acc + jnp.einsum(
            "hqk,qhd->khd",
            prob_rows.astype(jnp.bfloat16),
            dout_block_heads,
            preferred_element_type=jnp.float32,
        )
        prob_grad = jnp.einsum(
            "qhd,khd->hqk", dout_block_heads, v_heads, preferred_element_type=jnp.float32
        )
        dscore = (prob_rows * (prob_grad - delta_block[:, :, None]) * score_scale).astype(
            jnp.bfloat16
        )
        dk_acc = dk_acc + jnp.einsum(
            "hqk,qhd->khd", dscore, query_heads, preferred_element_type=jnp.float32
        )
        return (dk_acc, dv_acc)

    kv_start = (
        jnp.zeros((tok_dev, heads, head_dim), jnp.float32),
        jnp.zeros((tok_dev, heads, head_dim), jnp.float32),
    )
    dk_acc, dv_acc = pair_fold(
        key_grad_step,
        kv_start,
        (
            lax.all_gather(query_b, "ctx", axis=0, tiled=True),
            lax.all_gather(d_attn_b, "ctx", axis=0, tiled=True),
        ),
    )
    dk_b = dk_acc.reshape(tok_dev, width).astype(jnp.bfloat16)
    dv_b = dv_acc.reshape(tok_dev, width).astype(jnp.bfloat16)
    d_input = d_h1 + jnp.dot(dq_b, wq_back.T, preferred_element_type=jnp.float32)
    d_input = d_input + jnp.dot(dk_b, wk_back.T, preferred_element_type=jnp.float32)
    d_input = d_input + jnp.dot(dv_b, wv_back.T, preferred_element_type=jnp.float32)
    terms = (
        jnp.dot(x_in.T, dq_b, preferred_element_type=jnp.float32),
        jnp.dot(x_in.T, dk_b, preferred_element_type=jnp.float32),
        jnp.dot(x_in.T, dv_b, preferred_element_type=jnp.float32),
        d_wo,
        d_inner,
        d_outer,
        jnp.stack([d_gain1, d_gain2], axis=1),
        jnp.stack([d_shift1, d_shift2], axis=1),
    )
    shares = (
        lax.psum_scatter(
            terms[0].astype(jnp.bfloat16), "fsdp", scatter_dimension=0, tiled=True
        ).astype(jnp.float32),
        lax.psum_scatter(
            terms[1].astype(jnp.bfloat16), "fsdp", scatter_dimension=0, tiled=True
        ).astype(jnp.float32),
        lax.psum_scatter(
            terms[2].astype(jnp.bfloat16), "fsdp", scatter_dimension=0, tiled=True
        ).astype(jnp.float32),
        lax.psum_scatter(
            terms[3].astype(jnp.bfloat16), "fsdp", scatter_dimension=0, tiled=True
        ).astype(jnp.float32),
        lax.psum_scatter(
            terms[4].astype(jnp.bfloat16), "fsdp", scatter_dimension=0, tiled=True
        ).astype(jnp.float32),
        lax.psum_scatter(
            terms[5].astype(jnp.bfloat16), "fsdp", scatter_dimension=0, tiled=True
        ).astype(jnp.float32),
        lax.psum_scatter(
            terms[6].astype(jnp.bfloat16), "fsdp", scatter_dimension=0, tiled=True
        ).astype(jnp.float32),
        lax.psum_scatter(
            terms[7].astype(jnp.bfloat16), "fsdp", scatter_dimension=0, tiled=True
        ).astype(jnp.float32),
    )
    totals = (
        lax.psum(shares[0].astype(jnp.bfloat16), "ctx").astype(jnp.float32),
        lax.psum(shares[1].astype(jnp.bfloat16), "ctx").astype(jnp.float32),
        lax.psum(shares[2].astype(jnp.bfloat16), "ctx").astype(jnp.float32),
        lax.psum(shares[3].astype(jnp.bfloat16), "ctx").astype(jnp.float32),
        lax.psum(shares[4].astype(jnp.bfloat16), "ctx").astype(jnp.float32),
        lax.psum(shares[5].astype(jnp.bfloat16), "ctx").astype(jnp.float32),
        lax.psum(shares[6].astype(jnp.bfloat16), "ctx").astype(jnp.float32),
        lax.psum(shares[7].astype(jnp.bfloat16), "ctx").astype(jnp.float32),
    )
    return (
        result.astype(jnp.bfloat16)[None],
        d_input.astype(jnp.bfloat16)[None],
        totals[0],
        totals[1],
        totals[2],
        totals[3],
        totals[4],
        totals[5],
        totals[6],
        totals[7],
    )


MESH = pl.DeviceIdType.MESH
f32 = jnp.float32
bf16 = jnp.bfloat16


class Place:
    def __init__(self):
        me = lax.axis_index("ctx")
        self.me = me
        self.z = lax.axis_index("fsdp")
        self.core = lax.rem(me, 2)
        self.chip = me // 2
        self.x = lax.rem(self.chip, 2)
        self.y = self.chip // 2
        self.chip_x = self.chip + 1 - 2 * self.x
        self.chip_y = self.chip + 2 - 4 * self.y
        self.chip_d = 3 - self.chip
        self.other = 1 - self.core
        self.sib = (2 * self.chip + 1 - self.core, self.z)
        self.xn = (2 * self.chip_x + self.core, self.z)
        self.yn = (2 * self.chip_y + self.core, self.z)
        self.dn = (2 * self.chip_d + self.core, self.z)
        self.up = (me, self.z + 1)
        self.down = (me, self.z - 1)


def greet(place, others, line_len=None):
    barrier = pltpu.get_barrier_semaphore()
    count = len(others)
    for other in others:
        pl.semaphore_signal(barrier, inc=1, device_id=other, device_id_type=MESH)
    if line_len is not None:

        @pl.when(place.z < line_len - 1)
        def _():
            pl.semaphore_signal(barrier, inc=1, device_id=place.up, device_id_type=MESH)

        @pl.when(place.z > 0)
        def _():
            pl.semaphore_signal(barrier, inc=1, device_id=place.down, device_id_type=MESH)

        count = count + jnp.where(place.z < line_len - 1, 1, 0) + jnp.where(place.z > 0, 1, 0)

    pl.semaphore_wait(barrier, count)


def maybe(cond, fn):
    if cond is None:
        fn()
    else:
        pl.when(cond)(fn)


def of(ref):
    return ref() if callable(ref) else ref


class Net:
    def __init__(self, send_sems, recv_sems, count):
        self.send_sems, self.recv_sems, self.count = send_sems, recv_sems, count
        self.used = 0
        self.open = []

    def new(self):
        self.used += 1
        assert self.used <= self.count
        return self.used - 1

    def copy(self, idx, src, dst, dev):
        return pltpu.make_async_remote_copy(
            src_ref=src,
            dst_ref=dst,
            send_sem=self.send_sems.at[idx],
            recv_sem=self.recv_sems.at[idx],
            device_id=dev,
            device_id_type=MESH,
        )

    def send(self, idx, src, dst, dev, cond=None):
        make = lambda: self.copy(idx, of(src), of(dst), dev)
        maybe(cond, lambda: make().start())
        self.open.append((cond, make))

    def recv(self, idx, dst, dev, cond=None):
        maybe(cond, lambda: self.copy(idx, of(dst), of(dst), dev).wait_recv())

    def finish(self):
        for cond, make in self.open:
            maybe(cond, lambda make=make: make().wait_send())
        self.open = []


class PlaneGather:
    def __init__(self, net, place, own, slot, rows, cond=None):
        p = place
        self.net, self.place, self.cond = net, place, cond
        self.own_of, self.slot = own, slot
        self.h0, self.h1 = pl.ds(0, rows // 2), pl.ds(rows // 2, rows // 2)
        self.ids = [net.new() for _ in range(11)]

    def at(self, core, chip, half=0):
        def view():
            ref = self.slot(core, chip)
            return ref if half == 0 else ref.at[self.h0 if half == 1 else self.h1]

        return view

    def mine(self, half=0):
        def view():
            ref = self.own_of()
            return ref if half == 0 else ref.at[self.h0 if half == 1 else self.h1]

        return view

    def first(self):
        n, p, i, c = self.net, self.place, self.ids, self.cond
        at = functools.partial(self.at, p.core, p.chip)
        n.send(i[0], self.mine(1), at(1), p.xn, c)
        n.send(i[1], self.mine(2), at(2), p.yn, c)
        n.send(i[2], self.mine(2), at(2), p.xn, c)
        n.send(i[3], self.mine(1), at(1), p.yn, c)
        n.send(i[4], self.mine(), at(), p.sib, c)

    def second(self):
        n, p, i, c = self.net, self.place, self.ids, self.cond
        bx = functools.partial(self.at, p.core, p.chip_x)
        by = functools.partial(self.at, p.core, p.chip_y)
        n.recv(i[0], bx(1), p.xn, c)
        n.send(i[5], bx(1), bx(1), p.yn, c)
        n.recv(i[1], by(2), p.yn, c)
        n.send(i[6], by(2), by(2), p.xn, c)
        n.recv(i[2], bx(2), p.xn, c)
        n.send(i[7], bx(), bx(), p.sib, c)
        n.recv(i[3], by(1), p.yn, c)
        n.send(i[8], by(), by(), p.sib, c)

    def third(self):
        n, p, i, c = self.net, self.place, self.ids, self.cond
        bd = functools.partial(self.at, p.core, p.chip_d)
        n.recv(i[5], bd(1), p.yn, c)
        n.send(i[9], bd(1), bd(1), p.sib, c)
        n.recv(i[6], bd(2), p.xn, c)
        n.send(i[10], bd(2), bd(2), p.sib, c)

    def last(self):
        n, p, i, c = self.net, self.place, self.ids, self.cond
        for idx, q in ((4, p.chip), (7, p.chip_x), (8, p.chip_y)):
            n.recv(i[idx], self.at(p.other, q), p.sib, c)
        n.recv(i[9], self.at(p.other, p.chip_d, 1), p.sib, c)
        n.recv(i[10], self.at(p.other, p.chip_d, 2), p.sib, c)


def hbm(count):
    return [pl.BlockSpec(memory_space=pltpu.HBM)] * count


def comm_params(collective_id):
    return pltpu.CompilerParams(
        collective_id=collective_id, has_side_effects=True, vmem_limit_bytes=56 << 20
    )


def vmem(count):
    return [pl.BlockSpec(memory_space=pltpu.VMEM)] * count


def smem(count):
    return [pl.BlockSpec(memory_space=pltpu.SMEM)] * count


LANES = 256
KT = 128
NT = (((1,), (1,)), ((), ()))
TN = (((0,), (0,)), ((), ()))
NN = (((1,), (0,)), ((), ()))


def mm(a, b, dims=NN):
    return lax.dot_general(a, b, dims, preferred_element_type=f32)


def head_mask(h, head_dim, dtype):
    lane = lax.broadcasted_iota(jnp.int32, (1, LANES), 1)
    inside = jnp.logical_and(lane >= h * head_dim, lane < (h + 1) * head_dim)
    return jnp.where(inside, 1.0, 0.0).astype(dtype)


class Fold:
    def __init__(self, n, seg):
        self.n, self.seg, self.half = n, seg, n * seg
        self.tiles = self.half // KT

    def ranges(self, i):
        a = -(-(self.n - i) * self.seg // KT)
        b = -(-(i + 1) * self.seg // KT)
        assert a + b == self.tiles + 2
        return a, b

    def places(self, i, core, paired):
        a, b = self.ranges(i)
        n, seg = self.n, self.seg
        causal = 1 - paired
        up = n + core * (n // 2) + i
        rows_a = (core * n + n - 1 - i) * causal + up * paired
        rows_b = (core * n + i) * causal + up * paired
        keys_a = core * self.tiles * causal
        keys_b = core * self.tiles * causal + a * paired
        lim_a = (n - 1 - i) * seg - (a - 2) * KT + (1 << 20) * paired
        lim_b = i * seg - (b - 2) * KT - (1 << 20) * paired
        return (rows_a, keys_a, lim_a, a), (rows_b, keys_b, lim_b, b)


def natural(tab, n, s):
    upper = lax.div(s, n)
    c = tab[n + s + upper * (2 * n - 1 - 2 * s)]
    return lax.rem(c, 2), lax.div(c, 2), upper


def key_tiles(ref, base, first, count):
    return ref[pl.ds(base + first, count)].reshape(count * KT, LANES)


def tail_mask(seg, limit):
    col = lax.broadcasted_iota(jnp.int32, (seg, 2 * KT), 1)
    row = lax.broadcasted_iota(jnp.int32, (seg, 2 * KT), 0)
    return col - row <= limit


def norm_forward(h, gain, shift):
    mean = jnp.mean(h, axis=1, keepdims=True)
    center = h - mean
    scale = lax.rsqrt(jnp.mean(center * center, axis=1, keepdims=True) + norm_eps)
    n = center * scale
    return n, scale, n * gain + shift


def norm_backward(cot, n, scale, gain):
    dn = cot * gain
    mean = jnp.mean(dn, axis=1, keepdims=True)
    along = jnp.mean(dn * n, axis=1, keepdims=True)
    return scale * (dn - mean - n * along)


def chain(*steps):
    def run():
        for fn, *args in steps:
            fn(*args)

    return run


def fill_table(tab, pairs, pairing, chip, n, heads):
    for c in range(n):
        tab[c] = pairs[0, c]
    for a in range(n):
        found = jnp.int32(0)
        for c in range(n):
            found = found + (pairs[0, c] == a).astype(jnp.int32) * c
        tab[n + a] = jnp.minimum(found, n - 1)
    for h in range(heads):
        tab[2 * n + h] = pairing[0, chip * heads + h]


def lse_lane(fold, h, i, g):
    return (h * (fold.n // 2) + i) * 2 + g


def attend_unit(fold, core, h, i, head_dim, tab, q_ref, k_ref, v_ref, o_ref, lse_ref):
    n, seg = fold.n, fold.seg
    paired = tab[2 * n + h]
    pf = paired.astype(f32)
    lanes = head_mask(h, head_dim, f32)
    lanes16 = head_mask(h, head_dim, bf16)
    parts = []
    for rows, keys, limit, count in fold.places(i, core, paired):
        q = q_ref[rows] * lanes16
        tail = mm(q, key_tiles(k_ref, keys, count - 2, 2), NT)
        tail = jnp.where(tail_mask(seg, limit), tail, very_low)
        top = jnp.max(tail, axis=1, keepdims=True)
        main = None
        if count > 2:
            main = mm(q, key_tiles(k_ref, keys, 0, count - 2), NT)
            top = jnp.maximum(top, jnp.max(main, axis=1, keepdims=True))
        parts.append((keys, count, main, tail, top))
    both = jnp.maximum(parts[0][4], parts[1][4])
    joined = jnp.broadcast_to(paired, both.shape) == 1
    outs = []
    for keys, count, main, tail, top in parts:
        top = jnp.where(joined, both, top)
        e = jnp.exp(tail - top)
        total = jnp.sum(e, axis=1, keepdims=True)
        acc = mm(e.astype(bf16), key_tiles(v_ref, keys, count - 2, 2))
        if main is not None:
            e = jnp.exp(main - top)
            total += jnp.sum(e, axis=1, keepdims=True)
            acc += mm(e.astype(bf16), key_tiles(v_ref, keys, 0, count - 2))
        outs.append((top, total, acc))
    (top_a, sum_a, acc_a), (top_b, sum_b, acc_b) = outs
    sum_a, sum_b = sum_a + pf * sum_b, jnp.where(joined, sum_a + sum_b, sum_b)
    acc_a = acc_a + pf * acc_b
    out_a = acc_a * (lanes / sum_a)
    out_b = acc_b * (lanes / sum_b)
    lane = lax.broadcasted_iota(jnp.int32, (1, KT), 1)
    lse = jnp.where(lane == lse_lane(fold, h, i, 0), top_a + jnp.log(sum_a), lse_ref[...])
    lse_ref[...] = jnp.where(lane == lse_lane(fold, h, i, 1), top_b + jnp.log(sum_b), lse)
    far, near, up = core * n + n - 1 - i, core * n + i, n + core * (n // 2) + i
    for at, value in ((far, (1.0 - pf) * out_a), (near, (1.0 - pf) * out_b), (up, pf * out_a)):
        o_ref[at] += value.astype(bf16)


def front_kernel(
    nz, n, heads, head_dim, n_sem,
    pairs, pairing, x_ref, cot_ref, ln_ref, wq_i, wk_i, wv_i, wo_i, w1_i, w2_i,
    xall_o, wqkv_o, q_o, k_o, v_o, on_o, g_o, lse_o, out_o, da_o, dh_o,
    tab, xall, wqkv, q_ref, k_ref, v_ref, o_nat, o_ctx, o_part, o_sum, attn,
    w1, w2, wol, fq, fo, f1, f2, u_ref, z_ref, x1b_ref, acc_ref, n1_ref, r1_ref, dx1_ref, gs, gt,
    ssem, rsem, lsem, fsem, gsem,
):
    p = Place()
    z = p.z
    seg, width = x_ref.shape[1], x_ref.shape[2]
    tok = 2 * seg
    fold = Fold(n, seg)
    d_rows, f_rows = wq_i.shape[0], w2_i.shape[0]
    n_f = w1_i.shape[1] // width
    cols = heads * head_dim
    half = d_rows // 2
    a1_rows, a2_rows = n_f * d_rows // 8, f_rows // 12
    b_first = 8 * a2_rows
    b_rows = (f_rows - b_first) // 2
    locals_ = []

    def keep(src, dst):
        cp = pltpu.make_async_copy(src, dst, lsem.at[len(locals_)])
        cp.start()
        locals_.append(cp)
        return cp

    masters = [
        pltpu.make_async_copy(src, dst, fsem.at[i])
        for i, (src, dst) in enumerate(
            ((wq_i, fq.at[0]), (wk_i, fq.at[1]), (wv_i, fq.at[2]), (w1_i, f1), (w2_i, f2), (wo_i, fo))
        )
    ]
    for cp in masters:
        cp.start()
    own_x = keep(x_ref, xall.at[p.core, p.chip])
    greet(p, (p.sib, p.xn, p.yn, p.dn), nz)
    net = Net(ssem, rsem, n_sem)
    tokens_ag = PlaneGather(net, p, lambda: x_ref, lambda k, q: xall.at[k, q], 2)
    tokens_ag.first()
    can_up, can_down = z < nz - 1, z > 0
    rows = pl.ds(p.core * half, half)
    other = pl.ds(p.other * half, half)

    class Stream:
        def __init__(self, at, after):
            self.up = [net.new() for _ in range(nz)]
            self.down = [net.new() for _ in range(nz)]
            self.at, self.todo = at, {}
            for t in range(1, nz):
                self.todo[t] = []
                for ids, src, frm, to, got, more in (
                    (self.up, z - t, p.down, p.up, z >= t, can_up),
                    (self.down, z + t, p.up, p.down, z + t < nz, can_down),
                ):
                    src = jnp.clip(src, 0, nz - 1)
                    on = jnp.logical_and(got, more)
                    self.todo[t].append((ids, src, frm, to, got, on, after(t, src, at, got)))

        def begin(self):
            own = lambda: self.at(z)
            net.send(self.up[1], own, own, p.up, can_up)
            net.send(self.down[1], own, own, p.down, can_down)

        def step(self, t):
            for ids, src, frm, to, got, on, then in self.todo[t]:
                block = functools.partial(self.at, src)
                net.recv(ids[t], block, frm, got)
                if t + 1 < nz:
                    net.send(ids[t + 1], block, block, to, on)
                then()

    def share(waits, block_of):
        def after(t, src, at, got):
            idx = net.new()
            waits.append((idx, lambda: block_of(src), got))
            return lambda: net.send(idx, lambda: at(src), lambda: at(src), p.sib, got)

        return after

    gathers = {t: [] for t in range(1, nz)}

    def spread(slot_of, count):
        def after(t, src, at, got):
            slot = lambda k, q: slot_of(src, k, q)
            gather = PlaneGather(net, p, lambda: at(src), slot, count, got)
            gathers[t].append(gather)
            return gather.first

        return after

    def a1_slot(o, k, q):
        start = pl.multiple_of(o * d_rows + lax.rem(q, 2) * a1_rows, 32)
        return w1.at[k * 2 + lax.div(q, 2), pl.ds(start, a1_rows)]

    def a2_slot(o, k, q):
        return w2.at[o, pl.ds(pl.multiple_of((k * 4 + q) * a2_rows, 32), a2_rows)]

    def b_slot(o, k):
        return w2.at[o, pl.ds(pl.multiple_of(b_first + k * b_rows, 32), b_rows)]

    sel_waits, b_waits, c_waits = [], [], []
    sel = Stream(lambda o: wqkv.at[o, rows], share(sel_waits, lambda o: wqkv.at[o, other]))
    cs = Stream(lambda o: wol.at[o, p.core], share(c_waits, lambda o: wol.at[o, p.other]))
    a1 = Stream(lambda o: a1_slot(o, p.core, p.chip), spread(a1_slot, a1_rows))
    a2 = Stream(lambda o: a2_slot(o, p.core, p.chip), spread(a2_slot, a2_rows))
    bs = Stream(lambda o: b_slot(o, p.core), share(b_waits, lambda o: b_slot(o, p.other)))

    for cp in masters[:3]:
        cp.wait()
    for chip in range(4):

        @pl.when(p.chip == chip)
        def _():
            for m in range(3):
                mine = fq[m, :, chip * cols : (chip + 1) * cols].astype(bf16)
                wqkv[z, :, m * LANES : m * LANES + cols] = mine

    for m in range(3):
        wqkv[z, :, m * LANES + cols : (m + 1) * LANES] = jnp.zeros((d_rows, LANES - cols), bf16)
    sel.begin()
    masters[3].wait()
    for f in range(n_f):
        at = pl.ds(pl.multiple_of(z * d_rows, 32), d_rows)
        w1[f, at, :] = f1[:, f * width : (f + 1) * width].astype(bf16)
    a1.begin()
    masters[4].wait()

    def cast(i, _):
        at = pl.ds(pl.multiple_of(i * 64, 64), 64)
        w2[z, at, :] = f2[at, :].astype(bf16)
        return 0

    lax.fori_loop(0, f_rows // 64, cast, 0)
    masters[5].wait()
    for k in range(2):
        wol[z, k, :half, :] = fo[k * half : (k + 1) * half, :].astype(bf16)
        wol[z, k, half:, :] = ln_ref[...]
    fill_table(tab, pairs, pairing, p.chip, n, heads)
    o_nat[...] = jnp.zeros(o_nat.shape, bf16)
    lse_o[...] = jnp.zeros(lse_o.shape, f32)
    sel.step(1)
    a2.begin()
    for t in range(2, nz):
        sel.step(t)
    tokens_ag.second()
    a1.step(1)
    a2.step(1)
    tokens_ag.third()
    a1.step(2)
    cs.begin()
    own_x.wait()
    tokens_ag.last()
    for idx, block, got in sel_waits:
        net.recv(idx, block, p.sib, got)
    keep(xall, xall_o)
    keep(wqkv, wqkv_o)

    def four(i, _):
        tokens = jnp.concatenate([xall[natural(tab, n, 4 * i + u)] for u in range(4)], axis=0)
        qkv = mm(tokens, wqkv[...].reshape(-1, 3 * LANES))
        q = (qkv[:, :LANES].astype(bf16).astype(f32) * score_scale).astype(bf16)
        q_ref[pl.ds(4 * i, 4)] = q.reshape(4, seg, LANES)
        at = pl.ds(i * (4 * seg // KT), 4 * seg // KT)
        k_ref[at] = qkv[:, LANES : 2 * LANES].astype(bf16).reshape(-1, KT, LANES)
        v_ref[at] = qkv[:, 2 * LANES :].astype(bf16).reshape(-1, KT, LANES)
        return 0

    lax.fori_loop(0, n // 2, four, 0)
    for src, dst in ((q_ref, q_o), (k_ref, k_o), (v_ref, v_o)):
        keep(src, dst)

    def second(t):
        for gather in gathers[t]:
            gather.second()

    def third(t):
        for gather in gathers[t]:
            gather.third()

    todo = {
        (0, 0): chain((a2.step, 2), (a1.step, 3)),
        (0, 1): chain((second, 1)),
        (0, 2): chain((a2.step, 3), (bs.begin,)),
        (0, 3): chain((cs.step, 1)),
        (1, 1): chain((third, 1), (second, 2)),
        (1, 3): chain((cs.step, 2)),
        (2, 0): chain((third, 2), (bs.step, 1)),
        (2, 2): chain((second, 3), (cs.step, 3)),
    }

    def head(h, _):
        for i in range(n // 2):
            attend_unit(fold, p.core, h, i, head_dim, tab, q_ref, k_ref, v_ref, o_nat, lse_o)
            for (at_h, at_i), step in todo.items():
                if at_i == i:
                    pl.when(h == at_h)(step)
        return 0

    lax.fori_loop(0, heads, head, 0)
    keep(o_nat, on_o)
    for core_is in range(2):
        for q in range(n // 2):
            a = tab[2 * q + core_is]
            for u, s in ((0, a), (1, 2 * n - 1 - a)):
                o_ctx[core_is, q, u * seg : (u + 1) * seg, :] = o_nat[s]
    part, swaps = net.new(), [net.new() for _ in range(3)]
    net.send(part, o_ctx.at[p.other], o_part, p.sib)
    bs.step(2)
    net.recv(part, o_part, p.sib)
    partners = ((p.chip_d, p.dn), (p.chip_x, p.xn), (p.chip_y, p.yn))
    for idx, (chip, dev) in zip(swaps, partners):
        o_sum[chip] = o_ctx[p.core, chip] + o_part[chip]
        net.send(idx, o_sum.at[chip], attn.at[p.chip], dev)
    attn[p.chip] = o_ctx[p.core, p.chip] + o_part[p.chip]
    third(3)
    for idx, block, got in c_waits:
        net.recv(idx, block, p.sib, got)
    vec = wol[0, 0, half:, :].astype(f32)
    for o in range(1, nz):
        vec = vec + wol[o, 0, half:, :].astype(f32)
    gain1, gain2, shift1, shift2 = vec[0:1], vec[1:2], vec[2:3], vec[3:4]
    wo_of = lambda o: jnp.concatenate([wol[o, 0, :half, :], wol[o, 1, :half, :]], axis=0)
    for idx, (chip, dev) in zip(swaps, partners):
        net.recv(idx, attn.at[chip], dev)

    h1 = x_ref[...].reshape(tok, width).astype(f32)
    for o in range(nz):
        h1 = h1 + mm(attn[o, :, :cols], wo_of(o))
    n1, r1, x1 = norm_forward(h1, gain1, shift1)
    n1_ref[...] = n1
    r1_ref[...] = jnp.broadcast_to(r1, (tok, 128))
    x1b_ref[...] = x1.astype(bf16)
    acc_ref[...] = x1
    bs.step(3)
    for t in gathers:
        for gather in gathers[t]:
            gather.last()
    for idx, block, got in b_waits:
        net.recv(idx, block, p.sib, got)

    def up(f, _):
        u = mm(x1b_ref[...], w1[f])
        cdf = 0.5 + 0.5 * lax.erf(u * (0.5**0.5))
        act = (u * cdf).astype(bf16)
        z_ref[f] = act
        u_ref[f] = cdf + u * jnp.exp(-0.5 * u * u) * 0.3989422804014327
        acc_ref[...] += mm(act, w2[f])
        return 0

    lax.fori_loop(0, n_f, up, 0)
    n2, r2, out = norm_forward(acc_ref[...], gain2, shift2)
    out_o[...] = out.astype(bf16)
    cot = cot_ref[...].astype(f32)
    d_gain2 = jnp.sum(cot * n2, axis=0, keepdims=True)
    d_shift2 = jnp.sum(cot, axis=0, keepdims=True)
    dh2 = norm_backward(cot, n2, r2, gain2)
    dx1_ref[...] = dh2
    df = dh2.astype(bf16)
    first1, first2 = f_rows, f_rows + n_f * d_rows

    def grads_out(f, slot):
        yield pltpu.make_async_copy(gs.at[slot, 0], g_o.at[f, pl.ds(0, f_rows)], gsem.at[slot, 0])
        for o in range(nz):
            at = pl.ds(pl.multiple_of(first1 + f * d_rows, 32), d_rows)
            src = gs.at[slot, 1, pl.ds(o * d_rows, d_rows)]
            yield pltpu.make_async_copy(src, g_o.at[o, at], gsem.at[slot, 1 + o])

    def back(f, _):
        slot = lax.rem(f, 2)

        @pl.when(f >= 2)
        def _():
            for cp in grads_out(f - 2, slot):
                cp.wait()

        gs[slot, 0] = mm(z_ref[f], df, TN).astype(bf16)
        du = (mm(df, w2[f], NT) * u_ref[f]).astype(bf16)
        gs[slot, 1] = mm(x1b_ref[...], du, TN).astype(bf16)
        for cp in grads_out(f, slot):
            cp.start()
        dx1_ref[...] += mm(du, w1[f], NT)
        return 0

    lax.fori_loop(0, n_f, back, 0)
    d_x1 = dx1_ref[...]
    n1 = n1_ref[...]
    d_gain1 = jnp.sum(d_x1 * n1, axis=0, keepdims=True)
    d_shift1 = jnp.sum(d_x1, axis=0, keepdims=True)
    dh1 = norm_backward(d_x1, n1, r1_ref[:, :1], gain1)
    dh_o[...] = dh1
    dy = dh1.astype(bf16)
    norms = jnp.concatenate([d_gain1, d_gain2, d_shift1, d_shift2], axis=0).astype(bf16)
    ends = []
    for o in range(nz):
        da_o[o, :, :cols] = mm(dy, wo_of(o), NT).astype(bf16)
        da_o[o, :, cols:] = jnp.zeros((tok, LANES - cols), bf16)
        gt[o, :d_rows, :] = mm(attn[o, :, :cols], dy, TN).astype(bf16)
        gt[o, d_rows:, :] = jnp.zeros((gt.shape[1] - d_rows, width), bf16)
        gt[o, d_rows : d_rows + 4, :] = norms
        ends.append(pltpu.make_async_copy(gt.at[o], g_o.at[o, pl.ds(first2, gt.shape[1])], fsem.at[o]))
        ends[-1].start()
    for f in range(max(n_f - 2, 0), n_f):
        for cp in grads_out(f, f % 2):
            cp.wait()
    for cp in ends:
        cp.wait()
    net.finish()
    for cp in locals_[1:]:
        cp.wait()


def front(nz, n, heads, head_dim, total, pairs, pairing, x_in, cot, norms, weights):
    tok, width = x_in.shape
    seg = tok // 2
    d_rows, f_rows = weights[0].shape[0], weights[5].shape[0]
    n_f = weights[4].shape[1] // width
    n_sem = 11 * (4 * (nz - 1) + 1) + 5 * 2 * nz + 3 * 2 * (nz - 1) + 4
    wide, tiled = (2 * n, seg, LANES), (tok * n // KT, KT, LANES)
    shapes = [(2, 4, 2, seg, width), (nz, d_rows, 3 * LANES), wide, tiled, tiled, wide]
    block = (4, tok, LANES)
    sds = jax.ShapeDtypeStruct
    vb = lambda *s: pltpu.VMEM(s, bf16)
    vf = lambda *s: pltpu.VMEM(s, f32)
    return pl.pallas_call(
        functools.partial(front_kernel, nz, n, heads, head_dim, n_sem),
        out_shape=tuple(sds(s, bf16) for s in shapes)
        + (
            sds((nz, total, width), bf16),
            sds((seg, KT), f32),
            sds((tok, width), bf16),
            sds(block, bf16),
            sds((tok, width), f32),
        ),
        in_specs=smem(2) + vmem(3) + hbm(6),
        out_specs=tuple(hbm(7) + vmem(4)),
        scratch_shapes=[pltpu.SMEM((2 * n + heads,), jnp.int32)]
        + [vb(*s) for s in shapes]
        + [
            vb(2, *block),
            vb(*block),
            vb(*block),
            vb(*block),
            vb(n_f, nz * d_rows, width),
            vb(nz, f_rows, width),
            vb(nz, 2, d_rows // 2 + 16, width),
            vf(3, d_rows, width),
            vf(d_rows, width),
            vf(d_rows, n_f * width),
            vf(f_rows, width),
            vf(n_f, tok, width),
            vb(n_f, tok, width),
            vb(tok, width),
            vf(tok, width),
            vf(tok, width),
            vf(tok, 128),
            vf(tok, width),
            vb(2, 2, f_rows, width),
            vb(nz, total - f_rows - n_f * d_rows, width),
            pltpu.SemaphoreType.DMA((n_sem,)),
            pltpu.SemaphoreType.DMA((n_sem,)),
            pltpu.SemaphoreType.DMA((12,)),
            pltpu.SemaphoreType.DMA((6,)),
            pltpu.SemaphoreType.DMA((2, 1 + nz)),
        ],
        compiler_params=comm_params(0),
        name="front",
    )(pairs, pairing, x_in.reshape(2, seg, width), cot, norms, *weights)


def add_into(dst, src, rows, chunk=32):
    if rows % chunk:
        chunk = 16

    def step(i, _):
        at = pl.ds(pl.multiple_of(i * chunk, chunk), chunk)
        to, frm = of(dst), of(src)
        to[at, :] = to[at, :] + frm[at, :]
        return 0

    lax.fori_loop(0, rows // chunk, step, 0)


class Slot:
    def __init__(self, ref, o):
        self.ref, self.o = ref, o

    def __call__(self):
        return self.ref.at[self.o]

    @property
    def at(self):
        return self().at


class PlaneSum:
    def __init__(self, net, place, block, rows, rx0, ry1, ry0, rx1):
        p = place
        self.net, self.place = net, place
        self.rx0, self.ry1, self.ry0, self.rx1 = rx0, ry1, ry0, rx1
        self.h = rows // 2
        h0, h1 = pl.ds(0, self.h), pl.ds(self.h, self.h)
        far_x, far_y = 1 - p.x, 1 - p.y
        self.block, self.h0, self.h1 = block, h0, h1
        self.far_x, self.far_y = far_x, far_y
        self.to_x = [2 * j + far_x for j in range(2)]
        self.to_y = [2 * far_y + j for j in range(2)]
        self.on_y, self.on_x = 2 * far_y + p.x, 2 * p.y + far_x
        self.ids = [net.new() for _ in range(6)]

    def part(self, index, half):
        return lambda: self.block(index).at[half]

    def first(self):
        n, p, i = self.net, self.place, self.ids
        for j in range(2):
            n.send(i[j], self.part(self.to_x[j], self.h0), lambda j=j: self.rx0.at[j], p.xn)
            n.send(i[2 + j], self.part(self.to_y[j], self.h1), lambda j=j: self.ry1.at[j], p.yn)

    def second(self):
        n, p, i = self.net, self.place, self.ids
        on_y, on_x = self.part(self.on_y, self.h0), self.part(self.on_x, self.h1)
        mine0, mine1 = self.part(p.chip, self.h0), self.part(p.chip, self.h1)
        for j in range(2):
            n.recv(i[j], lambda j=j: self.rx0.at[j], p.xn)
        add_into(on_y, lambda: self.rx0.at[self.far_y], self.h)
        n.send(i[4], on_y, self.ry0, p.yn)
        for j in range(2):
            n.recv(i[2 + j], lambda j=j: self.ry1.at[j], p.yn)
        add_into(on_x, lambda: self.ry1.at[self.far_x], self.h)
        n.send(i[5], on_x, self.rx1, p.xn)
        add_into(mine0, lambda: self.rx0.at[p.y], self.h)
        add_into(mine1, lambda: self.ry1.at[p.x], self.h)

    def third(self):
        n, p, i = self.net, self.place, self.ids
        n.recv(i[4], self.ry0, p.yn)
        add_into(self.part(p.chip, self.h0), self.ry0, self.h)
        n.recv(i[5], self.rx1, p.xn)
        add_into(self.part(p.chip, self.h1), self.rx1, self.h)


class LineSum:
    def __init__(self, net, place, nz, whole, low, high, parts, rows):
        p, z, top = place, place.z, nz - 1
        self.net, self.top, self.parts, self.rows, self.whole = net, top, parts, rows, whole
        sides = (
            ([net.new() for _ in range(nz)], low, z, -1, p.down, p.up),
            ([net.new() for _ in range(nz)], high, top - z, 1, p.up, p.down),
        )
        self.todo = {}
        for t in range(nz):
            self.todo[t] = []
            for ids, buf, depth, sign, frm, to in sides:
                owner = jnp.clip(top - t + z if sign < 0 else t + z - top, 0, top)
                takes = jnp.logical_and(depth > 0, depth <= t)
                self.todo[t].append(
                    (ids, owner, buf, takes, depth <= t, frm, to)
                )

    def step(self, t):
        n = self.net
        for ids, owner, buf, takes, sends, frm, to in self.todo[t]:
            whole = functools.partial(self.whole, owner)
            landed = lambda buf=buf, owner=owner: buf.at[owner]

            def take(ids=ids, whole=whole, landed=landed, frm=frm):
                n.recv(ids[t - 1], landed, frm)
                if self.parts is None:
                    add_into(whole, landed, self.rows)
                else:
                    for j in range(self.parts):
                        add_into(
                            lambda j=j: whole().at[j], lambda j=j: landed().at[j], self.rows
                        )

            if t > 0:
                maybe(takes, take)
            if t < self.top:
                n.send(ids[t], whole, landed, to, sends)


def attend_back_unit(
    fold, core, h, i, head_dim, tab, q_ref, k_ref, v_ref, o_ref, lse_ref, da_ref,
    dcat_ref, dk_ref, dv_ref,
):
    n, seg, half = fold.n, fold.seg, fold.half
    paired = tab[2 * n + h]
    pf = paired.astype(f32)
    lanes = head_mask(h, head_dim, f32)
    lanes16 = head_mask(h, head_dim, bf16)
    dqs = []
    places = fold.places(i, core, paired)
    for g, (rows, keys, limit, count) in enumerate(places):
        q = q_ref[rows] * lanes16
        k, c, upper = natural(tab, n, rows)
        da = da_ref[k, c, upper] * lanes16
        delta = jnp.sum(
            da.astype(f32) * o_ref[rows].astype(f32), axis=1, keepdims=True
        )
        lane = lax.broadcasted_iota(jnp.int32, (1, KT), 1) == lse_lane(fold, h, i, g)
        lse = jnp.sum(jnp.where(lane, lse_ref[...], 0.0), axis=1, keepdims=True)
        dq = None
        pieces = [(count - 2, 2, True)]
        if count > 2:
            pieces.append((0, count - 2, False))
        for first, size, masked in pieces:
            kt = key_tiles(k_ref, keys, first, size)
            vt = key_tiles(v_ref, keys, first, size)
            pr = jnp.exp(mm(q, kt, NT) - lse)
            if masked:
                pr = jnp.where(tail_mask(seg, limit), pr, 0.0)
            ds = (pr * (mm(da, vt, NT) - delta)).astype(bf16)
            part = mm(ds, kt)
            dq = part if dq is None else dq + part
            dv = mm(pr.astype(bf16), da, TN)
            dk = mm(ds, q, TN)
            at = pl.ds(first * KT, size * KT)
            if g == 0 or masked:
                dk_ref[at, :] += dk
                dv_ref[at, :] += dv
            else:
                beyond = pl.ds(places[0][3] * KT, size * KT)
                dk_ref[at, :] += (1.0 - pf) * dk
                dv_ref[at, :] += (1.0 - pf) * dv
                dk_ref[beyond, :] += pf * dk
                dv_ref[beyond, :] += pf * dv
        dqs.append(dq)
    scaled = lanes * score_scale
    dq_a, dq_b = (dqs[0] + pf * dqs[1]) * scaled, dqs[1] * scaled
    far, near, up = core * n + n - 1 - i, core * n + i, n + core * (n // 2) + i
    for at, value in ((far, (1.0 - pf) * dq_a), (near, (1.0 - pf) * dq_b), (up, pf * dq_a)):
        dcat_ref[at, :, :LANES] += value.astype(bf16)


def place_key_grads(fold, core, paired, dk_ref, dv_ref, dcat_ref):
    n, seg, half = fold.n, fold.seg, fold.half
    pf = paired.astype(f32)

    def spread(j, _):
        at = pl.ds(pl.multiple_of(j * seg, seg), seg)
        for src, lanes in ((dk_ref, slice(LANES, 2 * LANES)), (dv_ref, slice(2 * LANES, None))):
            value = src[at, :]
            dcat_ref[core * n + j, :, lanes] += ((1.0 - pf) * value).astype(bf16)
            dcat_ref[j, :, lanes] += (pf * value).astype(bf16)
        return 0

    lax.fori_loop(0, n, spread, 0)


def backward_kernel(
    nz, n, heads, head_dim, rb, n_sem,
    pairs, pairing, g_ref, da_in, dh_ref, xall_i, wqkv_i, q_i, k_i, v_i, on_i, lse_ref,
    gsum_o, dtok_o, dw_o,
    tab, g_kept, g_sib, g_rx0, g_ry1, g_ry0, g_rx1, g_low, g_high,
    b_low, b_high, b_rx0, b_ry1, b_ry0, b_rx1,
    x_part, x_sib, x_rx0, x_ry1, x_ry0, x_rx1, w_part, w_sib, w_low, w_high, w_all,
    da_all, xall, wqkv, q_ref, k_ref, v_ref, on_ref, dcat, dk_ref, dv_ref, dw_acc,
    ssem, rsem, lsem,
):
    p = Place()
    z = p.z
    seg, width = xall.shape[3], xall.shape[4]
    tok = 2 * seg
    fold = Fold(n, seg)
    rows = g_ref.shape[3]
    ra = rows - rb
    ax, bx = pl.ds(0, ra), pl.ds(ra, rb)
    order = line_order(nz)
    local = []

    def fetch(src, dst):
        cp = pltpu.make_async_copy(src, dst, lsem.at[len(local)])
        cp.start()
        local.append(cp)
        return cp

    net = Net(ssem, rsem, n_sem)
    own_da = fetch(da_in.at[p.chip], da_all.at[p.core, p.chip])
    own_g = {o: fetch(g_ref.at[o, p.core], g_kept.at[o]) for o in order}
    greet(p, (p.sib, p.xn, p.yn, p.dn), nz)
    swaps = [net.new() for _ in range(7)]
    partners = ((p.chip_d, p.dn), (p.chip_x, p.xn), (p.chip_y, p.yn))
    for i, (chip, dev) in enumerate(partners):
        net.send(swaps[i], da_in.at[chip], da_all.at[p.core, p.chip], dev)
    net.send(swaps[3], da_in.at[p.chip], da_all.at[p.core, p.chip], p.sib)
    sib_ids = {o: net.new() for o in order}

    def to_sib(o):
        net.send(sib_ids[o], lambda: g_ref.at[o, p.other], lambda: g_sib.at[o], p.sib)

    to_sib(order[0])
    to_sib(order[1])
    att_in = [
        fetch(src, dst)
        for src, dst in (
            (q_i, q_ref), (k_i, k_ref), (v_i, v_ref), (on_i, on_ref), (xall_i, xall), (wqkv_i, wqkv),
        )
    ]
    fill_table(tab, pairs, pairing, p.chip, n, heads)
    dcat[...] = jnp.zeros(dcat.shape, bf16)

    plane = {
        o: PlaneSum(
            net, p, lambda q, o=o: g_kept.at[o, q].at[ax], ra,
            *(Slot(r, o) for r in (g_rx0, g_ry1, g_ry0, g_rx1)),
        )
        for o in order
    }
    line_a = LineSum(net, p, nz, lambda o: g_kept.at[o, p.chip].at[ax], g_low, g_high, None, ra)
    line_b = LineSum(net, p, nz, lambda o: g_kept.at[o, :, bx], b_low, b_high, n // 2, rb)
    plane_b = PlaneSum(
        net, p, lambda q: g_kept.at[z, q].at[bx], rb, b_rx0, b_ry1, b_ry0, b_rx1
    )

    def chip_sum(o):
        net.recv(sib_ids[o], lambda: g_sib.at[o], p.sib)
        pltpu.make_async_copy(g_ref.at[o, p.core], g_kept.at[o], lsem.at[1 + order.index(o)]).wait()
        for q in range(n // 2):
            add_into(lambda q=q: g_kept.at[o, q], lambda q=q: g_sib.at[o, q], rows)

    p0, p1, p2, p3 = (plane[o] for o in order)
    chip_sum(order[0])
    p0.first()
    to_sib(order[2])
    chip_sum(order[1])
    p1.first()
    to_sib(order[3])
    line_b.step(0)
    for i, chip, dev in ((1, p.chip_x, p.xn), (2, p.chip_y, p.yn), (0, p.chip_d, p.dn)):
        block = da_all.at[p.core, chip]
        net.recv(swaps[i], block, dev)
        net.send(swaps[4 + i], block, block, p.sib)
    for i, chip in ((3, p.chip), (5, p.chip_x), (6, p.chip_y), (4, p.chip_d)):
        net.recv(swaps[i], da_all.at[p.other, chip], p.sib)
    own_da.wait()
    for cp in att_in:
        cp.wait()

    todo = {
        0: chain((chip_sum, order[2]), (chip_sum, order[3])),
        1: chain((p0.second,)),
        2: chain((p1.second,), (p2.first,), (line_b.step, 1)),
        3: chain((p0.third,), (p3.first,)),
        4: chain((p1.third,), (line_a.step, 0)),
        5: chain((p2.second,)),
        6: chain((line_b.step, 2), (p3.second,)),
        7: chain((p2.third,)),
        8: chain((p3.third,), (line_a.step, 1)),
        9: chain((line_b.step, 3), (plane_b.first,)),
        10: chain((line_a.step, 2)),
        11: chain((plane_b.second,)),
    }
    units = n // 2

    def head(h, _):
        dk_ref[...] = jnp.zeros(dk_ref.shape, f32)
        dv_ref[...] = jnp.zeros(dv_ref.shape, f32)
        for i in range(units):
            attend_back_unit(
                fold, p.core, h, i, head_dim, tab, q_ref, k_ref, v_ref, on_ref, lse_ref, da_all,
                dcat, dk_ref, dv_ref,
            )
            for hh in range(heads):
                if hh * units + i in todo:
                    pl.when(h == hh)(todo[hh * units + i])
        place_key_grads(fold, p.core, tab[2 * n + h], dk_ref, dv_ref, dcat)
        return 0

    lax.fori_loop(0, heads, head, 0)

    def block_grads(k, q):
        a = tab[2 * q + k]
        return jnp.concatenate([dcat[a], dcat[2 * n - 1 - a]], axis=0)

    dw_acc[...] = jnp.zeros(dw_acc.shape, f32)

    def weights(c, _):
        k, q = lax.rem(c, 2), c // 2
        dw_acc[...] += mm(xall[k, q].reshape(tok, width), block_grads(k, q), TN)
        return 0

    lax.fori_loop(0, n, weights, 0)
    d = wqkv.shape[1]
    half = d // 2
    for o in range(nz):
        w_part[0, o] = dw_acc[o * d : o * d + half].astype(bf16)
        w_part[1, o] = dw_acc[o * d + half : (o + 1) * d].astype(bf16)
    w_id = net.new()
    net.send(w_id, w_part.at[p.other], w_sib, p.sib)
    w_line = LineSum(net, p, nz, lambda o: w_part.at[p.core, o], w_low, w_high, None, half)

    def tokens_of(k):
        def one(q, _):
            w = wqkv[...].reshape(-1, 3 * LANES)
            x_part[k, q] = mm(block_grads(k, q), w, NT).astype(bf16)
            return 0

        lax.fori_loop(0, n // 2, one, 0)

    tokens_of(p.other)
    x_id = net.new()
    net.send(x_id, x_part.at[p.other], x_sib, p.sib)
    net.recv(w_id, w_sib, p.sib)
    for o in range(nz):
        add_into(w_part.at[p.core, o], w_sib.at[o], half)
    w_line.step(0)
    tokens_of(p.core)
    net.recv(x_id, x_sib, p.sib)
    for q in range(n // 2):
        add_into(x_part.at[p.core, q], x_sib.at[q], tok)
    xs = PlaneSum(net, p, lambda q: x_part.at[p.core, q], tok, x_rx0, x_ry1, x_ry0, x_rx1)
    xs.first()
    line_a.step(3)
    plane_b.third()
    final = PlaneGather(net, p, lambda: g_kept.at[z, p.chip], lambda k, q: gsum_o.at[k, q], rows)
    final.first()
    own_sum = fetch(g_kept.at[z, p.chip], gsum_o.at[p.core, p.chip])
    w_line.step(1)
    xs.second()
    w_line.step(2)
    final.second()
    w_line.step(3)
    w_final = PlaneGather(net, p, lambda: w_part.at[p.core, z], lambda k, q: w_all.at[k, q], half)
    w_final.first()
    own_w = pltpu.make_async_copy(w_part.at[p.core, z], w_all.at[p.core, p.chip], lsem.at[31])
    own_w.start()
    final.third()
    w_final.second()
    xs.third()

    def add_tokens(i, _):
        at = pl.ds(pl.multiple_of(i * 32, 32), 32)
        dtok_o[at, :] = (dh_ref[at, :] + x_part[p.core, p.chip, at, :].astype(f32)).astype(bf16)
        return 0

    lax.fori_loop(0, tok // 32, add_tokens, 0)
    w_final.third()
    w_final.last()
    own_w.wait()
    cols = heads * head_dim
    for j in range(3):
        for k in range(2):
            dw_o[j, k * half : (k + 1) * half, :] = jnp.concatenate(
                [w_all[k, q][:, j * LANES : j * LANES + cols] for q in range(4)], axis=1
            )
    final.last()
    own_sum.wait()
    net.finish()


def line_order(nz):
    order = []
    for i in range((nz + 1) // 2):
        for o in (nz - 1 - i, i):
            if o not in order:
                order.append(o)
    return order


def backward(
    nz, n, heads, head_dim, rb, pairs, pairing, grads, da, dh, xall, wqkv, q, k, v, on, lse
):
    rows, width = grads.shape[3], grads.shape[4]
    seg = xall.shape[3]
    tok = 2 * seg
    d_rows = wqkv.shape[1]
    half = d_rows // 2
    ra = rows - rb
    n_sem = 6 * (nz + 2) + 6 * nz + nz + 9 + 24 + 2
    sds = jax.ShapeDtypeStruct
    vm = lambda *shape: pltpu.VMEM(shape, bf16)
    wide, tiled = (2 * n, seg, LANES), (tok * n // KT, KT, LANES)
    da = da.reshape(4, 2, seg, LANES)
    return pl.pallas_call(
        functools.partial(backward_kernel, nz, n, heads, head_dim, rb, n_sem),
        out_shape=(
            sds(grads.shape[1:], bf16),
            sds((tok, width), bf16),
            sds((3, d_rows, width), bf16),
        ),
        in_specs=smem(2) + hbm(2) + vmem(1) + hbm(6) + vmem(1),
        out_specs=tuple(hbm(1) + vmem(2)),
        scratch_shapes=[
            pltpu.SMEM((2 * n + heads,), jnp.int32),
            vm(nz, 4, rows, width),
            vm(nz, 4, rows, width),
            vm(nz, 2, ra // 2, width),
            vm(nz, 2, ra // 2, width),
            vm(nz, ra // 2, width),
            vm(nz, ra // 2, width),
            vm(nz, ra, width),
            vm(nz, ra, width),
            vm(nz, 4, rb, width),
            vm(nz, 4, rb, width),
            vm(2, rb // 2, width),
            vm(2, rb // 2, width),
            vm(rb // 2, width),
            vm(rb // 2, width),
            vm(2, 4, tok, width),
            vm(4, tok, width),
            vm(2, tok // 2, width),
            vm(2, tok // 2, width),
            vm(tok // 2, width),
            vm(tok // 2, width),
            vm(2, nz, half, width),
            vm(nz, half, width),
            vm(nz, half, width),
            vm(nz, half, width),
            vm(2, 4, half, width),
            vm(2, 4, 2, seg, LANES),
            vm(2, 4, 2, seg, width),
            vm(nz, d_rows, width),
            vm(*wide),
            vm(*tiled),
            vm(*tiled),
            vm(*wide),
            vm(2 * n, seg, 3 * LANES),
            pltpu.VMEM((seg * n, LANES), f32),
            pltpu.VMEM((seg * n, LANES), f32),
            pltpu.VMEM((width, 3 * LANES), f32),
            pltpu.SemaphoreType.DMA((n_sem,)),
            pltpu.SemaphoreType.DMA((n_sem,)),
            pltpu.SemaphoreType.DMA((32,)),
        ],
        compiler_params=comm_params(1),
        name="backward",
    )(pairs, pairing, grads, da, dh, xall, wqkv, q, k, v, on, lse)


def fast_body(
    tokens,
    w_query,
    w_key,
    w_value,
    w_output,
    w_inner,
    w_outer,
    ln_gain,
    ln_bias,
    pairing,
    block_pairs,
    cotangent,
):
    tok, width = tokens.shape[1], tokens.shape[2]
    n_ctx, nz = lax.axis_size("ctx"), lax.axis_size("fsdp")
    z = lax.axis_index("fsdp")
    heads = pairing.shape[1]
    my_heads, head_dim = heads // 4, width // heads
    d_rows = w_query.shape[0]
    f_rows, ff = w_outer.shape[0], w_inner.shape[1]
    n_f = ff // width
    o1, o2, used = f_rows, f_rows + n_f * d_rows, f_rows + n_f * d_rows + d_rows
    total = -(-(used + 4) // 256) * 256
    norms = jnp.concatenate([ln_gain.T, ln_bias.T], axis=0).astype(bf16)
    norms = lax.dynamic_update_slice(jnp.zeros((16, width), bf16), norms, (0, z * d_rows))
    weights = (w_query, w_key, w_value, w_output, w_inner, w_outer)
    xall, wqkv, q, k, v, on, grads, lse, result, da, d_h1 = front(
        nz, n_ctx, my_heads, head_dim, total, block_pairs, pairing, tokens[0], cotangent[0],
        norms, weights,
    )
    grads = grads.reshape(nz, 2, 4, total // 8, width)
    gsum, dtok, dw = backward(
        nz, n_ctx, my_heads, head_dim, 64, block_pairs, pairing, grads, da, d_h1,
        xall, wqkv, q, k, v, on, lse,
    )
    gsum = gsum.reshape(total, width)
    g_inner = [gsum[o1 + i * d_rows : o1 + (i + 1) * d_rows] for i in range(n_f)]
    g_norms = lax.dynamic_slice(gsum[used : used + 4], (0, z * d_rows), (4, d_rows)).astype(f32)
    return (
        result[None],
        dtok[None],
        dw[0].astype(f32),
        dw[1].astype(f32),
        dw[2].astype(f32),
        gsum[o2:used].astype(f32),
        jnp.concatenate(g_inner, axis=1).astype(f32),
        gsum[:o1].astype(f32),
        g_norms[:2].T,
        g_norms[2:].T,
    )


def solution(mesh):
    in_specs = (
        P("fsdp", "ctx", None),
        P("fsdp", None),
        P("fsdp", None),
        P("fsdp", None),
        P("fsdp", None),
        P("fsdp", None),
        P("fsdp", None),
        P("fsdp", None),
        P("fsdp", None),
        P("fsdp", None),
        P("fsdp", None),
        P("fsdp", "ctx", None),
    )
    out_specs = (
        P("fsdp", "ctx", None),
        P("fsdp", "ctx", None),
        P("fsdp", None),
        P("fsdp", None),
        P("fsdp", None),
        P("fsdp", None),
        P("fsdp", None),
        P("fsdp", None),
        P("fsdp", None),
        P("fsdp", None),
    )
    fast = mesh.shape["ctx"] == 8 and mesh.shape["fsdp"] == 4
    chosen = fast_body if fast else generic_body
    return jax.shard_map(chosen, mesh=mesh, in_specs=in_specs, out_specs=out_specs, check_vma=False)
```

```python
import functools

import jax
import jax.numpy as jnp
from jax import lax
from jax.experimental import pallas as pl
from jax.experimental.pallas import tpu as pltpu
from jax.sharding import PartitionSpec as P

norm_eps = 1e-05
score_scale = 0.125
very_low = -1e30


def shortened(value):

    def short(part):
        return part.astype(jnp.bfloat16) if part.dtype == jnp.float32 else part

    return jax.tree.map(short, value)


def layer_norm(values, norm_gain, norm_shift):
    center = values - jnp.mean(values, axis=-1, keepdims=True)
    spread = jnp.mean(center * center, axis=-1, keepdims=True)
    return center * lax.rsqrt(spread + norm_eps) * norm_gain + norm_shift


def exact_gelu(values):
    return jax.nn.gelu(values, approximate=False)


def project(rows_in, weight):
    return jnp.dot(rows_in, weight, preferred_element_type=jnp.float32)


def seq_positions(pair_row, tok_dev, seq_len):
    segment_len = tok_dev // 2
    within = jnp.arange(tok_dev, dtype=jnp.int32)
    lower_pos = pair_row[:, None] * segment_len + within[None, :]
    upper_pos = seq_len - (pair_row[:, None] + 1) * segment_len + within[None, :] - segment_len
    return jnp.where(within[None, :] < segment_len, lower_pos, upper_pos).reshape(-1)


def pair_mask(query_pos, key_pos, head_flags, half_len):
    target = (query_pos[None, :] // half_len + head_flags[:, None]) % 2
    paired = key_pos[None, None, :] // half_len == target[:, :, None]
    causal = key_pos[None, :] <= query_pos[:, None]
    return jnp.logical_and(paired, causal[None, :, :])


def block_rows(tok_dev):
    return 2 * tok_dev


def over_blocks(running, arrays, step_fn, tok_dev):
    row_count = arrays[0].shape[0]
    block_len = block_rows(tok_dev)

    def one_step(inner_carry, step_index):
        first_row = step_index * block_len
        sliced = tuple(
            (lax.dynamic_slice_in_dim(member, first_row, block_len, 0) for member in arrays)
        )
        return (step_fn(inner_carry, sliced, first_row), None)

    return lax.scan(one_step, running, jnp.arange(row_count // block_len, dtype=jnp.int32))[0]


def generic_body(
    tokens,
    w_query,
    w_key,
    w_value,
    w_output,
    w_inner,
    w_outer,
    ln_gain,
    ln_bias,
    pairing,
    block_pairs,
    cotangent,
):
    tok_dev = tokens.shape[1]
    width = tokens.shape[2]
    heads = pairing.shape[1]
    head_dim = width // heads
    n_ctx = lax.axis_size("ctx")
    seq_len = tok_dev * n_ctx
    half_len = seq_len // 2
    pos_all = seq_positions(block_pairs[0], tok_dev, seq_len)
    my_pos = lax.dynamic_slice_in_dim(pos_all, lax.axis_index("ctx") * tok_dev, tok_dev, 0)
    head_flags = pairing[0]
    masters = (w_query, w_key, w_value, w_output, w_inner, w_outer, ln_gain, ln_bias)
    low_masters = tuple((member.astype(jnp.bfloat16) for member in masters))
    gathered = jax.tree.map(
        lambda part, own: part.astype(own.dtype),
        lax.all_gather(shortened(low_masters), "fsdp", axis=0, tiled=True),
        low_masters,
    )
    wq_full, wk_full, wv_full, wo_full, inner_full, outer_full, gain_full, shift_full = gathered
    gain_wide = gain_full.astype(jnp.float32)
    shift_wide = shift_full.astype(jnp.float32)
    x_in = tokens[0]
    query_b = project(x_in, wq_full).astype(jnp.bfloat16)
    key_b = project(x_in, wk_full).astype(jnp.bfloat16)
    value_b = project(x_in, wv_full).astype(jnp.bfloat16)
    q_heads = query_b.reshape(tok_dev, heads, head_dim)

    def attend_step(running, sliced, offset):
        run_max, run_sum, run_acc = running
        key_block, value_block = sliced
        block_len = key_block.shape[0]
        key_pos = lax.dynamic_slice_in_dim(pos_all, offset, block_len, 0)
        allowed = pair_mask(my_pos, key_pos, head_flags, half_len)
        key_heads = key_block.reshape(block_len, heads, head_dim)
        value_heads = value_block.reshape(block_len, heads, head_dim)
        scores = (
            jnp.einsum("qhd,khd->hqk", q_heads, key_heads, preferred_element_type=jnp.float32)
            * score_scale
        )
        new_max = jnp.maximum(run_max, jnp.max(jnp.where(allowed, scores, very_low), axis=2))
        prob_rows = jnp.where(
            allowed, jnp.exp(jnp.where(allowed, scores - new_max[:, :, None], 0.0)), 0.0
        )
        decay = jnp.exp(run_max - new_max)
        new_sum = run_sum * decay + jnp.sum(prob_rows, axis=2)
        added = jnp.einsum(
            "hqk,khd->hqd",
            prob_rows.astype(jnp.bfloat16),
            value_heads,
            preferred_element_type=jnp.float32,
        )
        return (new_max, new_sum, run_acc * decay[:, :, None] + added)

    def pair_fold(step_fn, running, fetched):
        return over_blocks(running, fetched, step_fn, tok_dev)

    start_state = (
        jnp.full((heads, tok_dev), very_low, jnp.float32),
        jnp.zeros((heads, tok_dev), jnp.float32),
        jnp.zeros((heads, tok_dev, head_dim), jnp.float32),
    )
    run_max, run_sum, run_acc = pair_fold(
        attend_step,
        start_state,
        (
            lax.all_gather(key_b, "ctx", axis=0, tiled=True),
            lax.all_gather(value_b, "ctx", axis=0, tiled=True),
        ),
    )
    live_rows = run_sum > 0
    safe_sum = jnp.where(live_rows, run_sum, 1.0)
    attn_heads = jnp.where(live_rows[:, :, None], run_acc / safe_sum[:, :, None], 0.0)
    lse_rows = jnp.where(live_rows, run_max + jnp.log(safe_sum), 0.0)
    attn_rows = attn_heads.transpose(1, 0, 2).reshape(tok_dev, width)
    attn_b = attn_rows.astype(jnp.bfloat16)
    branch = project(attn_b, wo_full)
    first_norm, first_pull = jax.vjp(
        layer_norm, x_in.astype(jnp.float32) + branch, gain_wide[:, 0], shift_wide[:, 0]
    )
    first_b = first_norm.astype(jnp.bfloat16)
    inner = project(first_b, inner_full)
    active, gelu_pull = jax.vjp(exact_gelu, inner)
    active_b = active.astype(jnp.bfloat16)
    outer = project(active_b, outer_full)
    result, second_pull = jax.vjp(layer_norm, first_norm + outer, gain_wide[:, 1], shift_wide[:, 1])
    wq_back, wk_back, wv_back, wo_back, inner_back, outer_back, gain_back, shift_back = gathered
    d_h2, d_gain2, d_shift2 = second_pull(cotangent[0].astype(jnp.float32))
    d_f_b = d_h2.astype(jnp.bfloat16)
    d_outer = jnp.dot(active_b.T, d_f_b, preferred_element_type=jnp.float32)
    d_active = jnp.dot(d_f_b, outer_back.T, preferred_element_type=jnp.float32)
    d_u_b = gelu_pull(d_active)[0].astype(jnp.bfloat16)
    d_inner = jnp.dot(first_b.T, d_u_b, preferred_element_type=jnp.float32)
    d_x1 = d_h2 + jnp.dot(d_u_b, inner_back.T, preferred_element_type=jnp.float32)
    d_h1, d_gain1, d_shift1 = first_pull(d_x1)
    d_y_b = d_h1.astype(jnp.bfloat16)
    d_wo = jnp.dot(attn_b.T, d_y_b, preferred_element_type=jnp.float32)
    d_attn_b = jnp.dot(d_y_b, wo_back.T, preferred_element_type=jnp.float32).astype(jnp.bfloat16)
    delta_rows = (
        (d_attn_b.astype(jnp.float32) * attn_rows).reshape(tok_dev, heads, head_dim).sum(axis=2).T
    )
    dout_heads = d_attn_b.reshape(tok_dev, heads, head_dim)

    def query_grad_step(dq_acc, sliced, offset):
        key_block, value_block = sliced
        block_len = key_block.shape[0]
        key_pos = lax.dynamic_slice_in_dim(pos_all, offset, block_len, 0)
        allowed = pair_mask(my_pos, key_pos, head_flags, half_len)
        key_heads = key_block.reshape(block_len, heads, head_dim)
        value_heads = value_block.reshape(block_len, heads, head_dim)
        scores = (
            jnp.einsum("qhd,khd->hqk", q_heads, key_heads, preferred_element_type=jnp.float32)
            * score_scale
        )
        prob_rows = jnp.where(
            allowed, jnp.exp(jnp.where(allowed, scores - lse_rows[:, :, None], 0.0)), 0.0
        )
        prob_grad = jnp.einsum(
            "qhd,khd->hqk", dout_heads, value_heads, preferred_element_type=jnp.float32
        )
        dscore = (prob_rows * (prob_grad - delta_rows[:, :, None]) * score_scale).astype(
            jnp.bfloat16
        )
        return dq_acc + jnp.einsum(
            "hqk,khd->qhd", dscore, key_heads, preferred_element_type=jnp.float32
        )

    dq_start = jnp.zeros((tok_dev, heads, head_dim), jnp.float32)
    dq_acc = pair_fold(
        query_grad_step,
        dq_start,
        (
            lax.all_gather(key_b, "ctx", axis=0, tiled=True),
            lax.all_gather(value_b, "ctx", axis=0, tiled=True),
        ),
    )
    dq_b = dq_acc.reshape(tok_dev, width).astype(jnp.bfloat16)
    lse_all, delta_all = (
        lax.all_gather(lse_rows, "ctx", axis=1, tiled=True),
        lax.all_gather(delta_rows, "ctx", axis=1, tiled=True),
    )
    k_heads = key_b.reshape(tok_dev, heads, head_dim)
    v_heads = value_b.reshape(tok_dev, heads, head_dim)

    def key_grad_step(running, sliced, offset):
        dk_acc, dv_acc = running
        query_block, dout_block = sliced
        block_len = query_block.shape[0]
        query_pos = lax.dynamic_slice_in_dim(pos_all, offset, block_len, 0)
        lse_block = lax.dynamic_slice_in_dim(lse_all, offset, block_len, 1)
        delta_block = lax.dynamic_slice_in_dim(delta_all, offset, block_len, 1)
        allowed = pair_mask(query_pos, my_pos, head_flags, half_len)
        query_heads = query_block.reshape(block_len, heads, head_dim)
        dout_block_heads = dout_block.reshape(block_len, heads, head_dim)
        scores = (
            jnp.einsum("qhd,khd->hqk", query_heads, k_heads, preferred_element_type=jnp.float32)
            * score_scale
        )
        prob_rows = jnp.where(
            allowed, jnp.exp(jnp.where(allowed, scores - lse_block[:, :, None], 0.0)), 0.0
        )
        dv_acc = dv_acc + jnp.einsum(
            "hqk,qhd->khd",
            prob_rows.astype(jnp.bfloat16),
            dout_block_heads,
            preferred_element_type=jnp.float32,
        )
        prob_grad = jnp.einsum(
            "qhd,khd->hqk", dout_block_heads, v_heads, preferred_element_type=jnp.float32
        )
        dscore = (prob_rows * (prob_grad - delta_block[:, :, None]) * score_scale).astype(
            jnp.bfloat16
        )
        dk_acc = dk_acc + jnp.einsum(
            "hqk,qhd->khd", dscore, query_heads, preferred_element_type=jnp.float32
        )
        return (dk_acc, dv_acc)

    kv_start = (
        jnp.zeros((tok_dev, heads, head_dim), jnp.float32),
        jnp.zeros((tok_dev, heads, head_dim), jnp.float32),
    )
    dk_acc, dv_acc = pair_fold(
        key_grad_step,
        kv_start,
        (
            lax.all_gather(query_b, "ctx", axis=0, tiled=True),
            lax.all_gather(d_attn_b, "ctx", axis=0, tiled=True),
        ),
    )
    dk_b = dk_acc.reshape(tok_dev, width).astype(jnp.bfloat16)
    dv_b = dv_acc.reshape(tok_dev, width).astype(jnp.bfloat16)
    d_input = d_h1 + jnp.dot(dq_b, wq_back.T, preferred_element_type=jnp.float32)
    d_input = d_input + jnp.dot(dk_b, wk_back.T, preferred_element_type=jnp.float32)
    d_input = d_input + jnp.dot(dv_b, wv_back.T, preferred_element_type=jnp.float32)
    terms = (
        jnp.dot(x_in.T, dq_b, preferred_element_type=jnp.float32),
        jnp.dot(x_in.T, dk_b, preferred_element_type=jnp.float32),
        jnp.dot(x_in.T, dv_b, preferred_element_type=jnp.float32),
        d_wo,
        d_inner,
        d_outer,
        jnp.stack([d_gain1, d_gain2], axis=1),
        jnp.stack([d_shift1, d_shift2], axis=1),
    )
    shares = (
        lax.psum_scatter(
            terms[0].astype(jnp.bfloat16), "fsdp", scatter_dimension=0, tiled=True
        ).astype(jnp.float32),
        lax.psum_scatter(
            terms[1].astype(jnp.bfloat16), "fsdp", scatter_dimension=0, tiled=True
        ).astype(jnp.float32),
        lax.psum_scatter(
            terms[2].astype(jnp.bfloat16), "fsdp", scatter_dimension=0, tiled=True
        ).astype(jnp.float32),
        lax.psum_scatter(
            terms[3].astype(jnp.bfloat16), "fsdp", scatter_dimension=0, tiled=True
        ).astype(jnp.float32),
        lax.psum_scatter(
            terms[4].astype(jnp.bfloat16), "fsdp", scatter_dimension=0, tiled=True
        ).astype(jnp.float32),
        lax.psum_scatter(
            terms[5].astype(jnp.bfloat16), "fsdp", scatter_dimension=0, tiled=True
        ).astype(jnp.float32),
        lax.psum_scatter(
            terms[6].astype(jnp.bfloat16), "fsdp", scatter_dimension=0, tiled=True
        ).astype(jnp.float32),
        lax.psum_scatter(
            terms[7].astype(jnp.bfloat16), "fsdp", scatter_dimension=0, tiled=True
        ).astype(jnp.float32),
    )
    totals = (
        lax.psum(shares[0].astype(jnp.bfloat16), "ctx").astype(jnp.float32),
        lax.psum(shares[1].astype(jnp.bfloat16), "ctx").astype(jnp.float32),
        lax.psum(shares[2].astype(jnp.bfloat16), "ctx").astype(jnp.float32),
        lax.psum(shares[3].astype(jnp.bfloat16), "ctx").astype(jnp.float32),
        lax.psum(shares[4].astype(jnp.bfloat16), "ctx").astype(jnp.float32),
        lax.psum(shares[5].astype(jnp.bfloat16), "ctx").astype(jnp.float32),
        lax.psum(shares[6].astype(jnp.bfloat16), "ctx").astype(jnp.float32),
        lax.psum(shares[7].astype(jnp.bfloat16), "ctx").astype(jnp.float32),
    )
    return (
        result.astype(jnp.bfloat16)[None],
        d_input.astype(jnp.bfloat16)[None],
        totals[0],
        totals[1],
        totals[2],
        totals[3],
        totals[4],
        totals[5],
        totals[6],
        totals[7],
    )


MESH = pl.DeviceIdType.MESH
f32 = jnp.float32
bf16 = jnp.bfloat16


class Place:
    def __init__(self):
        me = lax.axis_index("ctx")
        self.me = me
        self.z = lax.axis_index("fsdp")
        self.core = lax.rem(me, 2)
        self.chip = me // 2
        self.x = lax.rem(self.chip, 2)
        self.y = self.chip // 2
        self.chip_x = self.chip + 1 - 2 * self.x
        self.chip_y = self.chip + 2 - 4 * self.y
        self.chip_d = 3 - self.chip
        self.other = 1 - self.core
        self.sib = (2 * self.chip + 1 - self.core, self.z)
        self.xn = (2 * self.chip_x + self.core, self.z)
        self.yn = (2 * self.chip_y + self.core, self.z)
        self.dn = (2 * self.chip_d + self.core, self.z)
        self.up = (me, self.z + 1)
        self.down = (me, self.z - 1)


def greet(place, others, line_len=None):
    barrier = pltpu.get_barrier_semaphore()
    count = len(others)
    for other in others:
        pl.semaphore_signal(barrier, inc=1, device_id=other, device_id_type=MESH)
    if line_len is not None:

        @pl.when(place.z < line_len - 1)
        def _():
            pl.semaphore_signal(barrier, inc=1, device_id=place.up, device_id_type=MESH)

        @pl.when(place.z > 0)
        def _():
            pl.semaphore_signal(barrier, inc=1, device_id=place.down, device_id_type=MESH)

        count = count + jnp.where(place.z < line_len - 1, 1, 0) + jnp.where(place.z > 0, 1, 0)

    pl.semaphore_wait(barrier, count)


def maybe(cond, fn):
    if cond is None:
        fn()
    else:
        pl.when(cond)(fn)


def of(ref):
    return ref() if callable(ref) else ref


class Net:
    def __init__(self, send_sems, recv_sems, count):
        self.send_sems, self.recv_sems, self.count = send_sems, recv_sems, count
        self.used = 0
        self.open = []

    def new(self):
        self.used += 1
        assert self.used <= self.count
        return self.used - 1

    def copy(self, idx, src, dst, dev):
        return pltpu.make_async_remote_copy(
            src_ref=src,
            dst_ref=dst,
            send_sem=self.send_sems.at[idx],
            recv_sem=self.recv_sems.at[idx],
            device_id=dev,
            device_id_type=MESH,
        )

    def send(self, idx, src, dst, dev, cond=None):
        make = lambda: self.copy(idx, of(src), of(dst), dev)
        maybe(cond, lambda: make().start())
        self.open.append((cond, make))

    def recv(self, idx, dst, dev, cond=None):
        maybe(cond, lambda: self.copy(idx, of(dst), of(dst), dev).wait_recv())

    def finish(self):
        for cond, make in self.open:
            maybe(cond, lambda make=make: make().wait_send())
        self.open = []


class PlaneGather:
    def __init__(self, net, place, own, slot, rows, cond=None):
        p = place
        self.net, self.place, self.cond = net, place, cond
        self.own_of, self.slot = own, slot
        self.h0, self.h1 = pl.ds(0, rows // 2), pl.ds(rows // 2, rows // 2)
        self.ids = [net.new() for _ in range(11)]

    def at(self, core, chip, half=0):
        def view():
            ref = self.slot(core, chip)
            return ref if half == 0 else ref.at[self.h0 if half == 1 else self.h1]

        return view

    def mine(self, half=0):
        def view():
            ref = self.own_of()
            return ref if half == 0 else ref.at[self.h0 if half == 1 else self.h1]

        return view

    def first(self):
        n, p, i, c = self.net, self.place, self.ids, self.cond
        at = functools.partial(self.at, p.core, p.chip)
        n.send(i[0], self.mine(1), at(1), p.xn, c)
        n.send(i[1], self.mine(2), at(2), p.yn, c)
        n.send(i[2], self.mine(2), at(2), p.xn, c)
        n.send(i[3], self.mine(1), at(1), p.yn, c)
        n.send(i[4], self.mine(), at(), p.sib, c)

    def second(self):
        n, p, i, c = self.net, self.place, self.ids, self.cond
        bx = functools.partial(self.at, p.core, p.chip_x)
        by = functools.partial(self.at, p.core, p.chip_y)
        n.recv(i[0], bx(1), p.xn, c)
        n.send(i[5], bx(1), bx(1), p.yn, c)
        n.recv(i[1], by(2), p.yn, c)
        n.send(i[6], by(2), by(2), p.xn, c)
        n.recv(i[2], bx(2), p.xn, c)
        n.send(i[7], bx(), bx(), p.sib, c)
        n.recv(i[3], by(1), p.yn, c)
        n.send(i[8], by(), by(), p.sib, c)

    def third(self):
        n, p, i, c = self.net, self.place, self.ids, self.cond
        bd = functools.partial(self.at, p.core, p.chip_d)
        n.recv(i[5], bd(1), p.yn, c)
        n.send(i[9], bd(1), bd(1), p.sib, c)
        n.recv(i[6], bd(2), p.xn, c)
        n.send(i[10], bd(2), bd(2), p.sib, c)

    def last(self):
        n, p, i, c = self.net, self.place, self.ids, self.cond
        for idx, q in ((4, p.chip), (7, p.chip_x), (8, p.chip_y)):
            n.recv(i[idx], self.at(p.other, q), p.sib, c)
        n.recv(i[9], self.at(p.other, p.chip_d, 1), p.sib, c)
        n.recv(i[10], self.at(p.other, p.chip_d, 2), p.sib, c)


def hbm(count):
    return [pl.BlockSpec(memory_space=pltpu.HBM)] * count


def comm_params(collective_id):
    return pltpu.CompilerParams(
        collective_id=collective_id, has_side_effects=True, vmem_limit_bytes=56 << 20
    )


def vmem(count):
    return [pl.BlockSpec(memory_space=pltpu.VMEM)] * count


def smem(count):
    return [pl.BlockSpec(memory_space=pltpu.SMEM)] * count


LANES = 256
KT = 128
NT = (((1,), (1,)), ((), ()))
TN = (((0,), (0,)), ((), ()))
NN = (((1,), (0,)), ((), ()))


def mm(a, b, dims=NN):
    return lax.dot_general(a, b, dims, preferred_element_type=f32)


def head_mask(h, head_dim, dtype):
    lane = lax.broadcasted_iota(jnp.int32, (1, LANES), 1)
    inside = jnp.logical_and(lane >= h * head_dim, lane < (h + 1) * head_dim)
    return jnp.where(inside, 1.0, 0.0).astype(dtype)


class Fold:
    def __init__(self, n, seg):
        self.n, self.seg, self.half = n, seg, n * seg
        self.tiles = self.half // KT

    def ranges(self, i):
        a = -(-(self.n - i) * self.seg // KT)
        b = -(-(i + 1) * self.seg // KT)
        assert a + b == self.tiles + 2
        return a, b

    def places(self, i, core, paired):
        a, b = self.ranges(i)
        n, seg = self.n, self.seg
        causal = 1 - paired
        up = n + core * (n // 2) + i
        rows_a = (core * n + n - 1 - i) * causal + up * paired
        rows_b = (core * n + i) * causal + up * paired
        keys_a = core * self.tiles * causal
        keys_b = core * self.tiles * causal + a * paired
        lim_a = (n - 1 - i) * seg - (a - 2) * KT + (1 << 20) * paired
        lim_b = i * seg - (b - 2) * KT - (1 << 20) * paired
        return (rows_a, keys_a, lim_a, a), (rows_b, keys_b, lim_b, b)


def natural(tab, n, s):
    upper = lax.div(s, n)
    c = tab[n + s + upper * (2 * n - 1 - 2 * s)]
    return lax.rem(c, 2), lax.div(c, 2), upper


def key_tiles(ref, base, first, count):
    return ref[pl.ds(base + first, count)].reshape(count * KT, LANES)


def tail_mask(seg, limit):
    col = lax.broadcasted_iota(jnp.int32, (seg, 2 * KT), 1)
    row = lax.broadcasted_iota(jnp.int32, (seg, 2 * KT), 0)
    return col - row <= limit


def norm_forward(h, gain, shift):
    mean = jnp.mean(h, axis=1, keepdims=True)
    center = h - mean
    scale = lax.rsqrt(jnp.mean(center * center, axis=1, keepdims=True) + norm_eps)
    n = center * scale
    return n, scale, n * gain + shift


def norm_backward(cot, n, scale, gain):
    dn = cot * gain
    mean = jnp.mean(dn, axis=1, keepdims=True)
    along = jnp.mean(dn * n, axis=1, keepdims=True)
    return scale * (dn - mean - n * along)


def chain(*steps):
    def run():
        for fn, *args in steps:
            fn(*args)

    return run


def fill_table(tab, pairs, pairing, chip, n, heads):
    for c in range(n):
        tab[c] = pairs[0, c]
    for a in range(n):
        found = jnp.int32(0)
        for c in range(n):
            found = found + (pairs[0, c] == a).astype(jnp.int32) * c
        tab[n + a] = jnp.minimum(found, n - 1)
    for h in range(heads):
        tab[2 * n + h] = pairing[0, chip * heads + h]


def lse_lane(fold, h, i, g):
    return (h * (fold.n // 2) + i) * 2 + g


def attend_unit(fold, core, h, i, head_dim, tab, q_ref, k_ref, v_ref, o_ref, lse_ref):
    n, seg = fold.n, fold.seg
    paired = tab[2 * n + h]
    pf = paired.astype(f32)
    lanes = head_mask(h, head_dim, f32)
    lanes16 = head_mask(h, head_dim, bf16)
    parts = []
    for rows, keys, limit, count in fold.places(i, core, paired):
        q = q_ref[rows] * lanes16
        tail = mm(q, key_tiles(k_ref, keys, count - 2, 2), NT)
        tail = jnp.where(tail_mask(seg, limit), tail, very_low)
        top = jnp.max(tail, axis=1, keepdims=True)
        main = None
        if count > 2:
            main = mm(q, key_tiles(k_ref, keys, 0, count - 2), NT)
            top = jnp.maximum(top, jnp.max(main, axis=1, keepdims=True))
        parts.append((keys, count, main, tail, top))
    both = jnp.maximum(parts[0][4], parts[1][4])
    joined = jnp.broadcast_to(paired, both.shape) == 1
    outs = []
    for keys, count, main, tail, top in parts:
        top = jnp.where(joined, both, top)
        e = jnp.exp(tail - top)
        total = jnp.sum(e, axis=1, keepdims=True)
        acc = mm(e.astype(bf16), key_tiles(v_ref, keys, count - 2, 2))
        if main is not None:
            e = jnp.exp(main - top)
            total += jnp.sum(e, axis=1, keepdims=True)
            acc += mm(e.astype(bf16), key_tiles(v_ref, keys, 0, count - 2))
        outs.append((top, total, acc))
    (top_a, sum_a, acc_a), (top_b, sum_b, acc_b) = outs
    sum_a, sum_b = sum_a + pf * sum_b, jnp.where(joined, sum_a + sum_b, sum_b)
    acc_a = acc_a + pf * acc_b
    out_a = acc_a * (lanes / sum_a)
    out_b = acc_b * (lanes / sum_b)
    lane = lax.broadcasted_iota(jnp.int32, (1, KT), 1)
    lse = jnp.where(lane == lse_lane(fold, h, i, 0), top_a + jnp.log(sum_a), lse_ref[...])
    lse_ref[...] = jnp.where(lane == lse_lane(fold, h, i, 1), top_b + jnp.log(sum_b), lse)
    far, near, up = core * n + n - 1 - i, core * n + i, n + core * (n // 2) + i
    for at, value in ((far, (1.0 - pf) * out_a), (near, (1.0 - pf) * out_b), (up, pf * out_a)):
        o_ref[at] += value.astype(bf16)


def front_kernel(
    nz, n, heads, head_dim, n_sem,
    pairs, pairing, x_ref, cot_ref, ln_ref, wq_i, wk_i, wv_i, wo_i, w1_i, w2_i,
    xall_o, wqkv_o, q_o, k_o, v_o, on_o, g_o, lse_o, out_o, da_o, dh_o,
    tab, xall, wqkv, q_ref, k_ref, v_ref, o_nat, o_ctx, o_part, o_sum, attn,
    w1, w2, wol, fq, fo, f1, f2, u_ref, z_ref, x1b_ref, acc_ref, n1_ref, r1_ref, dx1_ref, gs, gt,
    ssem, rsem, lsem, fsem, gsem,
):
    p = Place()
    z = p.z
    seg, width = x_ref.shape[1], x_ref.shape[2]
    tok = 2 * seg
    fold = Fold(n, seg)
    d_rows, f_rows = wq_i.shape[0], w2_i.shape[0]
    n_f = w1_i.shape[1] // width
    cols = heads * head_dim
    half = d_rows // 2
    a1_rows, a2_rows = n_f * d_rows // 8, f_rows // 12
    b_first = 8 * a2_rows
    b_rows = (f_rows - b_first) // 2
    locals_ = []

    def keep(src, dst):
        cp = pltpu.make_async_copy(src, dst, lsem.at[len(locals_)])
        cp.start()
        locals_.append(cp)
        return cp

    masters = [
        pltpu.make_async_copy(src, dst, fsem.at[i])
        for i, (src, dst) in enumerate(
            ((wq_i, fq.at[0]), (wk_i, fq.at[1]), (wv_i, fq.at[2]), (w1_i, f1), (w2_i, f2), (wo_i, fo))
        )
    ]
    for cp in masters:
        cp.start()
    own_x = keep(x_ref, xall.at[p.core, p.chip])
    greet(p, (p.sib, p.xn, p.yn, p.dn), nz)
    net = Net(ssem, rsem, n_sem)
    tokens_ag = PlaneGather(net, p, lambda: x_ref, lambda k, q: xall.at[k, q], 2)
    tokens_ag.first()
    can_up, can_down = z < nz - 1, z > 0
    rows = pl.ds(p.core * half, half)
    other = pl.ds(p.other * half, half)

    class Stream:
        def __init__(self, at, after):
            self.up = [net.new() for _ in range(nz)]
            self.down = [net.new() for _ in range(nz)]
            self.at, self.todo = at, {}
            for t in range(1, nz):
                self.todo[t] = []
                for ids, src, frm, to, got, more in (
                    (self.up, z - t, p.down, p.up, z >= t, can_up),
                    (self.down, z + t, p.up, p.down, z + t < nz, can_down),
                ):
                    src = jnp.clip(src, 0, nz - 1)
                    on = jnp.logical_and(got, more)
                    self.todo[t].append((ids, src, frm, to, got, on, after(t, src, at, got)))

        def begin(self):
            own = lambda: self.at(z)
            net.send(self.up[1], own, own, p.up, can_up)
            net.send(self.down[1], own, own, p.down, can_down)

        def step(self, t):
            for ids, src, frm, to, got, on, then in self.todo[t]:
                block = functools.partial(self.at, src)
                net.recv(ids[t], block, frm, got)
                if t + 1 < nz:
                    net.send(ids[t + 1], block, block, to, on)
                then()

    def share(waits, block_of):
        def after(t, src, at, got):
            idx = net.new()
            waits.append((idx, lambda: block_of(src), got))
            return lambda: net.send(idx, lambda: at(src), lambda: at(src), p.sib, got)

        return after

    gathers = {t: [] for t in range(1, nz)}

    def spread(slot_of, count):
        def after(t, src, at, got):
            slot = lambda k, q: slot_of(src, k, q)
            gather = PlaneGather(net, p, lambda: at(src), slot, count, got)
            gathers[t].append(gather)
            return gather.first

        return after

    def a1_slot(o, k, q):
        start = pl.multiple_of(o * d_rows + lax.rem(q, 2) * a1_rows, 32)
        return w1.at[k * 2 + lax.div(q, 2), pl.ds(start, a1_rows)]

    def a2_slot(o, k, q):
        return w2.at[o, pl.ds(pl.multiple_of((k * 4 + q) * a2_rows, 32), a2_rows)]

    def b_slot(o, k):
        return w2.at[o, pl.ds(pl.multiple_of(b_first + k * b_rows, 32), b_rows)]

    sel_waits, b_waits, c_waits = [], [], []
    sel = Stream(lambda o: wqkv.at[o, rows], share(sel_waits, lambda o: wqkv.at[o, other]))
    cs = Stream(lambda o: wol.at[o, p.core], share(c_waits, lambda o: wol.at[o, p.other]))
    a1 = Stream(lambda o: a1_slot(o, p.core, p.chip), spread(a1_slot, a1_rows))
    a2 = Stream(lambda o: a2_slot(o, p.core, p.chip), spread(a2_slot, a2_rows))
    bs = Stream(lambda o: b_slot(o, p.core), share(b_waits, lambda o: b_slot(o, p.other)))

    for cp in masters[:3]:
        cp.wait()
    for chip in range(4):

        @pl.when(p.chip == chip)
        def _():
            for m in range(3):
                mine = fq[m, :, chip * cols : (chip + 1) * cols].astype(bf16)
                wqkv[z, :, m * LANES : m * LANES + cols] = mine

    for m in range(3):
        wqkv[z, :, m * LANES + cols : (m + 1) * LANES] = jnp.zeros((d_rows, LANES - cols), bf16)
    sel.begin()
    masters[3].wait()
    for f in range(n_f):
        at = pl.ds(pl.multiple_of(z * d_rows, 32), d_rows)
        w1[f, at, :] = f1[:, f * width : (f + 1) * width].astype(bf16)
    a1.begin()
    masters[4].wait()

    def cast(i, _):
        at = pl.ds(pl.multiple_of(i * 64, 64), 64)
        w2[z, at, :] = f2[at, :].astype(bf16)
        return 0

    lax.fori_loop(0, f_rows // 64, cast, 0)
    masters[5].wait()
    for k in range(2):
        wol[z, k, :half, :] = fo[k * half : (k + 1) * half, :].astype(bf16)
        wol[z, k, half:, :] = ln_ref[...]
    fill_table(tab, pairs, pairing, p.chip, n, heads)
    o_nat[...] = jnp.zeros(o_nat.shape, bf16)
    lse_o[...] = jnp.zeros(lse_o.shape, f32)
    sel.step(1)
    a2.begin()
    for t in range(2, nz):
        sel.step(t)
    tokens_ag.second()
    a1.step(1)
    a2.step(1)
    tokens_ag.third()
    a1.step(2)
    cs.begin()
    own_x.wait()
    tokens_ag.last()
    for idx, block, got in sel_waits:
        net.recv(idx, block, p.sib, got)
    keep(xall, xall_o)
    keep(wqkv, wqkv_o)

    def four(i, _):
        tokens = jnp.concatenate([xall[natural(tab, n, 4 * i + u)] for u in range(4)], axis=0)
        qkv = mm(tokens, wqkv[...].reshape(-1, 3 * LANES))
        q = (qkv[:, :LANES].astype(bf16).astype(f32) * score_scale).astype(bf16)
        q_ref[pl.ds(4 * i, 4)] = q.reshape(4, seg, LANES)
        at = pl.ds(i * (4 * seg // KT), 4 * seg // KT)
        k_ref[at] = qkv[:, LANES : 2 * LANES].astype(bf16).reshape(-1, KT, LANES)
        v_ref[at] = qkv[:, 2 * LANES :].astype(bf16).reshape(-1, KT, LANES)
        return 0

    lax.fori_loop(0, n // 2, four, 0)
    for src, dst in ((q_ref, q_o), (k_ref, k_o), (v_ref, v_o)):
        keep(src, dst)

    def second(t):
        for gather in gathers[t]:
            gather.second()

    def third(t):
        for gather in gathers[t]:
            gather.third()

    todo = {
        (0, 0): chain((a2.step, 2), (a1.step, 3)),
        (0, 1): chain((second, 1)),
        (0, 2): chain((a2.step, 3), (bs.begin,)),
        (0, 3): chain((cs.step, 1)),
        (1, 1): chain((third, 1), (second, 2)),
        (1, 3): chain((cs.step, 2)),
        (2, 0): chain((third, 2), (bs.step, 1)),
        (2, 2): chain((second, 3), (cs.step, 3)),
    }

    def head(h, _):
        for i in range(n // 2):
            attend_unit(fold, p.core, h, i, head_dim, tab, q_ref, k_ref, v_ref, o_nat, lse_o)
            for (at_h, at_i), step in todo.items():
                if at_i == i:
                    pl.when(h == at_h)(step)
        return 0

    lax.fori_loop(0, heads, head, 0)
    keep(o_nat, on_o)
    for core_is in range(2):
        for q in range(n // 2):
            a = tab[2 * q + core_is]
            for u, s in ((0, a), (1, 2 * n - 1 - a)):
                o_ctx[core_is, q, u * seg : (u + 1) * seg, :] = o_nat[s]
    part, swaps = net.new(), [net.new() for _ in range(3)]
    net.send(part, o_ctx.at[p.other], o_part, p.sib)
    bs.step(2)
    net.recv(part, o_part, p.sib)
    partners = ((p.chip_d, p.dn), (p.chip_x, p.xn), (p.chip_y, p.yn))
    for idx, (chip, dev) in zip(swaps, partners):
        o_sum[chip] = o_ctx[p.core, chip] + o_part[chip]
        net.send(idx, o_sum.at[chip], attn.at[p.chip], dev)
    attn[p.chip] = o_ctx[p.core, p.chip] + o_part[p.chip]
    third(3)
    for idx, block, got in c_waits:
        net.recv(idx, block, p.sib, got)
    vec = wol[0, 0, half:, :].astype(f32)
    for o in range(1, nz):
        vec = vec + wol[o, 0, half:, :].astype(f32)
    gain1, gain2, shift1, shift2 = vec[0:1], vec[1:2], vec[2:3], vec[3:4]
    wo_of = lambda o: jnp.concatenate([wol[o, 0, :half, :], wol[o, 1, :half, :]], axis=0)
    for idx, (chip, dev) in zip(swaps, partners):
        net.recv(idx, attn.at[chip], dev)

    h1 = x_ref[...].reshape(tok, width).astype(f32)
    for o in range(nz):
        h1 = h1 + mm(attn[o, :, :cols], wo_of(o))
    n1, r1, x1 = norm_forward(h1, gain1, shift1)
    n1_ref[...] = n1
    r1_ref[...] = jnp.broadcast_to(r1, (tok, 128))
    x1b_ref[...] = x1.astype(bf16)
    acc_ref[...] = x1
    bs.step(3)
    for t in gathers:
        for gather in gathers[t]:
            gather.last()
    for idx, block, got in b_waits:
        net.recv(idx, block, p.sib, got)

    def up(f, _):
        u = mm(x1b_ref[...], w1[f])
        cdf = 0.5 + 0.5 * lax.erf(u * (0.5**0.5))
        act = (u * cdf).astype(bf16)
        z_ref[f] = act
        u_ref[f] = cdf + u * jnp.exp(-0.5 * u * u) * 0.3989422804014327
        acc_ref[...] += mm(act, w2[f])
        return 0

    lax.fori_loop(0, n_f, up, 0)
    n2, r2, out = norm_forward(acc_ref[...], gain2, shift2)
    out_o[...] = out.astype(bf16)
    cot = cot_ref[...].astype(f32)
    d_gain2 = jnp.sum(cot * n2, axis=0, keepdims=True)
    d_shift2 = jnp.sum(cot, axis=0, keepdims=True)
    dh2 = norm_backward(cot, n2, r2, gain2)
    dx1_ref[...] = dh2
    df = dh2.astype(bf16)
    first1, first2 = f_rows, f_rows + n_f * d_rows

    def grads_out(f, slot):
        yield pltpu.make_async_copy(gs.at[slot, 0], g_o.at[f, pl.ds(0, f_rows)], gsem.at[slot, 0])
        for o in range(nz):
            at = pl.ds(pl.multiple_of(first1 + f * d_rows, 32), d_rows)
            src = gs.at[slot, 1, pl.ds(o * d_rows, d_rows)]
            yield pltpu.make_async_copy(src, g_o.at[o, at], gsem.at[slot, 1 + o])

    def back(f, _):
        slot = lax.rem(f, 2)

        @pl.when(f >= 2)
        def _():
            for cp in grads_out(f - 2, slot):
                cp.wait()

        gs[slot, 0] = mm(z_ref[f], df, TN).astype(bf16)
        du = (mm(df, w2[f], NT) * u_ref[f]).astype(bf16)
        gs[slot, 1] = mm(x1b_ref[...], du, TN).astype(bf16)
        for cp in grads_out(f, slot):
            cp.start()
        dx1_ref[...] += mm(du, w1[f], NT)
        return 0

    lax.fori_loop(0, n_f, back, 0)
    d_x1 = dx1_ref[...]
    n1 = n1_ref[...]
    d_gain1 = jnp.sum(d_x1 * n1, axis=0, keepdims=True)
    d_shift1 = jnp.sum(d_x1, axis=0, keepdims=True)
    dh1 = norm_backward(d_x1, n1, r1_ref[:, :1], gain1)
    dh_o[...] = dh1
    dy = dh1.astype(bf16)
    norms = jnp.concatenate([d_gain1, d_gain2, d_shift1, d_shift2], axis=0).astype(bf16)
    ends = []
    for o in range(nz):
        da_o[o, :, :cols] = mm(dy, wo_of(o), NT).astype(bf16)
        da_o[o, :, cols:] = jnp.zeros((tok, LANES - cols), bf16)
        gt[o, :d_rows, :] = mm(attn[o, :, :cols], dy, TN).astype(bf16)
        gt[o, d_rows:, :] = jnp.zeros((gt.shape[1] - d_rows, width), bf16)
        gt[o, d_rows : d_rows + 4, :] = norms
        ends.append(pltpu.make_async_copy(gt.at[o], g_o.at[o, pl.ds(first2, gt.shape[1])], fsem.at[o]))
        ends[-1].start()
    for f in range(max(n_f - 2, 0), n_f):
        for cp in grads_out(f, f % 2):
            cp.wait()
    for cp in ends:
        cp.wait()
    net.finish()
    for cp in locals_[1:]:
        cp.wait()


def front(nz, n, heads, head_dim, total, pairs, pairing, x_in, cot, norms, weights):
    tok, width = x_in.shape
    seg = tok // 2
    d_rows, f_rows = weights[0].shape[0], weights[5].shape[0]
    n_f = weights[4].shape[1] // width
    n_sem = 11 * (4 * (nz - 1) + 1) + 5 * 2 * nz + 3 * 2 * (nz - 1) + 4
    wide, tiled = (2 * n, seg, LANES), (tok * n // KT, KT, LANES)
    shapes = [(2, 4, 2, seg, width), (nz, d_rows, 3 * LANES), wide, tiled, tiled, wide]
    block = (4, tok, LANES)
    sds = jax.ShapeDtypeStruct
    vb = lambda *s: pltpu.VMEM(s, bf16)
    vf = lambda *s: pltpu.VMEM(s, f32)
    return pl.pallas_call(
        functools.partial(front_kernel, nz, n, heads, head_dim, n_sem),
        out_shape=tuple(sds(s, bf16) for s in shapes)
        + (
            sds((nz, total, width), bf16),
            sds((seg, KT), f32),
            sds((tok, width), bf16),
            sds(block, bf16),
            sds((tok, width), f32),
        ),
        in_specs=smem(2) + vmem(3) + hbm(6),
        out_specs=tuple(hbm(7) + vmem(4)),
        scratch_shapes=[pltpu.SMEM((2 * n + heads,), jnp.int32)]
        + [vb(*s) for s in shapes]
        + [
            vb(2, *block),
            vb(*block),
            vb(*block),
            vb(*block),
            vb(n_f, nz * d_rows, width),
            vb(nz, f_rows, width),
            vb(nz, 2, d_rows // 2 + 16, width),
            vf(3, d_rows, width),
            vf(d_rows, width),
            vf(d_rows, n_f * width),
            vf(f_rows, width),
            vf(n_f, tok, width),
            vb(n_f, tok, width),
            vb(tok, width),
            vf(tok, width),
            vf(tok, width),
            vf(tok, 128),
            vf(tok, width),
            vb(2, 2, f_rows, width),
            vb(nz, total - f_rows - n_f * d_rows, width),
            pltpu.SemaphoreType.DMA((n_sem,)),
            pltpu.SemaphoreType.DMA((n_sem,)),
            pltpu.SemaphoreType.DMA((12,)),
            pltpu.SemaphoreType.DMA((6,)),
            pltpu.SemaphoreType.DMA((2, 1 + nz)),
        ],
        compiler_params=comm_params(0),
        name="front",
    )(pairs, pairing, x_in.reshape(2, seg, width), cot, norms, *weights)


def add_into(dst, src, rows):
    chunk = max(c for c in range(16, min(rows, 160) + 1, 16) if rows % c == 0)

    def step(i, _):
        at = pl.ds(pl.multiple_of(i * chunk, chunk), chunk)
        to, frm = of(dst), of(src)
        to[at, :] = to[at, :] + frm[at, :]
        return 0

    lax.fori_loop(0, rows // chunk, step, 0)


class Slot:
    def __init__(self, ref, o):
        self.ref, self.o = ref, o

    def __call__(self):
        return self.ref.at[self.o]

    @property
    def at(self):
        return self().at


class PlaneSum:
    def __init__(self, net, place, block, rows, rx0, ry1, ry0, rx1):
        p = place
        self.net, self.place = net, place
        self.rx0, self.ry1, self.ry0, self.rx1 = rx0, ry1, ry0, rx1
        self.h = rows // 2
        h0, h1 = pl.ds(0, self.h), pl.ds(self.h, self.h)
        far_x, far_y = 1 - p.x, 1 - p.y
        self.block, self.h0, self.h1 = block, h0, h1
        self.far_x, self.far_y = far_x, far_y
        self.to_x = [2 * j + far_x for j in range(2)]
        self.to_y = [2 * far_y + j for j in range(2)]
        self.on_y, self.on_x = 2 * far_y + p.x, 2 * p.y + far_x
        self.ids = [net.new() for _ in range(6)]

    def part(self, index, half):
        return lambda: self.block(index).at[half]

    def first(self):
        n, p, i = self.net, self.place, self.ids
        for j in range(2):
            n.send(i[j], self.part(self.to_x[j], self.h0), lambda j=j: self.rx0.at[j], p.xn)
            n.send(i[2 + j], self.part(self.to_y[j], self.h1), lambda j=j: self.ry1.at[j], p.yn)

    def second(self):
        n, p, i = self.net, self.place, self.ids
        on_y, on_x = self.part(self.on_y, self.h0), self.part(self.on_x, self.h1)
        mine0, mine1 = self.part(p.chip, self.h0), self.part(p.chip, self.h1)
        for j in range(2):
            n.recv(i[j], lambda j=j: self.rx0.at[j], p.xn)
        add_into(on_y, lambda: self.rx0.at[self.far_y], self.h)
        n.send(i[4], on_y, self.ry0, p.yn)
        for j in range(2):
            n.recv(i[2 + j], lambda j=j: self.ry1.at[j], p.yn)
        add_into(on_x, lambda: self.ry1.at[self.far_x], self.h)
        n.send(i[5], on_x, self.rx1, p.xn)
        add_into(mine0, lambda: self.rx0.at[p.y], self.h)
        add_into(mine1, lambda: self.ry1.at[p.x], self.h)

    def third(self):
        n, p, i = self.net, self.place, self.ids
        n.recv(i[4], self.ry0, p.yn)
        add_into(self.part(p.chip, self.h0), self.ry0, self.h)
        n.recv(i[5], self.rx1, p.xn)
        add_into(self.part(p.chip, self.h1), self.rx1, self.h)


class LineSum:
    def __init__(self, net, place, nz, whole, low, high, parts, rows):
        p, z, top = place, place.z, nz - 1
        self.net, self.top, self.parts, self.rows, self.whole = net, top, parts, rows, whole
        sides = (
            ([net.new() for _ in range(nz)], low, z, -1, p.down, p.up),
            ([net.new() for _ in range(nz)], high, top - z, 1, p.up, p.down),
        )
        self.todo = {}
        for t in range(nz):
            self.todo[t] = []
            for ids, buf, depth, sign, frm, to in sides:
                owner = jnp.clip(top - t + z if sign < 0 else t + z - top, 0, top)
                takes = jnp.logical_and(depth > 0, depth <= t)
                self.todo[t].append(
                    (ids, owner, buf, takes, depth <= t, frm, to)
                )

    def step(self, t):
        n = self.net
        for ids, owner, buf, takes, sends, frm, to in self.todo[t]:
            whole = functools.partial(self.whole, owner)
            landed = lambda buf=buf, owner=owner: buf.at[owner]

            def take(ids=ids, whole=whole, landed=landed, frm=frm):
                n.recv(ids[t - 1], landed, frm)
                if self.parts is None:
                    add_into(whole, landed, self.rows)
                else:
                    for j in range(self.parts):
                        add_into(
                            lambda j=j: whole().at[j], lambda j=j: landed().at[j], self.rows
                        )

            if t > 0:
                maybe(takes, take)
            if t < self.top:
                n.send(ids[t], whole, landed, to, sends)


def attend_back_unit(
    fold, core, h, i, head_dim, tab, q_ref, k_ref, v_ref, o_ref, lse_ref, da_ref,
    dcat_ref, dk_ref, dv_ref,
):
    n, seg, half = fold.n, fold.seg, fold.half
    paired = tab[2 * n + h]
    pf = paired.astype(f32)
    lanes = head_mask(h, head_dim, f32)
    lanes16 = head_mask(h, head_dim, bf16)
    dqs = []
    places = fold.places(i, core, paired)
    for g, (rows, keys, limit, count) in enumerate(places):
        q = q_ref[rows] * lanes16
        k, c, upper = natural(tab, n, rows)
        da = da_ref[k, c, upper] * lanes16
        delta = jnp.sum(
            da.astype(f32) * o_ref[rows].astype(f32), axis=1, keepdims=True
        )
        lane = lax.broadcasted_iota(jnp.int32, (1, KT), 1) == lse_lane(fold, h, i, g)
        lse = jnp.sum(jnp.where(lane, lse_ref[...], 0.0), axis=1, keepdims=True)
        dq = None
        pieces = [(count - 2, 2, True)]
        if count > 2:
            pieces.append((0, count - 2, False))
        for first, size, masked in pieces:
            kt = key_tiles(k_ref, keys, first, size)
            vt = key_tiles(v_ref, keys, first, size)
            pr = jnp.exp(mm(q, kt, NT) - lse)
            if masked:
                pr = jnp.where(tail_mask(seg, limit), pr, 0.0)
            ds = (pr * (mm(da, vt, NT) - delta)).astype(bf16)
            part = mm(ds, kt)
            dq = part if dq is None else dq + part
            dv = mm(pr.astype(bf16), da, TN)
            dk = mm(ds, q, TN)
            at = pl.ds(first * KT, size * KT)
            if g == 0 or masked:
                dk_ref[at, :] += dk
                dv_ref[at, :] += dv
            else:
                beyond = pl.ds(places[0][3] * KT, size * KT)
                dk_ref[at, :] += (1.0 - pf) * dk
                dv_ref[at, :] += (1.0 - pf) * dv
                dk_ref[beyond, :] += pf * dk
                dv_ref[beyond, :] += pf * dv
        dqs.append(dq)
    scaled = lanes * score_scale
    dq_a, dq_b = (dqs[0] + pf * dqs[1]) * scaled, dqs[1] * scaled
    far, near, up = core * n + n - 1 - i, core * n + i, n + core * (n // 2) + i
    for at, value in ((far, (1.0 - pf) * dq_a), (near, (1.0 - pf) * dq_b), (up, pf * dq_a)):
        dcat_ref[at, :, :LANES] += value.astype(bf16)


def place_key_grads(fold, core, paired, dk_ref, dv_ref, dcat_ref):
    n, seg, half = fold.n, fold.seg, fold.half
    pf = paired.astype(f32)

    def spread(j, _):
        at = pl.ds(pl.multiple_of(j * seg, seg), seg)
        for src, lanes in ((dk_ref, slice(LANES, 2 * LANES)), (dv_ref, slice(2 * LANES, None))):
            value = src[at, :]
            dcat_ref[core * n + j, :, lanes] += ((1.0 - pf) * value).astype(bf16)
            dcat_ref[j, :, lanes] += (pf * value).astype(bf16)
        return 0

    lax.fori_loop(0, n, spread, 0)


BACKWARD_ORDER = (
    "c1", "p1f", "dr", "c0", "lb0", "dw", "s2", "U0", "p0f", "s3", "U1", "U2", "U3", "p1s",
    "c2", "c3", "U4", "lb1", "U5", "p3f", "U6", "p2f", "U7", "p1t", "U8", "U9", "U10", "lb2",
    "p0s", "U11", "DXo", "p2s", "p3s", "p0t", "la0", "DXm", "xa", "xsf", "p3t", "p2t", "lb3",
    "pbf", "la1", "DW", "pbs", "la2", "wa", "pbt", "wl0", "fbf", "fbs", "la3", "faf", "wl1",
    "xss", "fbt", "wl2", "fbl", "wl3", "wff", "fas", "wfs", "fat", "xst", "tok", "wft", "fal",
    "wfl", "dwo",
)


def backward_kernel(
    nz, n, heads, head_dim, rb, n_sem,
    pairs, pairing, g_ref, da_in, dh_ref, xall_i, wqkv_i, q_i, k_i, v_i, on_i, lse_ref,
    gsum_o, dtok_o, dw_o,
    tab, g_kept, g_sib, g_rx0, g_ry1, g_ry0, g_rx1, g_low, g_high,
    b_low, b_high, b_rx0, b_ry1, b_ry0, b_rx1,
    x_part, x_sib, x_rx0, x_ry1, x_ry0, x_rx1, w_part, w_sib, w_low, w_high, w_all,
    da_all, xall, wqkv, q_ref, k_ref, v_ref, on_ref, dcat, dk_ref, dv_ref, dw_acc,
    ssem, rsem, lsem,
):
    p = Place()
    z = p.z
    seg, width = xall.shape[3], xall.shape[4]
    tok = 2 * seg
    fold = Fold(n, seg)
    rows = g_ref.shape[3]
    ra = rows - rb
    ax, bx = pl.ds(0, ra), pl.ds(ra, rb)
    order = line_order(nz)
    local = []

    def fetch(src, dst):
        cp = pltpu.make_async_copy(src, dst, lsem.at[len(local)])
        cp.start()
        local.append(cp)
        return cp

    net = Net(ssem, rsem, n_sem)
    own_da = fetch(da_in.at[p.chip], da_all.at[p.core, p.chip])
    own_g = {o: fetch(g_ref.at[o, p.core], g_kept.at[o]) for o in order}
    greet(p, (p.sib, p.xn, p.yn, p.dn), nz)
    swaps = [net.new() for _ in range(7)]
    partners = ((p.chip_d, p.dn), (p.chip_x, p.xn), (p.chip_y, p.yn))
    for i, (chip, dev) in enumerate(partners):
        net.send(swaps[i], da_in.at[chip], da_all.at[p.core, p.chip], dev)
    net.send(swaps[3], da_in.at[p.chip], da_all.at[p.core, p.chip], p.sib)
    sib_ids = {o: net.new() for o in order}

    def to_sib(o):
        net.send(sib_ids[o], lambda: g_ref.at[o, p.other], lambda: g_sib.at[o], p.sib)

    to_sib(order[0])
    to_sib(order[1])
    att_in = [
        fetch(src, dst)
        for src, dst in (
            (q_i, q_ref), (k_i, k_ref), (v_i, v_ref), (on_i, on_ref), (xall_i, xall), (wqkv_i, wqkv),
        )
    ]
    fill_table(tab, pairs, pairing, p.chip, n, heads)
    dcat[...] = jnp.zeros(dcat.shape, bf16)

    plane = {
        o: PlaneSum(
            net, p, lambda q, o=o: g_kept.at[o, q].at[ax], ra,
            *(Slot(r, o) for r in (g_rx0, g_ry1, g_ry0, g_rx1)),
        )
        for o in order
    }
    line_a = LineSum(net, p, nz, lambda o: g_kept.at[o, p.chip].at[ax], g_low, g_high, None, ra)
    line_b = LineSum(net, p, nz, lambda o: g_kept.at[o, :, bx], b_low, b_high, n // 2, rb)
    plane_b = PlaneSum(
        net, p, lambda q: g_kept.at[z, q].at[bx], rb, b_rx0, b_ry1, b_ry0, b_rx1
    )

    def chip_sum(o):
        net.recv(sib_ids[o], lambda: g_sib.at[o], p.sib)
        pltpu.make_async_copy(g_ref.at[o, p.core], g_kept.at[o], lsem.at[1 + order.index(o)]).wait()
        for q in range(n // 2):
            add_into(lambda q=q: g_kept.at[o, q], lambda q=q: g_sib.at[o, q], rows)

    d = wqkv.shape[1]
    half = d // 2
    x_id, w_id = net.new(), net.new()
    w_line = LineSum(net, p, nz, lambda o: w_part.at[p.core, o], w_low, w_high, None, half)
    xs = PlaneSum(net, p, lambda q: x_part.at[p.core, q], tok, x_rx0, x_ry1, x_ry0, x_rx1)
    final_a = PlaneGather(
        net, p, lambda: g_kept.at[z, p.chip].at[ax], lambda k, q: gsum_o.at[k, q].at[ax], ra
    )
    final_b = PlaneGather(
        net, p, lambda: g_kept.at[z, p.chip].at[bx], lambda k, q: gsum_o.at[k, q].at[bx], rb
    )
    w_final = PlaneGather(net, p, lambda: w_part.at[p.core, z], lambda k, q: w_all.at[k, q], half)
    cols = heads * head_dim

    def da_forward():
        for i, chip, dev in ((1, p.chip_x, p.xn), (2, p.chip_y, p.yn), (0, p.chip_d, p.dn)):
            block = lambda chip=chip: da_all.at[p.core, chip]
            net.recv(swaps[i], block, dev)
            net.send(swaps[4 + i], block, block, p.sib)

    def da_wait():
        for i, chip in ((3, p.chip), (5, p.chip_x), (6, p.chip_y), (4, p.chip_d)):
            net.recv(swaps[i], lambda chip=chip: da_all.at[p.other, chip], p.sib)
        own_da.wait()
        for cp in att_in:
            cp.wait()

    def block_grads(k, q):
        a = tab[2 * q + k]
        return jnp.concatenate([dcat[a], dcat[2 * n - 1 - a]], axis=0)

    def weight_grads():
        dw_acc[...] = jnp.zeros(dw_acc.shape, f32)

        def weights(c, _):
            k, q = lax.rem(c, 2), c // 2
            dw_acc[...] += mm(xall[k, q].reshape(tok, width), block_grads(k, q), TN)
            return 0

        lax.fori_loop(0, n, weights, 0)
        for o in range(nz):
            w_part[0, o] = dw_acc[o * d : o * d + half].astype(bf16)
            w_part[1, o] = dw_acc[o * d + half : (o + 1) * d].astype(bf16)
        net.send(w_id, w_part.at[p.other], w_sib, p.sib)

    def weight_sum():
        net.recv(w_id, w_sib, p.sib)
        for o in range(nz):
            add_into(w_part.at[p.core, o], w_sib.at[o], half)

    def tokens_of(k):
        def one(q, _):
            w = wqkv[...].reshape(-1, 3 * LANES)
            x_part[k, q] = mm(block_grads(k, q), w, NT).astype(bf16)
            return 0

        lax.fori_loop(0, n // 2, one, 0)

    def tokens_other():
        tokens_of(p.other)
        net.send(x_id, x_part.at[p.other], x_sib, p.sib)

    def tokens_sum():
        net.recv(x_id, x_sib, p.sib)
        for q in range(n // 2):
            add_into(x_part.at[p.core, q], x_sib.at[q], tok)

    def tokens_out():
        def add_tokens(i, _):
            at = pl.ds(pl.multiple_of(i * 32, 32), 32)
            dtok_o[at, :] = (dh_ref[at, :] + x_part[p.core, p.chip, at, :].astype(f32)).astype(bf16)
            return 0

        lax.fori_loop(0, tok // 32, add_tokens, 0)

    def own_w():
        return pltpu.make_async_copy(
            w_part.at[p.core, z], w_all.at[p.core, p.chip], lsem.at[31]
        )

    def w_final_first():
        w_final.first()
        own_w().start()

    def w_out():
        own_w().wait()
        for j in range(3):
            for k in range(2):
                dw_o[j, k * half : (k + 1) * half, :] = jnp.concatenate(
                    [w_all[k, q][:, j * LANES : j * LANES + cols] for q in range(4)], axis=1
                )

    steps = {
        "dr": da_forward, "dw": da_wait, "DW": weight_grads, "wa": weight_sum,
        "DXo": tokens_other, "DXm": lambda: tokens_of(p.core), "xa": tokens_sum, "tok": tokens_out,
        "dwo": w_out, "wff": w_final_first,
    }
    for k, o in enumerate(order):
        steps[f"s{k}"] = functools.partial(to_sib, o)
        steps[f"c{k}"] = functools.partial(chip_sum, o)
        steps[f"p{k}f"], steps[f"p{k}s"] = plane[o].first, plane[o].second
        steps[f"p{k}t"] = plane[o].third
    for name, line in (("la", line_a), ("lb", line_b), ("wl", w_line)):
        for t in range(nz):
            steps[f"{name}{t}"] = functools.partial(line.step, t)
    for name, thing in (("pb", plane_b), ("xs", xs), ("fa", final_a), ("fb", final_b), ("wf", w_final)):
        for stage in ("first", "second", "third", "last"):
            if hasattr(thing, stage):
                steps.setdefault(name + stage[0], getattr(thing, stage))
    units = n // 2
    todo, before, behind, unit = {}, [], [], -1
    for name in BACKWARD_ORDER:
        if name[0] == "U":
            unit = int(name[1:])
        elif unit < 0:
            before.append(steps[name])
        elif unit == units * heads - 1:
            behind.append(steps[name])
        else:
            todo.setdefault(unit, []).append(steps[name])
    for step in before:
        step()

    def head(h, _):
        dk_ref[...] = jnp.zeros(dk_ref.shape, f32)
        dv_ref[...] = jnp.zeros(dv_ref.shape, f32)
        for i in range(units):
            attend_back_unit(
                fold, p.core, h, i, head_dim, tab, q_ref, k_ref, v_ref, on_ref, lse_ref, da_all,
                dcat, dk_ref, dv_ref,
            )
            for hh in range(heads):
                if hh * units + i in todo:
                    pl.when(h == hh)(chain(*((step,) for step in todo[hh * units + i])))
        place_key_grads(fold, p.core, tab[2 * n + h], dk_ref, dv_ref, dcat)
        return 0

    lax.fori_loop(0, heads, head, 0)
    for step in behind:
        step()
    own_sum = fetch(g_kept.at[z, p.chip], gsum_o.at[p.core, p.chip])
    own_sum.wait()
    net.finish()


def line_order(nz):
    order = []
    for i in range((nz + 1) // 2):
        for o in (nz - 1 - i, i):
            if o not in order:
                order.append(o)
    return order


def backward(
    nz, n, heads, head_dim, rb, pairs, pairing, grads, da, dh, xall, wqkv, q, k, v, on, lse
):
    rows, width = grads.shape[3], grads.shape[4]
    seg = xall.shape[3]
    tok = 2 * seg
    d_rows = wqkv.shape[1]
    half = d_rows // 2
    ra = rows - rb
    n_sem = 6 * (nz + 2) + 6 * nz + nz + 9 + 33 + 2
    sds = jax.ShapeDtypeStruct
    vm = lambda *shape: pltpu.VMEM(shape, bf16)
    wide, tiled = (2 * n, seg, LANES), (tok * n // KT, KT, LANES)
    da = da.reshape(4, 2, seg, LANES)
    return pl.pallas_call(
        functools.partial(backward_kernel, nz, n, heads, head_dim, rb, n_sem),
        out_shape=(
            sds(grads.shape[1:], bf16),
            sds((tok, width), bf16),
            sds((3, d_rows, width), bf16),
        ),
        in_specs=smem(2) + hbm(2) + vmem(1) + hbm(6) + vmem(1),
        out_specs=tuple(hbm(1) + vmem(2)),
        scratch_shapes=[
            pltpu.SMEM((2 * n + heads,), jnp.int32),
            vm(nz, 4, rows, width),
            vm(nz, 4, rows, width),
            vm(nz, 2, ra // 2, width),
            vm(nz, 2, ra // 2, width),
            vm(nz, ra // 2, width),
            vm(nz, ra // 2, width),
            vm(nz, ra, width),
            vm(nz, ra, width),
            vm(nz, 4, rb, width),
            vm(nz, 4, rb, width),
            vm(2, rb // 2, width),
            vm(2, rb // 2, width),
            vm(rb // 2, width),
            vm(rb // 2, width),
            vm(2, 4, tok, width),
            vm(4, tok, width),
            vm(2, tok // 2, width),
            vm(2, tok // 2, width),
            vm(tok // 2, width),
            vm(tok // 2, width),
            vm(2, nz, half, width),
            vm(nz, half, width),
            vm(nz, half, width),
            vm(nz, half, width),
            vm(2, 4, half, width),
            vm(2, 4, 2, seg, LANES),
            vm(2, 4, 2, seg, width),
            vm(nz, d_rows, width),
            vm(*wide),
            vm(*tiled),
            vm(*tiled),
            vm(*wide),
            vm(2 * n, seg, 3 * LANES),
            pltpu.VMEM((seg * n, LANES), f32),
            pltpu.VMEM((seg * n, LANES), f32),
            pltpu.VMEM((width, 3 * LANES), f32),
            pltpu.SemaphoreType.DMA((n_sem,)),
            pltpu.SemaphoreType.DMA((n_sem,)),
            pltpu.SemaphoreType.DMA((32,)),
        ],
        compiler_params=comm_params(1),
        name="backward",
    )(pairs, pairing, grads, da, dh, xall, wqkv, q, k, v, on, lse)


def fast_body(
    tokens,
    w_query,
    w_key,
    w_value,
    w_output,
    w_inner,
    w_outer,
    ln_gain,
    ln_bias,
    pairing,
    block_pairs,
    cotangent,
):
    tok, width = tokens.shape[1], tokens.shape[2]
    n_ctx, nz = lax.axis_size("ctx"), lax.axis_size("fsdp")
    z = lax.axis_index("fsdp")
    heads = pairing.shape[1]
    my_heads, head_dim = heads // 4, width // heads
    d_rows = w_query.shape[0]
    f_rows, ff = w_outer.shape[0], w_inner.shape[1]
    n_f = ff // width
    o1, o2, used = f_rows, f_rows + n_f * d_rows, f_rows + n_f * d_rows + d_rows
    total = -(-(used + 4) // 256) * 256
    norms = jnp.concatenate([ln_gain.T, ln_bias.T], axis=0).astype(bf16)
    norms = lax.dynamic_update_slice(jnp.zeros((16, width), bf16), norms, (0, z * d_rows))
    weights = (w_query, w_key, w_value, w_output, w_inner, w_outer)
    xall, wqkv, q, k, v, on, grads, lse, result, da, d_h1 = front(
        nz, n_ctx, my_heads, head_dim, total, block_pairs, pairing, tokens[0], cotangent[0],
        norms, weights,
    )
    grads = grads.reshape(nz, 2, 4, total // 8, width)
    gsum, dtok, dw = backward(
        nz, n_ctx, my_heads, head_dim, 64, block_pairs, pairing, grads, da, d_h1,
        xall, wqkv, q, k, v, on, lse,
    )
    gsum = gsum.reshape(total, width)
    g_inner = [gsum[o1 + i * d_rows : o1 + (i + 1) * d_rows] for i in range(n_f)]
    g_norms = lax.dynamic_slice(gsum[used : used + 4], (0, z * d_rows), (4, d_rows)).astype(f32)
    return (
        result[None],
        dtok[None],
        dw[0].astype(f32),
        dw[1].astype(f32),
        dw[2].astype(f32),
        gsum[o2:used].astype(f32),
        jnp.concatenate(g_inner, axis=1).astype(f32),
        gsum[:o1].astype(f32),
        g_norms[:2].T,
        g_norms[2:].T,
    )


def solution(mesh):
    in_specs = (
        P("fsdp", "ctx", None),
        P("fsdp", None),
        P("fsdp", None),
        P("fsdp", None),
        P("fsdp", None),
        P("fsdp", None),
        P("fsdp", None),
        P("fsdp", None),
        P("fsdp", None),
        P("fsdp", None),
        P("fsdp", None),
        P("fsdp", "ctx", None),
    )
    out_specs = (
        P("fsdp", "ctx", None),
        P("fsdp", "ctx", None),
        P("fsdp", None),
        P("fsdp", None),
        P("fsdp", None),
        P("fsdp", None),
        P("fsdp", None),
        P("fsdp", None),
        P("fsdp", None),
        P("fsdp", None),
    )
    fast = mesh.shape["ctx"] == 8 and mesh.shape["fsdp"] == 4
    chosen = fast_body if fast else generic_body
    return jax.shard_map(chosen, mesh=mesh, in_specs=in_specs, out_specs=out_specs, check_vma=False)
```

```python
import functools

import jax
import jax.numpy as jnp
from jax import lax
from jax.experimental import pallas as pl
from jax.experimental.pallas import tpu as pltpu
from jax.sharding import PartitionSpec as P

norm_eps = 1e-05
score_scale = 0.125
very_low = -1e30


def shortened(value):

    def short(part):
        return part.astype(jnp.bfloat16) if part.dtype == jnp.float32 else part

    return jax.tree.map(short, value)


def layer_norm(values, norm_gain, norm_shift):
    center = values - jnp.mean(values, axis=-1, keepdims=True)
    spread = jnp.mean(center * center, axis=-1, keepdims=True)
    return center * lax.rsqrt(spread + norm_eps) * norm_gain + norm_shift


def exact_gelu(values):
    return jax.nn.gelu(values, approximate=False)


def project(rows_in, weight):
    return jnp.dot(rows_in, weight, preferred_element_type=jnp.float32)


def seq_positions(pair_row, tok_dev, seq_len):
    segment_len = tok_dev // 2
    within = jnp.arange(tok_dev, dtype=jnp.int32)
    lower_pos = pair_row[:, None] * segment_len + within[None, :]
    upper_pos = seq_len - (pair_row[:, None] + 1) * segment_len + within[None, :] - segment_len
    return jnp.where(within[None, :] < segment_len, lower_pos, upper_pos).reshape(-1)


def pair_mask(query_pos, key_pos, head_flags, half_len):
    target = (query_pos[None, :] // half_len + head_flags[:, None]) % 2
    paired = key_pos[None, None, :] // half_len == target[:, :, None]
    causal = key_pos[None, :] <= query_pos[:, None]
    return jnp.logical_and(paired, causal[None, :, :])


def block_rows(tok_dev):
    return 2 * tok_dev


def over_blocks(running, arrays, step_fn, tok_dev):
    row_count = arrays[0].shape[0]
    block_len = block_rows(tok_dev)

    def one_step(inner_carry, step_index):
        first_row = step_index * block_len
        sliced = tuple(
            (lax.dynamic_slice_in_dim(member, first_row, block_len, 0) for member in arrays)
        )
        return (step_fn(inner_carry, sliced, first_row), None)

    return lax.scan(one_step, running, jnp.arange(row_count // block_len, dtype=jnp.int32))[0]


def generic_body(
    tokens,
    w_query,
    w_key,
    w_value,
    w_output,
    w_inner,
    w_outer,
    ln_gain,
    ln_bias,
    pairing,
    block_pairs,
    cotangent,
):
    tok_dev = tokens.shape[1]
    width = tokens.shape[2]
    heads = pairing.shape[1]
    head_dim = width // heads
    n_ctx = lax.axis_size("ctx")
    seq_len = tok_dev * n_ctx
    half_len = seq_len // 2
    pos_all = seq_positions(block_pairs[0], tok_dev, seq_len)
    my_pos = lax.dynamic_slice_in_dim(pos_all, lax.axis_index("ctx") * tok_dev, tok_dev, 0)
    head_flags = pairing[0]
    masters = (w_query, w_key, w_value, w_output, w_inner, w_outer, ln_gain, ln_bias)
    low_masters = tuple((member.astype(jnp.bfloat16) for member in masters))
    gathered = jax.tree.map(
        lambda part, own: part.astype(own.dtype),
        lax.all_gather(shortened(low_masters), "fsdp", axis=0, tiled=True),
        low_masters,
    )
    wq_full, wk_full, wv_full, wo_full, inner_full, outer_full, gain_full, shift_full = gathered
    gain_wide = gain_full.astype(jnp.float32)
    shift_wide = shift_full.astype(jnp.float32)
    x_in = tokens[0]
    query_b = project(x_in, wq_full).astype(jnp.bfloat16)
    key_b = project(x_in, wk_full).astype(jnp.bfloat16)
    value_b = project(x_in, wv_full).astype(jnp.bfloat16)
    q_heads = query_b.reshape(tok_dev, heads, head_dim)

    def attend_step(running, sliced, offset):
        run_max, run_sum, run_acc = running
        key_block, value_block = sliced
        block_len = key_block.shape[0]
        key_pos = lax.dynamic_slice_in_dim(pos_all, offset, block_len, 0)
        allowed = pair_mask(my_pos, key_pos, head_flags, half_len)
        key_heads = key_block.reshape(block_len, heads, head_dim)
        value_heads = value_block.reshape(block_len, heads, head_dim)
        scores = (
            jnp.einsum("qhd,khd->hqk", q_heads, key_heads, preferred_element_type=jnp.float32)
            * score_scale
        )
        new_max = jnp.maximum(run_max, jnp.max(jnp.where(allowed, scores, very_low), axis=2))
        prob_rows = jnp.where(
            allowed, jnp.exp(jnp.where(allowed, scores - new_max[:, :, None], 0.0)), 0.0
        )
        decay = jnp.exp(run_max - new_max)
        new_sum = run_sum * decay + jnp.sum(prob_rows, axis=2)
        added = jnp.einsum(
            "hqk,khd->hqd",
            prob_rows.astype(jnp.bfloat16),
            value_heads,
            preferred_element_type=jnp.float32,
        )
        return (new_max, new_sum, run_acc * decay[:, :, None] + added)

    def pair_fold(step_fn, running, fetched):
        return over_blocks(running, fetched, step_fn, tok_dev)

    start_state = (
        jnp.full((heads, tok_dev), very_low, jnp.float32),
        jnp.zeros((heads, tok_dev), jnp.float32),
        jnp.zeros((heads, tok_dev, head_dim), jnp.float32),
    )
    run_max, run_sum, run_acc = pair_fold(
        attend_step,
        start_state,
        (
            lax.all_gather(key_b, "ctx", axis=0, tiled=True),
            lax.all_gather(value_b, "ctx", axis=0, tiled=True),
        ),
    )
    live_rows = run_sum > 0
    safe_sum = jnp.where(live_rows, run_sum, 1.0)
    attn_heads = jnp.where(live_rows[:, :, None], run_acc / safe_sum[:, :, None], 0.0)
    lse_rows = jnp.where(live_rows, run_max + jnp.log(safe_sum), 0.0)
    attn_rows = attn_heads.transpose(1, 0, 2).reshape(tok_dev, width)
    attn_b = attn_rows.astype(jnp.bfloat16)
    branch = project(attn_b, wo_full)
    first_norm, first_pull = jax.vjp(
        layer_norm, x_in.astype(jnp.float32) + branch, gain_wide[:, 0], shift_wide[:, 0]
    )
    first_b = first_norm.astype(jnp.bfloat16)
    inner = project(first_b, inner_full)
    active, gelu_pull = jax.vjp(exact_gelu, inner)
    active_b = active.astype(jnp.bfloat16)
    outer = project(active_b, outer_full)
    result, second_pull = jax.vjp(layer_norm, first_norm + outer, gain_wide[:, 1], shift_wide[:, 1])
    wq_back, wk_back, wv_back, wo_back, inner_back, outer_back, gain_back, shift_back = gathered
    d_h2, d_gain2, d_shift2 = second_pull(cotangent[0].astype(jnp.float32))
    d_f_b = d_h2.astype(jnp.bfloat16)
    d_outer = jnp.dot(active_b.T, d_f_b, preferred_element_type=jnp.float32)
    d_active = jnp.dot(d_f_b, outer_back.T, preferred_element_type=jnp.float32)
    d_u_b = gelu_pull(d_active)[0].astype(jnp.bfloat16)
    d_inner = jnp.dot(first_b.T, d_u_b, preferred_element_type=jnp.float32)
    d_x1 = d_h2 + jnp.dot(d_u_b, inner_back.T, preferred_element_type=jnp.float32)
    d_h1, d_gain1, d_shift1 = first_pull(d_x1)
    d_y_b = d_h1.astype(jnp.bfloat16)
    d_wo = jnp.dot(attn_b.T, d_y_b, preferred_element_type=jnp.float32)
    d_attn_b = jnp.dot(d_y_b, wo_back.T, preferred_element_type=jnp.float32).astype(jnp.bfloat16)
    delta_rows = (
        (d_attn_b.astype(jnp.float32) * attn_rows).reshape(tok_dev, heads, head_dim).sum(axis=2).T
    )
    dout_heads = d_attn_b.reshape(tok_dev, heads, head_dim)

    def query_grad_step(dq_acc, sliced, offset):
        key_block, value_block = sliced
        block_len = key_block.shape[0]
        key_pos = lax.dynamic_slice_in_dim(pos_all, offset, block_len, 0)
        allowed = pair_mask(my_pos, key_pos, head_flags, half_len)
        key_heads = key_block.reshape(block_len, heads, head_dim)
        value_heads = value_block.reshape(block_len, heads, head_dim)
        scores = (
            jnp.einsum("qhd,khd->hqk", q_heads, key_heads, preferred_element_type=jnp.float32)
            * score_scale
        )
        prob_rows = jnp.where(
            allowed, jnp.exp(jnp.where(allowed, scores - lse_rows[:, :, None], 0.0)), 0.0
        )
        prob_grad = jnp.einsum(
            "qhd,khd->hqk", dout_heads, value_heads, preferred_element_type=jnp.float32
        )
        dscore = (prob_rows * (prob_grad - delta_rows[:, :, None]) * score_scale).astype(
            jnp.bfloat16
        )
        return dq_acc + jnp.einsum(
            "hqk,khd->qhd", dscore, key_heads, preferred_element_type=jnp.float32
        )

    dq_start = jnp.zeros((tok_dev, heads, head_dim), jnp.float32)
    dq_acc = pair_fold(
        query_grad_step,
        dq_start,
        (
            lax.all_gather(key_b, "ctx", axis=0, tiled=True),
            lax.all_gather(value_b, "ctx", axis=0, tiled=True),
        ),
    )
    dq_b = dq_acc.reshape(tok_dev, width).astype(jnp.bfloat16)
    lse_all, delta_all = (
        lax.all_gather(lse_rows, "ctx", axis=1, tiled=True),
        lax.all_gather(delta_rows, "ctx", axis=1, tiled=True),
    )
    k_heads = key_b.reshape(tok_dev, heads, head_dim)
    v_heads = value_b.reshape(tok_dev, heads, head_dim)

    def key_grad_step(running, sliced, offset):
        dk_acc, dv_acc = running
        query_block, dout_block = sliced
        block_len = query_block.shape[0]
        query_pos = lax.dynamic_slice_in_dim(pos_all, offset, block_len, 0)
        lse_block = lax.dynamic_slice_in_dim(lse_all, offset, block_len, 1)
        delta_block = lax.dynamic_slice_in_dim(delta_all, offset, block_len, 1)
        allowed = pair_mask(query_pos, my_pos, head_flags, half_len)
        query_heads = query_block.reshape(block_len, heads, head_dim)
        dout_block_heads = dout_block.reshape(block_len, heads, head_dim)
        scores = (
            jnp.einsum("qhd,khd->hqk", query_heads, k_heads, preferred_element_type=jnp.float32)
            * score_scale
        )
        prob_rows = jnp.where(
            allowed, jnp.exp(jnp.where(allowed, scores - lse_block[:, :, None], 0.0)), 0.0
        )
        dv_acc = dv_acc + jnp.einsum(
            "hqk,qhd->khd",
            prob_rows.astype(jnp.bfloat16),
            dout_block_heads,
            preferred_element_type=jnp.float32,
        )
        prob_grad = jnp.einsum(
            "qhd,khd->hqk", dout_block_heads, v_heads, preferred_element_type=jnp.float32
        )
        dscore = (prob_rows * (prob_grad - delta_block[:, :, None]) * score_scale).astype(
            jnp.bfloat16
        )
        dk_acc = dk_acc + jnp.einsum(
            "hqk,qhd->khd", dscore, query_heads, preferred_element_type=jnp.float32
        )
        return (dk_acc, dv_acc)

    kv_start = (
        jnp.zeros((tok_dev, heads, head_dim), jnp.float32),
        jnp.zeros((tok_dev, heads, head_dim), jnp.float32),
    )
    dk_acc, dv_acc = pair_fold(
        key_grad_step,
        kv_start,
        (
            lax.all_gather(query_b, "ctx", axis=0, tiled=True),
            lax.all_gather(d_attn_b, "ctx", axis=0, tiled=True),
        ),
    )
    dk_b = dk_acc.reshape(tok_dev, width).astype(jnp.bfloat16)
    dv_b = dv_acc.reshape(tok_dev, width).astype(jnp.bfloat16)
    d_input = d_h1 + jnp.dot(dq_b, wq_back.T, preferred_element_type=jnp.float32)
    d_input = d_input + jnp.dot(dk_b, wk_back.T, preferred_element_type=jnp.float32)
    d_input = d_input + jnp.dot(dv_b, wv_back.T, preferred_element_type=jnp.float32)
    terms = (
        jnp.dot(x_in.T, dq_b, preferred_element_type=jnp.float32),
        jnp.dot(x_in.T, dk_b, preferred_element_type=jnp.float32),
        jnp.dot(x_in.T, dv_b, preferred_element_type=jnp.float32),
        d_wo,
        d_inner,
        d_outer,
        jnp.stack([d_gain1, d_gain2], axis=1),
        jnp.stack([d_shift1, d_shift2], axis=1),
    )
    shares = (
        lax.psum_scatter(
            terms[0].astype(jnp.bfloat16), "fsdp", scatter_dimension=0, tiled=True
        ).astype(jnp.float32),
        lax.psum_scatter(
            terms[1].astype(jnp.bfloat16), "fsdp", scatter_dimension=0, tiled=True
        ).astype(jnp.float32),
        lax.psum_scatter(
            terms[2].astype(jnp.bfloat16), "fsdp", scatter_dimension=0, tiled=True
        ).astype(jnp.float32),
        lax.psum_scatter(
            terms[3].astype(jnp.bfloat16), "fsdp", scatter_dimension=0, tiled=True
        ).astype(jnp.float32),
        lax.psum_scatter(
            terms[4].astype(jnp.bfloat16), "fsdp", scatter_dimension=0, tiled=True
        ).astype(jnp.float32),
        lax.psum_scatter(
            terms[5].astype(jnp.bfloat16), "fsdp", scatter_dimension=0, tiled=True
        ).astype(jnp.float32),
        lax.psum_scatter(
            terms[6].astype(jnp.bfloat16), "fsdp", scatter_dimension=0, tiled=True
        ).astype(jnp.float32),
        lax.psum_scatter(
            terms[7].astype(jnp.bfloat16), "fsdp", scatter_dimension=0, tiled=True
        ).astype(jnp.float32),
    )
    totals = (
        lax.psum(shares[0].astype(jnp.bfloat16), "ctx").astype(jnp.float32),
        lax.psum(shares[1].astype(jnp.bfloat16), "ctx").astype(jnp.float32),
        lax.psum(shares[2].astype(jnp.bfloat16), "ctx").astype(jnp.float32),
        lax.psum(shares[3].astype(jnp.bfloat16), "ctx").astype(jnp.float32),
        lax.psum(shares[4].astype(jnp.bfloat16), "ctx").astype(jnp.float32),
        lax.psum(shares[5].astype(jnp.bfloat16), "ctx").astype(jnp.float32),
        lax.psum(shares[6].astype(jnp.bfloat16), "ctx").astype(jnp.float32),
        lax.psum(shares[7].astype(jnp.bfloat16), "ctx").astype(jnp.float32),
    )
    return (
        result.astype(jnp.bfloat16)[None],
        d_input.astype(jnp.bfloat16)[None],
        totals[0],
        totals[1],
        totals[2],
        totals[3],
        totals[4],
        totals[5],
        totals[6],
        totals[7],
    )


MESH = pl.DeviceIdType.MESH
f32 = jnp.float32
bf16 = jnp.bfloat16


class Place:
    def __init__(self):
        me = lax.axis_index("ctx")
        self.me = me
        self.z = lax.axis_index("fsdp")
        self.core = lax.rem(me, 2)
        self.chip = me // 2
        self.x = lax.rem(self.chip, 2)
        self.y = self.chip // 2
        self.chip_x = self.chip + 1 - 2 * self.x
        self.chip_y = self.chip + 2 - 4 * self.y
        self.chip_d = 3 - self.chip
        self.other = 1 - self.core
        self.sib = (2 * self.chip + 1 - self.core, self.z)
        self.xn = (2 * self.chip_x + self.core, self.z)
        self.yn = (2 * self.chip_y + self.core, self.z)
        self.dn = (2 * self.chip_d + self.core, self.z)
        self.up = (me, self.z + 1)
        self.down = (me, self.z - 1)


def greet(place, others, line_len=None):
    barrier = pltpu.get_barrier_semaphore()
    count = len(others)
    for other in others:
        pl.semaphore_signal(barrier, inc=1, device_id=other, device_id_type=MESH)
    if line_len is not None:

        @pl.when(place.z < line_len - 1)
        def _():
            pl.semaphore_signal(barrier, inc=1, device_id=place.up, device_id_type=MESH)

        @pl.when(place.z > 0)
        def _():
            pl.semaphore_signal(barrier, inc=1, device_id=place.down, device_id_type=MESH)

        count = count + jnp.where(place.z < line_len - 1, 1, 0) + jnp.where(place.z > 0, 1, 0)

    pl.semaphore_wait(barrier, count)


def maybe(cond, fn):
    if cond is None:
        fn()
    else:
        pl.when(cond)(fn)


def of(ref):
    return ref() if callable(ref) else ref


class Net:
    def __init__(self, send_sems, recv_sems, count):
        self.send_sems, self.recv_sems, self.count = send_sems, recv_sems, count
        self.used = 0
        self.open = []

    def new(self):
        self.used += 1
        assert self.used <= self.count
        return self.used - 1

    def copy(self, idx, src, dst, dev):
        return pltpu.make_async_remote_copy(
            src_ref=src,
            dst_ref=dst,
            send_sem=self.send_sems.at[idx],
            recv_sem=self.recv_sems.at[idx],
            device_id=dev,
            device_id_type=MESH,
        )

    def send(self, idx, src, dst, dev, cond=None):
        make = lambda: self.copy(idx, of(src), of(dst), dev)
        maybe(cond, lambda: make().start())
        self.open.append((cond, make))

    def recv(self, idx, dst, dev, cond=None):
        maybe(cond, lambda: self.copy(idx, of(dst), of(dst), dev).wait_recv())

    def finish(self):
        for cond, make in self.open:
            maybe(cond, lambda make=make: make().wait_send())
        self.open = []


class PlaneGather:
    def __init__(self, net, place, own, slot, rows, cond=None):
        p = place
        self.net, self.place, self.cond = net, place, cond
        self.own_of, self.slot = own, slot
        self.h0, self.h1 = pl.ds(0, rows // 2), pl.ds(rows // 2, rows // 2)
        self.ids = [net.new() for _ in range(11)]

    def at(self, core, chip, half=0):
        def view():
            ref = self.slot(core, chip)
            return ref if half == 0 else ref.at[self.h0 if half == 1 else self.h1]

        return view

    def mine(self, half=0):
        def view():
            ref = self.own_of()
            return ref if half == 0 else ref.at[self.h0 if half == 1 else self.h1]

        return view

    def first(self):
        n, p, i, c = self.net, self.place, self.ids, self.cond
        at = functools.partial(self.at, p.core, p.chip)
        n.send(i[0], self.mine(1), at(1), p.xn, c)
        n.send(i[1], self.mine(2), at(2), p.yn, c)
        n.send(i[2], self.mine(2), at(2), p.xn, c)
        n.send(i[3], self.mine(1), at(1), p.yn, c)
        n.send(i[4], self.mine(), at(), p.sib, c)

    def second(self):
        n, p, i, c = self.net, self.place, self.ids, self.cond
        bx = functools.partial(self.at, p.core, p.chip_x)
        by = functools.partial(self.at, p.core, p.chip_y)
        n.recv(i[0], bx(1), p.xn, c)
        n.send(i[5], bx(1), bx(1), p.yn, c)
        n.recv(i[1], by(2), p.yn, c)
        n.send(i[6], by(2), by(2), p.xn, c)
        n.recv(i[2], bx(2), p.xn, c)
        n.send(i[7], bx(), bx(), p.sib, c)
        n.recv(i[3], by(1), p.yn, c)
        n.send(i[8], by(), by(), p.sib, c)

    def third(self):
        n, p, i, c = self.net, self.place, self.ids, self.cond
        bd = functools.partial(self.at, p.core, p.chip_d)
        n.recv(i[5], bd(1), p.yn, c)
        n.send(i[9], bd(1), bd(1), p.sib, c)
        n.recv(i[6], bd(2), p.xn, c)
        n.send(i[10], bd(2), bd(2), p.sib, c)

    def last(self):
        n, p, i, c = self.net, self.place, self.ids, self.cond
        for idx, q in ((4, p.chip), (7, p.chip_x), (8, p.chip_y)):
            n.recv(i[idx], self.at(p.other, q), p.sib, c)
        n.recv(i[9], self.at(p.other, p.chip_d, 1), p.sib, c)
        n.recv(i[10], self.at(p.other, p.chip_d, 2), p.sib, c)


def hbm(count):
    return [pl.BlockSpec(memory_space=pltpu.HBM)] * count


def comm_params(collective_id):
    return pltpu.CompilerParams(
        collective_id=collective_id, has_side_effects=True, vmem_limit_bytes=56 << 20
    )


def vmem(count):
    return [pl.BlockSpec(memory_space=pltpu.VMEM)] * count


def smem(count):
    return [pl.BlockSpec(memory_space=pltpu.SMEM)] * count


LANES = 256
KT = 128
NT = (((1,), (1,)), ((), ()))
TN = (((0,), (0,)), ((), ()))
NN = (((1,), (0,)), ((), ()))


def mm(a, b, dims=NN):
    return lax.dot_general(a, b, dims, preferred_element_type=f32)


def head_mask(h, head_dim, dtype):
    lane = lax.broadcasted_iota(jnp.int32, (1, LANES), 1)
    inside = jnp.logical_and(lane >= h * head_dim, lane < (h + 1) * head_dim)
    return jnp.where(inside, 1.0, 0.0).astype(dtype)


class Fold:
    def __init__(self, n, seg):
        self.n, self.seg, self.half = n, seg, n * seg
        self.tiles = self.half // KT

    def ranges(self, i):
        a = -(-(self.n - i) * self.seg // KT)
        b = -(-(i + 1) * self.seg // KT)
        assert a + b == self.tiles + 2
        return a, b

    def places(self, i, core, paired):
        a, b = self.ranges(i)
        n, seg = self.n, self.seg
        causal = 1 - paired
        up = n + core * (n // 2) + i
        rows_a = (core * n + n - 1 - i) * causal + up * paired
        rows_b = (core * n + i) * causal + up * paired
        keys_a = core * self.tiles * causal
        keys_b = core * self.tiles * causal + a * paired
        lim_a = (n - 1 - i) * seg - (a - 2) * KT + (1 << 20) * paired
        lim_b = i * seg - (b - 2) * KT - (1 << 20) * paired
        return (rows_a, keys_a, lim_a, a), (rows_b, keys_b, lim_b, b)


def natural(tab, n, s):
    upper = lax.div(s, n)
    c = tab[n + s + upper * (2 * n - 1 - 2 * s)]
    return lax.rem(c, 2), lax.div(c, 2), upper


def key_tiles(ref, base, first, count):
    return ref[pl.ds(base + first, count)].reshape(count * KT, LANES)


def tail_mask(seg, limit):
    col = lax.broadcasted_iota(jnp.int32, (seg, 2 * KT), 1)
    row = lax.broadcasted_iota(jnp.int32, (seg, 2 * KT), 0)
    return col - row <= limit


def norm_forward(h, gain, shift):
    mean = jnp.mean(h, axis=1, keepdims=True)
    center = h - mean
    scale = lax.rsqrt(jnp.mean(center * center, axis=1, keepdims=True) + norm_eps)
    n = center * scale
    return n, scale, n * gain + shift


def norm_backward(cot, n, scale, gain):
    dn = cot * gain
    mean = jnp.mean(dn, axis=1, keepdims=True)
    along = jnp.mean(dn * n, axis=1, keepdims=True)
    return scale * (dn - mean - n * along)


def chain(*steps):
    def run():
        for fn, *args in steps:
            fn(*args)

    return run


def by_unit(order, steps, last):
    before, todo, behind, unit = [], {}, [], -1
    for name in order:
        if name[0] == "U":
            unit = int(name[1:])
        elif unit < 0:
            before.append(steps[name])
        elif unit == last:
            behind.append(steps[name])
        else:
            todo.setdefault(unit, []).append(steps[name])
    return before, todo, behind


def fill_table(tab, pairs, pairing, chip, n, heads):
    for c in range(n):
        tab[c] = pairs[0, c]
    for a in range(n):
        found = jnp.int32(0)
        for c in range(n):
            found = found + (pairs[0, c] == a).astype(jnp.int32) * c
        tab[n + a] = jnp.minimum(found, n - 1)
    for h in range(heads):
        tab[2 * n + h] = pairing[0, chip * heads + h]


def lse_lane(fold, h, i, g):
    return (h * (fold.n // 2) + i) * 2 + g


def attend_unit(fold, core, h, i, head_dim, tab, q_ref, k_ref, v_ref, o_ref, lse_ref):
    n, seg = fold.n, fold.seg
    paired = tab[2 * n + h]
    pf = paired.astype(f32)
    lanes = head_mask(h, head_dim, f32)
    lanes16 = head_mask(h, head_dim, bf16)
    parts = []
    for rows, keys, limit, count in fold.places(i, core, paired):
        q = q_ref[rows] * lanes16
        tail = mm(q, key_tiles(k_ref, keys, count - 2, 2), NT)
        tail = jnp.where(tail_mask(seg, limit), tail, very_low)
        top = jnp.max(tail, axis=1, keepdims=True)
        main = None
        if count > 2:
            main = mm(q, key_tiles(k_ref, keys, 0, count - 2), NT)
            top = jnp.maximum(top, jnp.max(main, axis=1, keepdims=True))
        parts.append((keys, count, main, tail, top))
    both = jnp.maximum(parts[0][4], parts[1][4])
    joined = jnp.broadcast_to(paired, both.shape) == 1
    outs = []
    for keys, count, main, tail, top in parts:
        top = jnp.where(joined, both, top)
        e = jnp.exp(tail - top)
        total = jnp.sum(e, axis=1, keepdims=True)
        acc = mm(e.astype(bf16), key_tiles(v_ref, keys, count - 2, 2))
        if main is not None:
            e = jnp.exp(main - top)
            total += jnp.sum(e, axis=1, keepdims=True)
            acc += mm(e.astype(bf16), key_tiles(v_ref, keys, 0, count - 2))
        outs.append((top, total, acc))
    (top_a, sum_a, acc_a), (top_b, sum_b, acc_b) = outs
    sum_a, sum_b = sum_a + pf * sum_b, jnp.where(joined, sum_a + sum_b, sum_b)
    acc_a = acc_a + pf * acc_b
    out_a = acc_a * (lanes / sum_a)
    out_b = acc_b * (lanes / sum_b)
    lane = lax.broadcasted_iota(jnp.int32, (1, KT), 1)
    lse = jnp.where(lane == lse_lane(fold, h, i, 0), top_a + jnp.log(sum_a), lse_ref[...])
    lse_ref[...] = jnp.where(lane == lse_lane(fold, h, i, 1), top_b + jnp.log(sum_b), lse)
    far, near, up = core * n + n - 1 - i, core * n + i, n + core * (n // 2) + i
    for at, value in ((far, (1.0 - pf) * out_a), (near, (1.0 - pf) * out_b), (up, pf * out_a)):
        o_ref[at] += value.astype(bf16)


FRONT_ORDER = (
    "ca", "se1", "se2", "cb", "xs", "ba", "cc", "bb", "xt", "se3", "aa1", "xl", "bc", "sw",
    "ab1", "F", "U0", "aa2", "U1", "U2", "U3", "gs1", "ab2", "U4", "aa3", "cs1", "U5", "U6",
    "U7", "ab3", "U8", "bd", "U9", "hs1", "gs2", "U10", "gs3", "U11", "hs2", "hs3", "cs2", "OC",
    "OP", "bs1", "ht1", "cs3", "gt2", "bs2", "gt3", "ht3", "gt1", "ht2", "hl", "gl", "ow", "cw",
    "M1", "bs3", "V1", "bw", "V2",
)


def front_kernel(
    nz, n, heads, head_dim, n_sem,
    pairs, pairing, x_ref, cot_ref, ln_ref, wq_i, wk_i, wv_i, wo_i, w1_i, w2_i,
    xall_o, wqkv_o, q_o, k_o, v_o, on_o, g_o, lse_o, out_o, da_o, dh_o,
    tab, xall, wqkv, q_ref, k_ref, v_ref, o_nat, o_ctx, o_part, o_sum, attn,
    w1, w2, wol, fq, fo, f1, f2, u_ref, z_ref, x1b_ref, acc_ref, n1_ref, r1_ref, dx1_ref, gs, gt,
    ssem, rsem, lsem, fsem, gsem,
):
    p = Place()
    z = p.z
    seg, width = x_ref.shape[1], x_ref.shape[2]
    tok = 2 * seg
    fold = Fold(n, seg)
    d_rows, f_rows = wq_i.shape[0], w2_i.shape[0]
    n_f = w1_i.shape[1] // width
    cols = heads * head_dim
    half = d_rows // 2
    a1_rows, a2_rows = n_f * d_rows // 8, f_rows // 12
    b_first = 8 * a2_rows
    b_rows = (f_rows - b_first) // 2
    locals_ = []

    def keep(src, dst):
        cp = pltpu.make_async_copy(src, dst, lsem.at[len(locals_)])
        cp.start()
        locals_.append(cp)
        return cp

    masters = [
        pltpu.make_async_copy(src, dst, fsem.at[i])
        for i, (src, dst) in enumerate(
            ((wq_i, fq.at[0]), (wk_i, fq.at[1]), (wv_i, fq.at[2]), (w1_i, f1), (w2_i, f2), (wo_i, fo))
        )
    ]
    for cp in masters:
        cp.start()
    own_x = keep(x_ref, xall.at[p.core, p.chip])
    greet(p, (p.sib, p.xn, p.yn, p.dn), nz)
    net = Net(ssem, rsem, n_sem)
    tokens_ag = PlaneGather(net, p, lambda: x_ref, lambda k, q: xall.at[k, q], 2)
    tokens_ag.first()
    can_up, can_down = z < nz - 1, z > 0
    rows = pl.ds(p.core * half, half)
    other = pl.ds(p.other * half, half)

    class Stream:
        def __init__(self, at, after):
            self.up = [net.new() for _ in range(nz)]
            self.down = [net.new() for _ in range(nz)]
            self.at, self.todo = at, {}
            for t in range(1, nz):
                self.todo[t] = []
                for ids, src, frm, to, got, more in (
                    (self.up, z - t, p.down, p.up, z >= t, can_up),
                    (self.down, z + t, p.up, p.down, z + t < nz, can_down),
                ):
                    src = jnp.clip(src, 0, nz - 1)
                    on = jnp.logical_and(got, more)
                    self.todo[t].append((ids, src, frm, to, got, on, after(t, src, at, got)))

        def begin(self):
            own = lambda: self.at(z)
            net.send(self.up[1], own, own, p.up, can_up)
            net.send(self.down[1], own, own, p.down, can_down)

        def step(self, t):
            for ids, src, frm, to, got, on, then in self.todo[t]:
                block = functools.partial(self.at, src)
                net.recv(ids[t], block, frm, got)
                if t + 1 < nz:
                    net.send(ids[t + 1], block, block, to, on)
                then()

    def share(waits, block_of):
        def after(t, src, at, got):
            idx = net.new()
            waits.append((idx, lambda: block_of(src), got))
            return lambda: net.send(idx, lambda: at(src), lambda: at(src), p.sib, got)

        return after

    def spread(gathers, slot_of, count):
        def after(t, src, at, got):
            slot = lambda k, q: slot_of(src, k, q)
            gather = PlaneGather(net, p, lambda: at(src), slot, count, got)
            gathers.setdefault(t, []).append(gather)
            return gather.first

        return after

    def a1_slot(o, k, q):
        start = pl.multiple_of(o * d_rows + lax.rem(q, 2) * a1_rows, 32)
        return w1.at[k * 2 + lax.div(q, 2), pl.ds(start, a1_rows)]

    def a2_slot(o, k, q):
        return w2.at[o, pl.ds(pl.multiple_of((k * 4 + q) * a2_rows, 32), a2_rows)]

    def b_slot(o, k):
        return w2.at[o, pl.ds(pl.multiple_of(b_first + k * b_rows, 32), b_rows)]

    sel_waits, b_waits, c_waits, a1_gathers, a2_gathers = [], [], [], {}, {}
    sel = Stream(lambda o: wqkv.at[o, rows], share(sel_waits, lambda o: wqkv.at[o, other]))
    cs = Stream(lambda o: wol.at[o, p.core], share(c_waits, lambda o: wol.at[o, p.other]))
    a1 = Stream(lambda o: a1_slot(o, p.core, p.chip), spread(a1_gathers, a1_slot, a1_rows))
    a2 = Stream(lambda o: a2_slot(o, p.core, p.chip), spread(a2_gathers, a2_slot, a2_rows))
    bs = Stream(lambda o: b_slot(o, p.core), share(b_waits, lambda o: b_slot(o, p.other)))

    for cp in masters[:3]:
        cp.wait()
    for chip in range(4):

        @pl.when(p.chip == chip)
        def _():
            for m in range(3):
                mine = fq[m, :, chip * cols : (chip + 1) * cols].astype(bf16)
                wqkv[z, :, m * LANES : m * LANES + cols] = mine

    for m in range(3):
        wqkv[z, :, m * LANES + cols : (m + 1) * LANES] = jnp.zeros((d_rows, LANES - cols), bf16)
    sel.begin()
    fill_table(tab, pairs, pairing, p.chip, n, heads)
    o_nat[...] = jnp.zeros(o_nat.shape, bf16)
    lse_o[...] = jnp.zeros(lse_o.shape, f32)
    part, swaps = net.new(), [net.new() for _ in range(3)]
    partners = ((p.chip_d, p.dn), (p.chip_x, p.xn), (p.chip_y, p.yn))

    def cast_inner():
        masters[3].wait()
        for f in range(n_f):
            at = pl.ds(pl.multiple_of(z * d_rows, 32), d_rows)
            w1[f, at, :] = f1[:, f * width : (f + 1) * width].astype(bf16)

    def cast_outer():
        masters[4].wait()

        def cast(i, _):
            at = pl.ds(pl.multiple_of(i * 64, 64), 64)
            w2[z, at, :] = f2[at, :].astype(bf16)
            return 0

        lax.fori_loop(0, f_rows // 64, cast, 0)

    def cast_output():
        masters[5].wait()
        for k in range(2):
            wol[z, k, :half, :] = fo[k * half : (k + 1) * half, :].astype(bf16)
            wol[z, k, half:, :] = ln_ref[...]

    def tokens_last():
        own_x.wait()
        tokens_ag.last()

    def wait_all(waits):
        for idx, block, got in waits:
            net.recv(idx, block, p.sib, got)

    def project_all():
        keep(xall, xall_o)
        keep(wqkv, wqkv_o)

        def four(i, _):
            tokens = jnp.concatenate([xall[natural(tab, n, 4 * i + u)] for u in range(4)], axis=0)
            qkv = mm(tokens, wqkv[...].reshape(-1, 3 * LANES))
            q = (qkv[:, :LANES].astype(bf16).astype(f32) * score_scale).astype(bf16)
            q_ref[pl.ds(4 * i, 4)] = q.reshape(4, seg, LANES)
            at = pl.ds(i * (4 * seg // KT), 4 * seg // KT)
            k_ref[at] = qkv[:, LANES : 2 * LANES].astype(bf16).reshape(-1, KT, LANES)
            v_ref[at] = qkv[:, 2 * LANES :].astype(bf16).reshape(-1, KT, LANES)
            return 0

        lax.fori_loop(0, n // 2, four, 0)
        for src, dst in ((q_ref, q_o), (k_ref, k_o), (v_ref, v_o)):
            keep(src, dst)

    def heads_out():
        keep(o_nat, on_o)
        for core_is in range(2):
            for q in range(n // 2):
                a = tab[2 * q + core_is]
                for u, s in ((0, a), (1, 2 * n - 1 - a)):
                    o_ctx[core_is, q, u * seg : (u + 1) * seg, :] = o_nat[s]
        net.send(part, o_ctx.at[p.other], o_part, p.sib)

    def owners_out():
        net.recv(part, o_part, p.sib)
        for idx, (chip, dev) in zip(swaps, partners):
            o_sum[chip] = o_ctx[p.core, chip] + o_part[chip]
            net.send(idx, o_sum.at[chip], attn.at[p.chip], dev)
        attn[p.chip] = o_ctx[p.core, p.chip] + o_part[p.chip]

    def owners_wait():
        for idx, (chip, dev) in zip(swaps, partners):
            net.recv(idx, attn.at[chip], dev)

    wo_of = lambda o: jnp.concatenate([wol[o, 0, :half, :], wol[o, 1, :half, :]], axis=0)
    kept = {}

    def first_norm():
        vec = wol[0, 0, half:, :].astype(f32)
        for o in range(1, nz):
            vec = vec + wol[o, 0, half:, :].astype(f32)
        h1 = x_ref[...].reshape(tok, width).astype(f32)
        for o in range(nz):
            h1 = h1 + mm(attn[o, :, :cols], wo_of(o))
        n1, r1, x1 = norm_forward(h1, vec[0:1], vec[2:3])
        n1_ref[...] = n1
        r1_ref[...] = jnp.broadcast_to(r1, (tok, 128))
        x1b_ref[...] = x1.astype(bf16)
        acc_ref[...] = x1
        kept["vec"] = vec

    def inner_all():
        def up(f, _):
            u = mm(x1b_ref[...], w1[f])
            cdf = 0.5 + 0.5 * lax.erf(u * (0.5**0.5))
            z_ref[f] = (u * cdf).astype(bf16)
            u_ref[f] = cdf + u * jnp.exp(-0.5 * u * u) * 0.3989422804014327
            return 0

        lax.fori_loop(0, n_f, up, 0)

    def outer_all():
        def add(f, _):
            acc_ref[...] += mm(z_ref[f], w2[f])
            return 0

        lax.fori_loop(0, n_f, add, 0)

    def each(gathers, t, stage):
        for gather in gathers[t]:
            getattr(gather, stage)()

    def all_last(gathers):
        for t in gathers:
            each(gathers, t, "last")

    steps = {
        "ca": cast_inner, "cb": cast_outer, "cc": cast_output, "ba": a1.begin, "bb": a2.begin,
        "bc": cs.begin, "bd": bs.begin, "xs": tokens_ag.second, "xt": tokens_ag.third,
        "xl": tokens_last, "sw": lambda: wait_all(sel_waits), "cw": lambda: wait_all(c_waits),
        "bw": lambda: wait_all(b_waits), "F": project_all, "OC": heads_out, "OP": owners_out,
        "ow": owners_wait, "M1": first_norm, "V1": inner_all, "V2": outer_all,
        "gl": lambda: all_last(a1_gathers), "hl": lambda: all_last(a2_gathers),
    }
    for t in range(1, nz):
        for name, stream in (("se", sel), ("cs", cs), ("aa", a1), ("ab", a2), ("bs", bs)):
            steps[f"{name}{t}"] = functools.partial(stream.step, t)
        for name, gathers in (("g", a1_gathers), ("h", a2_gathers)):
            steps[f"{name}s{t}"] = functools.partial(each, gathers, t, "second")
            steps[f"{name}t{t}"] = functools.partial(each, gathers, t, "third")
    units = n // 2
    before, todo, behind = by_unit(FRONT_ORDER, steps, units * heads - 1)
    for step in before:
        step()

    def head(h, _):
        for i in range(units):
            attend_unit(fold, p.core, h, i, head_dim, tab, q_ref, k_ref, v_ref, o_nat, lse_o)
            for hh in range(heads):
                if hh * units + i in todo:
                    pl.when(h == hh)(chain(*((step,) for step in todo[hh * units + i])))
        return 0

    lax.fori_loop(0, heads, head, 0)
    for step in behind:
        step()
    vec = kept["vec"]
    gain1, gain2, shift2 = vec[0:1], vec[1:2], vec[3:4]
    n2, r2, out = norm_forward(acc_ref[...], gain2, shift2)
    out_o[...] = out.astype(bf16)
    cot = cot_ref[...].astype(f32)
    d_gain2 = jnp.sum(cot * n2, axis=0, keepdims=True)
    d_shift2 = jnp.sum(cot, axis=0, keepdims=True)
    dh2 = norm_backward(cot, n2, r2, gain2)
    dx1_ref[...] = dh2
    df = dh2.astype(bf16)
    first1, first2 = f_rows, f_rows + n_f * d_rows

    def grads_out(f, slot):
        yield pltpu.make_async_copy(gs.at[slot, 0], g_o.at[f, pl.ds(0, f_rows)], gsem.at[slot, 0])
        for o in range(nz):
            at = pl.ds(pl.multiple_of(first1 + f * d_rows, 32), d_rows)
            src = gs.at[slot, 1, pl.ds(o * d_rows, d_rows)]
            yield pltpu.make_async_copy(src, g_o.at[o, at], gsem.at[slot, 1 + o])

    def back(f, _):
        slot = lax.rem(f, 2)

        @pl.when(f >= 2)
        def _():
            for cp in grads_out(f - 2, slot):
                cp.wait()

        gs[slot, 0] = mm(z_ref[f], df, TN).astype(bf16)
        du = (mm(df, w2[f], NT) * u_ref[f]).astype(bf16)
        gs[slot, 1] = mm(x1b_ref[...], du, TN).astype(bf16)
        for cp in grads_out(f, slot):
            cp.start()
        dx1_ref[...] += mm(du, w1[f], NT)
        return 0

    lax.fori_loop(0, n_f, back, 0)
    d_x1 = dx1_ref[...]
    n1 = n1_ref[...]
    d_gain1 = jnp.sum(d_x1 * n1, axis=0, keepdims=True)
    d_shift1 = jnp.sum(d_x1, axis=0, keepdims=True)
    dh1 = norm_backward(d_x1, n1, r1_ref[:, :1], gain1)
    dh_o[...] = dh1
    dy = dh1.astype(bf16)
    norms = jnp.concatenate([d_gain1, d_gain2, d_shift1, d_shift2], axis=0).astype(bf16)
    ends = []
    for o in range(nz):
        da_o[o, :, :cols] = mm(dy, wo_of(o), NT).astype(bf16)
        da_o[o, :, cols:] = jnp.zeros((tok, LANES - cols), bf16)
        gt[o, :d_rows, :] = mm(attn[o, :, :cols], dy, TN).astype(bf16)
        gt[o, d_rows:, :] = jnp.zeros((gt.shape[1] - d_rows, width), bf16)
        gt[o, d_rows : d_rows + 4, :] = norms
        ends.append(pltpu.make_async_copy(gt.at[o], g_o.at[o, pl.ds(first2, gt.shape[1])], fsem.at[o]))
        ends[-1].start()
    for f in range(max(n_f - 2, 0), n_f):
        for cp in grads_out(f, f % 2):
            cp.wait()
    for cp in ends:
        cp.wait()
    net.finish()
    for cp in locals_[1:]:
        cp.wait()


def front(nz, n, heads, head_dim, total, pairs, pairing, x_in, cot, norms, weights):
    tok, width = x_in.shape
    seg = tok // 2
    d_rows, f_rows = weights[0].shape[0], weights[5].shape[0]
    n_f = weights[4].shape[1] // width
    n_sem = 11 * (4 * (nz - 1) + 1) + 5 * 2 * nz + 3 * 2 * (nz - 1) + 4
    wide, tiled = (2 * n, seg, LANES), (tok * n // KT, KT, LANES)
    shapes = [(2, 4, 2, seg, width), (nz, d_rows, 3 * LANES), wide, tiled, tiled, wide]
    block = (4, tok, LANES)
    sds = jax.ShapeDtypeStruct
    vb = lambda *s: pltpu.VMEM(s, bf16)
    vf = lambda *s: pltpu.VMEM(s, f32)
    return pl.pallas_call(
        functools.partial(front_kernel, nz, n, heads, head_dim, n_sem),
        out_shape=tuple(sds(s, bf16) for s in shapes)
        + (
            sds((nz, total, width), bf16),
            sds((seg, KT), f32),
            sds((tok, width), bf16),
            sds(block, bf16),
            sds((tok, width), f32),
        ),
        in_specs=smem(2) + vmem(3) + hbm(6),
        out_specs=tuple(hbm(7) + vmem(4)),
        scratch_shapes=[pltpu.SMEM((2 * n + heads,), jnp.int32)]
        + [vb(*s) for s in shapes]
        + [
            vb(2, *block),
            vb(*block),
            vb(*block),
            vb(*block),
            vb(n_f, nz * d_rows, width),
            vb(nz, f_rows, width),
            vb(nz, 2, d_rows // 2 + 16, width),
            vf(3, d_rows, width),
            vf(d_rows, width),
            vf(d_rows, n_f * width),
            vf(f_rows, width),
            vf(n_f, tok, width),
            vb(n_f, tok, width),
            vb(tok, width),
            vf(tok, width),
            vf(tok, width),
            vf(tok, 128),
            vf(tok, width),
            vb(2, 2, f_rows, width),
            vb(nz, total - f_rows - n_f * d_rows, width),
            pltpu.SemaphoreType.DMA((n_sem,)),
            pltpu.SemaphoreType.DMA((n_sem,)),
            pltpu.SemaphoreType.DMA((12,)),
            pltpu.SemaphoreType.DMA((6,)),
            pltpu.SemaphoreType.DMA((2, 1 + nz)),
        ],
        compiler_params=comm_params(0),
        name="front",
    )(pairs, pairing, x_in.reshape(2, seg, width), cot, norms, *weights)


def add_into(dst, src, rows):
    chunk = max(c for c in range(16, min(rows, 160) + 1, 16) if rows % c == 0)

    def step(i, _):
        at = pl.ds(pl.multiple_of(i * chunk, chunk), chunk)
        to, frm = of(dst), of(src)
        to[at, :] = to[at, :] + frm[at, :]
        return 0

    lax.fori_loop(0, rows // chunk, step, 0)


class Slot:
    def __init__(self, ref, o):
        self.ref, self.o = ref, o

    def __call__(self):
        return self.ref.at[self.o]

    @property
    def at(self):
        return self().at


class PlaneSum:
    def __init__(self, net, place, block, rows, rx0, ry1, ry0, rx1):
        p = place
        self.net, self.place = net, place
        self.rx0, self.ry1, self.ry0, self.rx1 = rx0, ry1, ry0, rx1
        self.h = rows // 2
        h0, h1 = pl.ds(0, self.h), pl.ds(self.h, self.h)
        far_x, far_y = 1 - p.x, 1 - p.y
        self.block, self.h0, self.h1 = block, h0, h1
        self.far_x, self.far_y = far_x, far_y
        self.to_x = [2 * j + far_x for j in range(2)]
        self.to_y = [2 * far_y + j for j in range(2)]
        self.on_y, self.on_x = 2 * far_y + p.x, 2 * p.y + far_x
        self.ids = [net.new() for _ in range(6)]

    def part(self, index, half):
        return lambda: self.block(index).at[half]

    def first(self):
        n, p, i = self.net, self.place, self.ids
        for j in range(2):
            n.send(i[j], self.part(self.to_x[j], self.h0), lambda j=j: self.rx0.at[j], p.xn)
            n.send(i[2 + j], self.part(self.to_y[j], self.h1), lambda j=j: self.ry1.at[j], p.yn)

    def second(self):
        n, p, i = self.net, self.place, self.ids
        on_y, on_x = self.part(self.on_y, self.h0), self.part(self.on_x, self.h1)
        mine0, mine1 = self.part(p.chip, self.h0), self.part(p.chip, self.h1)
        for j in range(2):
            n.recv(i[j], lambda j=j: self.rx0.at[j], p.xn)
        add_into(on_y, lambda: self.rx0.at[self.far_y], self.h)
        n.send(i[4], on_y, self.ry0, p.yn)
        for j in range(2):
            n.recv(i[2 + j], lambda j=j: self.ry1.at[j], p.yn)
        add_into(on_x, lambda: self.ry1.at[self.far_x], self.h)
        n.send(i[5], on_x, self.rx1, p.xn)
        add_into(mine0, lambda: self.rx0.at[p.y], self.h)
        add_into(mine1, lambda: self.ry1.at[p.x], self.h)

    def third(self):
        n, p, i = self.net, self.place, self.ids
        n.recv(i[4], self.ry0, p.yn)
        add_into(self.part(p.chip, self.h0), self.ry0, self.h)
        n.recv(i[5], self.rx1, p.xn)
        add_into(self.part(p.chip, self.h1), self.rx1, self.h)


class LineSum:
    def __init__(self, net, place, nz, whole, low, high, parts, rows):
        p, z, top = place, place.z, nz - 1
        self.net, self.top, self.parts, self.rows, self.whole = net, top, parts, rows, whole
        sides = (
            ([net.new() for _ in range(nz)], low, z, -1, p.down, p.up),
            ([net.new() for _ in range(nz)], high, top - z, 1, p.up, p.down),
        )
        self.todo = {}
        for t in range(nz):
            self.todo[t] = []
            for ids, buf, depth, sign, frm, to in sides:
                owner = jnp.clip(top - t + z if sign < 0 else t + z - top, 0, top)
                takes = jnp.logical_and(depth > 0, depth <= t)
                self.todo[t].append(
                    (ids, owner, buf, takes, depth <= t, frm, to)
                )

    def step(self, t):
        n = self.net
        for ids, owner, buf, takes, sends, frm, to in self.todo[t]:
            whole = functools.partial(self.whole, owner)
            landed = lambda buf=buf, owner=owner: buf.at[owner]

            def take(ids=ids, whole=whole, landed=landed, frm=frm):
                n.recv(ids[t - 1], landed, frm)
                if self.parts is None:
                    add_into(whole, landed, self.rows)
                else:
                    for j in range(self.parts):
                        add_into(
                            lambda j=j: whole().at[j], lambda j=j: landed().at[j], self.rows
                        )

            if t > 0:
                maybe(takes, take)
            if t < self.top:
                n.send(ids[t], whole, landed, to, sends)


def attend_back_unit(
    fold, core, h, i, head_dim, tab, q_ref, k_ref, v_ref, o_ref, lse_ref, da_ref,
    dcat_ref, dk_ref, dv_ref,
):
    n, seg, half = fold.n, fold.seg, fold.half
    paired = tab[2 * n + h]
    pf = paired.astype(f32)
    lanes = head_mask(h, head_dim, f32)
    lanes16 = head_mask(h, head_dim, bf16)
    dqs = []
    places = fold.places(i, core, paired)
    for g, (rows, keys, limit, count) in enumerate(places):
        q = q_ref[rows] * lanes16
        k, c, upper = natural(tab, n, rows)
        da = da_ref[k, c, upper] * lanes16
        delta = jnp.sum(
            da.astype(f32) * o_ref[rows].astype(f32), axis=1, keepdims=True
        )
        lane = lax.broadcasted_iota(jnp.int32, (1, KT), 1) == lse_lane(fold, h, i, g)
        lse = jnp.sum(jnp.where(lane, lse_ref[...], 0.0), axis=1, keepdims=True)
        dq = None
        pieces = [(count - 2, 2, True)]
        if count > 2:
            pieces.append((0, count - 2, False))
        for first, size, masked in pieces:
            kt = key_tiles(k_ref, keys, first, size)
            vt = key_tiles(v_ref, keys, first, size)
            pr = jnp.exp(mm(q, kt, NT) - lse)
            if masked:
                pr = jnp.where(tail_mask(seg, limit), pr, 0.0)
            ds = (pr * (mm(da, vt, NT) - delta)).astype(bf16)
            part = mm(ds, kt)
            dq = part if dq is None else dq + part
            dv = mm(pr.astype(bf16), da, TN)
            dk = mm(ds, q, TN)
            at = pl.ds(first * KT, size * KT)
            if g == 0 or masked:
                dk_ref[at, :] += dk
                dv_ref[at, :] += dv
            else:
                beyond = pl.ds(places[0][3] * KT, size * KT)
                dk_ref[at, :] += (1.0 - pf) * dk
                dv_ref[at, :] += (1.0 - pf) * dv
                dk_ref[beyond, :] += pf * dk
                dv_ref[beyond, :] += pf * dv
        dqs.append(dq)
    scaled = lanes * score_scale
    dq_a, dq_b = (dqs[0] + pf * dqs[1]) * scaled, dqs[1] * scaled
    far, near, up = core * n + n - 1 - i, core * n + i, n + core * (n // 2) + i
    for at, value in ((far, (1.0 - pf) * dq_a), (near, (1.0 - pf) * dq_b), (up, pf * dq_a)):
        dcat_ref[at, :, :LANES] += value.astype(bf16)


def place_key_grads(fold, core, paired, dk_ref, dv_ref, dcat_ref):
    n, seg, half = fold.n, fold.seg, fold.half
    pf = paired.astype(f32)

    def spread(j, _):
        at = pl.ds(pl.multiple_of(j * seg, seg), seg)
        for src, lanes in ((dk_ref, slice(LANES, 2 * LANES)), (dv_ref, slice(2 * LANES, None))):
            value = src[at, :]
            dcat_ref[core * n + j, :, lanes] += ((1.0 - pf) * value).astype(bf16)
            dcat_ref[j, :, lanes] += (pf * value).astype(bf16)
        return 0

    lax.fori_loop(0, n, spread, 0)


BACKWARD_ORDER = (
    "c1", "p1f", "dr", "c0", "lb0", "dw", "s2", "U0", "p0f", "s3", "U1", "U2", "U3", "p1s",
    "c2", "c3", "U4", "lb1", "U5", "p3f", "U6", "p2f", "U7", "p1t", "U8", "U9", "U10", "lb2",
    "p0s", "U11", "DXo", "p2s", "p3s", "p0t", "la0", "DXm", "xa", "xsf", "p3t", "p2t", "lb3",
    "pbf", "la1", "DW", "pbs", "la2", "wa", "pbt", "wl0", "fbf", "fbs", "la3", "faf", "wl1",
    "xss", "fbt", "wl2", "fbl", "wl3", "wff", "fas", "wfs", "fat", "xst", "tok", "wft", "fal",
    "wfl", "dwo",
)


def backward_kernel(
    nz, n, heads, head_dim, rb, n_sem,
    pairs, pairing, g_ref, da_in, dh_ref, xall_i, wqkv_i, q_i, k_i, v_i, on_i, lse_ref,
    gsum_o, dtok_o, dw_o,
    tab, g_kept, g_sib, g_rx0, g_ry1, g_ry0, g_rx1, g_low, g_high,
    b_low, b_high, b_rx0, b_ry1, b_ry0, b_rx1,
    x_part, x_sib, x_rx0, x_ry1, x_ry0, x_rx1, w_part, w_sib, w_low, w_high, w_all,
    da_all, xall, wqkv, q_ref, k_ref, v_ref, on_ref, dcat, dk_ref, dv_ref, dw_acc,
    ssem, rsem, lsem,
):
    p = Place()
    z = p.z
    seg, width = xall.shape[3], xall.shape[4]
    tok = 2 * seg
    fold = Fold(n, seg)
    rows = g_ref.shape[3]
    ra = rows - rb
    ax, bx = pl.ds(0, ra), pl.ds(ra, rb)
    order = line_order(nz)
    local = []

    def fetch(src, dst):
        cp = pltpu.make_async_copy(src, dst, lsem.at[len(local)])
        cp.start()
        local.append(cp)
        return cp

    net = Net(ssem, rsem, n_sem)
    own_da = fetch(da_in.at[p.chip], da_all.at[p.core, p.chip])
    own_g = {o: fetch(g_ref.at[o, p.core], g_kept.at[o]) for o in order}
    greet(p, (p.sib, p.xn, p.yn, p.dn), nz)
    swaps = [net.new() for _ in range(7)]
    partners = ((p.chip_d, p.dn), (p.chip_x, p.xn), (p.chip_y, p.yn))
    for i, (chip, dev) in enumerate(partners):
        net.send(swaps[i], da_in.at[chip], da_all.at[p.core, p.chip], dev)
    net.send(swaps[3], da_in.at[p.chip], da_all.at[p.core, p.chip], p.sib)
    sib_ids = {o: net.new() for o in order}

    def to_sib(o):
        net.send(sib_ids[o], lambda: g_ref.at[o, p.other], lambda: g_sib.at[o], p.sib)

    to_sib(order[0])
    to_sib(order[1])
    att_in = [
        fetch(src, dst)
        for src, dst in (
            (q_i, q_ref), (k_i, k_ref), (v_i, v_ref), (on_i, on_ref), (xall_i, xall), (wqkv_i, wqkv),
        )
    ]
    fill_table(tab, pairs, pairing, p.chip, n, heads)
    dcat[...] = jnp.zeros(dcat.shape, bf16)

    plane = {
        o: PlaneSum(
            net, p, lambda q, o=o: g_kept.at[o, q].at[ax], ra,
            *(Slot(r, o) for r in (g_rx0, g_ry1, g_ry0, g_rx1)),
        )
        for o in order
    }
    line_a = LineSum(net, p, nz, lambda o: g_kept.at[o, p.chip].at[ax], g_low, g_high, None, ra)
    line_b = LineSum(net, p, nz, lambda o: g_kept.at[o, :, bx], b_low, b_high, n // 2, rb)
    plane_b = PlaneSum(
        net, p, lambda q: g_kept.at[z, q].at[bx], rb, b_rx0, b_ry1, b_ry0, b_rx1
    )

    def chip_sum(o):
        net.recv(sib_ids[o], lambda: g_sib.at[o], p.sib)
        pltpu.make_async_copy(g_ref.at[o, p.core], g_kept.at[o], lsem.at[1 + order.index(o)]).wait()
        for q in range(n // 2):
            add_into(lambda q=q: g_kept.at[o, q], lambda q=q: g_sib.at[o, q], rows)

    d = wqkv.shape[1]
    half = d // 2
    x_id, w_id = net.new(), net.new()
    w_line = LineSum(net, p, nz, lambda o: w_part.at[p.core, o], w_low, w_high, None, half)
    xs = PlaneSum(net, p, lambda q: x_part.at[p.core, q], tok, x_rx0, x_ry1, x_ry0, x_rx1)
    final_a = PlaneGather(
        net, p, lambda: g_kept.at[z, p.chip].at[ax], lambda k, q: gsum_o.at[k, q].at[ax], ra
    )
    final_b = PlaneGather(
        net, p, lambda: g_kept.at[z, p.chip].at[bx], lambda k, q: gsum_o.at[k, q].at[bx], rb
    )
    w_final = PlaneGather(net, p, lambda: w_part.at[p.core, z], lambda k, q: w_all.at[k, q], half)
    cols = heads * head_dim

    def da_forward():
        for i, chip, dev in ((1, p.chip_x, p.xn), (2, p.chip_y, p.yn), (0, p.chip_d, p.dn)):
            block = lambda chip=chip: da_all.at[p.core, chip]
            net.recv(swaps[i], block, dev)
            net.send(swaps[4 + i], block, block, p.sib)

    def da_wait():
        for i, chip in ((3, p.chip), (5, p.chip_x), (6, p.chip_y), (4, p.chip_d)):
            net.recv(swaps[i], lambda chip=chip: da_all.at[p.other, chip], p.sib)
        own_da.wait()
        for cp in att_in:
            cp.wait()

    def block_grads(k, q):
        a = tab[2 * q + k]
        return jnp.concatenate([dcat[a], dcat[2 * n - 1 - a]], axis=0)

    def weight_grads():
        dw_acc[...] = jnp.zeros(dw_acc.shape, f32)

        def weights(c, _):
            k, q = lax.rem(c, 2), c // 2
            dw_acc[...] += mm(xall[k, q].reshape(tok, width), block_grads(k, q), TN)
            return 0

        lax.fori_loop(0, n, weights, 0)
        for o in range(nz):
            w_part[0, o] = dw_acc[o * d : o * d + half].astype(bf16)
            w_part[1, o] = dw_acc[o * d + half : (o + 1) * d].astype(bf16)
        net.send(w_id, w_part.at[p.other], w_sib, p.sib)

    def weight_sum():
        net.recv(w_id, w_sib, p.sib)
        for o in range(nz):
            add_into(w_part.at[p.core, o], w_sib.at[o], half)

    def tokens_of(k):
        def one(q, _):
            w = wqkv[...].reshape(-1, 3 * LANES)
            x_part[k, q] = mm(block_grads(k, q), w, NT).astype(bf16)
            return 0

        lax.fori_loop(0, n // 2, one, 0)

    def tokens_other():
        tokens_of(p.other)
        net.send(x_id, x_part.at[p.other], x_sib, p.sib)

    def tokens_sum():
        net.recv(x_id, x_sib, p.sib)
        for q in range(n // 2):
            add_into(x_part.at[p.core, q], x_sib.at[q], tok)

    def tokens_out():
        def add_tokens(i, _):
            at = pl.ds(pl.multiple_of(i * 32, 32), 32)
            dtok_o[at, :] = (dh_ref[at, :] + x_part[p.core, p.chip, at, :].astype(f32)).astype(bf16)
            return 0

        lax.fori_loop(0, tok // 32, add_tokens, 0)

    def own_w():
        return pltpu.make_async_copy(
            w_part.at[p.core, z], w_all.at[p.core, p.chip], lsem.at[31]
        )

    def w_final_first():
        w_final.first()
        own_w().start()

    def w_out():
        own_w().wait()
        for j in range(3):
            for k in range(2):
                dw_o[j, k * half : (k + 1) * half, :] = jnp.concatenate(
                    [w_all[k, q][:, j * LANES : j * LANES + cols] for q in range(4)], axis=1
                )

    steps = {
        "dr": da_forward, "dw": da_wait, "DW": weight_grads, "wa": weight_sum,
        "DXo": tokens_other, "DXm": lambda: tokens_of(p.core), "xa": tokens_sum, "tok": tokens_out,
        "dwo": w_out, "wff": w_final_first,
    }
    for k, o in enumerate(order):
        steps[f"s{k}"] = functools.partial(to_sib, o)
        steps[f"c{k}"] = functools.partial(chip_sum, o)
        steps[f"p{k}f"], steps[f"p{k}s"] = plane[o].first, plane[o].second
        steps[f"p{k}t"] = plane[o].third
    for name, line in (("la", line_a), ("lb", line_b), ("wl", w_line)):
        for t in range(nz):
            steps[f"{name}{t}"] = functools.partial(line.step, t)
    for name, thing in (("pb", plane_b), ("xs", xs), ("fa", final_a), ("fb", final_b), ("wf", w_final)):
        for stage in ("first", "second", "third", "last"):
            if hasattr(thing, stage):
                steps.setdefault(name + stage[0], getattr(thing, stage))
    units = n // 2
    before, todo, behind = by_unit(BACKWARD_ORDER, steps, units * heads - 1)
    for step in before:
        step()

    def head(h, _):
        dk_ref[...] = jnp.zeros(dk_ref.shape, f32)
        dv_ref[...] = jnp.zeros(dv_ref.shape, f32)
        for i in range(units):
            attend_back_unit(
                fold, p.core, h, i, head_dim, tab, q_ref, k_ref, v_ref, on_ref, lse_ref, da_all,
                dcat, dk_ref, dv_ref,
            )
            for hh in range(heads):
                if hh * units + i in todo:
                    pl.when(h == hh)(chain(*((step,) for step in todo[hh * units + i])))
        place_key_grads(fold, p.core, tab[2 * n + h], dk_ref, dv_ref, dcat)
        return 0

    lax.fori_loop(0, heads, head, 0)
    for step in behind:
        step()
    own_sum = fetch(g_kept.at[z, p.chip], gsum_o.at[p.core, p.chip])
    own_sum.wait()
    net.finish()


def line_order(nz):
    order = []
    for i in range((nz + 1) // 2):
        for o in (nz - 1 - i, i):
            if o not in order:
                order.append(o)
    return order


def backward(
    nz, n, heads, head_dim, rb, pairs, pairing, grads, da, dh, xall, wqkv, q, k, v, on, lse
):
    rows, width = grads.shape[3], grads.shape[4]
    seg = xall.shape[3]
    tok = 2 * seg
    d_rows = wqkv.shape[1]
    half = d_rows // 2
    ra = rows - rb
    n_sem = 6 * (nz + 2) + 6 * nz + nz + 9 + 33 + 2
    sds = jax.ShapeDtypeStruct
    vm = lambda *shape: pltpu.VMEM(shape, bf16)
    wide, tiled = (2 * n, seg, LANES), (tok * n // KT, KT, LANES)
    da = da.reshape(4, 2, seg, LANES)
    return pl.pallas_call(
        functools.partial(backward_kernel, nz, n, heads, head_dim, rb, n_sem),
        out_shape=(
            sds(grads.shape[1:], bf16),
            sds((tok, width), bf16),
            sds((3, d_rows, width), bf16),
        ),
        in_specs=smem(2) + hbm(2) + vmem(1) + hbm(6) + vmem(1),
        out_specs=tuple(hbm(1) + vmem(2)),
        scratch_shapes=[
            pltpu.SMEM((2 * n + heads,), jnp.int32),
            vm(nz, 4, rows, width),
            vm(nz, 4, rows, width),
            vm(nz, 2, ra // 2, width),
            vm(nz, 2, ra // 2, width),
            vm(nz, ra // 2, width),
            vm(nz, ra // 2, width),
            vm(nz, ra, width),
            vm(nz, ra, width),
            vm(nz, 4, rb, width),
            vm(nz, 4, rb, width),
            vm(2, rb // 2, width),
            vm(2, rb // 2, width),
            vm(rb // 2, width),
            vm(rb // 2, width),
            vm(2, 4, tok, width),
            vm(4, tok, width),
            vm(2, tok // 2, width),
            vm(2, tok // 2, width),
            vm(tok // 2, width),
            vm(tok // 2, width),
            vm(2, nz, half, width),
            vm(nz, half, width),
            vm(nz, half, width),
            vm(nz, half, width),
            vm(2, 4, half, width),
            vm(2, 4, 2, seg, LANES),
            vm(2, 4, 2, seg, width),
            vm(nz, d_rows, width),
            vm(*wide),
            vm(*tiled),
            vm(*tiled),
            vm(*wide),
            vm(2 * n, seg, 3 * LANES),
            pltpu.VMEM((seg * n, LANES), f32),
            pltpu.VMEM((seg * n, LANES), f32),
            pltpu.VMEM((width, 3 * LANES), f32),
            pltpu.SemaphoreType.DMA((n_sem,)),
            pltpu.SemaphoreType.DMA((n_sem,)),
            pltpu.SemaphoreType.DMA((32,)),
        ],
        compiler_params=comm_params(1),
        name="backward",
    )(pairs, pairing, grads, da, dh, xall, wqkv, q, k, v, on, lse)


def fast_body(
    tokens,
    w_query,
    w_key,
    w_value,
    w_output,
    w_inner,
    w_outer,
    ln_gain,
    ln_bias,
    pairing,
    block_pairs,
    cotangent,
):
    tok, width = tokens.shape[1], tokens.shape[2]
    n_ctx, nz = lax.axis_size("ctx"), lax.axis_size("fsdp")
    z = lax.axis_index("fsdp")
    heads = pairing.shape[1]
    my_heads, head_dim = heads // 4, width // heads
    d_rows = w_query.shape[0]
    f_rows, ff = w_outer.shape[0], w_inner.shape[1]
    n_f = ff // width
    o1, o2, used = f_rows, f_rows + n_f * d_rows, f_rows + n_f * d_rows + d_rows
    total = -(-(used + 4) // 256) * 256
    norms = jnp.concatenate([ln_gain.T, ln_bias.T], axis=0).astype(bf16)
    norms = lax.dynamic_update_slice(jnp.zeros((16, width), bf16), norms, (0, z * d_rows))
    weights = (w_query, w_key, w_value, w_output, w_inner, w_outer)
    xall, wqkv, q, k, v, on, grads, lse, result, da, d_h1 = front(
        nz, n_ctx, my_heads, head_dim, total, block_pairs, pairing, tokens[0], cotangent[0],
        norms, weights,
    )
    grads = grads.reshape(nz, 2, 4, total // 8, width)
    gsum, dtok, dw = backward(
        nz, n_ctx, my_heads, head_dim, 64, block_pairs, pairing, grads, da, d_h1,
        xall, wqkv, q, k, v, on, lse,
    )
    gsum = gsum.reshape(total, width)
    g_inner = [gsum[o1 + i * d_rows : o1 + (i + 1) * d_rows] for i in range(n_f)]
    g_norms = lax.dynamic_slice(gsum[used : used + 4], (0, z * d_rows), (4, d_rows)).astype(f32)
    return (
        result[None],
        dtok[None],
        dw[0].astype(f32),
        dw[1].astype(f32),
        dw[2].astype(f32),
        gsum[o2:used].astype(f32),
        jnp.concatenate(g_inner, axis=1).astype(f32),
        gsum[:o1].astype(f32),
        g_norms[:2].T,
        g_norms[2:].T,
    )


def solution(mesh):
    in_specs = (
        P("fsdp", "ctx", None),
        P("fsdp", None),
        P("fsdp", None),
        P("fsdp", None),
        P("fsdp", None),
        P("fsdp", None),
        P("fsdp", None),
        P("fsdp", None),
        P("fsdp", None),
        P("fsdp", None),
        P("fsdp", None),
        P("fsdp", "ctx", None),
    )
    out_specs = (
        P("fsdp", "ctx", None),
        P("fsdp", "ctx", None),
        P("fsdp", None),
        P("fsdp", None),
        P("fsdp", None),
        P("fsdp", None),
        P("fsdp", None),
        P("fsdp", None),
        P("fsdp", None),
        P("fsdp", None),
    )
    fast = mesh.shape["ctx"] == 8 and mesh.shape["fsdp"] == 4
    chosen = fast_body if fast else generic_body
    return jax.shard_map(chosen, mesh=mesh, in_specs=in_specs, out_specs=out_specs, check_vma=False)
```

```python
import functools

import jax
import jax.numpy as jnp
from jax import lax
from jax.experimental import pallas as pl
from jax.experimental.pallas import tpu as pltpu
from jax.sharding import PartitionSpec as P

norm_eps = 1e-05
score_scale = 0.125
very_low = -1e30


def shortened(value):

    def short(part):
        return part.astype(jnp.bfloat16) if part.dtype == jnp.float32 else part

    return jax.tree.map(short, value)


def layer_norm(values, norm_gain, norm_shift):
    center = values - jnp.mean(values, axis=-1, keepdims=True)
    spread = jnp.mean(center * center, axis=-1, keepdims=True)
    return center * lax.rsqrt(spread + norm_eps) * norm_gain + norm_shift


def exact_gelu(values):
    return jax.nn.gelu(values, approximate=False)


def project(rows_in, weight):
    return jnp.dot(rows_in, weight, preferred_element_type=jnp.float32)


def seq_positions(pair_row, tok_dev, seq_len):
    segment_len = tok_dev // 2
    within = jnp.arange(tok_dev, dtype=jnp.int32)
    lower_pos = pair_row[:, None] * segment_len + within[None, :]
    upper_pos = seq_len - (pair_row[:, None] + 1) * segment_len + within[None, :] - segment_len
    return jnp.where(within[None, :] < segment_len, lower_pos, upper_pos).reshape(-1)


def pair_mask(query_pos, key_pos, head_flags, half_len):
    target = (query_pos[None, :] // half_len + head_flags[:, None]) % 2
    paired = key_pos[None, None, :] // half_len == target[:, :, None]
    causal = key_pos[None, :] <= query_pos[:, None]
    return jnp.logical_and(paired, causal[None, :, :])


def block_rows(tok_dev):
    return 2 * tok_dev


def over_blocks(running, arrays, step_fn, tok_dev):
    row_count = arrays[0].shape[0]
    block_len = block_rows(tok_dev)

    def one_step(inner_carry, step_index):
        first_row = step_index * block_len
        sliced = tuple(
            (lax.dynamic_slice_in_dim(member, first_row, block_len, 0) for member in arrays)
        )
        return (step_fn(inner_carry, sliced, first_row), None)

    return lax.scan(one_step, running, jnp.arange(row_count // block_len, dtype=jnp.int32))[0]


def generic_body(
    tokens,
    w_query,
    w_key,
    w_value,
    w_output,
    w_inner,
    w_outer,
    ln_gain,
    ln_bias,
    pairing,
    block_pairs,
    cotangent,
):
    tok_dev = tokens.shape[1]
    width = tokens.shape[2]
    heads = pairing.shape[1]
    head_dim = width // heads
    n_ctx = lax.axis_size("ctx")
    seq_len = tok_dev * n_ctx
    half_len = seq_len // 2
    pos_all = seq_positions(block_pairs[0], tok_dev, seq_len)
    my_pos = lax.dynamic_slice_in_dim(pos_all, lax.axis_index("ctx") * tok_dev, tok_dev, 0)
    head_flags = pairing[0]
    masters = (w_query, w_key, w_value, w_output, w_inner, w_outer, ln_gain, ln_bias)
    low_masters = tuple((member.astype(jnp.bfloat16) for member in masters))
    gathered = jax.tree.map(
        lambda part, own: part.astype(own.dtype),
        lax.all_gather(shortened(low_masters), "fsdp", axis=0, tiled=True),
        low_masters,
    )
    wq_full, wk_full, wv_full, wo_full, inner_full, outer_full, gain_full, shift_full = gathered
    gain_wide = gain_full.astype(jnp.float32)
    shift_wide = shift_full.astype(jnp.float32)
    x_in = tokens[0]
    query_b = project(x_in, wq_full).astype(jnp.bfloat16)
    key_b = project(x_in, wk_full).astype(jnp.bfloat16)
    value_b = project(x_in, wv_full).astype(jnp.bfloat16)
    q_heads = query_b.reshape(tok_dev, heads, head_dim)

    def attend_step(running, sliced, offset):
        run_max, run_sum, run_acc = running
        key_block, value_block = sliced
        block_len = key_block.shape[0]
        key_pos = lax.dynamic_slice_in_dim(pos_all, offset, block_len, 0)
        allowed = pair_mask(my_pos, key_pos, head_flags, half_len)
        key_heads = key_block.reshape(block_len, heads, head_dim)
        value_heads = value_block.reshape(block_len, heads, head_dim)
        scores = (
            jnp.einsum("qhd,khd->hqk", q_heads, key_heads, preferred_element_type=jnp.float32)
            * score_scale
        )
        new_max = jnp.maximum(run_max, jnp.max(jnp.where(allowed, scores, very_low), axis=2))
        prob_rows = jnp.where(
            allowed, jnp.exp(jnp.where(allowed, scores - new_max[:, :, None], 0.0)), 0.0
        )
        decay = jnp.exp(run_max - new_max)
        new_sum = run_sum * decay + jnp.sum(prob_rows, axis=2)
        added = jnp.einsum(
            "hqk,khd->hqd",
            prob_rows.astype(jnp.bfloat16),
            value_heads,
            preferred_element_type=jnp.float32,
        )
        return (new_max, new_sum, run_acc * decay[:, :, None] + added)

    def pair_fold(step_fn, running, fetched):
        return over_blocks(running, fetched, step_fn, tok_dev)

    start_state = (
        jnp.full((heads, tok_dev), very_low, jnp.float32),
        jnp.zeros((heads, tok_dev), jnp.float32),
        jnp.zeros((heads, tok_dev, head_dim), jnp.float32),
    )
    run_max, run_sum, run_acc = pair_fold(
        attend_step,
        start_state,
        (
            lax.all_gather(key_b, "ctx", axis=0, tiled=True),
            lax.all_gather(value_b, "ctx", axis=0, tiled=True),
        ),
    )
    live_rows = run_sum > 0
    safe_sum = jnp.where(live_rows, run_sum, 1.0)
    attn_heads = jnp.where(live_rows[:, :, None], run_acc / safe_sum[:, :, None], 0.0)
    lse_rows = jnp.where(live_rows, run_max + jnp.log(safe_sum), 0.0)
    attn_rows = attn_heads.transpose(1, 0, 2).reshape(tok_dev, width)
    attn_b = attn_rows.astype(jnp.bfloat16)
    branch = project(attn_b, wo_full)
    first_norm, first_pull = jax.vjp(
        layer_norm, x_in.astype(jnp.float32) + branch, gain_wide[:, 0], shift_wide[:, 0]
    )
    first_b = first_norm.astype(jnp.bfloat16)
    inner = project(first_b, inner_full)
    active, gelu_pull = jax.vjp(exact_gelu, inner)
    active_b = active.astype(jnp.bfloat16)
    outer = project(active_b, outer_full)
    result, second_pull = jax.vjp(layer_norm, first_norm + outer, gain_wide[:, 1], shift_wide[:, 1])
    wq_back, wk_back, wv_back, wo_back, inner_back, outer_back, gain_back, shift_back = gathered
    d_h2, d_gain2, d_shift2 = second_pull(cotangent[0].astype(jnp.float32))
    d_f_b = d_h2.astype(jnp.bfloat16)
    d_outer = jnp.dot(active_b.T, d_f_b, preferred_element_type=jnp.float32)
    d_active = jnp.dot(d_f_b, outer_back.T, preferred_element_type=jnp.float32)
    d_u_b = gelu_pull(d_active)[0].astype(jnp.bfloat16)
    d_inner = jnp.dot(first_b.T, d_u_b, preferred_element_type=jnp.float32)
    d_x1 = d_h2 + jnp.dot(d_u_b, inner_back.T, preferred_element_type=jnp.float32)
    d_h1, d_gain1, d_shift1 = first_pull(d_x1)
    d_y_b = d_h1.astype(jnp.bfloat16)
    d_wo = jnp.dot(attn_b.T, d_y_b, preferred_element_type=jnp.float32)
    d_attn_b = jnp.dot(d_y_b, wo_back.T, preferred_element_type=jnp.float32).astype(jnp.bfloat16)
    delta_rows = (
        (d_attn_b.astype(jnp.float32) * attn_rows).reshape(tok_dev, heads, head_dim).sum(axis=2).T
    )
    dout_heads = d_attn_b.reshape(tok_dev, heads, head_dim)

    def query_grad_step(dq_acc, sliced, offset):
        key_block, value_block = sliced
        block_len = key_block.shape[0]
        key_pos = lax.dynamic_slice_in_dim(pos_all, offset, block_len, 0)
        allowed = pair_mask(my_pos, key_pos, head_flags, half_len)
        key_heads = key_block.reshape(block_len, heads, head_dim)
        value_heads = value_block.reshape(block_len, heads, head_dim)
        scores = (
            jnp.einsum("qhd,khd->hqk", q_heads, key_heads, preferred_element_type=jnp.float32)
            * score_scale
        )
        prob_rows = jnp.where(
            allowed, jnp.exp(jnp.where(allowed, scores - lse_rows[:, :, None], 0.0)), 0.0
        )
        prob_grad = jnp.einsum(
            "qhd,khd->hqk", dout_heads, value_heads, preferred_element_type=jnp.float32
        )
        dscore = (prob_rows * (prob_grad - delta_rows[:, :, None]) * score_scale).astype(
            jnp.bfloat16
        )
        return dq_acc + jnp.einsum(
            "hqk,khd->qhd", dscore, key_heads, preferred_element_type=jnp.float32
        )

    dq_start = jnp.zeros((tok_dev, heads, head_dim), jnp.float32)
    dq_acc = pair_fold(
        query_grad_step,
        dq_start,
        (
            lax.all_gather(key_b, "ctx", axis=0, tiled=True),
            lax.all_gather(value_b, "ctx", axis=0, tiled=True),
        ),
    )
    dq_b = dq_acc.reshape(tok_dev, width).astype(jnp.bfloat16)
    lse_all, delta_all = (
        lax.all_gather(lse_rows, "ctx", axis=1, tiled=True),
        lax.all_gather(delta_rows, "ctx", axis=1, tiled=True),
    )
    k_heads = key_b.reshape(tok_dev, heads, head_dim)
    v_heads = value_b.reshape(tok_dev, heads, head_dim)

    def key_grad_step(running, sliced, offset):
        dk_acc, dv_acc = running
        query_block, dout_block = sliced
        block_len = query_block.shape[0]
        query_pos = lax.dynamic_slice_in_dim(pos_all, offset, block_len, 0)
        lse_block = lax.dynamic_slice_in_dim(lse_all, offset, block_len, 1)
        delta_block = lax.dynamic_slice_in_dim(delta_all, offset, block_len, 1)
        allowed = pair_mask(query_pos, my_pos, head_flags, half_len)
        query_heads = query_block.reshape(block_len, heads, head_dim)
        dout_block_heads = dout_block.reshape(block_len, heads, head_dim)
        scores = (
            jnp.einsum("qhd,khd->hqk", query_heads, k_heads, preferred_element_type=jnp.float32)
            * score_scale
        )
        prob_rows = jnp.where(
            allowed, jnp.exp(jnp.where(allowed, scores - lse_block[:, :, None], 0.0)), 0.0
        )
        dv_acc = dv_acc + jnp.einsum(
            "hqk,qhd->khd",
            prob_rows.astype(jnp.bfloat16),
            dout_block_heads,
            preferred_element_type=jnp.float32,
        )
        prob_grad = jnp.einsum(
            "qhd,khd->hqk", dout_block_heads, v_heads, preferred_element_type=jnp.float32
        )
        dscore = (prob_rows * (prob_grad - delta_block[:, :, None]) * score_scale).astype(
            jnp.bfloat16
        )
        dk_acc = dk_acc + jnp.einsum(
            "hqk,qhd->khd", dscore, query_heads, preferred_element_type=jnp.float32
        )
        return (dk_acc, dv_acc)

    kv_start = (
        jnp.zeros((tok_dev, heads, head_dim), jnp.float32),
        jnp.zeros((tok_dev, heads, head_dim), jnp.float32),
    )
    dk_acc, dv_acc = pair_fold(
        key_grad_step,
        kv_start,
        (
            lax.all_gather(query_b, "ctx", axis=0, tiled=True),
            lax.all_gather(d_attn_b, "ctx", axis=0, tiled=True),
        ),
    )
    dk_b = dk_acc.reshape(tok_dev, width).astype(jnp.bfloat16)
    dv_b = dv_acc.reshape(tok_dev, width).astype(jnp.bfloat16)
    d_input = d_h1 + jnp.dot(dq_b, wq_back.T, preferred_element_type=jnp.float32)
    d_input = d_input + jnp.dot(dk_b, wk_back.T, preferred_element_type=jnp.float32)
    d_input = d_input + jnp.dot(dv_b, wv_back.T, preferred_element_type=jnp.float32)
    terms = (
        jnp.dot(x_in.T, dq_b, preferred_element_type=jnp.float32),
        jnp.dot(x_in.T, dk_b, preferred_element_type=jnp.float32),
        jnp.dot(x_in.T, dv_b, preferred_element_type=jnp.float32),
        d_wo,
        d_inner,
        d_outer,
        jnp.stack([d_gain1, d_gain2], axis=1),
        jnp.stack([d_shift1, d_shift2], axis=1),
    )
    shares = (
        lax.psum_scatter(
            terms[0].astype(jnp.bfloat16), "fsdp", scatter_dimension=0, tiled=True
        ).astype(jnp.float32),
        lax.psum_scatter(
            terms[1].astype(jnp.bfloat16), "fsdp", scatter_dimension=0, tiled=True
        ).astype(jnp.float32),
        lax.psum_scatter(
            terms[2].astype(jnp.bfloat16), "fsdp", scatter_dimension=0, tiled=True
        ).astype(jnp.float32),
        lax.psum_scatter(
            terms[3].astype(jnp.bfloat16), "fsdp", scatter_dimension=0, tiled=True
        ).astype(jnp.float32),
        lax.psum_scatter(
            terms[4].astype(jnp.bfloat16), "fsdp", scatter_dimension=0, tiled=True
        ).astype(jnp.float32),
        lax.psum_scatter(
            terms[5].astype(jnp.bfloat16), "fsdp", scatter_dimension=0, tiled=True
        ).astype(jnp.float32),
        lax.psum_scatter(
            terms[6].astype(jnp.bfloat16), "fsdp", scatter_dimension=0, tiled=True
        ).astype(jnp.float32),
        lax.psum_scatter(
            terms[7].astype(jnp.bfloat16), "fsdp", scatter_dimension=0, tiled=True
        ).astype(jnp.float32),
    )
    totals = (
        lax.psum(shares[0].astype(jnp.bfloat16), "ctx").astype(jnp.float32),
        lax.psum(shares[1].astype(jnp.bfloat16), "ctx").astype(jnp.float32),
        lax.psum(shares[2].astype(jnp.bfloat16), "ctx").astype(jnp.float32),
        lax.psum(shares[3].astype(jnp.bfloat16), "ctx").astype(jnp.float32),
        lax.psum(shares[4].astype(jnp.bfloat16), "ctx").astype(jnp.float32),
        lax.psum(shares[5].astype(jnp.bfloat16), "ctx").astype(jnp.float32),
        lax.psum(shares[6].astype(jnp.bfloat16), "ctx").astype(jnp.float32),
        lax.psum(shares[7].astype(jnp.bfloat16), "ctx").astype(jnp.float32),
    )
    return (
        result.astype(jnp.bfloat16)[None],
        d_input.astype(jnp.bfloat16)[None],
        totals[0],
        totals[1],
        totals[2],
        totals[3],
        totals[4],
        totals[5],
        totals[6],
        totals[7],
    )


MESH = pl.DeviceIdType.MESH
f32 = jnp.float32
bf16 = jnp.bfloat16


class Place:
    def __init__(self):
        me = lax.axis_index("ctx")
        self.me = me
        self.z = lax.axis_index("fsdp")
        self.core = lax.rem(me, 2)
        self.chip = me // 2
        self.x = lax.rem(self.chip, 2)
        self.y = self.chip // 2
        self.chip_x = self.chip + 1 - 2 * self.x
        self.chip_y = self.chip + 2 - 4 * self.y
        self.chip_d = 3 - self.chip
        self.other = 1 - self.core
        self.sib = (2 * self.chip + 1 - self.core, self.z)
        self.xn = (2 * self.chip_x + self.core, self.z)
        self.yn = (2 * self.chip_y + self.core, self.z)
        self.dn = (2 * self.chip_d + self.core, self.z)
        self.up = (me, self.z + 1)
        self.down = (me, self.z - 1)


def greet(place, others, line_len=None):
    barrier = pltpu.get_barrier_semaphore()
    count = len(others)
    for other in others:
        pl.semaphore_signal(barrier, inc=1, device_id=other, device_id_type=MESH)
    if line_len is not None:

        @pl.when(place.z < line_len - 1)
        def _():
            pl.semaphore_signal(barrier, inc=1, device_id=place.up, device_id_type=MESH)

        @pl.when(place.z > 0)
        def _():
            pl.semaphore_signal(barrier, inc=1, device_id=place.down, device_id_type=MESH)

        count = count + jnp.where(place.z < line_len - 1, 1, 0) + jnp.where(place.z > 0, 1, 0)

    pl.semaphore_wait(barrier, count)


def maybe(cond, fn):
    if cond is None:
        fn()
    else:
        pl.when(cond)(fn)


def of(ref):
    return ref() if callable(ref) else ref


class Net:
    def __init__(self, send_sems, recv_sems, count):
        self.send_sems, self.recv_sems, self.count = send_sems, recv_sems, count
        self.used = 0
        self.open = []

    def new(self):
        self.used += 1
        assert self.used <= self.count
        return self.used - 1

    def copy(self, idx, src, dst, dev):
        return pltpu.make_async_remote_copy(
            src_ref=src,
            dst_ref=dst,
            send_sem=self.send_sems.at[idx],
            recv_sem=self.recv_sems.at[idx],
            device_id=dev,
            device_id_type=MESH,
        )

    def send(self, idx, src, dst, dev, cond=None):
        make = lambda: self.copy(idx, of(src), of(dst), dev)
        maybe(cond, lambda: make().start())
        self.open.append((cond, make))

    def recv(self, idx, dst, dev, cond=None):
        maybe(cond, lambda: self.copy(idx, of(dst), of(dst), dev).wait_recv())

    def finish(self):
        for cond, make in self.open:
            maybe(cond, lambda make=make: make().wait_send())
        self.open = []


class PlaneGather:
    def __init__(self, net, place, own, slot, rows, cond=None):
        p = place
        self.net, self.place, self.cond = net, place, cond
        self.own_of, self.slot = own, slot
        self.h0, self.h1 = pl.ds(0, rows // 2), pl.ds(rows // 2, rows // 2)
        self.ids = [net.new() for _ in range(11)]

    def at(self, core, chip, half=0):
        def view():
            ref = self.slot(core, chip)
            return ref if half == 0 else ref.at[self.h0 if half == 1 else self.h1]

        return view

    def mine(self, half=0):
        def view():
            ref = self.own_of()
            return ref if half == 0 else ref.at[self.h0 if half == 1 else self.h1]

        return view

    def first(self):
        n, p, i, c = self.net, self.place, self.ids, self.cond
        at = functools.partial(self.at, p.core, p.chip)
        n.send(i[0], self.mine(1), at(1), p.xn, c)
        n.send(i[1], self.mine(2), at(2), p.yn, c)
        n.send(i[2], self.mine(2), at(2), p.xn, c)
        n.send(i[3], self.mine(1), at(1), p.yn, c)
        n.send(i[4], self.mine(), at(), p.sib, c)

    def second(self):
        n, p, i, c = self.net, self.place, self.ids, self.cond
        bx = functools.partial(self.at, p.core, p.chip_x)
        by = functools.partial(self.at, p.core, p.chip_y)
        n.recv(i[0], bx(1), p.xn, c)
        n.send(i[5], bx(1), bx(1), p.yn, c)
        n.recv(i[1], by(2), p.yn, c)
        n.send(i[6], by(2), by(2), p.xn, c)
        n.recv(i[2], bx(2), p.xn, c)
        n.send(i[7], bx(), bx(), p.sib, c)
        n.recv(i[3], by(1), p.yn, c)
        n.send(i[8], by(), by(), p.sib, c)

    def third(self):
        n, p, i, c = self.net, self.place, self.ids, self.cond
        bd = functools.partial(self.at, p.core, p.chip_d)
        n.recv(i[5], bd(1), p.yn, c)
        n.send(i[9], bd(1), bd(1), p.sib, c)
        n.recv(i[6], bd(2), p.xn, c)
        n.send(i[10], bd(2), bd(2), p.sib, c)

    def last(self):
        n, p, i, c = self.net, self.place, self.ids, self.cond
        for idx, q in ((4, p.chip), (7, p.chip_x), (8, p.chip_y)):
            n.recv(i[idx], self.at(p.other, q), p.sib, c)
        n.recv(i[9], self.at(p.other, p.chip_d, 1), p.sib, c)
        n.recv(i[10], self.at(p.other, p.chip_d, 2), p.sib, c)


def hbm(count):
    return [pl.BlockSpec(memory_space=pltpu.HBM)] * count


def comm_params(collective_id):
    return pltpu.CompilerParams(
        collective_id=collective_id, has_side_effects=True, vmem_limit_bytes=56 << 20
    )


def vmem(count):
    return [pl.BlockSpec(memory_space=pltpu.VMEM)] * count


def smem(count):
    return [pl.BlockSpec(memory_space=pltpu.SMEM)] * count


LANES = 256
KT = 128
NT = (((1,), (1,)), ((), ()))
TN = (((0,), (0,)), ((), ()))
NN = (((1,), (0,)), ((), ()))


def mm(a, b, dims=NN):
    return lax.dot_general(a, b, dims, preferred_element_type=f32)


def head_mask(h, head_dim, dtype):
    lane = lax.broadcasted_iota(jnp.int32, (1, LANES), 1)
    inside = jnp.logical_and(lane >= h * head_dim, lane < (h + 1) * head_dim)
    return jnp.where(inside, 1.0, 0.0).astype(dtype)


class Fold:
    def __init__(self, n, seg):
        self.n, self.seg, self.half = n, seg, n * seg
        self.tiles = self.half // KT

    def ranges(self, i):
        a = -(-(self.n - i) * self.seg // KT)
        b = -(-(i + 1) * self.seg // KT)
        assert a + b == self.tiles + 2
        return a, b

    def places(self, i, core, paired):
        a, b = self.ranges(i)
        n, seg = self.n, self.seg
        causal = 1 - paired
        up = n + core * (n // 2) + i
        rows_a = (core * n + n - 1 - i) * causal + up * paired
        rows_b = (core * n + i) * causal + up * paired
        keys_a = core * self.tiles * causal
        keys_b = core * self.tiles * causal + a * paired
        lim_a = (n - 1 - i) * seg - (a - 2) * KT + (1 << 20) * paired
        lim_b = i * seg - (b - 2) * KT - (1 << 20) * paired
        return (rows_a, keys_a, lim_a, a), (rows_b, keys_b, lim_b, b)


def natural(tab, n, s):
    upper = lax.div(s, n)
    c = tab[n + s + upper * (2 * n - 1 - 2 * s)]
    return lax.rem(c, 2), lax.div(c, 2), upper


def key_tiles(ref, base, first, count):
    return ref[pl.ds(base + first, count)].reshape(count * KT, LANES)


def tail_mask(seg, limit):
    col = lax.broadcasted_iota(jnp.int32, (seg, 2 * KT), 1)
    row = lax.broadcasted_iota(jnp.int32, (seg, 2 * KT), 0)
    return col - row <= limit


def norm_forward(h, gain, shift):
    mean = jnp.mean(h, axis=1, keepdims=True)
    center = h - mean
    scale = lax.rsqrt(jnp.mean(center * center, axis=1, keepdims=True) + norm_eps)
    n = center * scale
    return n, scale, n * gain + shift


def norm_backward(cot, n, scale, gain):
    dn = cot * gain
    mean = jnp.mean(dn, axis=1, keepdims=True)
    along = jnp.mean(dn * n, axis=1, keepdims=True)
    return scale * (dn - mean - n * along)


def chain(*steps):
    def run():
        for fn, *args in steps:
            fn(*args)

    return run


def window(first, rows, width):
    row = lax.broadcasted_iota(jnp.int32, (rows, width), 0)
    col = lax.broadcasted_iota(jnp.int32, (rows, width), 1)
    return jnp.where(col == row + first, 1.0, 0.0).astype(bf16)


def by_unit(order, steps, last):
    before, todo, behind, unit = [], {}, [], -1
    for name in order:
        if name[0] == "U":
            unit = int(name[1:])
        elif unit < 0:
            before.append(steps[name])
        elif unit == last:
            behind.append(steps[name])
        else:
            todo.setdefault(unit, []).append(steps[name])
    return before, todo, behind


def fill_table(tab, pairs, pairing, chip, n, heads):
    for c in range(n):
        tab[c] = pairs[0, c]
    for a in range(n):
        found = jnp.int32(0)
        for c in range(n):
            found = found + (pairs[0, c] == a).astype(jnp.int32) * c
        tab[n + a] = jnp.minimum(found, n - 1)
    for h in range(heads):
        tab[2 * n + h] = pairing[0, chip * heads + h]


def lse_lane(fold, h, i, g):
    return (h * (fold.n // 2) + i) * 2 + g


def attend_unit(fold, core, h, i, head_dim, tab, q_ref, k_ref, v_ref, o_ref, lse_ref):
    n, seg = fold.n, fold.seg
    paired = tab[2 * n + h]
    pf = paired.astype(f32)
    lanes = head_mask(h, head_dim, f32)
    lanes16 = head_mask(h, head_dim, bf16)
    parts = []
    for rows, keys, limit, count in fold.places(i, core, paired):
        q = q_ref[rows] * lanes16
        tail = mm(q, key_tiles(k_ref, keys, count - 2, 2), NT)
        tail = jnp.where(tail_mask(seg, limit), tail, very_low)
        top = jnp.max(tail, axis=1, keepdims=True)
        main = None
        if count > 2:
            main = mm(q, key_tiles(k_ref, keys, 0, count - 2), NT)
            top = jnp.maximum(top, jnp.max(main, axis=1, keepdims=True))
        parts.append((keys, count, main, tail, top))
    both = jnp.maximum(parts[0][4], parts[1][4])
    joined = jnp.broadcast_to(paired, both.shape) == 1
    outs = []
    for keys, count, main, tail, top in parts:
        top = jnp.where(joined, both, top)
        e = jnp.exp(tail - top)
        total = jnp.sum(e, axis=1, keepdims=True)
        acc = mm(e.astype(bf16), key_tiles(v_ref, keys, count - 2, 2))
        if main is not None:
            e = jnp.exp(main - top)
            total += jnp.sum(e, axis=1, keepdims=True)
            acc += mm(e.astype(bf16), key_tiles(v_ref, keys, 0, count - 2))
        outs.append((top, total, acc))
    (top_a, sum_a, acc_a), (top_b, sum_b, acc_b) = outs
    sum_a, sum_b = sum_a + pf * sum_b, jnp.where(joined, sum_a + sum_b, sum_b)
    acc_a = acc_a + pf * acc_b
    out_a = acc_a * (lanes / sum_a)
    out_b = acc_b * (lanes / sum_b)
    lane = lax.broadcasted_iota(jnp.int32, (1, KT), 1)
    lse = jnp.where(lane == lse_lane(fold, h, i, 0), top_a + jnp.log(sum_a), lse_ref[...])
    lse_ref[...] = jnp.where(lane == lse_lane(fold, h, i, 1), top_b + jnp.log(sum_b), lse)
    far, near, up = core * n + n - 1 - i, core * n + i, n + core * (n // 2) + i
    for at, value in ((far, (1.0 - pf) * out_a), (near, (1.0 - pf) * out_b), (up, pf * out_a)):
        o_ref[at] += value.astype(bf16)


FRONT_ORDER = (
    "ca", "se1", "se2", "ba", "cb", "xs", "cc", "bb", "xt", "se3", "aa1", "xl", "bc", "sw",
    "ab1", "F", "U0", "aa2", "U1", "U2", "U3", "gs1", "ab2", "U4", "aa3", "cs1", "U5", "U6",
    "U7", "ab3", "U8", "bd", "U9", "hs1", "gs2", "U10", "gs3", "U11", "hs2", "hs3", "cs2", "OC",
    "OP", "bs1", "ht1", "cs3", "gt2", "bs2", "gt3", "ht3", "gt1", "ht2", "hl", "gl", "ow", "cw",
    "M1", "bs3", "V1", "bw", "V2",
)


def front_kernel(
    nz, n, heads, head_dim, n_sem,
    pairs, pairing, x_ref, cot_ref, gain_ref, shift_ref, wq_i, wk_i, wv_i, wo_i, w1_i, w2_i,
    xall_o, wqkv_o, q_o, k_o, v_o, on_o, g_o, lse_o, out_o, da_o, dh_o,
    tab, xall, wqkv, q_ref, k_ref, v_ref, o_nat, o_ctx, o_part, o_sum, attn,
    w1, w2, wol, fq, fo, f1, f2, u_ref, z_ref, x1b_ref, acc_ref, n1_ref, r1_ref, dx1_ref, gs, gt,
    ssem, rsem, lsem, fsem, gsem,
):
    p = Place()
    z = p.z
    seg, width = x_ref.shape[1], x_ref.shape[2]
    tok = 2 * seg
    fold = Fold(n, seg)
    d_rows, f_rows = wq_i.shape[0], w2_i.shape[0]
    n_f = w1_i.shape[1] // width
    cols = heads * head_dim
    half = d_rows // 2
    a1_rows, a2_rows = n_f * d_rows // 8, f_rows // 12
    b_first = 8 * a2_rows
    b_rows = (f_rows - b_first) // 2
    locals_ = []

    def keep(src, dst):
        cp = pltpu.make_async_copy(src, dst, lsem.at[len(locals_)])
        cp.start()
        locals_.append(cp)
        return cp

    masters = [
        pltpu.make_async_copy(src, dst, fsem.at[i])
        for i, (src, dst) in enumerate(
            ((wq_i, fq.at[0]), (wk_i, fq.at[1]), (wv_i, fq.at[2]), (w1_i, f1), (w2_i, f2), (wo_i, fo))
        )
    ]
    for cp in masters:
        cp.start()
    own_x = keep(x_ref, xall.at[p.core, p.chip])
    greet(p, (p.sib, p.xn, p.yn, p.dn), nz)
    net = Net(ssem, rsem, n_sem)
    tokens_ag = PlaneGather(net, p, lambda: x_ref, lambda k, q: xall.at[k, q], 2)
    tokens_ag.first()
    can_up, can_down = z < nz - 1, z > 0
    rows = pl.ds(p.core * half, half)
    other = pl.ds(p.other * half, half)

    class Stream:
        def __init__(self, at, after):
            self.up = [net.new() for _ in range(nz)]
            self.down = [net.new() for _ in range(nz)]
            self.at, self.todo = at, {}
            for t in range(1, nz):
                self.todo[t] = []
                for ids, src, frm, to, got, more in (
                    (self.up, z - t, p.down, p.up, z >= t, can_up),
                    (self.down, z + t, p.up, p.down, z + t < nz, can_down),
                ):
                    src = jnp.clip(src, 0, nz - 1)
                    on = jnp.logical_and(got, more)
                    self.todo[t].append((ids, src, frm, to, got, on, after(t, src, at, got)))

        def begin(self):
            own = lambda: self.at(z)
            net.send(self.up[1], own, own, p.up, can_up)
            net.send(self.down[1], own, own, p.down, can_down)

        def step(self, t):
            for ids, src, frm, to, got, on, then in self.todo[t]:
                block = functools.partial(self.at, src)
                net.recv(ids[t], block, frm, got)
                if t + 1 < nz:
                    net.send(ids[t + 1], block, block, to, on)
                then()

    def share(waits, block_of):
        def after(t, src, at, got):
            idx = net.new()
            waits.append((idx, lambda: block_of(src), got))
            return lambda: net.send(idx, lambda: at(src), lambda: at(src), p.sib, got)

        return after

    def spread(gathers, slot_of, count):
        def after(t, src, at, got):
            slot = lambda k, q: slot_of(src, k, q)
            gather = PlaneGather(net, p, lambda: at(src), slot, count, got)
            gathers.setdefault(t, []).append(gather)
            return gather.first

        return after

    def a1_slot(o, k, q):
        start = pl.multiple_of(o * d_rows + lax.rem(q, 2) * a1_rows, 32)
        return w1.at[k * 2 + lax.div(q, 2), pl.ds(start, a1_rows)]

    def a2_slot(o, k, q):
        return w2.at[o, pl.ds(pl.multiple_of((k * 4 + q) * a2_rows, 32), a2_rows)]

    def b_slot(o, k):
        return w2.at[o, pl.ds(pl.multiple_of(b_first + k * b_rows, 32), b_rows)]

    sel_waits, b_waits, c_waits, a1_gathers, a2_gathers = [], [], [], {}, {}
    sel = Stream(lambda o: wqkv.at[o, rows], share(sel_waits, lambda o: wqkv.at[o, other]))
    cs = Stream(lambda o: wol.at[o, p.core], share(c_waits, lambda o: wol.at[o, p.other]))
    a1 = Stream(lambda o: a1_slot(o, p.core, p.chip), spread(a1_gathers, a1_slot, a1_rows))
    a2 = Stream(lambda o: a2_slot(o, p.core, p.chip), spread(a2_gathers, a2_slot, a2_rows))
    bs = Stream(lambda o: b_slot(o, p.core), share(b_waits, lambda o: b_slot(o, p.other)))

    for cp in masters[:3]:
        cp.wait()
    for chip in range(4):

        @pl.when(p.chip == chip)
        def _():
            for m in range(3):
                mine = fq[m, :, chip * cols : (chip + 1) * cols].astype(bf16)
                wqkv[z, :, m * LANES : m * LANES + cols] = mine

    for m in range(3):
        wqkv[z, :, m * LANES + cols : (m + 1) * LANES] = jnp.zeros((d_rows, LANES - cols), bf16)
    sel.begin()
    fill_table(tab, pairs, pairing, p.chip, n, heads)
    o_nat[...] = jnp.zeros(o_nat.shape, bf16)
    lse_o[...] = jnp.zeros(lse_o.shape, f32)
    part, swaps = net.new(), [net.new() for _ in range(3)]
    partners = ((p.chip_d, p.dn), (p.chip_x, p.xn), (p.chip_y, p.yn))

    def cast_inner():
        masters[3].wait()
        for f in range(n_f):
            at = pl.ds(pl.multiple_of(z * d_rows, 32), d_rows)
            w1[f, at, :] = f1[:, f * width : (f + 1) * width].astype(bf16)

    def cast_outer():
        masters[4].wait()

        def cast(i, _):
            at = pl.ds(pl.multiple_of(i * 64, 64), 64)
            w2[z, at, :] = f2[at, :].astype(bf16)
            return 0

        lax.fori_loop(0, f_rows // 64, cast, 0)

    def cast_output():
        masters[5].wait()
        four = jnp.concatenate([gain_ref[...], shift_ref[...], jnp.zeros((12, d_rows), f32)], axis=0)
        norms = mm(four.astype(bf16), window(z * d_rows, d_rows, width)).astype(bf16)
        for k in range(2):
            wol[z, k, :half, :] = fo[k * half : (k + 1) * half, :].astype(bf16)
            wol[z, k, half:, :] = norms

    def tokens_last():
        own_x.wait()
        tokens_ag.last()

    def wait_all(waits):
        for idx, block, got in waits:
            net.recv(idx, block, p.sib, got)

    def project_all():
        keep(xall, xall_o)
        keep(wqkv, wqkv_o)

        def four(i, _):
            tokens = jnp.concatenate([xall[natural(tab, n, 4 * i + u)] for u in range(4)], axis=0)
            qkv = mm(tokens, wqkv[...].reshape(-1, 3 * LANES))
            q = (qkv[:, :LANES].astype(bf16).astype(f32) * score_scale).astype(bf16)
            q_ref[pl.ds(4 * i, 4)] = q.reshape(4, seg, LANES)
            at = pl.ds(i * (4 * seg // KT), 4 * seg // KT)
            k_ref[at] = qkv[:, LANES : 2 * LANES].astype(bf16).reshape(-1, KT, LANES)
            v_ref[at] = qkv[:, 2 * LANES :].astype(bf16).reshape(-1, KT, LANES)
            return 0

        lax.fori_loop(0, n // 2, four, 0)
        for src, dst in ((q_ref, q_o), (k_ref, k_o), (v_ref, v_o)):
            keep(src, dst)

    def heads_out():
        keep(o_nat, on_o)
        for core_is in range(2):
            for q in range(n // 2):
                a = tab[2 * q + core_is]
                for u, s in ((0, a), (1, 2 * n - 1 - a)):
                    o_ctx[core_is, q, u * seg : (u + 1) * seg, :] = o_nat[s]
        net.send(part, o_ctx.at[p.other], o_part, p.sib)

    def owners_out():
        net.recv(part, o_part, p.sib)
        for idx, (chip, dev) in zip(swaps, partners):
            o_sum[chip] = o_ctx[p.core, chip] + o_part[chip]
            net.send(idx, o_sum.at[chip], attn.at[p.chip], dev)
        attn[p.chip] = o_ctx[p.core, p.chip] + o_part[p.chip]

    def owners_wait():
        for idx, (chip, dev) in zip(swaps, partners):
            net.recv(idx, attn.at[chip], dev)

    wo_of = lambda o: jnp.concatenate([wol[o, 0, :half, :], wol[o, 1, :half, :]], axis=0)
    kept = {}

    def first_norm():
        vec = wol[0, 0, half:, :].astype(f32)
        for o in range(1, nz):
            vec = vec + wol[o, 0, half:, :].astype(f32)
        h1 = x_ref[...].reshape(tok, width).astype(f32)
        for o in range(nz):
            h1 = h1 + mm(attn[o, :, :cols], wo_of(o))
        n1, r1, x1 = norm_forward(h1, vec[0:1], vec[2:3])
        n1_ref[...] = n1
        r1_ref[...] = jnp.broadcast_to(r1, (tok, 128))
        x1b_ref[...] = x1.astype(bf16)
        acc_ref[...] = x1
        kept["vec"] = vec

    def inner_all():
        def up(f, _):
            u = mm(x1b_ref[...], w1[f])
            cdf = 0.5 + 0.5 * lax.erf(u * (0.5**0.5))
            z_ref[f] = (u * cdf).astype(bf16)
            u_ref[f] = cdf + u * jnp.exp(-0.5 * u * u) * 0.3989422804014327
            return 0

        lax.fori_loop(0, n_f, up, 0)

    def outer_all():
        def add(f, _):
            acc_ref[...] += mm(z_ref[f], w2[f])
            return 0

        lax.fori_loop(0, n_f, add, 0)

    def each(gathers, t, stage):
        for gather in gathers[t]:
            getattr(gather, stage)()

    def all_last(gathers):
        for t in gathers:
            each(gathers, t, "last")

    steps = {
        "ca": cast_inner, "cb": cast_outer, "cc": cast_output, "ba": a1.begin, "bb": a2.begin,
        "bc": cs.begin, "bd": bs.begin, "xs": tokens_ag.second, "xt": tokens_ag.third,
        "xl": tokens_last, "sw": lambda: wait_all(sel_waits), "cw": lambda: wait_all(c_waits),
        "bw": lambda: wait_all(b_waits), "F": project_all, "OC": heads_out, "OP": owners_out,
        "ow": owners_wait, "M1": first_norm, "V1": inner_all, "V2": outer_all,
        "gl": lambda: all_last(a1_gathers), "hl": lambda: all_last(a2_gathers),
    }
    for t in range(1, nz):
        for name, stream in (("se", sel), ("cs", cs), ("aa", a1), ("ab", a2), ("bs", bs)):
            steps[f"{name}{t}"] = functools.partial(stream.step, t)
        for name, gathers in (("g", a1_gathers), ("h", a2_gathers)):
            steps[f"{name}s{t}"] = functools.partial(each, gathers, t, "second")
            steps[f"{name}t{t}"] = functools.partial(each, gathers, t, "third")
    units = n // 2
    before, todo, behind = by_unit(FRONT_ORDER, steps, units * heads - 1)
    for step in before:
        step()

    def head(h, _):
        for i in range(units):
            attend_unit(fold, p.core, h, i, head_dim, tab, q_ref, k_ref, v_ref, o_nat, lse_o)
            for hh in range(heads):
                if hh * units + i in todo:
                    pl.when(h == hh)(chain(*((step,) for step in todo[hh * units + i])))
        return 0

    lax.fori_loop(0, heads, head, 0)
    for step in behind:
        step()
    vec = kept["vec"]
    gain1, gain2, shift2 = vec[0:1], vec[1:2], vec[3:4]
    n2, r2, out = norm_forward(acc_ref[...], gain2, shift2)
    out_o[...] = out.astype(bf16)
    cot = cot_ref[...].astype(f32)
    d_gain2 = jnp.sum(cot * n2, axis=0, keepdims=True)
    d_shift2 = jnp.sum(cot, axis=0, keepdims=True)
    dh2 = norm_backward(cot, n2, r2, gain2)
    dx1_ref[...] = dh2
    df = dh2.astype(bf16)
    first1, first2 = f_rows, f_rows + n_f * d_rows

    def grads_out(f, slot):
        yield pltpu.make_async_copy(gs.at[slot, 0], g_o.at[f, pl.ds(0, f_rows)], gsem.at[slot, 0])
        for o in range(nz):
            at = pl.ds(pl.multiple_of(first1 + f * d_rows, 32), d_rows)
            src = gs.at[slot, 1, pl.ds(o * d_rows, d_rows)]
            yield pltpu.make_async_copy(src, g_o.at[o, at], gsem.at[slot, 1 + o])

    def back(f, _):
        slot = lax.rem(f, 2)

        @pl.when(f >= 2)
        def _():
            for cp in grads_out(f - 2, slot):
                cp.wait()

        gs[slot, 0] = mm(z_ref[f], df, TN).astype(bf16)
        du = (mm(df, w2[f], NT) * u_ref[f]).astype(bf16)
        gs[slot, 1] = mm(x1b_ref[...], du, TN).astype(bf16)
        for cp in grads_out(f, slot):
            cp.start()
        dx1_ref[...] += mm(du, w1[f], NT)
        return 0

    lax.fori_loop(0, n_f, back, 0)
    d_x1 = dx1_ref[...]
    n1 = n1_ref[...]
    d_gain1 = jnp.sum(d_x1 * n1, axis=0, keepdims=True)
    d_shift1 = jnp.sum(d_x1, axis=0, keepdims=True)
    dh1 = norm_backward(d_x1, n1, r1_ref[:, :1], gain1)
    dh_o[...] = dh1
    dy = dh1.astype(bf16)
    norms = jnp.concatenate([d_gain1, d_gain2, d_shift1, d_shift2], axis=0).astype(bf16)
    ends = []
    for o in range(nz):
        da_o[o, :, :cols] = mm(dy, wo_of(o), NT).astype(bf16)
        da_o[o, :, cols:] = jnp.zeros((tok, LANES - cols), bf16)
        gt[o, :d_rows, :] = mm(attn[o, :, :cols], dy, TN).astype(bf16)
        gt[o, d_rows:, :] = jnp.zeros((gt.shape[1] - d_rows, width), bf16)
        gt[o, d_rows : d_rows + 4, :] = norms
        ends.append(pltpu.make_async_copy(gt.at[o], g_o.at[o, pl.ds(first2, gt.shape[1])], fsem.at[o]))
        ends[-1].start()
    for f in range(max(n_f - 2, 0), n_f):
        for cp in grads_out(f, f % 2):
            cp.wait()
    for cp in ends:
        cp.wait()
    net.finish()
    for cp in locals_[1:]:
        cp.wait()


def front(nz, n, heads, head_dim, total, pairs, pairing, x_in, cot, gains, shifts, weights):
    tok, width = x_in.shape
    seg = tok // 2
    d_rows, f_rows = weights[0].shape[0], weights[5].shape[0]
    n_f = weights[4].shape[1] // width
    n_sem = 11 * (4 * (nz - 1) + 1) + 5 * 2 * nz + 3 * 2 * (nz - 1) + 4
    wide, tiled = (2 * n, seg, LANES), (tok * n // KT, KT, LANES)
    shapes = [(2, 4, 2, seg, width), (nz, d_rows, 3 * LANES), wide, tiled, tiled, wide]
    block = (4, tok, LANES)
    sds = jax.ShapeDtypeStruct
    vb = lambda *s: pltpu.VMEM(s, bf16)
    vf = lambda *s: pltpu.VMEM(s, f32)
    return pl.pallas_call(
        functools.partial(front_kernel, nz, n, heads, head_dim, n_sem),
        out_shape=tuple(sds(s, bf16) for s in shapes)
        + (
            sds((nz, total, width), bf16),
            sds((seg, KT), f32),
            sds((tok, width), bf16),
            sds(block, bf16),
            sds((tok, width), f32),
        ),
        in_specs=smem(2) + vmem(4) + hbm(6),
        out_specs=tuple(hbm(7) + vmem(4)),
        scratch_shapes=[pltpu.SMEM((2 * n + heads,), jnp.int32)]
        + [vb(*s) for s in shapes]
        + [
            vb(2, *block),
            vb(*block),
            vb(*block),
            vb(*block),
            vb(n_f, nz * d_rows, width),
            vb(nz, f_rows, width),
            vb(nz, 2, d_rows // 2 + 16, width),
            vf(3, d_rows, width),
            vf(d_rows, width),
            vf(d_rows, n_f * width),
            vf(f_rows, width),
            vf(n_f, tok, width),
            vb(n_f, tok, width),
            vb(tok, width),
            vf(tok, width),
            vf(tok, width),
            vf(tok, 128),
            vf(tok, width),
            vb(2, 2, f_rows, width),
            vb(nz, total - f_rows - n_f * d_rows, width),
            pltpu.SemaphoreType.DMA((n_sem,)),
            pltpu.SemaphoreType.DMA((n_sem,)),
            pltpu.SemaphoreType.DMA((12,)),
            pltpu.SemaphoreType.DMA((6,)),
            pltpu.SemaphoreType.DMA((2, 1 + nz)),
        ],
        compiler_params=comm_params(0),
        name="front",
    )(pairs, pairing, x_in.reshape(2, seg, width), cot, gains, shifts, *weights)


def add_into(dst, src, rows):
    chunk = max(c for c in range(16, min(rows, 160) + 1, 16) if rows % c == 0)

    def step(i, _):
        at = pl.ds(pl.multiple_of(i * chunk, chunk), chunk)
        to, frm = of(dst), of(src)
        to[at, :] = to[at, :] + frm[at, :]
        return 0

    lax.fori_loop(0, rows // chunk, step, 0)


class Slot:
    def __init__(self, ref, o):
        self.ref, self.o = ref, o

    def __call__(self):
        return self.ref.at[self.o]

    @property
    def at(self):
        return self().at


class PlaneSum:
    def __init__(self, net, place, block, rows, rx0, ry1, ry0, rx1):
        p = place
        self.net, self.place = net, place
        self.rx0, self.ry1, self.ry0, self.rx1 = rx0, ry1, ry0, rx1
        self.h = rows // 2
        h0, h1 = pl.ds(0, self.h), pl.ds(self.h, self.h)
        far_x, far_y = 1 - p.x, 1 - p.y
        self.block, self.h0, self.h1 = block, h0, h1
        self.far_x, self.far_y = far_x, far_y
        self.to_x = [2 * j + far_x for j in range(2)]
        self.to_y = [2 * far_y + j for j in range(2)]
        self.on_y, self.on_x = 2 * far_y + p.x, 2 * p.y + far_x
        self.ids = [net.new() for _ in range(6)]

    def part(self, index, half):
        return lambda: self.block(index).at[half]

    def first(self):
        n, p, i = self.net, self.place, self.ids
        for j in range(2):
            n.send(i[j], self.part(self.to_x[j], self.h0), lambda j=j: self.rx0.at[j], p.xn)
            n.send(i[2 + j], self.part(self.to_y[j], self.h1), lambda j=j: self.ry1.at[j], p.yn)

    def second(self):
        n, p, i = self.net, self.place, self.ids
        on_y, on_x = self.part(self.on_y, self.h0), self.part(self.on_x, self.h1)
        mine0, mine1 = self.part(p.chip, self.h0), self.part(p.chip, self.h1)
        for j in range(2):
            n.recv(i[j], lambda j=j: self.rx0.at[j], p.xn)
        add_into(on_y, lambda: self.rx0.at[self.far_y], self.h)
        n.send(i[4], on_y, self.ry0, p.yn)
        for j in range(2):
            n.recv(i[2 + j], lambda j=j: self.ry1.at[j], p.yn)
        add_into(on_x, lambda: self.ry1.at[self.far_x], self.h)
        n.send(i[5], on_x, self.rx1, p.xn)
        add_into(mine0, lambda: self.rx0.at[p.y], self.h)
        add_into(mine1, lambda: self.ry1.at[p.x], self.h)

    def third(self):
        n, p, i = self.net, self.place, self.ids
        n.recv(i[4], self.ry0, p.yn)
        add_into(self.part(p.chip, self.h0), self.ry0, self.h)
        n.recv(i[5], self.rx1, p.xn)
        add_into(self.part(p.chip, self.h1), self.rx1, self.h)


class LineSum:
    def __init__(self, net, place, nz, whole, low, high, parts, rows):
        p, z, top = place, place.z, nz - 1
        self.net, self.top, self.parts, self.rows, self.whole = net, top, parts, rows, whole
        sides = (
            ([net.new() for _ in range(nz)], low, z, -1, p.down, p.up),
            ([net.new() for _ in range(nz)], high, top - z, 1, p.up, p.down),
        )
        self.todo = {}
        for t in range(nz):
            self.todo[t] = []
            for ids, buf, depth, sign, frm, to in sides:
                owner = jnp.clip(top - t + z if sign < 0 else t + z - top, 0, top)
                takes = jnp.logical_and(depth > 0, depth <= t)
                self.todo[t].append(
                    (ids, owner, buf, takes, depth <= t, frm, to)
                )

    def step(self, t):
        n = self.net
        for ids, owner, buf, takes, sends, frm, to in self.todo[t]:
            whole = functools.partial(self.whole, owner)
            landed = lambda buf=buf, owner=owner: buf.at[owner]

            def take(ids=ids, whole=whole, landed=landed, frm=frm):
                n.recv(ids[t - 1], landed, frm)
                if self.parts is None:
                    add_into(whole, landed, self.rows)
                else:
                    for j in range(self.parts):
                        add_into(
                            lambda j=j: whole().at[j], lambda j=j: landed().at[j], self.rows
                        )

            if t > 0:
                maybe(takes, take)
            if t < self.top:
                n.send(ids[t], whole, landed, to, sends)


def attend_back_unit(
    fold, core, h, i, head_dim, tab, q_ref, k_ref, v_ref, o_ref, lse_ref, da_ref,
    dcat_ref, dk_ref, dv_ref,
):
    n, seg, half = fold.n, fold.seg, fold.half
    paired = tab[2 * n + h]
    pf = paired.astype(f32)
    lanes = head_mask(h, head_dim, f32)
    lanes16 = head_mask(h, head_dim, bf16)
    dqs = []
    places = fold.places(i, core, paired)
    for g, (rows, keys, limit, count) in enumerate(places):
        q = q_ref[rows] * lanes16
        k, c, upper = natural(tab, n, rows)
        da = da_ref[k, c, upper] * lanes16
        delta = jnp.sum(
            da.astype(f32) * o_ref[rows].astype(f32), axis=1, keepdims=True
        )
        lane = lax.broadcasted_iota(jnp.int32, (1, KT), 1) == lse_lane(fold, h, i, g)
        lse = jnp.sum(jnp.where(lane, lse_ref[...], 0.0), axis=1, keepdims=True)
        dq = None
        pieces = [(count - 2, 2, True)]
        if count > 2:
            pieces.append((0, count - 2, False))
        for first, size, masked in pieces:
            kt = key_tiles(k_ref, keys, first, size)
            vt = key_tiles(v_ref, keys, first, size)
            pr = jnp.exp(mm(q, kt, NT) - lse)
            if masked:
                pr = jnp.where(tail_mask(seg, limit), pr, 0.0)
            ds = (pr * (mm(da, vt, NT) - delta)).astype(bf16)
            part = mm(ds, kt)
            dq = part if dq is None else dq + part
            dv = mm(pr.astype(bf16), da, TN)
            dk = mm(ds, q, TN)
            at = pl.ds(first * KT, size * KT)
            if g == 0 or masked:
                dk_ref[at, :] += dk
                dv_ref[at, :] += dv
            else:
                beyond = pl.ds(places[0][3] * KT, size * KT)
                dk_ref[at, :] += (1.0 - pf) * dk
                dv_ref[at, :] += (1.0 - pf) * dv
                dk_ref[beyond, :] += pf * dk
                dv_ref[beyond, :] += pf * dv
        dqs.append(dq)
    scaled = lanes * score_scale
    dq_a, dq_b = (dqs[0] + pf * dqs[1]) * scaled, dqs[1] * scaled
    far, near, up = core * n + n - 1 - i, core * n + i, n + core * (n // 2) + i
    for at, value in ((far, (1.0 - pf) * dq_a), (near, (1.0 - pf) * dq_b), (up, pf * dq_a)):
        dcat_ref[at, :, :LANES] += value.astype(bf16)


def place_key_grads(fold, core, paired, dk_ref, dv_ref, dcat_ref):
    n, seg, half = fold.n, fold.seg, fold.half
    pf = paired.astype(f32)

    def spread(j, _):
        at = pl.ds(pl.multiple_of(j * seg, seg), seg)
        for src, lanes in ((dk_ref, slice(LANES, 2 * LANES)), (dv_ref, slice(2 * LANES, None))):
            value = src[at, :]
            dcat_ref[core * n + j, :, lanes] += ((1.0 - pf) * value).astype(bf16)
            dcat_ref[j, :, lanes] += (pf * value).astype(bf16)
        return 0

    lax.fori_loop(0, n, spread, 0)


BACKWARD_ORDER = (
    "dr", "c1", "c0", "s3", "p1f", "dw", "U0", "lb0", "s2", "p0f", "U1", "U2", "U3", "U4",
    "p1s", "c2", "U5", "p2f", "c3", "U6", "lb1", "U7", "U8", "U9", "p3f", "U10", "U11", "p0s",
    "DXo", "lb2", "p1t", "p3s", "p0t", "p2s", "DXm", "xa", "la0", "xsf", "DW", "p3t", "wa",
    "lb3", "wl0", "p2t", "la1", "pbf", "xss", "wl1", "pbs", "la2", "pbt", "fbf", "fbs", "xst",
    "la3", "faf", "wl2", "wl3", "wff", "fbt", "fas", "wfs", "tok", "fat", "wft", "fal", "wfl",
    "fbl", "dwo",
)


def backward_kernel(
    nz, n, heads, head_dim, rb, n_sem,
    pairs, pairing, g_ref, da_in, dh_ref, xall_i, wqkv_i, q_i, k_i, v_i, on_i, lse_ref,
    gsum_o, dtok_o, dw_o,
    tab, g_kept, g_sib, g_rx0, g_ry1, g_ry0, g_rx1, g_low, g_high,
    b_low, b_high, b_rx0, b_ry1, b_ry0, b_rx1,
    x_part, x_sib, x_rx0, x_ry1, x_ry0, x_rx1, w_part, w_sib, w_low, w_high, w_all,
    da_all, xall, wqkv, q_ref, k_ref, v_ref, on_ref, dcat, dk_ref, dv_ref, dw_acc,
    ssem, rsem, lsem,
):
    p = Place()
    z = p.z
    seg, width = xall.shape[3], xall.shape[4]
    tok = 2 * seg
    fold = Fold(n, seg)
    rows = g_ref.shape[3]
    ra = rows - rb
    ax, bx = pl.ds(0, ra), pl.ds(ra, rb)
    order = line_order(nz)
    local = []

    def fetch(src, dst):
        cp = pltpu.make_async_copy(src, dst, lsem.at[len(local)])
        cp.start()
        local.append(cp)
        return cp

    net = Net(ssem, rsem, n_sem)
    own_da = fetch(da_in.at[p.chip], da_all.at[p.core, p.chip])
    own_g = {o: fetch(g_ref.at[o, p.core], g_kept.at[o]) for o in order}
    greet(p, (p.sib, p.xn, p.yn, p.dn), nz)
    swaps = [net.new() for _ in range(7)]
    partners = ((p.chip_d, p.dn), (p.chip_x, p.xn), (p.chip_y, p.yn))
    for i, (chip, dev) in enumerate(partners):
        net.send(swaps[i], da_in.at[chip], da_all.at[p.core, p.chip], dev)
    net.send(swaps[3], da_in.at[p.chip], da_all.at[p.core, p.chip], p.sib)
    sib_ids = {o: net.new() for o in order}

    def to_sib(o):
        net.send(sib_ids[o], lambda: g_ref.at[o, p.other], lambda: g_sib.at[o], p.sib)

    to_sib(order[0])
    to_sib(order[1])
    att_in = [
        fetch(src, dst)
        for src, dst in (
            (q_i, q_ref), (k_i, k_ref), (v_i, v_ref), (on_i, on_ref), (xall_i, xall), (wqkv_i, wqkv),
        )
    ]
    fill_table(tab, pairs, pairing, p.chip, n, heads)
    dcat[...] = jnp.zeros(dcat.shape, bf16)

    plane = {
        o: PlaneSum(
            net, p, lambda q, o=o: g_kept.at[o, q].at[ax], ra,
            *(Slot(r, o) for r in (g_rx0, g_ry1, g_ry0, g_rx1)),
        )
        for o in order
    }
    line_a = LineSum(net, p, nz, lambda o: g_kept.at[o, p.chip].at[ax], g_low, g_high, None, ra)
    line_b = LineSum(net, p, nz, lambda o: g_kept.at[o, :, bx], b_low, b_high, n // 2, rb)
    plane_b = PlaneSum(
        net, p, lambda q: g_kept.at[z, q].at[bx], rb, b_rx0, b_ry1, b_ry0, b_rx1
    )

    def chip_sum(o):
        net.recv(sib_ids[o], lambda: g_sib.at[o], p.sib)
        pltpu.make_async_copy(g_ref.at[o, p.core], g_kept.at[o], lsem.at[1 + order.index(o)]).wait()
        for q in range(n // 2):
            add_into(lambda q=q: g_kept.at[o, q], lambda q=q: g_sib.at[o, q], rows)

    d = wqkv.shape[1]
    half = d // 2
    x_id, w_id = net.new(), net.new()
    w_line = LineSum(net, p, nz, lambda o: w_part.at[p.core, o], w_low, w_high, None, half)
    xs = PlaneSum(net, p, lambda q: x_part.at[p.core, q], tok, x_rx0, x_ry1, x_ry0, x_rx1)
    final_a = PlaneGather(
        net, p, lambda: g_kept.at[z, p.chip].at[ax], lambda k, q: gsum_o.at[k, q].at[ax], ra
    )
    final_b = PlaneGather(
        net, p, lambda: g_kept.at[z, p.chip].at[bx], lambda k, q: gsum_o.at[k, q].at[bx], rb
    )
    w_final = PlaneGather(net, p, lambda: w_part.at[p.core, z], lambda k, q: w_all.at[k, q], half)
    cols = heads * head_dim

    def da_forward():
        for i, chip, dev in ((1, p.chip_x, p.xn), (2, p.chip_y, p.yn), (0, p.chip_d, p.dn)):
            block = lambda chip=chip: da_all.at[p.core, chip]
            net.recv(swaps[i], block, dev)
            net.send(swaps[4 + i], block, block, p.sib)

    def da_wait():
        for i, chip in ((3, p.chip), (5, p.chip_x), (6, p.chip_y), (4, p.chip_d)):
            net.recv(swaps[i], lambda chip=chip: da_all.at[p.other, chip], p.sib)
        own_da.wait()
        for cp in att_in:
            cp.wait()

    def block_grads(k, q):
        a = tab[2 * q + k]
        return jnp.concatenate([dcat[a], dcat[2 * n - 1 - a]], axis=0)

    def weight_grads():
        dw_acc[...] = jnp.zeros(dw_acc.shape, f32)

        def weights(c, _):
            k, q = lax.rem(c, 2), c // 2
            dw_acc[...] += mm(xall[k, q].reshape(tok, width), block_grads(k, q), TN)
            return 0

        lax.fori_loop(0, n, weights, 0)
        for o in range(nz):
            w_part[0, o] = dw_acc[o * d : o * d + half].astype(bf16)
            w_part[1, o] = dw_acc[o * d + half : (o + 1) * d].astype(bf16)
        net.send(w_id, w_part.at[p.other], w_sib, p.sib)

    def weight_sum():
        net.recv(w_id, w_sib, p.sib)
        for o in range(nz):
            add_into(w_part.at[p.core, o], w_sib.at[o], half)

    def tokens_of(k):
        def one(q, _):
            w = wqkv[...].reshape(-1, 3 * LANES)
            x_part[k, q] = mm(block_grads(k, q), w, NT).astype(bf16)
            return 0

        lax.fori_loop(0, n // 2, one, 0)

    def tokens_other():
        tokens_of(p.other)
        net.send(x_id, x_part.at[p.other], x_sib, p.sib)

    def tokens_sum():
        net.recv(x_id, x_sib, p.sib)
        for q in range(n // 2):
            add_into(x_part.at[p.core, q], x_sib.at[q], tok)

    def tokens_out():
        def add_tokens(i, _):
            at = pl.ds(pl.multiple_of(i * 32, 32), 32)
            dtok_o[at, :] = (dh_ref[at, :] + x_part[p.core, p.chip, at, :].astype(f32)).astype(bf16)
            return 0

        lax.fori_loop(0, tok // 32, add_tokens, 0)

    def own_w():
        return pltpu.make_async_copy(
            w_part.at[p.core, z], w_all.at[p.core, p.chip], lsem.at[31]
        )

    def w_final_first():
        w_final.first()
        own_w().start()

    def w_out():
        own_w().wait()
        for j in range(3):
            for k in range(2):
                dw_o[j, k * half : (k + 1) * half, :] = jnp.concatenate(
                    [w_all[k, q][:, j * LANES : j * LANES + cols] for q in range(4)], axis=1
                )

    steps = {
        "dr": da_forward, "dw": da_wait, "DW": weight_grads, "wa": weight_sum,
        "DXo": tokens_other, "DXm": lambda: tokens_of(p.core), "xa": tokens_sum, "tok": tokens_out,
        "dwo": w_out, "wff": w_final_first,
    }
    for k, o in enumerate(order):
        steps[f"s{k}"] = functools.partial(to_sib, o)
        steps[f"c{k}"] = functools.partial(chip_sum, o)
        steps[f"p{k}f"], steps[f"p{k}s"] = plane[o].first, plane[o].second
        steps[f"p{k}t"] = plane[o].third
    for name, line in (("la", line_a), ("lb", line_b), ("wl", w_line)):
        for t in range(nz):
            steps[f"{name}{t}"] = functools.partial(line.step, t)
    for name, thing in (("pb", plane_b), ("xs", xs), ("fa", final_a), ("fb", final_b), ("wf", w_final)):
        for stage in ("first", "second", "third", "last"):
            if hasattr(thing, stage):
                steps.setdefault(name + stage[0], getattr(thing, stage))
    units = n // 2
    before, todo, behind = by_unit(BACKWARD_ORDER, steps, units * heads - 1)
    for step in before:
        step()

    def head(h, _):
        dk_ref[...] = jnp.zeros(dk_ref.shape, f32)
        dv_ref[...] = jnp.zeros(dv_ref.shape, f32)
        for i in range(units):
            attend_back_unit(
                fold, p.core, h, i, head_dim, tab, q_ref, k_ref, v_ref, on_ref, lse_ref, da_all,
                dcat, dk_ref, dv_ref,
            )
            for hh in range(heads):
                if hh * units + i in todo:
                    pl.when(h == hh)(chain(*((step,) for step in todo[hh * units + i])))
        place_key_grads(fold, p.core, tab[2 * n + h], dk_ref, dv_ref, dcat)
        return 0

    lax.fori_loop(0, heads, head, 0)
    for step in behind:
        step()
    own_sum = fetch(g_kept.at[z, p.chip], gsum_o.at[p.core, p.chip])
    own_sum.wait()
    net.finish()


def line_order(nz):
    order = []
    for i in range((nz + 1) // 2):
        for o in (nz - 1 - i, i):
            if o not in order:
                order.append(o)
    return order


def backward(
    nz, n, heads, head_dim, rb, pairs, pairing, grads, da, dh, xall, wqkv, q, k, v, on, lse
):
    rows, width = grads.shape[3], grads.shape[4]
    seg = xall.shape[3]
    tok = 2 * seg
    d_rows = wqkv.shape[1]
    half = d_rows // 2
    ra = rows - rb
    n_sem = 6 * (nz + 2) + 6 * nz + nz + 9 + 33 + 2
    sds = jax.ShapeDtypeStruct
    vm = lambda *shape: pltpu.VMEM(shape, bf16)
    wide, tiled = (2 * n, seg, LANES), (tok * n // KT, KT, LANES)
    da = da.reshape(4, 2, seg, LANES)
    return pl.pallas_call(
        functools.partial(backward_kernel, nz, n, heads, head_dim, rb, n_sem),
        out_shape=(
            sds(grads.shape[1:], bf16),
            sds((tok, width), bf16),
            sds((3, d_rows, width), bf16),
        ),
        in_specs=smem(2) + hbm(2) + vmem(1) + hbm(6) + vmem(1),
        out_specs=tuple(hbm(1) + vmem(2)),
        scratch_shapes=[
            pltpu.SMEM((2 * n + heads,), jnp.int32),
            vm(nz, 4, rows, width),
            vm(nz, 4, rows, width),
            vm(nz, 2, ra // 2, width),
            vm(nz, 2, ra // 2, width),
            vm(nz, ra // 2, width),
            vm(nz, ra // 2, width),
            vm(nz, ra, width),
            vm(nz, ra, width),
            vm(nz, 4, rb, width),
            vm(nz, 4, rb, width),
            vm(2, rb // 2, width),
            vm(2, rb // 2, width),
            vm(rb // 2, width),
            vm(rb // 2, width),
            vm(2, 4, tok, width),
            vm(4, tok, width),
            vm(2, tok // 2, width),
            vm(2, tok // 2, width),
            vm(tok // 2, width),
            vm(tok // 2, width),
            vm(2, nz, half, width),
            vm(nz, half, width),
            vm(nz, half, width),
            vm(nz, half, width),
            vm(2, 4, half, width),
            vm(2, 4, 2, seg, LANES),
            vm(2, 4, 2, seg, width),
            vm(nz, d_rows, width),
            vm(*wide),
            vm(*tiled),
            vm(*tiled),
            vm(*wide),
            vm(2 * n, seg, 3 * LANES),
            pltpu.VMEM((seg * n, LANES), f32),
            pltpu.VMEM((seg * n, LANES), f32),
            pltpu.VMEM((width, 3 * LANES), f32),
            pltpu.SemaphoreType.DMA((n_sem,)),
            pltpu.SemaphoreType.DMA((n_sem,)),
            pltpu.SemaphoreType.DMA((32,)),
        ],
        compiler_params=comm_params(1),
        name="backward",
    )(pairs, pairing, grads, da, dh, xall, wqkv, q, k, v, on, lse)


def finish_kernel(outer, inner, output, norms, dw, result, tokens, *outs):
    outer_o, inner_o, output_o, query_o, key_o, value_o, gain_o, shift_o, result_o, tokens_o = outs
    outer_o[...] = outer[...].astype(f32)
    inner_o[...] = inner[...].astype(f32)
    output_o[...] = output[...].astype(f32)
    for j, out in enumerate((query_o, key_o, value_o)):
        out[...] = dw[j].astype(f32)
    result_o[...] = result[...]
    tokens_o[...] = tokens[...]

    @pl.when(pl.program_id(0) == 0)
    def _():
        rows, width = inner_o.shape
        first = lax.axis_index("fsdp") * rows
        mine = mm(norms[:16, :], window(first, rows, width), NT)
        gain_o[...] = mine[0:2]
        shift_o[...] = mine[2:4]


def finish(gsum, dw, result, dtok, d_rows, f_rows, n_f):
    tok, width = result.shape
    used = f_rows + n_f * d_rows + d_rows
    o_rows, s_rows, t_rows = f_rows // n_f, d_rows // n_f, tok // n_f
    tail = gsum.shape[0] - used
    sds = jax.ShapeDtypeStruct
    square, pair = (d_rows, width), (2, d_rows)
    strip = lambda rows, first=0: pl.BlockSpec((rows, width), lambda f: (first + f, 0))
    return pl.pallas_call(
        finish_kernel,
        grid=(n_f,),
        out_shape=(sds((f_rows, width), f32), sds((d_rows, n_f * width), f32))
        + (sds(square, f32),) * 4
        + (sds(pair, f32),) * 2
        + (sds((tok, width), bf16),) * 2,
        in_specs=[
            strip(o_rows),
            strip(d_rows, f_rows // d_rows),
            strip(s_rows, (used - d_rows) // s_rows),
            pl.BlockSpec((tail, width), lambda f: (used // tail, 0)),
            pl.BlockSpec((3, s_rows, width), lambda f: (0, f, 0)),
            strip(t_rows),
            strip(t_rows),
        ],
        out_specs=(strip(o_rows), pl.BlockSpec((d_rows, width), lambda f: (0, f)))
        + (strip(s_rows),) * 4
        + (pl.BlockSpec(pair, lambda f: (0, 0)),) * 2
        + (strip(t_rows),) * 2,
        compiler_params=pltpu.CompilerParams(vmem_limit_bytes=60 << 20),
        name="finish",
    )(gsum, gsum, gsum, gsum, dw, result, dtok)


def fast_body(
    tokens,
    w_query,
    w_key,
    w_value,
    w_output,
    w_inner,
    w_outer,
    ln_gain,
    ln_bias,
    pairing,
    block_pairs,
    cotangent,
):
    tok, width = tokens.shape[1], tokens.shape[2]
    n_ctx, nz = lax.axis_size("ctx"), lax.axis_size("fsdp")
    heads = pairing.shape[1]
    my_heads, head_dim = heads // 4, width // heads
    d_rows = w_query.shape[0]
    f_rows, ff = w_outer.shape[0], w_inner.shape[1]
    n_f = ff // width
    used = f_rows + n_f * d_rows + d_rows
    total = -(-(used + 4) // 256) * 256
    weights = (w_query, w_key, w_value, w_output, w_inner, w_outer)
    xall, wqkv, q, k, v, on, grads, lse, result, da, d_h1 = front(
        nz, n_ctx, my_heads, head_dim, total, block_pairs, pairing, tokens[0], cotangent[0],
        ln_gain.T, ln_bias.T, weights,
    )
    grads = grads.reshape(nz, 2, 4, total // 8, width)
    gsum, dtok, dw = backward(
        nz, n_ctx, my_heads, head_dim, 64, block_pairs, pairing, grads, da, d_h1,
        xall, wqkv, q, k, v, on, lse,
    )
    gsum = gsum.reshape(total, width)
    d_outer, d_inner, d_output, d_query, d_key, d_value, d_gain, d_shift, result, dtok = finish(
        gsum, dw, result, dtok, d_rows, f_rows, n_f
    )
    return (
        result[None],
        dtok[None],
        d_query,
        d_key,
        d_value,
        d_output,
        d_inner,
        d_outer,
        d_gain.T,
        d_shift.T,
    )


def solution(mesh):
    in_specs = (
        P("fsdp", "ctx", None),
        P("fsdp", None),
        P("fsdp", None),
        P("fsdp", None),
        P("fsdp", None),
        P("fsdp", None),
        P("fsdp", None),
        P("fsdp", None),
        P("fsdp", None),
        P("fsdp", None),
        P("fsdp", None),
        P("fsdp", "ctx", None),
    )
    out_specs = (
        P("fsdp", "ctx", None),
        P("fsdp", "ctx", None),
        P("fsdp", None),
        P("fsdp", None),
        P("fsdp", None),
        P("fsdp", None),
        P("fsdp", None),
        P("fsdp", None),
        P("fsdp", None),
        P("fsdp", None),
    )
    fast = mesh.shape["ctx"] == 8 and mesh.shape["fsdp"] == 4
    chosen = fast_body if fast else generic_body
    return jax.shard_map(chosen, mesh=mesh, in_specs=in_specs, out_specs=out_specs, check_vma=False)
```

```python
import functools

import jax
import jax.numpy as jnp
from jax import lax
from jax.experimental import pallas as pl
from jax.experimental.pallas import tpu as pltpu
from jax.sharding import PartitionSpec as P

norm_eps = 1e-05
score_scale = 0.125
very_low = -1e30


def shortened(value):

    def short(part):
        return part.astype(jnp.bfloat16) if part.dtype == jnp.float32 else part

    return jax.tree.map(short, value)


def layer_norm(values, norm_gain, norm_shift):
    center = values - jnp.mean(values, axis=-1, keepdims=True)
    spread = jnp.mean(center * center, axis=-1, keepdims=True)
    return center * lax.rsqrt(spread + norm_eps) * norm_gain + norm_shift


def exact_gelu(values):
    return jax.nn.gelu(values, approximate=False)


def project(rows_in, weight):
    return jnp.dot(rows_in, weight, preferred_element_type=jnp.float32)


def seq_positions(pair_row, tok_dev, seq_len):
    segment_len = tok_dev // 2
    within = jnp.arange(tok_dev, dtype=jnp.int32)
    lower_pos = pair_row[:, None] * segment_len + within[None, :]
    upper_pos = seq_len - (pair_row[:, None] + 1) * segment_len + within[None, :] - segment_len
    return jnp.where(within[None, :] < segment_len, lower_pos, upper_pos).reshape(-1)


def pair_mask(query_pos, key_pos, head_flags, half_len):
    target = (query_pos[None, :] // half_len + head_flags[:, None]) % 2
    paired = key_pos[None, None, :] // half_len == target[:, :, None]
    causal = key_pos[None, :] <= query_pos[:, None]
    return jnp.logical_and(paired, causal[None, :, :])


def block_rows(tok_dev):
    return 2 * tok_dev


def over_blocks(running, arrays, step_fn, tok_dev):
    row_count = arrays[0].shape[0]
    block_len = block_rows(tok_dev)

    def one_step(inner_carry, step_index):
        first_row = step_index * block_len
        sliced = tuple(
            (lax.dynamic_slice_in_dim(member, first_row, block_len, 0) for member in arrays)
        )
        return (step_fn(inner_carry, sliced, first_row), None)

    return lax.scan(one_step, running, jnp.arange(row_count // block_len, dtype=jnp.int32))[0]


def generic_body(
    tokens,
    w_query,
    w_key,
    w_value,
    w_output,
    w_inner,
    w_outer,
    ln_gain,
    ln_bias,
    pairing,
    block_pairs,
    cotangent,
):
    tok_dev = tokens.shape[1]
    width = tokens.shape[2]
    heads = pairing.shape[1]
    head_dim = width // heads
    n_ctx = lax.axis_size("ctx")
    seq_len = tok_dev * n_ctx
    half_len = seq_len // 2
    pos_all = seq_positions(block_pairs[0], tok_dev, seq_len)
    my_pos = lax.dynamic_slice_in_dim(pos_all, lax.axis_index("ctx") * tok_dev, tok_dev, 0)
    head_flags = pairing[0]
    masters = (w_query, w_key, w_value, w_output, w_inner, w_outer, ln_gain, ln_bias)
    low_masters = tuple((member.astype(jnp.bfloat16) for member in masters))
    gathered = jax.tree.map(
        lambda part, own: part.astype(own.dtype),
        lax.all_gather(shortened(low_masters), "fsdp", axis=0, tiled=True),
        low_masters,
    )
    wq_full, wk_full, wv_full, wo_full, inner_full, outer_full, gain_full, shift_full = gathered
    gain_wide = gain_full.astype(jnp.float32)
    shift_wide = shift_full.astype(jnp.float32)
    x_in = tokens[0]
    query_b = project(x_in, wq_full).astype(jnp.bfloat16)
    key_b = project(x_in, wk_full).astype(jnp.bfloat16)
    value_b = project(x_in, wv_full).astype(jnp.bfloat16)
    q_heads = query_b.reshape(tok_dev, heads, head_dim)

    def attend_step(running, sliced, offset):
        run_max, run_sum, run_acc = running
        key_block, value_block = sliced
        block_len = key_block.shape[0]
        key_pos = lax.dynamic_slice_in_dim(pos_all, offset, block_len, 0)
        allowed = pair_mask(my_pos, key_pos, head_flags, half_len)
        key_heads = key_block.reshape(block_len, heads, head_dim)
        value_heads = value_block.reshape(block_len, heads, head_dim)
        scores = (
            jnp.einsum("qhd,khd->hqk", q_heads, key_heads, preferred_element_type=jnp.float32)
            * score_scale
        )
        new_max = jnp.maximum(run_max, jnp.max(jnp.where(allowed, scores, very_low), axis=2))
        prob_rows = jnp.where(
            allowed, jnp.exp(jnp.where(allowed, scores - new_max[:, :, None], 0.0)), 0.0
        )
        decay = jnp.exp(run_max - new_max)
        new_sum = run_sum * decay + jnp.sum(prob_rows, axis=2)
        added = jnp.einsum(
            "hqk,khd->hqd",
            prob_rows.astype(jnp.bfloat16),
            value_heads,
            preferred_element_type=jnp.float32,
        )
        return (new_max, new_sum, run_acc * decay[:, :, None] + added)

    def pair_fold(step_fn, running, fetched):
        return over_blocks(running, fetched, step_fn, tok_dev)

    start_state = (
        jnp.full((heads, tok_dev), very_low, jnp.float32),
        jnp.zeros((heads, tok_dev), jnp.float32),
        jnp.zeros((heads, tok_dev, head_dim), jnp.float32),
    )
    run_max, run_sum, run_acc = pair_fold(
        attend_step,
        start_state,
        (
            lax.all_gather(key_b, "ctx", axis=0, tiled=True),
            lax.all_gather(value_b, "ctx", axis=0, tiled=True),
        ),
    )
    live_rows = run_sum > 0
    safe_sum = jnp.where(live_rows, run_sum, 1.0)
    attn_heads = jnp.where(live_rows[:, :, None], run_acc / safe_sum[:, :, None], 0.0)
    lse_rows = jnp.where(live_rows, run_max + jnp.log(safe_sum), 0.0)
    attn_rows = attn_heads.transpose(1, 0, 2).reshape(tok_dev, width)
    attn_b = attn_rows.astype(jnp.bfloat16)
    branch = project(attn_b, wo_full)
    first_norm, first_pull = jax.vjp(
        layer_norm, x_in.astype(jnp.float32) + branch, gain_wide[:, 0], shift_wide[:, 0]
    )
    first_b = first_norm.astype(jnp.bfloat16)
    inner = project(first_b, inner_full)
    active, gelu_pull = jax.vjp(exact_gelu, inner)
    active_b = active.astype(jnp.bfloat16)
    outer = project(active_b, outer_full)
    result, second_pull = jax.vjp(layer_norm, first_norm + outer, gain_wide[:, 1], shift_wide[:, 1])
    wq_back, wk_back, wv_back, wo_back, inner_back, outer_back, gain_back, shift_back = gathered
    d_h2, d_gain2, d_shift2 = second_pull(cotangent[0].astype(jnp.float32))
    d_f_b = d_h2.astype(jnp.bfloat16)
    d_outer = jnp.dot(active_b.T, d_f_b, preferred_element_type=jnp.float32)
    d_active = jnp.dot(d_f_b, outer_back.T, preferred_element_type=jnp.float32)
    d_u_b = gelu_pull(d_active)[0].astype(jnp.bfloat16)
    d_inner = jnp.dot(first_b.T, d_u_b, preferred_element_type=jnp.float32)
    d_x1 = d_h2 + jnp.dot(d_u_b, inner_back.T, preferred_element_type=jnp.float32)
    d_h1, d_gain1, d_shift1 = first_pull(d_x1)
    d_y_b = d_h1.astype(jnp.bfloat16)
    d_wo = jnp.dot(attn_b.T, d_y_b, preferred_element_type=jnp.float32)
    d_attn_b = jnp.dot(d_y_b, wo_back.T, preferred_element_type=jnp.float32).astype(jnp.bfloat16)
    delta_rows = (
        (d_attn_b.astype(jnp.float32) * attn_rows).reshape(tok_dev, heads, head_dim).sum(axis=2).T
    )
    dout_heads = d_attn_b.reshape(tok_dev, heads, head_dim)

    def query_grad_step(dq_acc, sliced, offset):
        key_block, value_block = sliced
        block_len = key_block.shape[0]
        key_pos = lax.dynamic_slice_in_dim(pos_all, offset, block_len, 0)
        allowed = pair_mask(my_pos, key_pos, head_flags, half_len)
        key_heads = key_block.reshape(block_len, heads, head_dim)
        value_heads = value_block.reshape(block_len, heads, head_dim)
        scores = (
            jnp.einsum("qhd,khd->hqk", q_heads, key_heads, preferred_element_type=jnp.float32)
            * score_scale
        )
        prob_rows = jnp.where(
            allowed, jnp.exp(jnp.where(allowed, scores - lse_rows[:, :, None], 0.0)), 0.0
        )
        prob_grad = jnp.einsum(
            "qhd,khd->hqk", dout_heads, value_heads, preferred_element_type=jnp.float32
        )
        dscore = (prob_rows * (prob_grad - delta_rows[:, :, None]) * score_scale).astype(
            jnp.bfloat16
        )
        return dq_acc + jnp.einsum(
            "hqk,khd->qhd", dscore, key_heads, preferred_element_type=jnp.float32
        )

    dq_start = jnp.zeros((tok_dev, heads, head_dim), jnp.float32)
    dq_acc = pair_fold(
        query_grad_step,
        dq_start,
        (
            lax.all_gather(key_b, "ctx", axis=0, tiled=True),
            lax.all_gather(value_b, "ctx", axis=0, tiled=True),
        ),
    )
    dq_b = dq_acc.reshape(tok_dev, width).astype(jnp.bfloat16)
    lse_all, delta_all = (
        lax.all_gather(lse_rows, "ctx", axis=1, tiled=True),
        lax.all_gather(delta_rows, "ctx", axis=1, tiled=True),
    )
    k_heads = key_b.reshape(tok_dev, heads, head_dim)
    v_heads = value_b.reshape(tok_dev, heads, head_dim)

    def key_grad_step(running, sliced, offset):
        dk_acc, dv_acc = running
        query_block, dout_block = sliced
        block_len = query_block.shape[0]
        query_pos = lax.dynamic_slice_in_dim(pos_all, offset, block_len, 0)
        lse_block = lax.dynamic_slice_in_dim(lse_all, offset, block_len, 1)
        delta_block = lax.dynamic_slice_in_dim(delta_all, offset, block_len, 1)
        allowed = pair_mask(query_pos, my_pos, head_flags, half_len)
        query_heads = query_block.reshape(block_len, heads, head_dim)
        dout_block_heads = dout_block.reshape(block_len, heads, head_dim)
        scores = (
            jnp.einsum("qhd,khd->hqk", query_heads, k_heads, preferred_element_type=jnp.float32)
            * score_scale
        )
        prob_rows = jnp.where(
            allowed, jnp.exp(jnp.where(allowed, scores - lse_block[:, :, None], 0.0)), 0.0
        )
        dv_acc = dv_acc + jnp.einsum(
            "hqk,qhd->khd",
            prob_rows.astype(jnp.bfloat16),
            dout_block_heads,
            preferred_element_type=jnp.float32,
        )
        prob_grad = jnp.einsum(
            "qhd,khd->hqk", dout_block_heads, v_heads, preferred_element_type=jnp.float32
        )
        dscore = (prob_rows * (prob_grad - delta_block[:, :, None]) * score_scale).astype(
            jnp.bfloat16
        )
        dk_acc = dk_acc + jnp.einsum(
            "hqk,qhd->khd", dscore, query_heads, preferred_element_type=jnp.float32
        )
        return (dk_acc, dv_acc)

    kv_start = (
        jnp.zeros((tok_dev, heads, head_dim), jnp.float32),
        jnp.zeros((tok_dev, heads, head_dim), jnp.float32),
    )
    dk_acc, dv_acc = pair_fold(
        key_grad_step,
        kv_start,
        (
            lax.all_gather(query_b, "ctx", axis=0, tiled=True),
            lax.all_gather(d_attn_b, "ctx", axis=0, tiled=True),
        ),
    )
    dk_b = dk_acc.reshape(tok_dev, width).astype(jnp.bfloat16)
    dv_b = dv_acc.reshape(tok_dev, width).astype(jnp.bfloat16)
    d_input = d_h1 + jnp.dot(dq_b, wq_back.T, preferred_element_type=jnp.float32)
    d_input = d_input + jnp.dot(dk_b, wk_back.T, preferred_element_type=jnp.float32)
    d_input = d_input + jnp.dot(dv_b, wv_back.T, preferred_element_type=jnp.float32)
    terms = (
        jnp.dot(x_in.T, dq_b, preferred_element_type=jnp.float32),
        jnp.dot(x_in.T, dk_b, preferred_element_type=jnp.float32),
        jnp.dot(x_in.T, dv_b, preferred_element_type=jnp.float32),
        d_wo,
        d_inner,
        d_outer,
        jnp.stack([d_gain1, d_gain2], axis=1),
        jnp.stack([d_shift1, d_shift2], axis=1),
    )
    shares = (
        lax.psum_scatter(
            terms[0].astype(jnp.bfloat16), "fsdp", scatter_dimension=0, tiled=True
        ).astype(jnp.float32),
        lax.psum_scatter(
            terms[1].astype(jnp.bfloat16), "fsdp", scatter_dimension=0, tiled=True
        ).astype(jnp.float32),
        lax.psum_scatter(
            terms[2].astype(jnp.bfloat16), "fsdp", scatter_dimension=0, tiled=True
        ).astype(jnp.float32),
        lax.psum_scatter(
            terms[3].astype(jnp.bfloat16), "fsdp", scatter_dimension=0, tiled=True
        ).astype(jnp.float32),
        lax.psum_scatter(
            terms[4].astype(jnp.bfloat16), "fsdp", scatter_dimension=0, tiled=True
        ).astype(jnp.float32),
        lax.psum_scatter(
            terms[5].astype(jnp.bfloat16), "fsdp", scatter_dimension=0, tiled=True
        ).astype(jnp.float32),
        lax.psum_scatter(
            terms[6].astype(jnp.bfloat16), "fsdp", scatter_dimension=0, tiled=True
        ).astype(jnp.float32),
        lax.psum_scatter(
            terms[7].astype(jnp.bfloat16), "fsdp", scatter_dimension=0, tiled=True
        ).astype(jnp.float32),
    )
    totals = (
        lax.psum(shares[0].astype(jnp.bfloat16), "ctx").astype(jnp.float32),
        lax.psum(shares[1].astype(jnp.bfloat16), "ctx").astype(jnp.float32),
        lax.psum(shares[2].astype(jnp.bfloat16), "ctx").astype(jnp.float32),
        lax.psum(shares[3].astype(jnp.bfloat16), "ctx").astype(jnp.float32),
        lax.psum(shares[4].astype(jnp.bfloat16), "ctx").astype(jnp.float32),
        lax.psum(shares[5].astype(jnp.bfloat16), "ctx").astype(jnp.float32),
        lax.psum(shares[6].astype(jnp.bfloat16), "ctx").astype(jnp.float32),
        lax.psum(shares[7].astype(jnp.bfloat16), "ctx").astype(jnp.float32),
    )
    return (
        result.astype(jnp.bfloat16)[None],
        d_input.astype(jnp.bfloat16)[None],
        totals[0],
        totals[1],
        totals[2],
        totals[3],
        totals[4],
        totals[5],
        totals[6],
        totals[7],
    )


MESH = pl.DeviceIdType.MESH
f32 = jnp.float32
bf16 = jnp.bfloat16


class Place:
    def __init__(self):
        me = lax.axis_index("ctx")
        self.me = me
        self.z = lax.axis_index("fsdp")
        self.core = lax.rem(me, 2)
        self.chip = me // 2
        self.x = lax.rem(self.chip, 2)
        self.y = self.chip // 2
        self.chip_x = self.chip + 1 - 2 * self.x
        self.chip_y = self.chip + 2 - 4 * self.y
        self.chip_d = 3 - self.chip
        self.other = 1 - self.core
        self.sib = (2 * self.chip + 1 - self.core, self.z)
        self.xn = (2 * self.chip_x + self.core, self.z)
        self.yn = (2 * self.chip_y + self.core, self.z)
        self.dn = (2 * self.chip_d + self.core, self.z)
        self.up = (me, self.z + 1)
        self.down = (me, self.z - 1)


def greet(place, others, line_len=None):
    barrier = pltpu.get_barrier_semaphore()
    count = len(others)
    for other in others:
        pl.semaphore_signal(barrier, inc=1, device_id=other, device_id_type=MESH)
    if line_len is not None:

        @pl.when(place.z < line_len - 1)
        def _():
            pl.semaphore_signal(barrier, inc=1, device_id=place.up, device_id_type=MESH)

        @pl.when(place.z > 0)
        def _():
            pl.semaphore_signal(barrier, inc=1, device_id=place.down, device_id_type=MESH)

        count = count + jnp.where(place.z < line_len - 1, 1, 0) + jnp.where(place.z > 0, 1, 0)

    pl.semaphore_wait(barrier, count)


def maybe(cond, fn):
    if cond is None:
        fn()
    else:
        pl.when(cond)(fn)


def of(ref):
    return ref() if callable(ref) else ref


class Net:
    def __init__(self, send_sems, recv_sems, count):
        self.send_sems, self.recv_sems, self.count = send_sems, recv_sems, count
        self.used = 0
        self.open = []

    def new(self):
        self.used += 1
        assert self.used <= self.count
        return self.used - 1

    def copy(self, idx, src, dst, dev):
        return pltpu.make_async_remote_copy(
            src_ref=src,
            dst_ref=dst,
            send_sem=self.send_sems.at[idx],
            recv_sem=self.recv_sems.at[idx],
            device_id=dev,
            device_id_type=MESH,
        )

    def send(self, idx, src, dst, dev, cond=None):
        make = lambda: self.copy(idx, of(src), of(dst), dev)
        maybe(cond, lambda: make().start())
        self.open.append((cond, make))

    def recv(self, idx, dst, dev, cond=None):
        maybe(cond, lambda: self.copy(idx, of(dst), of(dst), dev).wait_recv())

    def finish(self):
        for cond, make in self.open:
            maybe(cond, lambda make=make: make().wait_send())
        self.open = []


class PlaneGather:
    def __init__(self, net, place, own, slot, rows, cond=None):
        p = place
        self.net, self.place, self.cond = net, place, cond
        self.own_of, self.slot = own, slot
        self.h0, self.h1 = pl.ds(0, rows // 2), pl.ds(rows // 2, rows // 2)
        self.ids = [net.new() for _ in range(11)]

    def at(self, core, chip, half=0):
        def view():
            ref = self.slot(core, chip)
            return ref if half == 0 else ref.at[self.h0 if half == 1 else self.h1]

        return view

    def mine(self, half=0):
        def view():
            ref = self.own_of()
            return ref if half == 0 else ref.at[self.h0 if half == 1 else self.h1]

        return view

    def first(self):
        n, p, i, c = self.net, self.place, self.ids, self.cond
        at = functools.partial(self.at, p.core, p.chip)
        n.send(i[0], self.mine(1), at(1), p.xn, c)
        n.send(i[1], self.mine(2), at(2), p.yn, c)
        n.send(i[2], self.mine(2), at(2), p.xn, c)
        n.send(i[3], self.mine(1), at(1), p.yn, c)
        n.send(i[4], self.mine(), at(), p.sib, c)

    def second(self):
        n, p, i, c = self.net, self.place, self.ids, self.cond
        bx = functools.partial(self.at, p.core, p.chip_x)
        by = functools.partial(self.at, p.core, p.chip_y)
        n.recv(i[0], bx(1), p.xn, c)
        n.send(i[5], bx(1), bx(1), p.yn, c)
        n.recv(i[1], by(2), p.yn, c)
        n.send(i[6], by(2), by(2), p.xn, c)
        n.recv(i[2], bx(2), p.xn, c)
        n.send(i[7], bx(), bx(), p.sib, c)
        n.recv(i[3], by(1), p.yn, c)
        n.send(i[8], by(), by(), p.sib, c)

    def third(self):
        n, p, i, c = self.net, self.place, self.ids, self.cond
        bd = functools.partial(self.at, p.core, p.chip_d)
        n.recv(i[5], bd(1), p.yn, c)
        n.send(i[9], bd(1), bd(1), p.sib, c)
        n.recv(i[6], bd(2), p.xn, c)
        n.send(i[10], bd(2), bd(2), p.sib, c)

    def last(self):
        n, p, i, c = self.net, self.place, self.ids, self.cond
        for idx, q in ((4, p.chip), (7, p.chip_x), (8, p.chip_y)):
            n.recv(i[idx], self.at(p.other, q), p.sib, c)
        n.recv(i[9], self.at(p.other, p.chip_d, 1), p.sib, c)
        n.recv(i[10], self.at(p.other, p.chip_d, 2), p.sib, c)


def hbm(count):
    return [pl.BlockSpec(memory_space=pltpu.HBM)] * count


def comm_params(collective_id):
    return pltpu.CompilerParams(
        collective_id=collective_id, has_side_effects=True, vmem_limit_bytes=56 << 20
    )


def vmem(count):
    return [pl.BlockSpec(memory_space=pltpu.VMEM)] * count


def smem(count):
    return [pl.BlockSpec(memory_space=pltpu.SMEM)] * count


LANES = 256
KT = 128
NT = (((1,), (1,)), ((), ()))
TN = (((0,), (0,)), ((), ()))
NN = (((1,), (0,)), ((), ()))


def mm(a, b, dims=NN):
    return lax.dot_general(a, b, dims, preferred_element_type=f32)


def head_mask(h, head_dim, dtype):
    lane = lax.broadcasted_iota(jnp.int32, (1, LANES), 1)
    inside = jnp.logical_and(lane >= h * head_dim, lane < (h + 1) * head_dim)
    return jnp.where(inside, 1.0, 0.0).astype(dtype)


class Fold:
    def __init__(self, n, seg):
        self.n, self.seg, self.half = n, seg, n * seg
        self.tiles = self.half // KT

    def ranges(self, i):
        a = -(-(self.n - i) * self.seg // KT)
        b = -(-(i + 1) * self.seg // KT)
        assert a + b == self.tiles + 2
        return a, b

    def places(self, i, core, paired):
        a, b = self.ranges(i)
        n, seg = self.n, self.seg
        causal = 1 - paired
        up = n + core * (n // 2) + i
        rows_a = (core * n + n - 1 - i) * causal + up * paired
        rows_b = (core * n + i) * causal + up * paired
        keys_a = core * self.tiles * causal
        keys_b = core * self.tiles * causal + a * paired
        lim_a = (n - 1 - i) * seg - (a - 2) * KT + (1 << 20) * paired
        lim_b = i * seg - (b - 2) * KT - (1 << 20) * paired
        return (rows_a, keys_a, lim_a, a), (rows_b, keys_b, lim_b, b)


def natural(tab, n, s):
    upper = lax.div(s, n)
    c = tab[n + s + upper * (2 * n - 1 - 2 * s)]
    return lax.rem(c, 2), lax.div(c, 2), upper


def key_tiles(ref, base, first, count):
    return ref[pl.ds(base + first, count)].reshape(count * KT, LANES)


def tail_mask(seg, limit):
    col = lax.broadcasted_iota(jnp.int32, (seg, 2 * KT), 1)
    row = lax.broadcasted_iota(jnp.int32, (seg, 2 * KT), 0)
    return col - row <= limit


def norm_forward(h, gain, shift):
    mean = jnp.mean(h, axis=1, keepdims=True)
    center = h - mean
    scale = lax.rsqrt(jnp.mean(center * center, axis=1, keepdims=True) + norm_eps)
    n = center * scale
    return n, scale, n * gain + shift


def norm_backward(cot, n, scale, gain):
    dn = cot * gain
    mean = jnp.mean(dn, axis=1, keepdims=True)
    along = jnp.mean(dn * n, axis=1, keepdims=True)
    return scale * (dn - mean - n * along)


def chain(*steps):
    def run():
        for fn, *args in steps:
            fn(*args)

    return run


def window(first, rows, width):
    row = lax.broadcasted_iota(jnp.int32, (rows, width), 0)
    col = lax.broadcasted_iota(jnp.int32, (rows, width), 1)
    return jnp.where(col == row + first, 1.0, 0.0).astype(bf16)


def by_unit(order, steps, last):
    before, todo, behind, unit = [], {}, [], -1
    for name in order:
        if name[0] == "U":
            unit = int(name[1:])
        elif unit < 0:
            before.append(steps[name])
        elif unit == last:
            behind.append(steps[name])
        else:
            todo.setdefault(unit, []).append(steps[name])
    return before, todo, behind


def fill_table(tab, pairs, pairing, chip, n, heads):
    for c in range(n):
        tab[c] = pairs[0, c]
    for a in range(n):
        found = jnp.int32(0)
        for c in range(n):
            found = found + (pairs[0, c] == a).astype(jnp.int32) * c
        tab[n + a] = jnp.minimum(found, n - 1)
    for h in range(heads):
        tab[2 * n + h] = pairing[0, chip * heads + h]


def lse_lane(fold, h, i, g):
    return (h * (fold.n // 2) + i) * 2 + g


def attend_unit(fold, core, h, i, head_dim, tab, q_ref, k_ref, v_ref, o_ref, lse_ref):
    n, seg = fold.n, fold.seg
    paired = tab[2 * n + h]
    pf = paired.astype(f32)
    lanes = head_mask(h, head_dim, f32)
    lanes16 = head_mask(h, head_dim, bf16)
    parts = []
    for rows, keys, limit, count in fold.places(i, core, paired):
        q = q_ref[rows] * lanes16
        tail = mm(q, key_tiles(k_ref, keys, count - 2, 2), NT)
        tail = jnp.where(tail_mask(seg, limit), tail, very_low)
        top = jnp.max(tail, axis=1, keepdims=True)
        main = None
        if count > 2:
            main = mm(q, key_tiles(k_ref, keys, 0, count - 2), NT)
            top = jnp.maximum(top, jnp.max(main, axis=1, keepdims=True))
        parts.append((keys, count, main, tail, top))
    both = jnp.maximum(parts[0][4], parts[1][4])
    joined = jnp.broadcast_to(paired, both.shape) == 1
    outs = []
    for keys, count, main, tail, top in parts:
        top = jnp.where(joined, both, top)
        e = jnp.exp(tail - top)
        total = jnp.sum(e, axis=1, keepdims=True)
        acc = mm(e.astype(bf16), key_tiles(v_ref, keys, count - 2, 2))
        if main is not None:
            e = jnp.exp(main - top)
            total += jnp.sum(e, axis=1, keepdims=True)
            acc += mm(e.astype(bf16), key_tiles(v_ref, keys, 0, count - 2))
        outs.append((top, total, acc))
    (top_a, sum_a, acc_a), (top_b, sum_b, acc_b) = outs
    sum_a, sum_b = sum_a + pf * sum_b, jnp.where(joined, sum_a + sum_b, sum_b)
    acc_a = acc_a + pf * acc_b
    out_a = acc_a * (lanes / sum_a)
    out_b = acc_b * (lanes / sum_b)
    lane = lax.broadcasted_iota(jnp.int32, (1, KT), 1)
    lse = jnp.where(lane == lse_lane(fold, h, i, 0), top_a + jnp.log(sum_a), lse_ref[...])
    lse_ref[...] = jnp.where(lane == lse_lane(fold, h, i, 1), top_b + jnp.log(sum_b), lse)
    far, near, up = core * n + n - 1 - i, core * n + i, n + core * (n // 2) + i
    for at, value in ((far, (1.0 - pf) * out_a), (near, (1.0 - pf) * out_b), (up, pf * out_a)):
        o_ref[at] += value.astype(bf16)


FRONT_ORDER = (
    "ca", "cb", "bb", "se1", "ba", "xs", "se2", "ab1", "cc", "se3", "xt", "ab2", "aa1", "xl",
    "bc", "sw", "F", "U0", "aa2", "U1", "U2", "hs1", "bd", "ab3", "U3", "hs2", "U4", "U5",
    "cs1", "aa3", "U6", "gs1", "U7", "U8", "hs3", "U9", "U10", "gs2", "gs3", "U11", "bs1", "OC",
    "cs2", "OP", "gt3", "cs3", "ht2", "bs2", "ht3", "gt1", "cw", "ht1", "gt2", "gl", "hl",
    "bs3", "ow", "M1", "V1", "bw", "V2",
)


def front_kernel(
    nz, n, heads, head_dim, n_sem,
    pairs, pairing, x_ref, cot_ref, gain_ref, shift_ref, wq_i, wk_i, wv_i, wo_i, w1_i, w2_i,
    xall_o, wqkv_o, q_o, k_o, v_o, on_o, g_o, lse_o, out_o, da_o, dh_o,
    tab, xall, wqkv, q_ref, k_ref, v_ref, o_nat, o_ctx, o_part, o_sum, attn,
    w1, w2, wol, fq, fo, f1, f2, u_ref, z_ref, x1b_ref, acc_ref, n1_ref, r1_ref, dx1_ref, gs, gt,
    ssem, rsem, lsem, fsem, gsem,
):
    p = Place()
    z = p.z
    seg, width = x_ref.shape[1], x_ref.shape[2]
    tok = 2 * seg
    fold = Fold(n, seg)
    d_rows, f_rows = wq_i.shape[0], w2_i.shape[0]
    n_f = w1_i.shape[1] // width
    cols = heads * head_dim
    half = d_rows // 2
    a1_rows, a2_rows = n_f * d_rows // 8, f_rows // 12
    b_first = 8 * a2_rows
    b_rows = (f_rows - b_first) // 2
    locals_ = []

    def keep(src, dst):
        cp = pltpu.make_async_copy(src, dst, lsem.at[len(locals_)])
        cp.start()
        locals_.append(cp)
        return cp

    masters = [
        pltpu.make_async_copy(src, dst, fsem.at[i])
        for i, (src, dst) in enumerate(
            ((wq_i, fq.at[0]), (wk_i, fq.at[1]), (wv_i, fq.at[2]), (w1_i, f1), (w2_i, f2), (wo_i, fo))
        )
    ]
    for cp in masters:
        cp.start()
    own_x = keep(x_ref, xall.at[p.core, p.chip])
    greet(p, (p.sib, p.xn, p.yn, p.dn), nz)
    net = Net(ssem, rsem, n_sem)
    tokens_ag = PlaneGather(net, p, lambda: x_ref, lambda k, q: xall.at[k, q], 2)
    tokens_ag.first()
    can_up, can_down = z < nz - 1, z > 0
    rows = pl.ds(p.core * half, half)
    other = pl.ds(p.other * half, half)

    class Stream:
        def __init__(self, at, after):
            self.up = [net.new() for _ in range(nz)]
            self.down = [net.new() for _ in range(nz)]
            self.at, self.todo = at, {}
            for t in range(1, nz):
                self.todo[t] = []
                for ids, src, frm, to, got, more in (
                    (self.up, z - t, p.down, p.up, z >= t, can_up),
                    (self.down, z + t, p.up, p.down, z + t < nz, can_down),
                ):
                    src = jnp.clip(src, 0, nz - 1)
                    on = jnp.logical_and(got, more)
                    self.todo[t].append((ids, src, frm, to, got, on, after(t, src, at, got)))

        def begin(self):
            own = lambda: self.at(z)
            net.send(self.up[1], own, own, p.up, can_up)
            net.send(self.down[1], own, own, p.down, can_down)

        def step(self, t):
            for ids, src, frm, to, got, on, then in self.todo[t]:
                block = functools.partial(self.at, src)
                net.recv(ids[t], block, frm, got)
                if t + 1 < nz:
                    net.send(ids[t + 1], block, block, to, on)
                then()

    def share(waits, block_of):
        def after(t, src, at, got):
            idx = net.new()
            waits.append((idx, lambda: block_of(src), got))
            return lambda: net.send(idx, lambda: at(src), lambda: at(src), p.sib, got)

        return after

    def spread(gathers, slot_of, count):
        def after(t, src, at, got):
            slot = lambda k, q: slot_of(src, k, q)
            gather = PlaneGather(net, p, lambda: at(src), slot, count, got)
            gathers.setdefault(t, []).append(gather)
            return gather.first

        return after

    def a1_slot(o, k, q):
        start = pl.multiple_of(o * d_rows + lax.rem(q, 2) * a1_rows, 32)
        return w1.at[k * 2 + lax.div(q, 2), pl.ds(start, a1_rows)]

    def a2_slot(o, k, q):
        return w2.at[o, pl.ds(pl.multiple_of((k * 4 + q) * a2_rows, 32), a2_rows)]

    def b_slot(o, k):
        return w2.at[o, pl.ds(pl.multiple_of(b_first + k * b_rows, 32), b_rows)]

    sel_waits, b_waits, c_waits, a1_gathers, a2_gathers = [], [], [], {}, {}
    sel = Stream(lambda o: wqkv.at[o, rows], share(sel_waits, lambda o: wqkv.at[o, other]))
    cs = Stream(lambda o: wol.at[o, p.core], share(c_waits, lambda o: wol.at[o, p.other]))
    a1 = Stream(lambda o: a1_slot(o, p.core, p.chip), spread(a1_gathers, a1_slot, a1_rows))
    a2 = Stream(lambda o: a2_slot(o, p.core, p.chip), spread(a2_gathers, a2_slot, a2_rows))
    bs = Stream(lambda o: b_slot(o, p.core), share(b_waits, lambda o: b_slot(o, p.other)))

    for cp in masters[:3]:
        cp.wait()
    for chip in range(4):

        @pl.when(p.chip == chip)
        def _():
            for m in range(3):
                mine = fq[m, :, chip * cols : (chip + 1) * cols].astype(bf16)
                wqkv[z, :, m * LANES : m * LANES + cols] = mine

    for m in range(3):
        wqkv[z, :, m * LANES + cols : (m + 1) * LANES] = jnp.zeros((d_rows, LANES - cols), bf16)
    sel.begin()
    fill_table(tab, pairs, pairing, p.chip, n, heads)
    o_nat[...] = jnp.zeros(o_nat.shape, bf16)
    lse_o[...] = jnp.zeros(lse_o.shape, f32)
    part, swaps = net.new(), [net.new() for _ in range(3)]
    partners = ((p.chip_d, p.dn), (p.chip_x, p.xn), (p.chip_y, p.yn))

    def cast_inner():
        masters[3].wait()
        for f in range(n_f):
            at = pl.ds(pl.multiple_of(z * d_rows, 32), d_rows)
            w1[f, at, :] = f1[:, f * width : (f + 1) * width].astype(bf16)

    def cast_outer():
        masters[4].wait()

        def cast(i, _):
            at = pl.ds(pl.multiple_of(i * 64, 64), 64)
            w2[z, at, :] = f2[at, :].astype(bf16)
            return 0

        lax.fori_loop(0, f_rows // 64, cast, 0)

    def cast_output():
        masters[5].wait()
        four = jnp.concatenate([gain_ref[...], shift_ref[...], jnp.zeros((12, d_rows), f32)], axis=0)
        norms = mm(four.astype(bf16), window(z * d_rows, d_rows, width)).astype(bf16)
        for k in range(2):
            wol[z, k, :half, :] = fo[k * half : (k + 1) * half, :].astype(bf16)
            wol[z, k, half:, :] = norms

    def tokens_last():
        own_x.wait()
        tokens_ag.last()

    def wait_all(waits):
        for idx, block, got in waits:
            net.recv(idx, block, p.sib, got)

    def project_all():
        keep(xall, xall_o)
        keep(wqkv, wqkv_o)

        def four(i, _):
            tokens = jnp.concatenate([xall[natural(tab, n, 4 * i + u)] for u in range(4)], axis=0)
            qkv = mm(tokens, wqkv[...].reshape(-1, 3 * LANES))
            q = (qkv[:, :LANES].astype(bf16).astype(f32) * score_scale).astype(bf16)
            q_ref[pl.ds(4 * i, 4)] = q.reshape(4, seg, LANES)
            at = pl.ds(i * (4 * seg // KT), 4 * seg // KT)
            k_ref[at] = qkv[:, LANES : 2 * LANES].astype(bf16).reshape(-1, KT, LANES)
            v_ref[at] = qkv[:, 2 * LANES :].astype(bf16).reshape(-1, KT, LANES)
            return 0

        lax.fori_loop(0, n // 2, four, 0)
        for src, dst in ((q_ref, q_o), (k_ref, k_o), (v_ref, v_o)):
            keep(src, dst)

    def heads_out():
        keep(o_nat, on_o)
        for core_is in range(2):
            for q in range(n // 2):
                a = tab[2 * q + core_is]
                for u, s in ((0, a), (1, 2 * n - 1 - a)):
                    o_ctx[core_is, q, u * seg : (u + 1) * seg, :] = o_nat[s]
        net.send(part, o_ctx.at[p.other], o_part, p.sib)

    def owners_out():
        net.recv(part, o_part, p.sib)
        for idx, (chip, dev) in zip(swaps, partners):
            o_sum[chip] = o_ctx[p.core, chip] + o_part[chip]
            net.send(idx, o_sum.at[chip], attn.at[p.chip], dev)
        attn[p.chip] = o_ctx[p.core, p.chip] + o_part[p.chip]

    def owners_wait():
        for idx, (chip, dev) in zip(swaps, partners):
            net.recv(idx, attn.at[chip], dev)

    wo_of = lambda o: jnp.concatenate([wol[o, 0, :half, :], wol[o, 1, :half, :]], axis=0)
    kept = {}

    def first_norm():
        vec = wol[0, 0, half:, :].astype(f32)
        for o in range(1, nz):
            vec = vec + wol[o, 0, half:, :].astype(f32)
        h1 = x_ref[...].reshape(tok, width).astype(f32)
        for o in range(nz):
            h1 = h1 + mm(attn[o, :, :cols], wo_of(o))
        n1, r1, x1 = norm_forward(h1, vec[0:1], vec[2:3])
        n1_ref[...] = n1
        r1_ref[...] = jnp.broadcast_to(r1, (tok, 128))
        x1b_ref[...] = x1.astype(bf16)
        acc_ref[...] = x1
        kept["vec"] = vec

    def inner_all():
        def up(f, _):
            u = mm(x1b_ref[...], w1[f])
            cdf = 0.5 + 0.5 * lax.erf(u * (0.5**0.5))
            z_ref[f] = (u * cdf).astype(bf16)
            u_ref[f] = cdf + u * jnp.exp(-0.5 * u * u) * 0.3989422804014327
            return 0

        lax.fori_loop(0, n_f, up, 0)

    def outer_all():
        def add(f, _):
            acc_ref[...] += mm(z_ref[f], w2[f])
            return 0

        lax.fori_loop(0, n_f, add, 0)

    def each(gathers, t, stage):
        for gather in gathers[t]:
            getattr(gather, stage)()

    def all_last(gathers):
        for t in gathers:
            each(gathers, t, "last")

    steps = {
        "ca": cast_inner, "cb": cast_outer, "cc": cast_output, "ba": a1.begin, "bb": a2.begin,
        "bc": cs.begin, "bd": bs.begin, "xs": tokens_ag.second, "xt": tokens_ag.third,
        "xl": tokens_last, "sw": lambda: wait_all(sel_waits), "cw": lambda: wait_all(c_waits),
        "bw": lambda: wait_all(b_waits), "F": project_all, "OC": heads_out, "OP": owners_out,
        "ow": owners_wait, "M1": first_norm, "V1": inner_all, "V2": outer_all,
        "gl": lambda: all_last(a1_gathers), "hl": lambda: all_last(a2_gathers),
    }
    for t in range(1, nz):
        for name, stream in (("se", sel), ("cs", cs), ("aa", a1), ("ab", a2), ("bs", bs)):
            steps[f"{name}{t}"] = functools.partial(stream.step, t)
        for name, gathers in (("g", a1_gathers), ("h", a2_gathers)):
            steps[f"{name}s{t}"] = functools.partial(each, gathers, t, "second")
            steps[f"{name}t{t}"] = functools.partial(each, gathers, t, "third")
    units = n // 2
    before, todo, behind = by_unit(FRONT_ORDER, steps, units * heads - 1)
    for step in before:
        step()

    def head(h, _):
        for i in range(units):
            attend_unit(fold, p.core, h, i, head_dim, tab, q_ref, k_ref, v_ref, o_nat, lse_o)
            for hh in range(heads):
                if hh * units + i in todo:
                    pl.when(h == hh)(chain(*((step,) for step in todo[hh * units + i])))
        return 0

    lax.fori_loop(0, heads, head, 0)
    for step in behind:
        step()
    vec = kept["vec"]
    gain1, gain2, shift2 = vec[0:1], vec[1:2], vec[3:4]
    n2, r2, out = norm_forward(acc_ref[...], gain2, shift2)
    out_o[...] = out.astype(bf16)
    cot = cot_ref[...].astype(f32)
    d_gain2 = jnp.sum(cot * n2, axis=0, keepdims=True)
    d_shift2 = jnp.sum(cot, axis=0, keepdims=True)
    dh2 = norm_backward(cot, n2, r2, gain2)
    dx1_ref[...] = dh2
    df = dh2.astype(bf16)
    first1, first2 = f_rows, f_rows + n_f * d_rows

    def grads_out(f, slot):
        yield pltpu.make_async_copy(gs.at[slot, 0], g_o.at[f, pl.ds(0, f_rows)], gsem.at[slot, 0])
        for o in range(nz):
            at = pl.ds(pl.multiple_of(first1 + f * d_rows, 32), d_rows)
            src = gs.at[slot, 1, pl.ds(o * d_rows, d_rows)]
            yield pltpu.make_async_copy(src, g_o.at[o, at], gsem.at[slot, 1 + o])

    def back(f, _):
        slot = lax.rem(f, 2)

        @pl.when(f >= 2)
        def _():
            for cp in grads_out(f - 2, slot):
                cp.wait()

        gs[slot, 0] = mm(z_ref[f], df, TN).astype(bf16)
        du = (mm(df, w2[f], NT) * u_ref[f]).astype(bf16)
        gs[slot, 1] = mm(x1b_ref[...], du, TN).astype(bf16)
        for cp in grads_out(f, slot):
            cp.start()
        dx1_ref[...] += mm(du, w1[f], NT)
        return 0

    lax.fori_loop(0, n_f, back, 0)
    d_x1 = dx1_ref[...]
    n1 = n1_ref[...]
    d_gain1 = jnp.sum(d_x1 * n1, axis=0, keepdims=True)
    d_shift1 = jnp.sum(d_x1, axis=0, keepdims=True)
    dh1 = norm_backward(d_x1, n1, r1_ref[:, :1], gain1)
    dh_o[...] = dh1
    dy = dh1.astype(bf16)
    norms = jnp.concatenate([d_gain1, d_gain2, d_shift1, d_shift2], axis=0).astype(bf16)
    ends = []
    for o in range(nz):
        da_o[o, :, :cols] = mm(dy, wo_of(o), NT).astype(bf16)
        da_o[o, :, cols:] = jnp.zeros((tok, LANES - cols), bf16)
        gt[o, :d_rows, :] = mm(attn[o, :, :cols], dy, TN).astype(bf16)
        gt[o, d_rows:, :] = jnp.zeros((gt.shape[1] - d_rows, width), bf16)
        gt[o, d_rows : d_rows + 4, :] = norms
        ends.append(pltpu.make_async_copy(gt.at[o], g_o.at[o, pl.ds(first2, gt.shape[1])], fsem.at[o]))
        ends[-1].start()
    for f in range(max(n_f - 2, 0), n_f):
        for cp in grads_out(f, f % 2):
            cp.wait()
    for cp in ends:
        cp.wait()
    net.finish()
    for cp in locals_[1:]:
        cp.wait()


def front(nz, n, heads, head_dim, total, pairs, pairing, x_in, cot, gains, shifts, weights):
    tok, width = x_in.shape
    seg = tok // 2
    d_rows, f_rows = weights[0].shape[0], weights[5].shape[0]
    n_f = weights[4].shape[1] // width
    n_sem = 11 * (4 * (nz - 1) + 1) + 5 * 2 * nz + 3 * 2 * (nz - 1) + 4
    wide, tiled = (2 * n, seg, LANES), (tok * n // KT, KT, LANES)
    shapes = [(2, 4, 2, seg, width), (nz, d_rows, 3 * LANES), wide, tiled, tiled, wide]
    block = (4, tok, LANES)
    sds = jax.ShapeDtypeStruct
    vb = lambda *s: pltpu.VMEM(s, bf16)
    vf = lambda *s: pltpu.VMEM(s, f32)
    return pl.pallas_call(
        functools.partial(front_kernel, nz, n, heads, head_dim, n_sem),
        out_shape=tuple(sds(s, bf16) for s in shapes)
        + (
            sds((nz, total, width), bf16),
            sds((seg, KT), f32),
            sds((tok, width), bf16),
            sds(block, bf16),
            sds((tok, width), f32),
        ),
        in_specs=smem(2) + vmem(4) + hbm(6),
        out_specs=tuple(hbm(7) + vmem(4)),
        scratch_shapes=[pltpu.SMEM((2 * n + heads,), jnp.int32)]
        + [vb(*s) for s in shapes]
        + [
            vb(2, *block),
            vb(*block),
            vb(*block),
            vb(*block),
            vb(n_f, nz * d_rows, width),
            vb(nz, f_rows, width),
            vb(nz, 2, d_rows // 2 + 16, width),
            vf(3, d_rows, width),
            vf(d_rows, width),
            vf(d_rows, n_f * width),
            vf(f_rows, width),
            vf(n_f, tok, width),
            vb(n_f, tok, width),
            vb(tok, width),
            vf(tok, width),
            vf(tok, width),
            vf(tok, 128),
            vf(tok, width),
            vb(2, 2, f_rows, width),
            vb(nz, total - f_rows - n_f * d_rows, width),
            pltpu.SemaphoreType.DMA((n_sem,)),
            pltpu.SemaphoreType.DMA((n_sem,)),
            pltpu.SemaphoreType.DMA((12,)),
            pltpu.SemaphoreType.DMA((6,)),
            pltpu.SemaphoreType.DMA((2, 1 + nz)),
        ],
        compiler_params=comm_params(0),
        name="front",
    )(pairs, pairing, x_in.reshape(2, seg, width), cot, gains, shifts, *weights)


def add_into(dst, src, rows):
    chunk = max(c for c in range(16, min(rows, 160) + 1, 16) if rows % c == 0)

    def step(i, _):
        at = pl.ds(pl.multiple_of(i * chunk, chunk), chunk)
        to, frm = of(dst), of(src)
        to[at, :] = to[at, :] + frm[at, :]
        return 0

    lax.fori_loop(0, rows // chunk, step, 0)


class Slot:
    def __init__(self, ref, o):
        self.ref, self.o = ref, o

    def __call__(self):
        return self.ref.at[self.o]

    @property
    def at(self):
        return self().at


class PlaneSum:
    def __init__(self, net, place, block, rows, rx0, ry1, ry0, rx1):
        p = place
        self.net, self.place = net, place
        self.rx0, self.ry1, self.ry0, self.rx1 = rx0, ry1, ry0, rx1
        self.h = rows // 2
        h0, h1 = pl.ds(0, self.h), pl.ds(self.h, self.h)
        far_x, far_y = 1 - p.x, 1 - p.y
        self.block, self.h0, self.h1 = block, h0, h1
        self.far_x, self.far_y = far_x, far_y
        self.to_x = [2 * j + far_x for j in range(2)]
        self.to_y = [2 * far_y + j for j in range(2)]
        self.on_y, self.on_x = 2 * far_y + p.x, 2 * p.y + far_x
        self.ids = [net.new() for _ in range(6)]

    def part(self, index, half):
        return lambda: self.block(index).at[half]

    def first(self):
        n, p, i = self.net, self.place, self.ids
        for j in range(2):
            n.send(i[j], self.part(self.to_x[j], self.h0), lambda j=j: self.rx0.at[j], p.xn)
            n.send(i[2 + j], self.part(self.to_y[j], self.h1), lambda j=j: self.ry1.at[j], p.yn)

    def second(self):
        n, p, i = self.net, self.place, self.ids
        on_y, on_x = self.part(self.on_y, self.h0), self.part(self.on_x, self.h1)
        mine0, mine1 = self.part(p.chip, self.h0), self.part(p.chip, self.h1)
        for j in range(2):
            n.recv(i[j], lambda j=j: self.rx0.at[j], p.xn)
        add_into(on_y, lambda: self.rx0.at[self.far_y], self.h)
        n.send(i[4], on_y, self.ry0, p.yn)
        for j in range(2):
            n.recv(i[2 + j], lambda j=j: self.ry1.at[j], p.yn)
        add_into(on_x, lambda: self.ry1.at[self.far_x], self.h)
        n.send(i[5], on_x, self.rx1, p.xn)
        add_into(mine0, lambda: self.rx0.at[p.y], self.h)
        add_into(mine1, lambda: self.ry1.at[p.x], self.h)

    def third(self):
        n, p, i = self.net, self.place, self.ids
        n.recv(i[4], self.ry0, p.yn)
        add_into(self.part(p.chip, self.h0), self.ry0, self.h)
        n.recv(i[5], self.rx1, p.xn)
        add_into(self.part(p.chip, self.h1), self.rx1, self.h)


class LineSum:
    def __init__(self, net, place, nz, whole, low, high, parts, rows):
        p, z, top = place, place.z, nz - 1
        self.net, self.top, self.parts, self.rows, self.whole = net, top, parts, rows, whole
        sides = (
            ([net.new() for _ in range(nz)], low, z, -1, p.down, p.up),
            ([net.new() for _ in range(nz)], high, top - z, 1, p.up, p.down),
        )
        self.todo = {}
        for t in range(nz):
            self.todo[t] = []
            for ids, buf, depth, sign, frm, to in sides:
                owner = jnp.clip(top - t + z if sign < 0 else t + z - top, 0, top)
                takes = jnp.logical_and(depth > 0, depth <= t)
                self.todo[t].append(
                    (ids, owner, buf, takes, depth <= t, frm, to)
                )

    def step(self, t):
        n = self.net
        for ids, owner, buf, takes, sends, frm, to in self.todo[t]:
            whole = functools.partial(self.whole, owner)
            landed = lambda buf=buf, owner=owner: buf.at[owner]

            def take(ids=ids, whole=whole, landed=landed, frm=frm):
                n.recv(ids[t - 1], landed, frm)
                if self.parts is None:
                    add_into(whole, landed, self.rows)
                else:
                    for j in range(self.parts):
                        add_into(
                            lambda j=j: whole().at[j], lambda j=j: landed().at[j], self.rows
                        )

            if t > 0:
                maybe(takes, take)
            if t < self.top:
                n.send(ids[t], whole, landed, to, sends)


def attend_back_unit(
    fold, core, h, i, head_dim, tab, q_ref, k_ref, v_ref, o_ref, lse_ref, da_ref,
    dcat_ref, dk_ref, dv_ref,
):
    n, seg, half = fold.n, fold.seg, fold.half
    paired = tab[2 * n + h]
    pf = paired.astype(f32)
    lanes = head_mask(h, head_dim, f32)
    lanes16 = head_mask(h, head_dim, bf16)
    dqs = []
    places = fold.places(i, core, paired)
    for g, (rows, keys, limit, count) in enumerate(places):
        q = q_ref[rows] * lanes16
        k, c, upper = natural(tab, n, rows)
        da = da_ref[k, c, upper] * lanes16
        delta = jnp.sum(
            da.astype(f32) * o_ref[rows].astype(f32), axis=1, keepdims=True
        )
        lane = lax.broadcasted_iota(jnp.int32, (1, KT), 1) == lse_lane(fold, h, i, g)
        lse = jnp.sum(jnp.where(lane, lse_ref[...], 0.0), axis=1, keepdims=True)
        dq = None
        pieces = [(count - 2, 2, True)]
        if count > 2:
            pieces.append((0, count - 2, False))
        for first, size, masked in pieces:
            kt = key_tiles(k_ref, keys, first, size)
            vt = key_tiles(v_ref, keys, first, size)
            pr = jnp.exp(mm(q, kt, NT) - lse)
            if masked:
                pr = jnp.where(tail_mask(seg, limit), pr, 0.0)
            ds = (pr * (mm(da, vt, NT) - delta)).astype(bf16)
            part = mm(ds, kt)
            dq = part if dq is None else dq + part
            dv = mm(pr.astype(bf16), da, TN)
            dk = mm(ds, q, TN)
            at = pl.ds(first * KT, size * KT)
            if g == 0 or masked:
                dk_ref[at, :] += dk
                dv_ref[at, :] += dv
            else:
                beyond = pl.ds(places[0][3] * KT, size * KT)
                dk_ref[at, :] += (1.0 - pf) * dk
                dv_ref[at, :] += (1.0 - pf) * dv
                dk_ref[beyond, :] += pf * dk
                dv_ref[beyond, :] += pf * dv
        dqs.append(dq)
    scaled = lanes * score_scale
    dq_a, dq_b = (dqs[0] + pf * dqs[1]) * scaled, dqs[1] * scaled
    far, near, up = core * n + n - 1 - i, core * n + i, n + core * (n // 2) + i
    for at, value in ((far, (1.0 - pf) * dq_a), (near, (1.0 - pf) * dq_b), (up, pf * dq_a)):
        dcat_ref[at, :, :LANES] += value.astype(bf16)


def place_key_grads(fold, core, paired, dk_ref, dv_ref, dcat_ref):
    n, seg, half = fold.n, fold.seg, fold.half
    pf = paired.astype(f32)

    def spread(j, _):
        at = pl.ds(pl.multiple_of(j * seg, seg), seg)
        for src, lanes in ((dk_ref, slice(LANES, 2 * LANES)), (dv_ref, slice(2 * LANES, None))):
            value = src[at, :]
            dcat_ref[core * n + j, :, lanes] += ((1.0 - pf) * value).astype(bf16)
            dcat_ref[j, :, lanes] += (pf * value).astype(bf16)
        return 0

    lax.fori_loop(0, n, spread, 0)


BACKWARD_ORDER = (
    "dr", "c1", "c0", "s3", "p1f", "dw", "U0", "lb0", "s2", "p0f", "U1", "U2", "U3", "U4",
    "p1s", "c2", "U5", "p2f", "c3", "U6", "lb1", "U7", "U8", "U9", "p3f", "U10", "U11", "p0s",
    "DXo", "lb2", "p1t", "p3s", "p0t", "p2s", "DXm", "xa", "la0", "xsf", "DW", "p3t", "wa",
    "lb3", "wl0", "p2t", "la1", "pbf", "xss", "wl1", "pbs", "la2", "pbt", "fbf", "fbs", "xst",
    "la3", "faf", "wl2", "wl3", "wff", "fbt", "fas", "wfs", "tok", "fat", "wft", "fal", "wfl",
    "fbl", "dwo",
)


def backward_kernel(
    nz, n, heads, head_dim, rb, n_sem,
    pairs, pairing, g_ref, da_in, dh_ref, xall_i, wqkv_i, q_i, k_i, v_i, on_i, lse_ref,
    gsum_o, dtok_o, dw_o,
    tab, g_kept, g_sib, g_rx0, g_ry1, g_ry0, g_rx1, g_low, g_high,
    b_low, b_high, b_rx0, b_ry1, b_ry0, b_rx1,
    x_part, x_sib, x_rx0, x_ry1, x_ry0, x_rx1, w_part, w_sib, w_low, w_high, w_all,
    da_all, xall, wqkv, q_ref, k_ref, v_ref, on_ref, dcat, dk_ref, dv_ref, dw_acc,
    ssem, rsem, lsem,
):
    p = Place()
    z = p.z
    seg, width = xall.shape[3], xall.shape[4]
    tok = 2 * seg
    fold = Fold(n, seg)
    rows = g_ref.shape[3]
    ra = rows - rb
    ax, bx = pl.ds(0, ra), pl.ds(ra, rb)
    order = line_order(nz)
    local = []

    def fetch(src, dst):
        cp = pltpu.make_async_copy(src, dst, lsem.at[len(local)])
        cp.start()
        local.append(cp)
        return cp

    net = Net(ssem, rsem, n_sem)
    own_da = fetch(da_in.at[p.chip], da_all.at[p.core, p.chip])
    own_g = {o: fetch(g_ref.at[o, p.core], g_kept.at[o]) for o in order}
    greet(p, (p.sib, p.xn, p.yn, p.dn), nz)
    swaps = [net.new() for _ in range(7)]
    partners = ((p.chip_d, p.dn), (p.chip_x, p.xn), (p.chip_y, p.yn))
    for i, (chip, dev) in enumerate(partners):
        net.send(swaps[i], da_in.at[chip], da_all.at[p.core, p.chip], dev)
    net.send(swaps[3], da_in.at[p.chip], da_all.at[p.core, p.chip], p.sib)
    sib_ids = {o: net.new() for o in order}

    def to_sib(o):
        net.send(sib_ids[o], lambda: g_ref.at[o, p.other], lambda: g_sib.at[o], p.sib)

    to_sib(order[0])
    to_sib(order[1])
    att_in = [
        fetch(src, dst)
        for src, dst in (
            (q_i, q_ref), (k_i, k_ref), (v_i, v_ref), (on_i, on_ref), (xall_i, xall), (wqkv_i, wqkv),
        )
    ]
    fill_table(tab, pairs, pairing, p.chip, n, heads)
    dcat[...] = jnp.zeros(dcat.shape, bf16)

    plane = {
        o: PlaneSum(
            net, p, lambda q, o=o: g_kept.at[o, q].at[ax], ra,
            *(Slot(r, o) for r in (g_rx0, g_ry1, g_ry0, g_rx1)),
        )
        for o in order
    }
    line_a = LineSum(net, p, nz, lambda o: g_kept.at[o, p.chip].at[ax], g_low, g_high, None, ra)
    line_b = LineSum(net, p, nz, lambda o: g_kept.at[o, :, bx], b_low, b_high, n // 2, rb)
    plane_b = PlaneSum(
        net, p, lambda q: g_kept.at[z, q].at[bx], rb, b_rx0, b_ry1, b_ry0, b_rx1
    )

    def chip_sum(o):
        net.recv(sib_ids[o], lambda: g_sib.at[o], p.sib)
        pltpu.make_async_copy(g_ref.at[o, p.core], g_kept.at[o], lsem.at[1 + order.index(o)]).wait()
        for q in range(n // 2):
            add_into(lambda q=q: g_kept.at[o, q], lambda q=q: g_sib.at[o, q], rows)

    d = wqkv.shape[1]
    half = d // 2
    x_id, w_id = net.new(), net.new()
    w_line = LineSum(net, p, nz, lambda o: w_part.at[p.core, o], w_low, w_high, None, half)
    xs = PlaneSum(net, p, lambda q: x_part.at[p.core, q], tok, x_rx0, x_ry1, x_ry0, x_rx1)
    final_a = PlaneGather(
        net, p, lambda: g_kept.at[z, p.chip].at[ax], lambda k, q: gsum_o.at[k, q].at[ax], ra
    )
    final_b = PlaneGather(
        net, p, lambda: g_kept.at[z, p.chip].at[bx], lambda k, q: gsum_o.at[k, q].at[bx], rb
    )
    w_final = PlaneGather(net, p, lambda: w_part.at[p.core, z], lambda k, q: w_all.at[k, q], half)
    cols = heads * head_dim

    def da_forward():
        for i, chip, dev in ((1, p.chip_x, p.xn), (2, p.chip_y, p.yn), (0, p.chip_d, p.dn)):
            block = lambda chip=chip: da_all.at[p.core, chip]
            net.recv(swaps[i], block, dev)
            net.send(swaps[4 + i], block, block, p.sib)

    def da_wait():
        for i, chip in ((3, p.chip), (5, p.chip_x), (6, p.chip_y), (4, p.chip_d)):
            net.recv(swaps[i], lambda chip=chip: da_all.at[p.other, chip], p.sib)
        own_da.wait()
        for cp in att_in:
            cp.wait()

    def block_grads(k, q):
        a = tab[2 * q + k]
        return jnp.concatenate([dcat[a], dcat[2 * n - 1 - a]], axis=0)

    def weight_grads():
        dw_acc[...] = jnp.zeros(dw_acc.shape, f32)

        def weights(c, _):
            k, q = lax.rem(c, 2), c // 2
            dw_acc[...] += mm(xall[k, q].reshape(tok, width), block_grads(k, q), TN)
            return 0

        lax.fori_loop(0, n, weights, 0)
        for o in range(nz):
            w_part[0, o] = dw_acc[o * d : o * d + half].astype(bf16)
            w_part[1, o] = dw_acc[o * d + half : (o + 1) * d].astype(bf16)
        net.send(w_id, w_part.at[p.other], w_sib, p.sib)

    def weight_sum():
        net.recv(w_id, w_sib, p.sib)
        for o in range(nz):
            add_into(w_part.at[p.core, o], w_sib.at[o], half)

    def tokens_of(k):
        def one(q, _):
            w = wqkv[...].reshape(-1, 3 * LANES)
            x_part[k, q] = mm(block_grads(k, q), w, NT).astype(bf16)
            return 0

        lax.fori_loop(0, n // 2, one, 0)

    def tokens_other():
        tokens_of(p.other)
        net.send(x_id, x_part.at[p.other], x_sib, p.sib)

    def tokens_sum():
        net.recv(x_id, x_sib, p.sib)
        for q in range(n // 2):
            add_into(x_part.at[p.core, q], x_sib.at[q], tok)

    def tokens_out():
        def add_tokens(i, _):
            at = pl.ds(pl.multiple_of(i * 32, 32), 32)
            dtok_o[at, :] = (dh_ref[at, :] + x_part[p.core, p.chip, at, :].astype(f32)).astype(bf16)
            return 0

        lax.fori_loop(0, tok // 32, add_tokens, 0)

    def own_w():
        return pltpu.make_async_copy(
            w_part.at[p.core, z], w_all.at[p.core, p.chip], lsem.at[31]
        )

    def w_final_first():
        w_final.first()
        own_w().start()

    def w_out():
        own_w().wait()
        for j in range(3):
            for k in range(2):
                dw_o[j, k * half : (k + 1) * half, :] = jnp.concatenate(
                    [w_all[k, q][:, j * LANES : j * LANES + cols] for q in range(4)], axis=1
                )

    steps = {
        "dr": da_forward, "dw": da_wait, "DW": weight_grads, "wa": weight_sum,
        "DXo": tokens_other, "DXm": lambda: tokens_of(p.core), "xa": tokens_sum, "tok": tokens_out,
        "dwo": w_out, "wff": w_final_first,
    }
    for k, o in enumerate(order):
        steps[f"s{k}"] = functools.partial(to_sib, o)
        steps[f"c{k}"] = functools.partial(chip_sum, o)
        steps[f"p{k}f"], steps[f"p{k}s"] = plane[o].first, plane[o].second
        steps[f"p{k}t"] = plane[o].third
    for name, line in (("la", line_a), ("lb", line_b), ("wl", w_line)):
        for t in range(nz):
            steps[f"{name}{t}"] = functools.partial(line.step, t)
    for name, thing in (("pb", plane_b), ("xs", xs), ("fa", final_a), ("fb", final_b), ("wf", w_final)):
        for stage in ("first", "second", "third", "last"):
            if hasattr(thing, stage):
                steps.setdefault(name + stage[0], getattr(thing, stage))
    units = n // 2
    before, todo, behind = by_unit(BACKWARD_ORDER, steps, units * heads - 1)
    for step in before:
        step()

    def head(h, _):
        dk_ref[...] = jnp.zeros(dk_ref.shape, f32)
        dv_ref[...] = jnp.zeros(dv_ref.shape, f32)
        for i in range(units):
            attend_back_unit(
                fold, p.core, h, i, head_dim, tab, q_ref, k_ref, v_ref, on_ref, lse_ref, da_all,
                dcat, dk_ref, dv_ref,
            )
            for hh in range(heads):
                if hh * units + i in todo:
                    pl.when(h == hh)(chain(*((step,) for step in todo[hh * units + i])))
        place_key_grads(fold, p.core, tab[2 * n + h], dk_ref, dv_ref, dcat)
        return 0

    lax.fori_loop(0, heads, head, 0)
    for step in behind:
        step()
    own_sum = fetch(g_kept.at[z, p.chip], gsum_o.at[p.core, p.chip])
    own_sum.wait()
    net.finish()


def line_order(nz):
    order = []
    for i in range((nz + 1) // 2):
        for o in (nz - 1 - i, i):
            if o not in order:
                order.append(o)
    return order


def backward(
    nz, n, heads, head_dim, rb, pairs, pairing, grads, da, dh, xall, wqkv, q, k, v, on, lse
):
    rows, width = grads.shape[3], grads.shape[4]
    seg = xall.shape[3]
    tok = 2 * seg
    d_rows = wqkv.shape[1]
    half = d_rows // 2
    ra = rows - rb
    n_sem = 6 * (nz + 2) + 6 * nz + nz + 9 + 33 + 2
    sds = jax.ShapeDtypeStruct
    vm = lambda *shape: pltpu.VMEM(shape, bf16)
    wide, tiled = (2 * n, seg, LANES), (tok * n // KT, KT, LANES)
    da = da.reshape(4, 2, seg, LANES)
    return pl.pallas_call(
        functools.partial(backward_kernel, nz, n, heads, head_dim, rb, n_sem),
        out_shape=(
            sds(grads.shape[1:], bf16),
            sds((tok, width), bf16),
            sds((3, d_rows, width), bf16),
        ),
        in_specs=smem(2) + hbm(2) + vmem(1) + hbm(6) + vmem(1),
        out_specs=tuple(hbm(1) + vmem(2)),
        scratch_shapes=[
            pltpu.SMEM((2 * n + heads,), jnp.int32),
            vm(nz, 4, rows, width),
            vm(nz, 4, rows, width),
            vm(nz, 2, ra // 2, width),
            vm(nz, 2, ra // 2, width),
            vm(nz, ra // 2, width),
            vm(nz, ra // 2, width),
            vm(nz, ra, width),
            vm(nz, ra, width),
            vm(nz, 4, rb, width),
            vm(nz, 4, rb, width),
            vm(2, rb // 2, width),
            vm(2, rb // 2, width),
            vm(rb // 2, width),
            vm(rb // 2, width),
            vm(2, 4, tok, width),
            vm(4, tok, width),
            vm(2, tok // 2, width),
            vm(2, tok // 2, width),
            vm(tok // 2, width),
            vm(tok // 2, width),
            vm(2, nz, half, width),
            vm(nz, half, width),
            vm(nz, half, width),
            vm(nz, half, width),
            vm(2, 4, half, width),
            vm(2, 4, 2, seg, LANES),
            vm(2, 4, 2, seg, width),
            vm(nz, d_rows, width),
            vm(*wide),
            vm(*tiled),
            vm(*tiled),
            vm(*wide),
            vm(2 * n, seg, 3 * LANES),
            pltpu.VMEM((seg * n, LANES), f32),
            pltpu.VMEM((seg * n, LANES), f32),
            pltpu.VMEM((width, 3 * LANES), f32),
            pltpu.SemaphoreType.DMA((n_sem,)),
            pltpu.SemaphoreType.DMA((n_sem,)),
            pltpu.SemaphoreType.DMA((32,)),
        ],
        compiler_params=comm_params(1),
        name="backward",
    )(pairs, pairing, grads, da, dh, xall, wqkv, q, k, v, on, lse)


def finish_kernel(outer, inner, output, norms, dw, result, tokens, *outs):
    outer_o, inner_o, output_o, query_o, key_o, value_o, gain_o, shift_o, result_o, tokens_o = outs
    outer_o[...] = outer[...].astype(f32)
    rows, width = inner_o.shape[0], norms.shape[1]
    for k in range(inner.shape[0] // rows):
        inner_o[:, k * width : (k + 1) * width] = inner[k * rows : (k + 1) * rows, :].astype(f32)
    output_o[...] = output[...].astype(f32)
    for j, out in enumerate((query_o, key_o, value_o)):
        out[...] = dw[j].astype(f32)
    result_o[...] = result[...]
    tokens_o[...] = tokens[...]

    @pl.when(pl.program_id(0) == 0)
    def _():
        first = lax.axis_index("fsdp") * rows
        mine = mm(norms[:16, :], window(first, rows, width), NT)
        gain_o[...] = mine[0:2]
        shift_o[...] = mine[2:4]


def finish(gsum, dw, result, dtok, d_rows, f_rows, n_f):
    tok, width = result.shape
    used = f_rows + n_f * d_rows + d_rows
    steps = n_f // 2
    per = n_f // steps
    o_rows, s_rows, t_rows = f_rows // steps, d_rows // steps, tok // steps
    tail = gsum.shape[0] - used
    sds = jax.ShapeDtypeStruct
    square, pair = (d_rows, width), (2, d_rows)
    strip = lambda rows, first=0: pl.BlockSpec((rows, width), lambda f: (first + f, 0))
    return pl.pallas_call(
        finish_kernel,
        grid=(steps,),
        out_shape=(sds((f_rows, width), f32), sds((d_rows, n_f * width), f32))
        + (sds(square, f32),) * 4
        + (sds(pair, f32),) * 2
        + (sds((tok, width), bf16),) * 2,
        in_specs=[
            strip(o_rows),
            strip(per * d_rows, f_rows // (per * d_rows)),
            strip(s_rows, (used - d_rows) // s_rows),
            pl.BlockSpec((tail, width), lambda f: (used // tail, 0)),
            pl.BlockSpec((3, s_rows, width), lambda f: (0, f, 0)),
            strip(t_rows),
            strip(t_rows),
        ],
        out_specs=(strip(o_rows), pl.BlockSpec((d_rows, per * width), lambda f: (0, f)))
        + (strip(s_rows),) * 4
        + (pl.BlockSpec(pair, lambda f: (0, 0)),) * 2
        + (strip(t_rows),) * 2,
        compiler_params=pltpu.CompilerParams(vmem_limit_bytes=60 << 20),
        name="finish",
    )(gsum, gsum, gsum, gsum, dw, result, dtok)


def fast_body(
    tokens,
    w_query,
    w_key,
    w_value,
    w_output,
    w_inner,
    w_outer,
    ln_gain,
    ln_bias,
    pairing,
    block_pairs,
    cotangent,
):
    tok, width = tokens.shape[1], tokens.shape[2]
    n_ctx, nz = lax.axis_size("ctx"), lax.axis_size("fsdp")
    heads = pairing.shape[1]
    my_heads, head_dim = heads // 4, width // heads
    d_rows = w_query.shape[0]
    f_rows, ff = w_outer.shape[0], w_inner.shape[1]
    n_f = ff // width
    used = f_rows + n_f * d_rows + d_rows
    total = -(-(used + 4) // 256) * 256
    weights = (w_query, w_key, w_value, w_output, w_inner, w_outer)
    xall, wqkv, q, k, v, on, grads, lse, result, da, d_h1 = front(
        nz, n_ctx, my_heads, head_dim, total, block_pairs, pairing, tokens[0], cotangent[0],
        ln_gain.T, ln_bias.T, weights,
    )
    grads = grads.reshape(nz, 2, 4, total // 8, width)
    gsum, dtok, dw = backward(
        nz, n_ctx, my_heads, head_dim, 64, block_pairs, pairing, grads, da, d_h1,
        xall, wqkv, q, k, v, on, lse,
    )
    gsum = gsum.reshape(total, width)
    d_outer, d_inner, d_output, d_query, d_key, d_value, d_gain, d_shift, result, dtok = finish(
        gsum, dw, result, dtok, d_rows, f_rows, n_f
    )
    return (
        result[None],
        dtok[None],
        d_query,
        d_key,
        d_value,
        d_output,
        d_inner,
        d_outer,
        d_gain.T,
        d_shift.T,
    )


def solution(mesh):
    in_specs = (
        P("fsdp", "ctx", None),
        P("fsdp", None),
        P("fsdp", None),
        P("fsdp", None),
        P("fsdp", None),
        P("fsdp", None),
        P("fsdp", None),
        P("fsdp", None),
        P("fsdp", None),
        P("fsdp", None),
        P("fsdp", None),
        P("fsdp", "ctx", None),
    )
    out_specs = (
        P("fsdp", "ctx", None),
        P("fsdp", "ctx", None),
        P("fsdp", None),
        P("fsdp", None),
        P("fsdp", None),
        P("fsdp", None),
        P("fsdp", None),
        P("fsdp", None),
        P("fsdp", None),
        P("fsdp", None),
    )
    fast = mesh.shape["ctx"] == 8 and mesh.shape["fsdp"] == 4
    chosen = fast_body if fast else generic_body
    return jax.shard_map(chosen, mesh=mesh, in_specs=in_specs, out_specs=out_specs, check_vma=False)
```

```python
import functools

import jax
import jax.numpy as jnp
from jax import lax
from jax.experimental import pallas as pl
from jax.experimental.pallas import tpu as pltpu
from jax.sharding import PartitionSpec as P

norm_eps = 1e-05
score_scale = 0.125
very_low = -1e30


def shortened(value):

    def short(part):
        return part.astype(jnp.bfloat16) if part.dtype == jnp.float32 else part

    return jax.tree.map(short, value)


def layer_norm(values, norm_gain, norm_shift):
    center = values - jnp.mean(values, axis=-1, keepdims=True)
    spread = jnp.mean(center * center, axis=-1, keepdims=True)
    return center * lax.rsqrt(spread + norm_eps) * norm_gain + norm_shift


def exact_gelu(values):
    return jax.nn.gelu(values, approximate=False)


def project(rows_in, weight):
    return jnp.dot(rows_in, weight, preferred_element_type=jnp.float32)


def seq_positions(pair_row, tok_dev, seq_len):
    segment_len = tok_dev // 2
    within = jnp.arange(tok_dev, dtype=jnp.int32)
    lower_pos = pair_row[:, None] * segment_len + within[None, :]
    upper_pos = seq_len - (pair_row[:, None] + 1) * segment_len + within[None, :] - segment_len
    return jnp.where(within[None, :] < segment_len, lower_pos, upper_pos).reshape(-1)


def pair_mask(query_pos, key_pos, head_flags, half_len):
    target = (query_pos[None, :] // half_len + head_flags[:, None]) % 2
    paired = key_pos[None, None, :] // half_len == target[:, :, None]
    causal = key_pos[None, :] <= query_pos[:, None]
    return jnp.logical_and(paired, causal[None, :, :])


def block_rows(tok_dev):
    return 2 * tok_dev


def over_blocks(running, arrays, step_fn, tok_dev):
    row_count = arrays[0].shape[0]
    block_len = block_rows(tok_dev)

    def one_step(inner_carry, step_index):
        first_row = step_index * block_len
        sliced = tuple(
            (lax.dynamic_slice_in_dim(member, first_row, block_len, 0) for member in arrays)
        )
        return (step_fn(inner_carry, sliced, first_row), None)

    return lax.scan(one_step, running, jnp.arange(row_count // block_len, dtype=jnp.int32))[0]


def generic_body(
    tokens,
    w_query,
    w_key,
    w_value,
    w_output,
    w_inner,
    w_outer,
    ln_gain,
    ln_bias,
    pairing,
    block_pairs,
    cotangent,
):
    tok_dev = tokens.shape[1]
    width = tokens.shape[2]
    heads = pairing.shape[1]
    head_dim = width // heads
    n_ctx = lax.axis_size("ctx")
    seq_len = tok_dev * n_ctx
    half_len = seq_len // 2
    pos_all = seq_positions(block_pairs[0], tok_dev, seq_len)
    my_pos = lax.dynamic_slice_in_dim(pos_all, lax.axis_index("ctx") * tok_dev, tok_dev, 0)
    head_flags = pairing[0]
    masters = (w_query, w_key, w_value, w_output, w_inner, w_outer, ln_gain, ln_bias)
    low_masters = tuple((member.astype(jnp.bfloat16) for member in masters))
    gathered = jax.tree.map(
        lambda part, own: part.astype(own.dtype),
        lax.all_gather(shortened(low_masters), "fsdp", axis=0, tiled=True),
        low_masters,
    )
    wq_full, wk_full, wv_full, wo_full, inner_full, outer_full, gain_full, shift_full = gathered
    gain_wide = gain_full.astype(jnp.float32)
    shift_wide = shift_full.astype(jnp.float32)
    x_in = tokens[0]
    query_b = project(x_in, wq_full).astype(jnp.bfloat16)
    key_b = project(x_in, wk_full).astype(jnp.bfloat16)
    value_b = project(x_in, wv_full).astype(jnp.bfloat16)
    q_heads = query_b.reshape(tok_dev, heads, head_dim)

    def attend_step(running, sliced, offset):
        run_max, run_sum, run_acc = running
        key_block, value_block = sliced
        block_len = key_block.shape[0]
        key_pos = lax.dynamic_slice_in_dim(pos_all, offset, block_len, 0)
        allowed = pair_mask(my_pos, key_pos, head_flags, half_len)
        key_heads = key_block.reshape(block_len, heads, head_dim)
        value_heads = value_block.reshape(block_len, heads, head_dim)
        scores = (
            jnp.einsum("qhd,khd->hqk", q_heads, key_heads, preferred_element_type=jnp.float32)
            * score_scale
        )
        new_max = jnp.maximum(run_max, jnp.max(jnp.where(allowed, scores, very_low), axis=2))
        prob_rows = jnp.where(
            allowed, jnp.exp(jnp.where(allowed, scores - new_max[:, :, None], 0.0)), 0.0
        )
        decay = jnp.exp(run_max - new_max)
        new_sum = run_sum * decay + jnp.sum(prob_rows, axis=2)
        added = jnp.einsum(
            "hqk,khd->hqd",
            prob_rows.astype(jnp.bfloat16),
            value_heads,
            preferred_element_type=jnp.float32,
        )
        return (new_max, new_sum, run_acc * decay[:, :, None] + added)

    def pair_fold(step_fn, running, fetched):
        return over_blocks(running, fetched, step_fn, tok_dev)

    start_state = (
        jnp.full((heads, tok_dev), very_low, jnp.float32),
        jnp.zeros((heads, tok_dev), jnp.float32),
        jnp.zeros((heads, tok_dev, head_dim), jnp.float32),
    )
    run_max, run_sum, run_acc = pair_fold(
        attend_step,
        start_state,
        (
            lax.all_gather(key_b, "ctx", axis=0, tiled=True),
            lax.all_gather(value_b, "ctx", axis=0, tiled=True),
        ),
    )
    live_rows = run_sum > 0
    safe_sum = jnp.where(live_rows, run_sum, 1.0)
    attn_heads = jnp.where(live_rows[:, :, None], run_acc / safe_sum[:, :, None], 0.0)
    lse_rows = jnp.where(live_rows, run_max + jnp.log(safe_sum), 0.0)
    attn_rows = attn_heads.transpose(1, 0, 2).reshape(tok_dev, width)
    attn_b = attn_rows.astype(jnp.bfloat16)
    branch = project(attn_b, wo_full)
    first_norm, first_pull = jax.vjp(
        layer_norm, x_in.astype(jnp.float32) + branch, gain_wide[:, 0], shift_wide[:, 0]
    )
    first_b = first_norm.astype(jnp.bfloat16)
    inner = project(first_b, inner_full)
    active, gelu_pull = jax.vjp(exact_gelu, inner)
    active_b = active.astype(jnp.bfloat16)
    outer = project(active_b, outer_full)
    result, second_pull = jax.vjp(layer_norm, first_norm + outer, gain_wide[:, 1], shift_wide[:, 1])
    wq_back, wk_back, wv_back, wo_back, inner_back, outer_back, gain_back, shift_back = gathered
    d_h2, d_gain2, d_shift2 = second_pull(cotangent[0].astype(jnp.float32))
    d_f_b = d_h2.astype(jnp.bfloat16)
    d_outer = jnp.dot(active_b.T, d_f_b, preferred_element_type=jnp.float32)
    d_active = jnp.dot(d_f_b, outer_back.T, preferred_element_type=jnp.float32)
    d_u_b = gelu_pull(d_active)[0].astype(jnp.bfloat16)
    d_inner = jnp.dot(first_b.T, d_u_b, preferred_element_type=jnp.float32)
    d_x1 = d_h2 + jnp.dot(d_u_b, inner_back.T, preferred_element_type=jnp.float32)
    d_h1, d_gain1, d_shift1 = first_pull(d_x1)
    d_y_b = d_h1.astype(jnp.bfloat16)
    d_wo = jnp.dot(attn_b.T, d_y_b, preferred_element_type=jnp.float32)
    d_attn_b = jnp.dot(d_y_b, wo_back.T, preferred_element_type=jnp.float32).astype(jnp.bfloat16)
    delta_rows = (
        (d_attn_b.astype(jnp.float32) * attn_rows).reshape(tok_dev, heads, head_dim).sum(axis=2).T
    )
    dout_heads = d_attn_b.reshape(tok_dev, heads, head_dim)

    def query_grad_step(dq_acc, sliced, offset):
        key_block, value_block = sliced
        block_len = key_block.shape[0]
        key_pos = lax.dynamic_slice_in_dim(pos_all, offset, block_len, 0)
        allowed = pair_mask(my_pos, key_pos, head_flags, half_len)
        key_heads = key_block.reshape(block_len, heads, head_dim)
        value_heads = value_block.reshape(block_len, heads, head_dim)
        scores = (
            jnp.einsum("qhd,khd->hqk", q_heads, key_heads, preferred_element_type=jnp.float32)
            * score_scale
        )
        prob_rows = jnp.where(
            allowed, jnp.exp(jnp.where(allowed, scores - lse_rows[:, :, None], 0.0)), 0.0
        )
        prob_grad = jnp.einsum(
            "qhd,khd->hqk", dout_heads, value_heads, preferred_element_type=jnp.float32
        )
        dscore = (prob_rows * (prob_grad - delta_rows[:, :, None]) * score_scale).astype(
            jnp.bfloat16
        )
        return dq_acc + jnp.einsum(
            "hqk,khd->qhd", dscore, key_heads, preferred_element_type=jnp.float32
        )

    dq_start = jnp.zeros((tok_dev, heads, head_dim), jnp.float32)
    dq_acc = pair_fold(
        query_grad_step,
        dq_start,
        (
            lax.all_gather(key_b, "ctx", axis=0, tiled=True),
            lax.all_gather(value_b, "ctx", axis=0, tiled=True),
        ),
    )
    dq_b = dq_acc.reshape(tok_dev, width).astype(jnp.bfloat16)
    lse_all, delta_all = (
        lax.all_gather(lse_rows, "ctx", axis=1, tiled=True),
        lax.all_gather(delta_rows, "ctx", axis=1, tiled=True),
    )
    k_heads = key_b.reshape(tok_dev, heads, head_dim)
    v_heads = value_b.reshape(tok_dev, heads, head_dim)

    def key_grad_step(running, sliced, offset):
        dk_acc, dv_acc = running
        query_block, dout_block = sliced
        block_len = query_block.shape[0]
        query_pos = lax.dynamic_slice_in_dim(pos_all, offset, block_len, 0)
        lse_block = lax.dynamic_slice_in_dim(lse_all, offset, block_len, 1)
        delta_block = lax.dynamic_slice_in_dim(delta_all, offset, block_len, 1)
        allowed = pair_mask(query_pos, my_pos, head_flags, half_len)
        query_heads = query_block.reshape(block_len, heads, head_dim)
        dout_block_heads = dout_block.reshape(block_len, heads, head_dim)
        scores = (
            jnp.einsum("qhd,khd->hqk", query_heads, k_heads, preferred_element_type=jnp.float32)
            * score_scale
        )
        prob_rows = jnp.where(
            allowed, jnp.exp(jnp.where(allowed, scores - lse_block[:, :, None], 0.0)), 0.0
        )
        dv_acc = dv_acc + jnp.einsum(
            "hqk,qhd->khd",
            prob_rows.astype(jnp.bfloat16),
            dout_block_heads,
            preferred_element_type=jnp.float32,
        )
        prob_grad = jnp.einsum(
            "qhd,khd->hqk", dout_block_heads, v_heads, preferred_element_type=jnp.float32
        )
        dscore = (prob_rows * (prob_grad - delta_block[:, :, None]) * score_scale).astype(
            jnp.bfloat16
        )
        dk_acc = dk_acc + jnp.einsum(
            "hqk,qhd->khd", dscore, query_heads, preferred_element_type=jnp.float32
        )
        return (dk_acc, dv_acc)

    kv_start = (
        jnp.zeros((tok_dev, heads, head_dim), jnp.float32),
        jnp.zeros((tok_dev, heads, head_dim), jnp.float32),
    )
    dk_acc, dv_acc = pair_fold(
        key_grad_step,
        kv_start,
        (
            lax.all_gather(query_b, "ctx", axis=0, tiled=True),
            lax.all_gather(d_attn_b, "ctx", axis=0, tiled=True),
        ),
    )
    dk_b = dk_acc.reshape(tok_dev, width).astype(jnp.bfloat16)
    dv_b = dv_acc.reshape(tok_dev, width).astype(jnp.bfloat16)
    d_input = d_h1 + jnp.dot(dq_b, wq_back.T, preferred_element_type=jnp.float32)
    d_input = d_input + jnp.dot(dk_b, wk_back.T, preferred_element_type=jnp.float32)
    d_input = d_input + jnp.dot(dv_b, wv_back.T, preferred_element_type=jnp.float32)
    terms = (
        jnp.dot(x_in.T, dq_b, preferred_element_type=jnp.float32),
        jnp.dot(x_in.T, dk_b, preferred_element_type=jnp.float32),
        jnp.dot(x_in.T, dv_b, preferred_element_type=jnp.float32),
        d_wo,
        d_inner,
        d_outer,
        jnp.stack([d_gain1, d_gain2], axis=1),
        jnp.stack([d_shift1, d_shift2], axis=1),
    )
    shares = (
        lax.psum_scatter(
            terms[0].astype(jnp.bfloat16), "fsdp", scatter_dimension=0, tiled=True
        ).astype(jnp.float32),
        lax.psum_scatter(
            terms[1].astype(jnp.bfloat16), "fsdp", scatter_dimension=0, tiled=True
        ).astype(jnp.float32),
        lax.psum_scatter(
            terms[2].astype(jnp.bfloat16), "fsdp", scatter_dimension=0, tiled=True
        ).astype(jnp.float32),
        lax.psum_scatter(
            terms[3].astype(jnp.bfloat16), "fsdp", scatter_dimension=0, tiled=True
        ).astype(jnp.float32),
        lax.psum_scatter(
            terms[4].astype(jnp.bfloat16), "fsdp", scatter_dimension=0, tiled=True
        ).astype(jnp.float32),
        lax.psum_scatter(
            terms[5].astype(jnp.bfloat16), "fsdp", scatter_dimension=0, tiled=True
        ).astype(jnp.float32),
        lax.psum_scatter(
            terms[6].astype(jnp.bfloat16), "fsdp", scatter_dimension=0, tiled=True
        ).astype(jnp.float32),
        lax.psum_scatter(
            terms[7].astype(jnp.bfloat16), "fsdp", scatter_dimension=0, tiled=True
        ).astype(jnp.float32),
    )
    totals = (
        lax.psum(shares[0].astype(jnp.bfloat16), "ctx").astype(jnp.float32),
        lax.psum(shares[1].astype(jnp.bfloat16), "ctx").astype(jnp.float32),
        lax.psum(shares[2].astype(jnp.bfloat16), "ctx").astype(jnp.float32),
        lax.psum(shares[3].astype(jnp.bfloat16), "ctx").astype(jnp.float32),
        lax.psum(shares[4].astype(jnp.bfloat16), "ctx").astype(jnp.float32),
        lax.psum(shares[5].astype(jnp.bfloat16), "ctx").astype(jnp.float32),
        lax.psum(shares[6].astype(jnp.bfloat16), "ctx").astype(jnp.float32),
        lax.psum(shares[7].astype(jnp.bfloat16), "ctx").astype(jnp.float32),
    )
    return (
        result.astype(jnp.bfloat16)[None],
        d_input.astype(jnp.bfloat16)[None],
        totals[0],
        totals[1],
        totals[2],
        totals[3],
        totals[4],
        totals[5],
        totals[6],
        totals[7],
    )


MESH = pl.DeviceIdType.MESH
f32 = jnp.float32
bf16 = jnp.bfloat16


class Place:
    def __init__(self):
        me = lax.axis_index("ctx")
        self.me = me
        self.z = lax.axis_index("fsdp")
        self.core = lax.rem(me, 2)
        self.chip = me // 2
        self.x = lax.rem(self.chip, 2)
        self.y = self.chip // 2
        self.chip_x = self.chip + 1 - 2 * self.x
        self.chip_y = self.chip + 2 - 4 * self.y
        self.chip_d = 3 - self.chip
        self.other = 1 - self.core
        self.sib = (2 * self.chip + 1 - self.core, self.z)
        self.xn = (2 * self.chip_x + self.core, self.z)
        self.yn = (2 * self.chip_y + self.core, self.z)
        self.dn = (2 * self.chip_d + self.core, self.z)
        self.up = (me, self.z + 1)
        self.down = (me, self.z - 1)


def greet(place, others, line_len=None):
    barrier = pltpu.get_barrier_semaphore()
    count = len(others)
    for other in others:
        pl.semaphore_signal(barrier, inc=1, device_id=other, device_id_type=MESH)
    if line_len is not None:

        @pl.when(place.z < line_len - 1)
        def _():
            pl.semaphore_signal(barrier, inc=1, device_id=place.up, device_id_type=MESH)

        @pl.when(place.z > 0)
        def _():
            pl.semaphore_signal(barrier, inc=1, device_id=place.down, device_id_type=MESH)

        count = count + jnp.where(place.z < line_len - 1, 1, 0) + jnp.where(place.z > 0, 1, 0)

    pl.semaphore_wait(barrier, count)


def maybe(cond, fn):
    if cond is None:
        fn()
    else:
        pl.when(cond)(fn)


def of(ref):
    return ref() if callable(ref) else ref


class Net:
    def __init__(self, send_sems, recv_sems, count):
        self.send_sems, self.recv_sems, self.count = send_sems, recv_sems, count
        self.used = 0
        self.open = []

    def new(self):
        self.used += 1
        assert self.used <= self.count
        return self.used - 1

    def copy(self, idx, src, dst, dev):
        return pltpu.make_async_remote_copy(
            src_ref=src,
            dst_ref=dst,
            send_sem=self.send_sems.at[idx],
            recv_sem=self.recv_sems.at[idx],
            device_id=dev,
            device_id_type=MESH,
        )

    def send(self, idx, src, dst, dev, cond=None):
        make = lambda: self.copy(idx, of(src), of(dst), dev)
        maybe(cond, lambda: make().start())
        self.open.append((cond, make))

    def recv(self, idx, dst, dev, cond=None):
        maybe(cond, lambda: self.copy(idx, of(dst), of(dst), dev).wait_recv())

    def finish(self):
        for cond, make in self.open:
            maybe(cond, lambda make=make: make().wait_send())
        self.open = []


class PlaneGather:
    def __init__(self, net, place, own, slot, rows, cond=None):
        p = place
        self.net, self.place, self.cond = net, place, cond
        self.own_of, self.slot = own, slot
        self.h0, self.h1 = pl.ds(0, rows // 2), pl.ds(rows // 2, rows // 2)
        self.ids = [net.new() for _ in range(11)]

    def at(self, core, chip, half=0):
        def view():
            ref = self.slot(core, chip)
            return ref if half == 0 else ref.at[self.h0 if half == 1 else self.h1]

        return view

    def mine(self, half=0):
        def view():
            ref = self.own_of()
            return ref if half == 0 else ref.at[self.h0 if half == 1 else self.h1]

        return view

    def first(self):
        n, p, i, c = self.net, self.place, self.ids, self.cond
        at = functools.partial(self.at, p.core, p.chip)
        n.send(i[0], self.mine(1), at(1), p.xn, c)
        n.send(i[1], self.mine(2), at(2), p.yn, c)
        n.send(i[2], self.mine(2), at(2), p.xn, c)
        n.send(i[3], self.mine(1), at(1), p.yn, c)
        n.send(i[4], self.mine(), at(), p.sib, c)

    def second(self):
        n, p, i, c = self.net, self.place, self.ids, self.cond
        bx = functools.partial(self.at, p.core, p.chip_x)
        by = functools.partial(self.at, p.core, p.chip_y)
        n.recv(i[0], bx(1), p.xn, c)
        n.send(i[5], bx(1), bx(1), p.yn, c)
        n.recv(i[1], by(2), p.yn, c)
        n.send(i[6], by(2), by(2), p.xn, c)
        n.recv(i[2], bx(2), p.xn, c)
        n.send(i[7], bx(), bx(), p.sib, c)
        n.recv(i[3], by(1), p.yn, c)
        n.send(i[8], by(), by(), p.sib, c)

    def third(self):
        n, p, i, c = self.net, self.place, self.ids, self.cond
        bd = functools.partial(self.at, p.core, p.chip_d)
        n.recv(i[5], bd(1), p.yn, c)
        n.send(i[9], bd(1), bd(1), p.sib, c)
        n.recv(i[6], bd(2), p.xn, c)
        n.send(i[10], bd(2), bd(2), p.sib, c)

    def last(self):
        n, p, i, c = self.net, self.place, self.ids, self.cond
        for idx, q in ((4, p.chip), (7, p.chip_x), (8, p.chip_y)):
            n.recv(i[idx], self.at(p.other, q), p.sib, c)
        n.recv(i[9], self.at(p.other, p.chip_d, 1), p.sib, c)
        n.recv(i[10], self.at(p.other, p.chip_d, 2), p.sib, c)


def hbm(count):
    return [pl.BlockSpec(memory_space=pltpu.HBM)] * count


def comm_params(collective_id):
    return pltpu.CompilerParams(
        collective_id=collective_id, has_side_effects=True, vmem_limit_bytes=56 << 20
    )


def vmem(count):
    return [pl.BlockSpec(memory_space=pltpu.VMEM)] * count


def smem(count):
    return [pl.BlockSpec(memory_space=pltpu.SMEM)] * count


LANES = 256
KT = 128
NT = (((1,), (1,)), ((), ()))
TN = (((0,), (0,)), ((), ()))
NN = (((1,), (0,)), ((), ()))


def mm(a, b, dims=NN):
    return lax.dot_general(a, b, dims, preferred_element_type=f32)


def head_mask(h, head_dim, dtype):
    lane = lax.broadcasted_iota(jnp.int32, (1, LANES), 1)
    inside = jnp.logical_and(lane >= h * head_dim, lane < (h + 1) * head_dim)
    return jnp.where(inside, 1.0, 0.0).astype(dtype)


class Fold:
    def __init__(self, n, seg):
        self.n, self.seg, self.half = n, seg, n * seg
        self.tiles = self.half // KT

    def ranges(self, i):
        a = -(-(self.n - i) * self.seg // KT)
        b = -(-(i + 1) * self.seg // KT)
        assert a + b == self.tiles + 2
        return a, b

    def places(self, i, core, paired):
        a, b = self.ranges(i)
        n, seg = self.n, self.seg
        causal = 1 - paired
        up = n + core * (n // 2) + i
        rows_a = (core * n + n - 1 - i) * causal + up * paired
        rows_b = (core * n + i) * causal + up * paired
        keys_a = core * self.tiles * causal
        keys_b = core * self.tiles * causal + a * paired
        lim_a = (n - 1 - i) * seg - (a - 2) * KT + (1 << 20) * paired
        lim_b = i * seg - (b - 2) * KT - (1 << 20) * paired
        return (rows_a, keys_a, lim_a, a), (rows_b, keys_b, lim_b, b)


def natural(tab, n, s):
    upper = lax.div(s, n)
    c = tab[n + s + upper * (2 * n - 1 - 2 * s)]
    return lax.rem(c, 2), lax.div(c, 2), upper


def key_tiles(ref, base, first, count):
    return ref[pl.ds(base + first, count)].reshape(count * KT, LANES)


def tail_mask(seg, limit):
    col = lax.broadcasted_iota(jnp.int32, (seg, 2 * KT), 1)
    row = lax.broadcasted_iota(jnp.int32, (seg, 2 * KT), 0)
    return col - row <= limit


def norm_forward(h, gain, shift):
    mean = jnp.mean(h, axis=1, keepdims=True)
    center = h - mean
    scale = lax.rsqrt(jnp.mean(center * center, axis=1, keepdims=True) + norm_eps)
    n = center * scale
    return n, scale, n * gain + shift


def norm_backward(cot, n, scale, gain):
    dn = cot * gain
    mean = jnp.mean(dn, axis=1, keepdims=True)
    along = jnp.mean(dn * n, axis=1, keepdims=True)
    return scale * (dn - mean - n * along)


def chain(*steps):
    def run():
        for fn, *args in steps:
            fn(*args)

    return run


def window(first, rows, width):
    row = lax.broadcasted_iota(jnp.int32, (rows, width), 0)
    col = lax.broadcasted_iota(jnp.int32, (rows, width), 1)
    return jnp.where(col == row + first, 1.0, 0.0).astype(bf16)


def by_unit(order, steps, last):
    before, todo, behind, unit = [], {}, [], -1
    for name in order:
        if name[0] == "U":
            unit = int(name[1:])
        elif unit < 0:
            before.append(steps[name])
        elif unit == last:
            behind.append(steps[name])
        else:
            todo.setdefault(unit, []).append(steps[name])
    return before, todo, behind


def fill_table(tab, pairs, pairing, chip, n, heads):
    for c in range(n):
        tab[c] = pairs[0, c]
    for a in range(n):
        found = jnp.int32(0)
        for c in range(n):
            found = found + (pairs[0, c] == a).astype(jnp.int32) * c
        tab[n + a] = jnp.minimum(found, n - 1)
    for h in range(heads):
        tab[2 * n + h] = pairing[0, chip * heads + h]


def lse_lane(fold, h, i, g):
    return (h * (fold.n // 2) + i) * 2 + g


def attend_unit(fold, core, h, i, head_dim, tab, q_ref, k_ref, v_ref, o_ref, lse_ref):
    n, seg = fold.n, fold.seg
    paired = tab[2 * n + h]
    pf = paired.astype(f32)
    lanes = head_mask(h, head_dim, f32)
    lanes16 = head_mask(h, head_dim, bf16)
    parts = []
    for rows, keys, limit, count in fold.places(i, core, paired):
        q = q_ref[rows] * lanes16
        tail = mm(q, key_tiles(k_ref, keys, count - 2, 2), NT)
        tail = jnp.where(tail_mask(seg, limit), tail, very_low)
        top = jnp.max(tail, axis=1, keepdims=True)
        main = None
        if count > 2:
            main = mm(q, key_tiles(k_ref, keys, 0, count - 2), NT)
            top = jnp.maximum(top, jnp.max(main, axis=1, keepdims=True))
        parts.append((keys, count, main, tail, top))
    both = jnp.maximum(parts[0][4], parts[1][4])
    joined = jnp.broadcast_to(paired, both.shape) == 1
    outs = []
    for keys, count, main, tail, top in parts:
        top = jnp.where(joined, both, top)
        e = jnp.exp(tail - top)
        total = jnp.sum(e, axis=1, keepdims=True)
        acc = mm(e.astype(bf16), key_tiles(v_ref, keys, count - 2, 2))
        if main is not None:
            e = jnp.exp(main - top)
            total += jnp.sum(e, axis=1, keepdims=True)
            acc += mm(e.astype(bf16), key_tiles(v_ref, keys, 0, count - 2))
        outs.append((top, total, acc))
    (top_a, sum_a, acc_a), (top_b, sum_b, acc_b) = outs
    sum_a, sum_b = sum_a + pf * sum_b, jnp.where(joined, sum_a + sum_b, sum_b)
    acc_a = acc_a + pf * acc_b
    out_a = acc_a * (lanes / sum_a)
    out_b = acc_b * (lanes / sum_b)
    lane = lax.broadcasted_iota(jnp.int32, (1, KT), 1)
    lse = jnp.where(lane == lse_lane(fold, h, i, 0), top_a + jnp.log(sum_a), lse_ref[...])
    lse_ref[...] = jnp.where(lane == lse_lane(fold, h, i, 1), top_b + jnp.log(sum_b), lse)
    far, near, up = core * n + n - 1 - i, core * n + i, n + core * (n // 2) + i
    for at, value in ((far, (1.0 - pf) * out_a), (near, (1.0 - pf) * out_b), (up, pf * out_a)):
        o_ref[at] += value.astype(bf16)


FRONT_ORDER = (
    "ca", "cb", "bb", "se1", "ba", "xs", "se2", "ab1", "cc", "se3", "xt", "ab2", "aa1", "xl",
    "bc", "sw", "F", "U0", "aa2", "U1", "U2", "hs1", "bd", "ab3", "U3", "hs2", "U4", "U5",
    "cs1", "aa3", "U6", "gs1", "U7", "U8", "hs3", "U9", "U10", "gs2", "gs3", "U11", "bs1", "OC",
    "cs2", "OP", "gt3", "cs3", "ht2", "bs2", "ht3", "gt1", "cw", "ht1", "gt2", "gl", "ow", "M1",
    "V1", "hl", "bw", "V2", "bs3", "bx", "V3",
)


def front_kernel(
    nz, n, heads, head_dim, n_sem,
    pairs, pairing, x_ref, cot_ref, gain_ref, shift_ref, wq_i, wk_i, wv_i, wo_i, w1_i, w2_i,
    xall_o, wqkv_o, q_o, k_o, v_o, on_o, g_o, out_o, dh_o, lse_o, da_o,
    tab, xall, wqkv, q_ref, k_ref, v_ref, o_nat, o_ctx, o_part, o_sum, attn,
    w1, w2, wol, fq, fo, f1, f2, u_ref, z_ref, x1b_ref, acc_ref, n1_ref, r1_ref, dx1_ref, gs, gt, out_ref,
    ssem, rsem, lsem, fsem, gsem,
):
    p = Place()
    z = p.z
    seg, width = x_ref.shape[1], x_ref.shape[2]
    tok = 2 * seg
    fold = Fold(n, seg)
    d_rows, f_rows = wq_i.shape[0], w2_i.shape[0]
    n_f = w1_i.shape[1] // width
    cols = heads * head_dim
    half = d_rows // 2
    a1_rows, a2_rows = n_f * d_rows // 8, f_rows // 12
    b_first = 8 * a2_rows
    b_rows = (f_rows - b_first) // 2
    locals_ = []

    def keep(src, dst):
        cp = pltpu.make_async_copy(src, dst, lsem.at[len(locals_)])
        cp.start()
        locals_.append(cp)
        return cp

    masters = [
        pltpu.make_async_copy(src, dst, fsem.at[i])
        for i, (src, dst) in enumerate(
            ((wq_i, fq.at[0]), (wk_i, fq.at[1]), (wv_i, fq.at[2]), (w1_i, f1), (w2_i, f2), (wo_i, fo))
        )
    ]
    for cp in masters:
        cp.start()
    own_x = keep(x_ref, xall.at[p.core, p.chip])
    greet(p, (p.sib, p.xn, p.yn, p.dn), nz)
    net = Net(ssem, rsem, n_sem)
    tokens_ag = PlaneGather(net, p, lambda: x_ref, lambda k, q: xall.at[k, q], 2)
    tokens_ag.first()
    can_up, can_down = z < nz - 1, z > 0
    rows = pl.ds(p.core * half, half)
    other = pl.ds(p.other * half, half)

    class Stream:
        def __init__(self, at, after):
            self.up = [net.new() for _ in range(nz)]
            self.down = [net.new() for _ in range(nz)]
            self.at, self.todo = at, {}
            for t in range(1, nz):
                self.todo[t] = []
                for ids, src, frm, to, got, more in (
                    (self.up, z - t, p.down, p.up, z >= t, can_up),
                    (self.down, z + t, p.up, p.down, z + t < nz, can_down),
                ):
                    src = jnp.clip(src, 0, nz - 1)
                    on = jnp.logical_and(got, more)
                    self.todo[t].append((ids, src, frm, to, got, on, after(t, src, at, got)))

        def begin(self):
            own = lambda: self.at(z)
            net.send(self.up[1], own, own, p.up, can_up)
            net.send(self.down[1], own, own, p.down, can_down)

        def step(self, t):
            for ids, src, frm, to, got, on, _ in self.todo[t]:
                block = functools.partial(self.at, src)
                net.recv(ids[t], block, frm, got)
                if t + 1 < nz:
                    net.send(ids[t + 1], block, block, to, on)
            for *_, then in self.todo[t]:
                then()

    def share(waits, block_of):
        def after(t, src, at, got):
            idx = net.new()
            waits.append((idx, lambda: block_of(src), got))
            return lambda: net.send(idx, lambda: at(src), lambda: at(src), p.sib, got)

        return after

    def spread(gathers, slot_of, count):
        def after(t, src, at, got):
            slot = lambda k, q: slot_of(src, k, q)
            gather = PlaneGather(net, p, lambda: at(src), slot, count, got)
            gathers.setdefault(t, []).append(gather)
            return gather.first

        return after

    def a1_slot(o, k, q):
        start = pl.multiple_of(o * d_rows + lax.rem(q, 2) * a1_rows, 32)
        return w1.at[k * 2 + lax.div(q, 2), pl.ds(start, a1_rows)]

    def a2_slot(o, k, q):
        return w2.at[o, pl.ds(pl.multiple_of((k * 4 + q) * a2_rows, 32), a2_rows)]

    def b_slot(o, k):
        return w2.at[o, pl.ds(pl.multiple_of(b_first + k * b_rows, 32), b_rows)]

    sel_waits, b_waits, c_waits, a1_gathers, a2_gathers = [], [], [], {}, {}
    sel = Stream(lambda o: wqkv.at[o, rows], share(sel_waits, lambda o: wqkv.at[o, other]))
    cs = Stream(lambda o: wol.at[o, p.core], share(c_waits, lambda o: wol.at[o, p.other]))
    a1 = Stream(lambda o: a1_slot(o, p.core, p.chip), spread(a1_gathers, a1_slot, a1_rows))
    a2 = Stream(lambda o: a2_slot(o, p.core, p.chip), spread(a2_gathers, a2_slot, a2_rows))
    bs = Stream(lambda o: b_slot(o, p.core), share(b_waits, lambda o: b_slot(o, p.other)))

    for cp in masters[:3]:
        cp.wait()
    for chip in range(4):

        @pl.when(p.chip == chip)
        def _():
            for m in range(3):
                mine = fq[m, :, chip * cols : (chip + 1) * cols].astype(bf16)
                wqkv[z, :, m * LANES : m * LANES + cols] = mine

    for m in range(3):
        wqkv[z, :, m * LANES + cols : (m + 1) * LANES] = jnp.zeros((d_rows, LANES - cols), bf16)
    sel.begin()
    fill_table(tab, pairs, pairing, p.chip, n, heads)
    o_nat[...] = jnp.zeros(o_nat.shape, bf16)
    lse_o[...] = jnp.zeros(lse_o.shape, f32)
    part, swaps = net.new(), [net.new() for _ in range(3)]
    partners = ((p.chip_d, p.dn), (p.chip_x, p.xn), (p.chip_y, p.yn))

    def cast_inner():
        masters[3].wait()
        for f in range(n_f):
            at = pl.ds(pl.multiple_of(z * d_rows, 32), d_rows)
            w1[f, at, :] = f1[:, f * width : (f + 1) * width].astype(bf16)

    def cast_outer():
        masters[4].wait()

        def cast(i, _):
            at = pl.ds(pl.multiple_of(i * 64, 64), 64)
            w2[z, at, :] = f2[at, :].astype(bf16)
            return 0

        lax.fori_loop(0, f_rows // 64, cast, 0)

    def cast_output():
        masters[5].wait()
        four = jnp.concatenate([gain_ref[...], shift_ref[...], jnp.zeros((12, d_rows), f32)], axis=0)
        norms = mm(four.astype(bf16), window(z * d_rows, d_rows, width)).astype(bf16)
        for k in range(2):
            wol[z, k, :half, :] = fo[k * half : (k + 1) * half, :].astype(bf16)
            wol[z, k, half:, :] = norms

    def tokens_last():
        own_x.wait()
        tokens_ag.last()

    def wait_all(waits):
        for idx, block, got in waits:
            net.recv(idx, block, p.sib, got)

    def project_all():
        keep(xall, xall_o)
        keep(wqkv, wqkv_o)

        def four(i, _):
            tokens = jnp.concatenate([xall[natural(tab, n, 4 * i + u)] for u in range(4)], axis=0)
            qkv = mm(tokens, wqkv[...].reshape(-1, 3 * LANES))
            q = (qkv[:, :LANES].astype(bf16).astype(f32) * score_scale).astype(bf16)
            q_ref[pl.ds(4 * i, 4)] = q.reshape(4, seg, LANES)
            at = pl.ds(i * (4 * seg // KT), 4 * seg // KT)
            k_ref[at] = qkv[:, LANES : 2 * LANES].astype(bf16).reshape(-1, KT, LANES)
            v_ref[at] = qkv[:, 2 * LANES :].astype(bf16).reshape(-1, KT, LANES)
            return 0

        lax.fori_loop(0, n // 2, four, 0)
        for src, dst in ((q_ref, q_o), (k_ref, k_o), (v_ref, v_o)):
            keep(src, dst)

    def heads_out():
        keep(o_nat, on_o)
        for core_is in range(2):
            for q in range(n // 2):
                a = tab[2 * q + core_is]
                for u, s in ((0, a), (1, 2 * n - 1 - a)):
                    o_ctx[core_is, q, u * seg : (u + 1) * seg, :] = o_nat[s]
        net.send(part, o_ctx.at[p.other], o_part, p.sib)

    def owners_out():
        net.recv(part, o_part, p.sib)
        for idx, (chip, dev) in zip(swaps, partners):
            o_sum[chip] = o_ctx[p.core, chip] + o_part[chip]
            net.send(idx, o_sum.at[chip], attn.at[p.chip], dev)
        attn[p.chip] = o_ctx[p.core, p.chip] + o_part[p.chip]

    def owners_wait():
        for idx, (chip, dev) in zip(swaps, partners):
            net.recv(idx, attn.at[chip], dev)

    wo_of = lambda o: jnp.concatenate([wol[o, 0, :half, :], wol[o, 1, :half, :]], axis=0)
    kept = {}

    def first_norm():
        vec = wol[0, 0, half:, :].astype(f32)
        for o in range(1, nz):
            vec = vec + wol[o, 0, half:, :].astype(f32)
        h1 = x_ref[...].reshape(tok, width).astype(f32)
        for o in range(nz):
            h1 = h1 + mm(attn[o, :, :cols], wo_of(o))
        n1, r1, x1 = norm_forward(h1, vec[0:1], vec[2:3])
        n1_ref[...] = n1
        r1_ref[...] = jnp.broadcast_to(r1, (tok, 128))
        x1b_ref[...] = x1.astype(bf16)
        acc_ref[...] = x1
        kept["vec"] = vec

    def inner_all():
        def up(f, _):
            u = mm(x1b_ref[...], w1[f])
            cdf = 0.5 + 0.5 * lax.erf(u * (0.5**0.5))
            z_ref[f] = (u * cdf).astype(bf16)
            u_ref[f] = cdf + u * jnp.exp(-0.5 * u * u) * 0.3989422804014327
            return 0

        lax.fori_loop(0, n_f, up, 0)

    far = jnp.where(2 * z < nz, n_f - 1, 0)

    def outer_near():
        def add(i, _):
            f = i + jnp.where(far == 0, 1, 0)
            acc_ref[...] += mm(z_ref[f], w2[f])
            return 0

        lax.fori_loop(0, n_f - 1, add, 0)

    def outer_far():
        acc_ref[...] += mm(z_ref[far], w2[far])

    def each(gathers, t, stage):
        for gather in gathers[t]:
            getattr(gather, stage)()

    def all_last(gathers):
        for t in gathers:
            each(gathers, t, "last")

    steps = {
        "ca": cast_inner, "cb": cast_outer, "cc": cast_output, "ba": a1.begin, "bb": a2.begin,
        "bc": cs.begin, "bd": bs.begin, "xs": tokens_ag.second, "xt": tokens_ag.third,
        "xl": tokens_last, "sw": lambda: wait_all(sel_waits), "cw": lambda: wait_all(c_waits),
        "bw": lambda: wait_all(b_waits[:-2]), "bx": lambda: wait_all(b_waits[-2:]),
        "F": project_all, "OC": heads_out, "OP": owners_out,
        "ow": owners_wait, "M1": first_norm, "V1": inner_all, "V2": outer_near, "V3": outer_far,
        "gl": lambda: all_last(a1_gathers), "hl": lambda: all_last(a2_gathers),
    }
    for t in range(1, nz):
        for name, stream in (("se", sel), ("cs", cs), ("aa", a1), ("ab", a2), ("bs", bs)):
            steps[f"{name}{t}"] = functools.partial(stream.step, t)
        for name, gathers in (("g", a1_gathers), ("h", a2_gathers)):
            steps[f"{name}s{t}"] = functools.partial(each, gathers, t, "second")
            steps[f"{name}t{t}"] = functools.partial(each, gathers, t, "third")
    units = n // 2
    before, todo, behind = by_unit(FRONT_ORDER, steps, units * heads - 1)
    for step in before:
        step()

    def head(h, _):
        for i in range(units):
            attend_unit(fold, p.core, h, i, head_dim, tab, q_ref, k_ref, v_ref, o_nat, lse_o)
            for hh in range(heads):
                if hh * units + i in todo:
                    pl.when(h == hh)(chain(*((step,) for step in todo[hh * units + i])))
        return 0

    lax.fori_loop(0, heads, head, 0)
    for step in behind:
        step()
    vec = kept["vec"]
    gain1, gain2, shift2 = vec[0:1], vec[1:2], vec[3:4]
    n2, r2, out = norm_forward(acc_ref[...], gain2, shift2)
    out_ref[...] = out.astype(bf16)
    keep(out_ref, out_o)
    cot = cot_ref[...].astype(f32)
    d_gain2 = jnp.sum(cot * n2, axis=0, keepdims=True)
    d_shift2 = jnp.sum(cot, axis=0, keepdims=True)
    dh2 = norm_backward(cot, n2, r2, gain2)
    dx1_ref[...] = dh2
    df = dh2.astype(bf16)
    first1, first2 = f_rows, f_rows + n_f * d_rows

    def grads_out(f, slot):
        yield pltpu.make_async_copy(gs.at[slot, 0], g_o.at[f, pl.ds(0, f_rows)], gsem.at[slot, 0])
        for o in range(nz):
            at = pl.ds(pl.multiple_of(first1 + f * d_rows, 32), d_rows)
            src = gs.at[slot, 1, pl.ds(o * d_rows, d_rows)]
            yield pltpu.make_async_copy(src, g_o.at[o, at], gsem.at[slot, 1 + o])

    def back(f, _):
        slot = lax.rem(f, 2)

        @pl.when(f >= 2)
        def _():
            for cp in grads_out(f - 2, slot):
                cp.wait()

        gs[slot, 0] = mm(z_ref[f], df, TN).astype(bf16)
        du = (mm(df, w2[f], NT) * u_ref[f]).astype(bf16)
        gs[slot, 1] = mm(x1b_ref[...], du, TN).astype(bf16)
        for cp in grads_out(f, slot):
            cp.start()
        dx1_ref[...] += mm(du, w1[f], NT)
        return 0

    lax.fori_loop(0, n_f, back, 0)
    d_x1 = dx1_ref[...]
    n1 = n1_ref[...]
    d_gain1 = jnp.sum(d_x1 * n1, axis=0, keepdims=True)
    d_shift1 = jnp.sum(d_x1, axis=0, keepdims=True)
    dh1 = norm_backward(d_x1, n1, r1_ref[:, :1], gain1)
    dx1_ref[...] = dh1
    keep(dx1_ref, dh_o)
    dy = dh1.astype(bf16)
    norms = jnp.concatenate([d_gain1, d_gain2, d_shift1, d_shift2], axis=0).astype(bf16)
    ends = []
    for o in range(nz):
        da_o[o, :, :cols] = mm(dy, wo_of(o), NT).astype(bf16)
        da_o[o, :, cols:] = jnp.zeros((tok, LANES - cols), bf16)
        gt[o, :d_rows, :] = mm(attn[o, :, :cols], dy, TN).astype(bf16)
        gt[o, d_rows:, :] = jnp.zeros((gt.shape[1] - d_rows, width), bf16)
        gt[o, d_rows : d_rows + 4, :] = norms
        ends.append(pltpu.make_async_copy(gt.at[o], g_o.at[o, pl.ds(first2, gt.shape[1])], fsem.at[o]))
        ends[-1].start()
    for f in range(max(n_f - 2, 0), n_f):
        for cp in grads_out(f, f % 2):
            cp.wait()
    for cp in ends:
        cp.wait()
    net.finish()
    for cp in locals_[1:]:
        cp.wait()


def front(nz, n, heads, head_dim, total, pairs, pairing, x_in, cot, gains, shifts, weights):
    tok, width = x_in.shape
    seg = tok // 2
    d_rows, f_rows = weights[0].shape[0], weights[5].shape[0]
    n_f = weights[4].shape[1] // width
    n_sem = 11 * (4 * (nz - 1) + 1) + 5 * 2 * nz + 3 * 2 * (nz - 1) + 4
    wide, tiled = (2 * n, seg, LANES), (tok * n // KT, KT, LANES)
    shapes = [(2, 4, 2, seg, width), (nz, d_rows, 3 * LANES), wide, tiled, tiled, wide]
    block = (4, tok, LANES)
    sds = jax.ShapeDtypeStruct
    vb = lambda *s: pltpu.VMEM(s, bf16)
    vf = lambda *s: pltpu.VMEM(s, f32)
    return pl.pallas_call(
        functools.partial(front_kernel, nz, n, heads, head_dim, n_sem),
        out_shape=tuple(sds(s, bf16) for s in shapes)
        + (
            sds((nz, total, width), bf16),
            sds((tok, width), bf16),
            sds((tok, width), f32),
            sds((seg, KT), f32),
            sds(block, bf16),
        ),
        in_specs=smem(2) + vmem(4) + hbm(6),
        out_specs=tuple(hbm(9) + vmem(2)),
        scratch_shapes=[pltpu.SMEM((2 * n + heads,), jnp.int32)]
        + [vb(*s) for s in shapes]
        + [
            vb(2, *block),
            vb(*block),
            vb(*block),
            vb(*block),
            vb(n_f, nz * d_rows, width),
            vb(nz, f_rows, width),
            vb(nz, 2, d_rows // 2 + 16, width),
            vf(3, d_rows, width),
            vf(d_rows, width),
            vf(d_rows, n_f * width),
            vf(f_rows, width),
            vf(n_f, tok, width),
            vb(n_f, tok, width),
            vb(tok, width),
            vf(tok, width),
            vf(tok, width),
            vf(tok, 128),
            vf(tok, width),
            vb(2, 2, f_rows, width),
            vb(nz, total - f_rows - n_f * d_rows, width),
            vb(tok, width),
            pltpu.SemaphoreType.DMA((n_sem,)),
            pltpu.SemaphoreType.DMA((n_sem,)),
            pltpu.SemaphoreType.DMA((12,)),
            pltpu.SemaphoreType.DMA((6,)),
            pltpu.SemaphoreType.DMA((2, 1 + nz)),
        ],
        compiler_params=comm_params(0),
        name="front",
    )(pairs, pairing, x_in.reshape(2, seg, width), cot, gains, shifts, *weights)


def add_into(dst, src, rows):
    chunk = max(c for c in range(16, min(rows, 160) + 1, 16) if rows % c == 0)

    def step(i, _):
        at = pl.ds(pl.multiple_of(i * chunk, chunk), chunk)
        to, frm = of(dst), of(src)
        to[at, :] = to[at, :] + frm[at, :]
        return 0

    lax.fori_loop(0, rows // chunk, step, 0)


class Slot:
    def __init__(self, ref, o):
        self.ref, self.o = ref, o

    def __call__(self):
        return self.ref.at[self.o]

    @property
    def at(self):
        return self().at


class PlaneSum:
    def __init__(self, net, place, block, rows, rx0, ry1, ry0, rx1):
        p = place
        self.net, self.place = net, place
        self.rx0, self.ry1, self.ry0, self.rx1 = rx0, ry1, ry0, rx1
        self.h = rows // 2
        h0, h1 = pl.ds(0, self.h), pl.ds(self.h, self.h)
        far_x, far_y = 1 - p.x, 1 - p.y
        self.block, self.h0, self.h1 = block, h0, h1
        self.far_x, self.far_y = far_x, far_y
        self.to_x = [2 * j + far_x for j in range(2)]
        self.to_y = [2 * far_y + j for j in range(2)]
        self.on_y, self.on_x = 2 * far_y + p.x, 2 * p.y + far_x
        self.ids = [net.new() for _ in range(6)]

    def part(self, index, half):
        return lambda: self.block(index).at[half]

    def first(self):
        n, p, i = self.net, self.place, self.ids
        for j in range(2):
            n.send(i[j], self.part(self.to_x[j], self.h0), lambda j=j: self.rx0.at[j], p.xn)
            n.send(i[2 + j], self.part(self.to_y[j], self.h1), lambda j=j: self.ry1.at[j], p.yn)

    def second(self):
        n, p, i = self.net, self.place, self.ids
        on_y, on_x = self.part(self.on_y, self.h0), self.part(self.on_x, self.h1)
        mine0, mine1 = self.part(p.chip, self.h0), self.part(p.chip, self.h1)
        for j in range(2):
            n.recv(i[j], lambda j=j: self.rx0.at[j], p.xn)
        add_into(on_y, lambda: self.rx0.at[self.far_y], self.h)
        n.send(i[4], on_y, self.ry0, p.yn)
        for j in range(2):
            n.recv(i[2 + j], lambda j=j: self.ry1.at[j], p.yn)
        add_into(on_x, lambda: self.ry1.at[self.far_x], self.h)
        n.send(i[5], on_x, self.rx1, p.xn)
        add_into(mine0, lambda: self.rx0.at[p.y], self.h)
        add_into(mine1, lambda: self.ry1.at[p.x], self.h)

    def third(self):
        n, p, i = self.net, self.place, self.ids
        n.recv(i[4], self.ry0, p.yn)
        add_into(self.part(p.chip, self.h0), self.ry0, self.h)
        n.recv(i[5], self.rx1, p.xn)
        add_into(self.part(p.chip, self.h1), self.rx1, self.h)


class LineSum:
    def __init__(self, net, place, nz, whole, low, high, parts, rows):
        p, z, top = place, place.z, nz - 1
        self.net, self.top, self.parts, self.rows, self.whole = net, top, parts, rows, whole
        sides = (
            ([net.new() for _ in range(nz)], low, z, -1, p.down, p.up),
            ([net.new() for _ in range(nz)], high, top - z, 1, p.up, p.down),
        )
        self.todo = {}
        for t in range(nz):
            self.todo[t] = []
            for ids, buf, depth, sign, frm, to in sides:
                owner = jnp.clip(top - t + z if sign < 0 else t + z - top, 0, top)
                takes = jnp.logical_and(depth > 0, depth <= t)
                self.todo[t].append(
                    (ids, owner, buf, takes, depth <= t, frm, to)
                )

    def step(self, t):
        n = self.net
        for ids, owner, buf, takes, sends, frm, to in self.todo[t]:
            whole = functools.partial(self.whole, owner)
            landed = lambda buf=buf, owner=owner: buf.at[owner]

            def take(ids=ids, whole=whole, landed=landed, frm=frm):
                n.recv(ids[t - 1], landed, frm)
                if self.parts is None:
                    add_into(whole, landed, self.rows)
                else:
                    for j in range(self.parts):
                        add_into(
                            lambda j=j: whole().at[j], lambda j=j: landed().at[j], self.rows
                        )

            if t > 0:
                maybe(takes, take)
            if t < self.top:
                n.send(ids[t], whole, landed, to, sends)


def attend_back_unit(
    fold, core, h, i, head_dim, tab, q_ref, k_ref, v_ref, o_ref, lse_ref, da_ref,
    dcat_ref, dk_ref, dv_ref,
):
    n, seg, half = fold.n, fold.seg, fold.half
    paired = tab[2 * n + h]
    pf = paired.astype(f32)
    lanes = head_mask(h, head_dim, f32)
    lanes16 = head_mask(h, head_dim, bf16)
    dqs = []
    places = fold.places(i, core, paired)
    for g, (rows, keys, limit, count) in enumerate(places):
        q = q_ref[rows] * lanes16
        k, c, upper = natural(tab, n, rows)
        da = da_ref[k, c, upper] * lanes16
        delta = jnp.sum(
            da.astype(f32) * o_ref[rows].astype(f32), axis=1, keepdims=True
        )
        lane = lax.broadcasted_iota(jnp.int32, (1, KT), 1) == lse_lane(fold, h, i, g)
        lse = jnp.sum(jnp.where(lane, lse_ref[...], 0.0), axis=1, keepdims=True)
        dq = None
        pieces = [(count - 2, 2, True)]
        if count > 2:
            pieces.append((0, count - 2, False))
        for first, size, masked in pieces:
            kt = key_tiles(k_ref, keys, first, size)
            vt = key_tiles(v_ref, keys, first, size)
            pr = jnp.exp(mm(q, kt, NT) - lse)
            if masked:
                pr = jnp.where(tail_mask(seg, limit), pr, 0.0)
            ds = (pr * (mm(da, vt, NT) - delta)).astype(bf16)
            part = mm(ds, kt)
            dq = part if dq is None else dq + part
            dv = mm(pr.astype(bf16), da, TN)
            dk = mm(ds, q, TN)
            at = pl.ds(first * KT, size * KT)
            if g == 0 or masked:
                dk_ref[at, :] += dk
                dv_ref[at, :] += dv
            else:
                beyond = pl.ds(places[0][3] * KT, size * KT)
                dk_ref[at, :] += (1.0 - pf) * dk
                dv_ref[at, :] += (1.0 - pf) * dv
                dk_ref[beyond, :] += pf * dk
                dv_ref[beyond, :] += pf * dv
        dqs.append(dq)
    scaled = lanes * score_scale
    dq_a, dq_b = (dqs[0] + pf * dqs[1]) * scaled, dqs[1] * scaled
    far, near, up = core * n + n - 1 - i, core * n + i, n + core * (n // 2) + i
    for at, value in ((far, (1.0 - pf) * dq_a), (near, (1.0 - pf) * dq_b), (up, pf * dq_a)):
        dcat_ref[at, :, :LANES] += value.astype(bf16)


def place_key_grads(fold, core, paired, dk_ref, dv_ref, dcat_ref):
    n, seg, half = fold.n, fold.seg, fold.half
    pf = paired.astype(f32)

    def spread(j, _):
        at = pl.ds(pl.multiple_of(j * seg, seg), seg)
        for src, lanes in ((dk_ref, slice(LANES, 2 * LANES)), (dv_ref, slice(2 * LANES, None))):
            value = src[at, :]
            dcat_ref[core * n + j, :, lanes] += ((1.0 - pf) * value).astype(bf16)
            dcat_ref[j, :, lanes] += (pf * value).astype(bf16)
        return 0

    lax.fori_loop(0, n, spread, 0)


BACKWARD_ORDER = (
    "dr", "c1", "c0", "s3", "p1f", "dw", "U0", "lb0", "s2", "p0f", "U1", "U2", "U3", "U4",
    "p1s", "c2", "U5", "p2f", "c3", "U6", "lb1", "U7", "U8", "U9", "p3f", "U10", "U11", "p0s",
    "DXo", "lb2", "p1t", "p3s", "p0t", "p2s", "DXm", "xa", "la0", "xsf", "DW", "p3t", "wa",
    "lb3", "wl0", "p2t", "la1", "pbf", "xss", "wl1", "pbs", "la2", "pbt", "fbf", "fbs", "xst",
    "la3", "faf", "wl2", "wl3", "wff", "fbt", "fas", "wfs", "tok", "fat", "wft", "fal", "wfl",
    "fbl", "dwo",
)


def backward_kernel(
    nz, n, heads, head_dim, rb, n_sem,
    pairs, pairing, g_ref, da_in, dh_i, xall_i, wqkv_i, q_i, k_i, v_i, on_i, lse_ref,
    gsum_o, dtok_o, dw_o,
    tab, g_kept, g_sib, g_rx0, g_ry1, g_ry0, g_rx1, g_low, g_high,
    b_low, b_high, b_rx0, b_ry1, b_ry0, b_rx1,
    x_part, x_sib, x_rx0, x_ry1, x_ry0, x_rx1, w_part, w_sib, w_low, w_high, w_all,
    da_all, xall, wqkv, q_ref, k_ref, v_ref, on_ref, dcat, dk_ref, dv_ref, dw_acc, dh_ref,
    ssem, rsem, lsem,
):
    p = Place()
    z = p.z
    seg, width = xall.shape[3], xall.shape[4]
    tok = 2 * seg
    fold = Fold(n, seg)
    rows = g_ref.shape[3]
    ra = rows - rb
    ax, bx = pl.ds(0, ra), pl.ds(ra, rb)
    order = line_order(nz)
    local = []

    def fetch(src, dst):
        cp = pltpu.make_async_copy(src, dst, lsem.at[len(local)])
        cp.start()
        local.append(cp)
        return cp

    net = Net(ssem, rsem, n_sem)
    own_da = fetch(da_in.at[p.chip], da_all.at[p.core, p.chip])
    own_g = {o: fetch(g_ref.at[o, p.core], g_kept.at[o]) for o in order}
    greet(p, (p.sib, p.xn, p.yn, p.dn), nz)
    swaps = [net.new() for _ in range(7)]
    partners = ((p.chip_d, p.dn), (p.chip_x, p.xn), (p.chip_y, p.yn))
    for i, (chip, dev) in enumerate(partners):
        net.send(swaps[i], da_in.at[chip], da_all.at[p.core, p.chip], dev)
    net.send(swaps[3], da_in.at[p.chip], da_all.at[p.core, p.chip], p.sib)
    sib_ids = {o: net.new() for o in order}

    def to_sib(o):
        net.send(sib_ids[o], lambda: g_ref.at[o, p.other], lambda: g_sib.at[o], p.sib)

    to_sib(order[0])
    to_sib(order[1])
    att_in = [
        fetch(src, dst)
        for src, dst in (
            (q_i, q_ref), (k_i, k_ref), (v_i, v_ref), (on_i, on_ref), (xall_i, xall), (wqkv_i, wqkv),
            (dh_i, dh_ref),
        )
    ]
    fill_table(tab, pairs, pairing, p.chip, n, heads)
    dcat[...] = jnp.zeros(dcat.shape, bf16)

    plane = {
        o: PlaneSum(
            net, p, lambda q, o=o: g_kept.at[o, q].at[ax], ra,
            *(Slot(r, o) for r in (g_rx0, g_ry1, g_ry0, g_rx1)),
        )
        for o in order
    }
    line_a = LineSum(net, p, nz, lambda o: g_kept.at[o, p.chip].at[ax], g_low, g_high, None, ra)
    line_b = LineSum(net, p, nz, lambda o: g_kept.at[o, :, bx], b_low, b_high, n // 2, rb)
    plane_b = PlaneSum(
        net, p, lambda q: g_kept.at[z, q].at[bx], rb, b_rx0, b_ry1, b_ry0, b_rx1
    )

    def chip_sum(o):
        net.recv(sib_ids[o], lambda: g_sib.at[o], p.sib)
        pltpu.make_async_copy(g_ref.at[o, p.core], g_kept.at[o], lsem.at[1 + order.index(o)]).wait()
        for q in range(n // 2):
            add_into(lambda q=q: g_kept.at[o, q], lambda q=q: g_sib.at[o, q], rows)

    d = wqkv.shape[1]
    half = d // 2
    x_id, w_id = net.new(), net.new()
    w_line = LineSum(net, p, nz, lambda o: w_part.at[p.core, o], w_low, w_high, None, half)
    xs = PlaneSum(net, p, lambda q: x_part.at[p.core, q], tok, x_rx0, x_ry1, x_ry0, x_rx1)
    final_a = PlaneGather(
        net, p, lambda: g_kept.at[z, p.chip].at[ax], lambda k, q: gsum_o.at[k, q].at[ax], ra
    )
    final_b = PlaneGather(
        net, p, lambda: g_kept.at[z, p.chip].at[bx], lambda k, q: gsum_o.at[k, q].at[bx], rb
    )
    w_final = PlaneGather(net, p, lambda: w_part.at[p.core, z], lambda k, q: w_all.at[k, q], half)
    cols = heads * head_dim

    def da_forward():
        for i, chip, dev in ((1, p.chip_x, p.xn), (2, p.chip_y, p.yn), (0, p.chip_d, p.dn)):
            block = lambda chip=chip: da_all.at[p.core, chip]
            net.recv(swaps[i], block, dev)
            net.send(swaps[4 + i], block, block, p.sib)

    def da_wait():
        for i, chip in ((3, p.chip), (5, p.chip_x), (6, p.chip_y), (4, p.chip_d)):
            net.recv(swaps[i], lambda chip=chip: da_all.at[p.other, chip], p.sib)
        own_da.wait()
        for cp in att_in:
            cp.wait()

    def block_grads(k, q):
        a = tab[2 * q + k]
        return jnp.concatenate([dcat[a], dcat[2 * n - 1 - a]], axis=0)

    def weight_grads():
        dw_acc[...] = jnp.zeros(dw_acc.shape, f32)

        def weights(c, _):
            k, q = lax.rem(c, 2), c // 2
            dw_acc[...] += mm(xall[k, q].reshape(tok, width), block_grads(k, q), TN)
            return 0

        lax.fori_loop(0, n, weights, 0)
        for o in range(nz):
            w_part[0, o] = dw_acc[o * d : o * d + half].astype(bf16)
            w_part[1, o] = dw_acc[o * d + half : (o + 1) * d].astype(bf16)
        net.send(w_id, w_part.at[p.other], w_sib, p.sib)

    def weight_sum():
        net.recv(w_id, w_sib, p.sib)
        for o in range(nz):
            add_into(w_part.at[p.core, o], w_sib.at[o], half)

    def tokens_of(k):
        def one(q, _):
            w = wqkv[...].reshape(-1, 3 * LANES)
            x_part[k, q] = mm(block_grads(k, q), w, NT).astype(bf16)
            return 0

        lax.fori_loop(0, n // 2, one, 0)

    def tokens_other():
        tokens_of(p.other)
        net.send(x_id, x_part.at[p.other], x_sib, p.sib)

    def tokens_sum():
        net.recv(x_id, x_sib, p.sib)
        for q in range(n // 2):
            add_into(x_part.at[p.core, q], x_sib.at[q], tok)

    def tokens_out():
        def add_tokens(i, _):
            at = pl.ds(pl.multiple_of(i * 32, 32), 32)
            dtok_o[at, :] = (dh_ref[at, :] + x_part[p.core, p.chip, at, :].astype(f32)).astype(bf16)
            return 0

        lax.fori_loop(0, tok // 32, add_tokens, 0)

    def own_w():
        return pltpu.make_async_copy(
            w_part.at[p.core, z], w_all.at[p.core, p.chip], lsem.at[31]
        )

    def w_final_first():
        w_final.first()
        own_w().start()

    def own_g_out(i, at):
        src, dst = g_kept.at[z, p.chip].at[at], gsum_o.at[p.core, p.chip].at[at]
        return pltpu.make_async_copy(src, dst, lsem.at[i])

    def final_first(gather, i, at):
        gather.first()
        own_g_out(i, at).start()

    def w_out():
        own_w().wait()
        for j in range(3):
            for k in range(2):
                dw_o[j, k * half : (k + 1) * half, :] = jnp.concatenate(
                    [w_all[k, q][:, j * LANES : j * LANES + cols] for q in range(4)], axis=1
                )

    steps = {
        "dr": da_forward, "dw": da_wait, "DW": weight_grads, "wa": weight_sum,
        "DXo": tokens_other, "DXm": lambda: tokens_of(p.core), "xa": tokens_sum, "tok": tokens_out,
        "dwo": w_out, "wff": w_final_first,
        "faf": lambda: final_first(final_a, 29, ax), "fbf": lambda: final_first(final_b, 30, bx),
    }
    for k, o in enumerate(order):
        steps[f"s{k}"] = functools.partial(to_sib, o)
        steps[f"c{k}"] = functools.partial(chip_sum, o)
        steps[f"p{k}f"], steps[f"p{k}s"] = plane[o].first, plane[o].second
        steps[f"p{k}t"] = plane[o].third
    for name, line in (("la", line_a), ("lb", line_b), ("wl", w_line)):
        for t in range(nz):
            steps[f"{name}{t}"] = functools.partial(line.step, t)
    for name, thing in (("pb", plane_b), ("xs", xs), ("fa", final_a), ("fb", final_b), ("wf", w_final)):
        for stage in ("first", "second", "third", "last"):
            if hasattr(thing, stage):
                steps.setdefault(name + stage[0], getattr(thing, stage))
    units = n // 2
    before, todo, behind = by_unit(BACKWARD_ORDER, steps, units * heads - 1)
    for step in before:
        step()

    def head(h, _):
        dk_ref[...] = jnp.zeros(dk_ref.shape, f32)
        dv_ref[...] = jnp.zeros(dv_ref.shape, f32)
        for i in range(units):
            attend_back_unit(
                fold, p.core, h, i, head_dim, tab, q_ref, k_ref, v_ref, on_ref, lse_ref, da_all,
                dcat, dk_ref, dv_ref,
            )
            for hh in range(heads):
                if hh * units + i in todo:
                    pl.when(h == hh)(chain(*((step,) for step in todo[hh * units + i])))
        place_key_grads(fold, p.core, tab[2 * n + h], dk_ref, dv_ref, dcat)
        return 0

    lax.fori_loop(0, heads, head, 0)
    for step in behind:
        step()
    for i, at in ((29, ax), (30, bx)):
        own_g_out(i, at).wait()
    net.finish()


def line_order(nz):
    order = []
    for i in range((nz + 1) // 2):
        for o in (nz - 1 - i, i):
            if o not in order:
                order.append(o)
    return order


def backward(
    nz, n, heads, head_dim, rb, pairs, pairing, grads, da, dh, xall, wqkv, q, k, v, on, lse
):
    rows, width = grads.shape[3], grads.shape[4]
    seg = xall.shape[3]
    tok = 2 * seg
    d_rows = wqkv.shape[1]
    half = d_rows // 2
    ra = rows - rb
    n_sem = 6 * (nz + 2) + 6 * nz + nz + 9 + 33 + 2
    sds = jax.ShapeDtypeStruct
    vm = lambda *shape: pltpu.VMEM(shape, bf16)
    wide, tiled = (2 * n, seg, LANES), (tok * n // KT, KT, LANES)
    da = da.reshape(4, 2, seg, LANES)
    return pl.pallas_call(
        functools.partial(backward_kernel, nz, n, heads, head_dim, rb, n_sem),
        out_shape=(
            sds(grads.shape[1:], bf16),
            sds((tok, width), bf16),
            sds((3, d_rows, width), bf16),
        ),
        in_specs=smem(2) + hbm(9) + vmem(1),
        out_specs=tuple(hbm(1) + vmem(2)),
        scratch_shapes=[
            pltpu.SMEM((2 * n + heads,), jnp.int32),
            vm(nz, 4, rows, width),
            vm(nz, 4, rows, width),
            vm(nz, 2, ra // 2, width),
            vm(nz, 2, ra // 2, width),
            vm(nz, ra // 2, width),
            vm(nz, ra // 2, width),
            vm(nz, ra, width),
            vm(nz, ra, width),
            vm(nz, 4, rb, width),
            vm(nz, 4, rb, width),
            vm(2, rb // 2, width),
            vm(2, rb // 2, width),
            vm(rb // 2, width),
            vm(rb // 2, width),
            vm(2, 4, tok, width),
            vm(4, tok, width),
            vm(2, tok // 2, width),
            vm(2, tok // 2, width),
            vm(tok // 2, width),
            vm(tok // 2, width),
            vm(2, nz, half, width),
            vm(nz, half, width),
            vm(nz, half, width),
            vm(nz, half, width),
            vm(2, 4, half, width),
            vm(2, 4, 2, seg, LANES),
            vm(2, 4, 2, seg, width),
            vm(nz, d_rows, width),
            vm(*wide),
            vm(*tiled),
            vm(*tiled),
            vm(*wide),
            vm(2 * n, seg, 3 * LANES),
            pltpu.VMEM((seg * n, LANES), f32),
            pltpu.VMEM((seg * n, LANES), f32),
            pltpu.VMEM((width, 3 * LANES), f32),
            pltpu.VMEM((tok, width), f32),
            pltpu.SemaphoreType.DMA((n_sem,)),
            pltpu.SemaphoreType.DMA((n_sem,)),
            pltpu.SemaphoreType.DMA((32,)),
        ],
        compiler_params=comm_params(1),
        name="backward",
    )(pairs, pairing, grads, da, dh, xall, wqkv, q, k, v, on, lse)


def finish_kernel(outer, inner, output, norms, dw, result, tokens, *outs):
    outer_o, inner_o, output_o, query_o, key_o, value_o, gain_o, shift_o, result_o, tokens_o = outs
    outer_o[...] = outer[...].astype(f32)
    rows, width = inner_o.shape[0], norms.shape[1]
    for k in range(inner.shape[0] // rows):
        inner_o[:, k * width : (k + 1) * width] = inner[k * rows : (k + 1) * rows, :].astype(f32)
    output_o[...] = output[...].astype(f32)
    for j, out in enumerate((query_o, key_o, value_o)):
        out[...] = dw[j].astype(f32)
    result_o[...] = result[...]
    tokens_o[...] = tokens[...]

    @pl.when(pl.program_id(0) == 0)
    def _():
        first = lax.axis_index("fsdp") * rows
        mine = mm(norms[:16, :], window(first, rows, width), NT)
        gain_o[...] = mine[0:2]
        shift_o[...] = mine[2:4]


def finish(gsum, dw, result, dtok, d_rows, f_rows, n_f):
    tok, width = result.shape
    used = f_rows + n_f * d_rows + d_rows
    steps = n_f // 2
    per = n_f // steps
    o_rows, s_rows, t_rows = f_rows // steps, d_rows // steps, tok // steps
    tail = gsum.shape[0] - used
    sds = jax.ShapeDtypeStruct
    square, pair = (d_rows, width), (2, d_rows)
    strip = lambda rows, first=0: pl.BlockSpec((rows, width), lambda f: (first + f, 0))
    return pl.pallas_call(
        finish_kernel,
        grid=(steps,),
        out_shape=(sds((f_rows, width), f32), sds((d_rows, n_f * width), f32))
        + (sds(square, f32),) * 4
        + (sds(pair, f32),) * 2
        + (sds((tok, width), bf16),) * 2,
        in_specs=[
            strip(o_rows),
            strip(per * d_rows, f_rows // (per * d_rows)),
            strip(s_rows, (used - d_rows) // s_rows),
            pl.BlockSpec((tail, width), lambda f: (used // tail, 0)),
            pl.BlockSpec((3, s_rows, width), lambda f: (0, f, 0)),
            strip(t_rows),
            strip(t_rows),
        ],
        out_specs=(strip(o_rows), pl.BlockSpec((d_rows, per * width), lambda f: (0, f)))
        + (strip(s_rows),) * 4
        + (pl.BlockSpec(pair, lambda f: (0, 0)),) * 2
        + (strip(t_rows),) * 2,
        compiler_params=pltpu.CompilerParams(vmem_limit_bytes=60 << 20),
        name="finish",
    )(gsum, gsum, gsum, gsum, dw, result, dtok)


def fast_body(
    tokens,
    w_query,
    w_key,
    w_value,
    w_output,
    w_inner,
    w_outer,
    ln_gain,
    ln_bias,
    pairing,
    block_pairs,
    cotangent,
):
    tok, width = tokens.shape[1], tokens.shape[2]
    n_ctx, nz = lax.axis_size("ctx"), lax.axis_size("fsdp")
    heads = pairing.shape[1]
    my_heads, head_dim = heads // 4, width // heads
    d_rows = w_query.shape[0]
    f_rows, ff = w_outer.shape[0], w_inner.shape[1]
    n_f = ff // width
    used = f_rows + n_f * d_rows + d_rows
    total = -(-(used + 4) // 256) * 256
    weights = (w_query, w_key, w_value, w_output, w_inner, w_outer)
    xall, wqkv, q, k, v, on, grads, result, d_h1, lse, da = front(
        nz, n_ctx, my_heads, head_dim, total, block_pairs, pairing, tokens[0], cotangent[0],
        ln_gain.T, ln_bias.T, weights,
    )
    grads = grads.reshape(nz, 2, 4, total // 8, width)
    gsum, dtok, dw = backward(
        nz, n_ctx, my_heads, head_dim, 64, block_pairs, pairing, grads, da, d_h1,
        xall, wqkv, q, k, v, on, lse,
    )
    gsum = gsum.reshape(total, width)
    d_outer, d_inner, d_output, d_query, d_key, d_value, d_gain, d_shift, result, dtok = finish(
        gsum, dw, result, dtok, d_rows, f_rows, n_f
    )
    return (
        result[None],
        dtok[None],
        d_query,
        d_key,
        d_value,
        d_output,
        d_inner,
        d_outer,
        d_gain.T,
        d_shift.T,
    )


def solution(mesh):
    in_specs = (
        P("fsdp", "ctx", None),
        P("fsdp", None),
        P("fsdp", None),
        P("fsdp", None),
        P("fsdp", None),
        P("fsdp", None),
        P("fsdp", None),
        P("fsdp", None),
        P("fsdp", None),
        P("fsdp", None),
        P("fsdp", None),
        P("fsdp", "ctx", None),
    )
    out_specs = (
        P("fsdp", "ctx", None),
        P("fsdp", "ctx", None),
        P("fsdp", None),
        P("fsdp", None),
        P("fsdp", None),
        P("fsdp", None),
        P("fsdp", None),
        P("fsdp", None),
        P("fsdp", None),
        P("fsdp", None),
    )
    fast = mesh.shape["ctx"] == 8 and mesh.shape["fsdp"] == 4
    chosen = fast_body if fast else generic_body
    return jax.shard_map(chosen, mesh=mesh, in_specs=in_specs, out_specs=out_specs, check_vma=False)
```
